32 devices in a mesh: dp: 4 (over y, x), ctx: 2 (over core), expert: 4 (over z).
Axes of the slice: x: 2, y: 2, z: 4, core: 2. Of those that a mesh axis runs over, the one named last changes fastest.
Arguments:
- tokens: bfloat16 [96, 200, 512], P(('dp', 'expert'), 'ctx'), may hold values from -6 to 6
- gain_one: float32 [512], replicated, may hold values from 0.1 to 1.9
- w_qkv: bfloat16 [512, 1536], replicated, may hold values from -0.25 to 0.25
- w_out: bfloat16 [512, 512], replicated, may hold values from -1 to 1
- gain_two: float32 [512], replicated, may hold values from 0.1 to 1.9
- w_router: bfloat16 [512, 4], replicated, may hold values from -0.1875 to 0.1875
- w_in: bfloat16 [4, 512, 2048], P('expert'), may hold values from -0.25 to 0.25
- w_back: bfloat16 [4, 2048, 512], P('expert'), may hold values from -0.25 to 0.25
- route_ids: int32 [16, 2, 6, 100, 2], P(('dp', 'expert'), 'ctx'), may hold values from 0 to 3, all different within a row; in each aligned block of 600 rows (0 to 599, 600 to 1199, ..., all dimensions but the last counted through in order) at most 600 rows name the same one
- key_mask: int32 [96, 200], P(('dp', 'expert')), may hold values from 0 to 1, as said below
- cotangent: bfloat16 [96, 200, 512], P(('dp', 'expert'), 'ctx'), may hold values from -6 to 6
Outputs:
- mixed: bfloat16 [96, 200, 512], P(('dp', 'expert'), 'ctx')
- grad_tokens: bfloat16 [96, 200, 512], P(('dp', 'expert'), 'ctx')
- grad_gain_one: float32 [512], replicated
- grad_qkv: float32 [512, 1536], replicated
- grad_out: float32 [512, 512], replicated
- grad_gain_two: float32 [512], replicated
- grad_router: float32 [512, 4], replicated
- grad_in: float32 [4, 512, 2048], P('expert')
- grad_back: float32 [4, 2048, 512], P('expert')
The draws below stay inside these ranges and needn't reach their ends.
Inputs may be any that keep to these rules, and one draw needn't show every extreme that they name: Among the 600 tokens of one device (one aligned block of route_ids), at most 600 routes name the same expert, ; a token's two experts differ. `key_mask`: each image's mask is 1 on a first run of positions of length 150 to 200, then 0.
All inputs are finite; a program needn't handle non-finite values.
Results may differ from the reference program's by a relative error of at most 0.017.
Values may be sent and summed in bfloat16 or wider, within the bound.
No kernel may reach another device: no remote copies, remote signals or barrier semaphores. Data moves between devices by JAX's collectives and lax.ppermute only.
A program may use at most 192 MiB of HBM per device.

```python
import math
import jax
import jax.numpy as jnp
import numpy as np
from jax import lax

D = 512
HEADS = 8
HEAD_DIM = 64
FF = 2048
TOP = 2
SEQ = 200
IMG_DEV = 6
EXPERTS = 4
GROUPS = 16
IMAGES = 96
HALF = 100
TOK_DEV = 600
CAP = 600
N_CTX = 2


def draw_key_mask(key, part):
    lengths = jax.random.randint(key, (IMAGES,), SEQ - SEQ // 4, SEQ + 1)
    lengths = lengths.at[0].set(SEQ - SEQ // 4)
    positions = jnp.arange(SEQ, dtype=jnp.int32)
    return (positions[None, :] < lengths[:, None]).astype(jnp.int32)


def level_of(own_key, shape, split, low, top_value):
    def one(axis_at, blocks):
        draws = jax.random.uniform(jax.random.fold_in(jax.random.fold_in(own_key, 6), axis_at), (blocks,), jnp.float32, low / len(split), top_value / len(split))
        return jnp.repeat(jnp.exp(draws), shape[axis_at] // blocks).reshape((-1,) + (1,) * (len(shape) - axis_at - 1))

    level = one(*split[0])
    for cut in split[1:]:
        level = level * one(*cut)
    return level


def assign_block(own_key, own, number, rows, count, top, limit, slope):
    order = jax.random.permutation(own_key, count)
    packed, ordinary = load_shares(count, rows * top, limit, slope, True), load_shares(count, rows * top, limit, slope, False)
    places = jnp.arange(count)

    def named(sizes, turn):
        used = int((sizes > 0).sum())
        fixed = max(1, used // 4)
        shifted = fixed + (places - fixed + turn * (used - fixed)) % max(1, count - fixed)
        return jnp.zeros((count,), jnp.int32).at[order[jnp.where(places < fixed, places, shifted)]].set(jnp.asarray(sizes, jnp.int32))

    sizes = jnp.where(number % 4 == 0, named(packed, number // 4), named(ordinary, number - number // 4 - 1))
    mixed = jax.random.permutation(jax.random.fold_in(own, 3), count)
    source_of, receiver = mixed[0:count // 2 * 2:2], mixed[1:count // 2 * 2:2]
    slack = jnp.minimum(sizes[source_of] - 1, limit - sizes[receiver]) // 2
    slack = jnp.where((source_of == order[0]) | (receiver == order[0]) | (sizes[receiver] == 0), 0, jnp.maximum(slack, 0))
    shifted = jax.random.randint(jax.random.fold_in(own, 4), (count // 2,), 0, 1 << 20) % (slack + 1)
    sizes = sizes.at[source_of].add(-shifted).at[receiver].add(shifted)
    items = jnp.searchsorted(jnp.cumsum(sizes), jnp.arange(rows * top), side="right").astype(jnp.int32)
    grid = items.reshape(top, rows).T
    grid = grid[jax.random.permutation(jax.random.fold_in(own, 1), rows)]
    turn = jax.random.randint(jax.random.fold_in(own, 2), (rows, 1), 0, top)
    return jnp.take_along_axis(grid, (jnp.arange(top)[None, :] + turn) % top, axis=1)


def load_shares(amount, total, bound, slope, full):
    loads = [(1 << 20) // math.isqrt(standing ** slope) + 1 for standing in range(1, amount + 1)]
    largest = bound if full else min(bound, max(-(-total // amount), total * loads[0] // sum(loads)))
    least = 1 if total - largest >= amount - 1 else 0
    holding, surplus = [largest] + [least] * (amount - 1), total - largest - least * (amount - 1)
    while surplus > 0:
        movable = [i for i in range(1, amount) if holding[i] < largest] or [i for i in range(1, amount) if holding[i] < bound]
        mass, left = sum([loads[i] for i in movable]), surplus
        for i in movable:
            extra = min(bound - holding[i], max(1, left * loads[i] // mass), surplus)
            holding[i] = holding[i] + extra
            surplus = surplus - extra
    return np.array(holding)


def bell_draw(key, shape, scale, most, shards=(), held_as=jnp.bfloat16):
    values = jax.random.normal(key, shape, jnp.float32) * scale
    if len(shards) > 0:
        values = level_of(key, shape, shards, -0.22, 0.18) * values
    return jnp.clip(values, min=-most, max=most).astype(held_as)


def setup_inputs(seed: int = 0) -> dict:
    arg_keys = jax.random.split(jax.random.key(seed), 12)
    tokens = bell_draw(arg_keys[0], (IMAGES, SEQ, D), 1.0, 6.0, ((0, 16), (1, 2)))
    gain_one = jnp.clip(1.0 + 0.18 * jax.random.normal(arg_keys[1], (D,), jnp.float32), 0.1, 1.9)
    w_qkv = bell_draw(arg_keys[2], (D, 3 * D), D ** -0.5, 0.25)
    w_out = bell_draw(arg_keys[3], (D, D), (D // 16) ** -0.5, 1.0)
    gain_two = jnp.clip(1.0 + 0.18 * jax.random.normal(arg_keys[4], (D,), jnp.float32), 0.1, 1.9)
    w_router = bell_draw(arg_keys[5], (D, EXPERTS), (2 * D) ** -0.5, 0.1875)
    w_in = bell_draw(arg_keys[6], (EXPERTS, D, FF), D ** -0.5, 0.25, ((0, 4),))
    w_back = bell_draw(arg_keys[7], (EXPERTS, FF, D), (FF // 4) ** -0.5, 0.25, ((0, 4),))
    route_ids_keys = jax.random.split(jax.random.fold_in(arg_keys[8], 1), GROUPS * N_CTX * IMG_DEV * HALF // TOK_DEV)
    route_ids_turns = jax.random.permutation(jax.random.fold_in(arg_keys[8], 3), GROUPS * N_CTX * IMG_DEV * HALF // TOK_DEV)
    route_ids = jax.vmap(lambda own, number: assign_block(jax.random.fold_in(arg_keys[8], 2), own, number, TOK_DEV, EXPERTS, TOP, CAP, 1))(route_ids_keys, route_ids_turns).reshape((GROUPS, N_CTX, IMG_DEV, HALF, TOP))
    key_mask = draw_key_mask(jax.random.fold_in(arg_keys[11], 71), 0)
    cotangent = bell_draw(arg_keys[10], (IMAGES, SEQ, D), 1.0, 6.0, ((0, 16), (1, 2)))
    return {"tokens": tokens, "gain_one": gain_one, "w_qkv": w_qkv, "w_out": w_out, "gain_two": gain_two, "w_router": w_router, "w_in": w_in, "w_back": w_back, "route_ids": route_ids, "key_mask": key_mask, "cotangent": cotangent}


@jax.custom_vjp
def low(v):
    return lax.optimization_barrier(v.astype(jnp.bfloat16)).astype(jnp.float32)

@jax.custom_vjp
def low_back(v):
    return v

def low_keep(v):
    return (low(v), None)

def low_pass(kept, grad):
    return (grad,)

def back_keep(v):
    return (v, None)

def back_low(kept, grad):
    return (low(grad),)
low.defvjp(low_keep, low_pass)
low_back.defvjp(back_keep, back_low)

def norm_rows(value, gain):
    center = value - lax.optimization_barrier(jnp.mean(value, -1, keepdims=True))
    spread = lax.optimization_barrier(jnp.mean(center * center, -1, keepdims=True))
    return center * lax.rsqrt(spread + 1e-06) * gain

def smooth_gelu(value):
    return 0.5 * value * (1.0 + jnp.tanh(0.7978845608 * (value + 0.044715 * value * value * value)))

def block_forward(block_x, gain_one, w_qkv, w_out, gain_two, w_router, w_in, w_back, block_ids, block_mask):
    high = lax.Precision.HIGHEST
    nimg, seq, width = block_x.shape
    normed = low(norm_rows(block_x, gain_one))
    qkv = jnp.einsum('bsd,de->bse', normed, w_qkv, precision=high)
    query = low_back(low(qkv[..., :width])).reshape(nimg, seq, HEADS, HEAD_DIM)
    keys = low_back(low(qkv[..., width:2 * width])).reshape(nimg, seq, HEADS, HEAD_DIM)
    values = low_back(low(qkv[..., 2 * width:])).reshape(nimg, seq, HEADS, HEAD_DIM)
    scale = HEAD_DIM ** (-0.5)
    scores = low_back(jnp.einsum('bqhc,bkhc->bhqk', query, keys, precision=high) * scale)
    live = block_mask[:, None, None, :] > 0
    masked = jnp.where(live, scores, -1000000000.0)
    topmost = lax.optimization_barrier(jnp.max(masked, -1, keepdims=True))
    expo = jnp.where(live, jnp.exp(masked - topmost), 0.0)
    probs = expo / lax.optimization_barrier(jnp.sum(expo, -1, keepdims=True))
    mix = jnp.einsum('bhqk,bkhc->bqhc', low(probs), values, precision=high).reshape(nimg, seq, width)
    mix = low_back(low(mix))
    branch = low_back(jnp.einsum('bsd,de->bse', mix, w_out, precision=high))
    mid = block_x + branch
    routed = low(norm_rows(mid, gain_two)).reshape(nimg * seq, width)
    logits = jnp.dot(routed, w_router, precision=high)
    flat_ids = block_ids.reshape(nimg * seq, TOP)
    chosen = jnp.take_along_axis(logits, flat_ids, axis=1)
    expo_gate = jnp.exp(chosen)
    gates = expo_gate / lax.optimization_barrier(jnp.sum(expo_gate, -1, keepdims=True))

    def expert_term(total, inputs):
        index, weight_a, weight_b = inputs
        entering = low_back(routed)
        pre = low_back(jnp.dot(entering, weight_a, precision=high))
        act = low(smooth_gelu(pre))
        made = low_back(low(jnp.dot(act, weight_b, precision=high)))
        weight = lax.optimization_barrier(jnp.sum(jnp.where(flat_ids == index, gates, 0.0), -1))
        return (total + weight[:, None] * made, None)
    start = jnp.zeros((nimg * seq, width), jnp.float32)
    total, _ = lax.scan(jax.checkpoint(expert_term), start, (jnp.arange(EXPERTS, dtype=jnp.int32), w_in, w_back))
    return mid + total.reshape(nimg, seq, width)

def reference(tokens, gain_one, w_qkv, w_out, gain_two, w_router, w_in, w_back, route_ids, key_mask, cotangent):
    ids = jnp.transpose(route_ids, (0, 2, 1, 3, 4)).reshape(IMAGES, SEQ, TOP)
    blocks = IMAGES // IMG_DEV
    x_blocks = tokens.astype(jnp.float32).reshape(blocks, IMG_DEV, SEQ, D)
    id_blocks = ids.reshape(blocks, IMG_DEV, SEQ, TOP)
    mask_blocks = key_mask.reshape(blocks, IMG_DEV, SEQ)
    cot_blocks = cotangent.astype(jnp.float32).reshape(blocks, IMG_DEV, SEQ, D)
    params = (gain_one.astype(jnp.float32), w_qkv.astype(jnp.float32), w_out.astype(jnp.float32), gain_two.astype(jnp.float32), w_router.astype(jnp.float32), w_in.astype(jnp.float32), w_back.astype(jnp.float32))

    def one_block(totals, inputs):
        block_x, block_ids, block_mask, block_cot = inputs

        def forward(xv, g1, wq, wo, g2, wr, wa, wb):
            return block_forward(xv, g1, wq, wo, g2, wr, wa, wb, block_ids, block_mask)
        output, pull = jax.vjp(forward, block_x, *params)
        grads = pull(block_cot)
        totals = tuple((a + b for a, b in zip(totals, grads[1:])))
        return (totals, (output.astype(jnp.bfloat16), grads[0].astype(jnp.bfloat16)))
    start = tuple((jnp.zeros_like(p) for p in params))
    totals, (outputs, input_grads) = lax.scan(one_block, start, (x_blocks, id_blocks, mask_blocks, cot_blocks))
    mixed = outputs.reshape(IMAGES, SEQ, D)
    grad_tokens = input_grads.reshape(IMAGES, SEQ, D)
    return (mixed, grad_tokens, totals[0], totals[1], totals[2], totals[3], totals[4], totals[5], totals[6])
```

```python
import functools
import jax
import jax.numpy as jnp
from jax import lax
from jax.experimental import pallas as pl
from jax.experimental.pallas import tpu as pltpu
from jax.sharding import PartitionSpec as P

HEADS = 8
HEAD_DIM = 64
TOP = 2
EPS = 1e-06
SCALE = HEAD_DIM ** (-0.5)
F32 = jnp.float32
BF16 = jnp.bfloat16
NT = (((1,), (1,)), ((), ()))
TN = (((0,), (0,)), ((), ()))
NN = (((1,), (0,)), ((), ()))


def mm(a, b, dims=NN):
    return lax.dot_general(a, b, dims, preferred_element_type=F32)


def two_halves(a):
    high = a.astype(BF16)
    return high, (a - high.astype(F32)).astype(BF16)


def stats(value):
    center = value - jnp.mean(value, -1, keepdims=True)
    rstd = lax.rsqrt(jnp.mean(center * center, -1, keepdims=True) + EPS)
    return center * rstd, rstd


def norm_vjp(d_value, unit, rstd, gain):
    d_unit = d_value * gain
    return rstd * (
        d_unit
        - jnp.mean(d_unit, -1, keepdims=True)
        - unit * jnp.mean(d_unit * unit, -1, keepdims=True)
    )


def head_pair(value):
    lane = lax.broadcasted_iota(jnp.int32, value.shape, 1)
    first = lane < HEAD_DIM
    return jnp.concatenate(
        [jnp.where(first, value, 0.0), jnp.where(first, 0.0, value)], axis=0
    ).astype(BF16)


def join_pair(value):
    rows = value.shape[0] // 2
    lane = lax.broadcasted_iota(jnp.int32, (rows, value.shape[1]), 1)
    return jnp.where(lane < HEAD_DIM, value[:rows], value[rows:])


def attend_kernel(
    own_ref, other_ref, open_ref, g1_ref, wqkv_ref, wout_ref, g2_ref,
    x_ref, normed_ref, qkv_ref, probs_ref, mix_ref, mid_ref, routed_ref,
    x_s, qkv_s, mix_s,
):
    half = own_ref.shape[1]
    width = own_ref.shape[2]
    pair = 2 * HEAD_DIM
    x_s[0:half, :] = own_ref[0].astype(F32)
    x_s[half : 2 * half, :] = other_ref[0].astype(F32)
    x = x_s[...]
    x_ref[...] = x.astype(BF16)
    unit, _ = stats(x)
    normed = (unit * g1_ref[...]).astype(BF16)
    normed_ref[...] = normed
    qkv_s[...] = mm(normed, wqkv_ref[...])
    qkv_ref[...] = qkv_s[...].astype(BF16)
    is_open = open_ref[0] > 0
    for n in range(width // pair):
        at = n * pair
        query = head_pair(qkv_s[:, at : at + pair])
        keys = qkv_s[:, width + at : width + at + pair].astype(BF16)
        vals = qkv_s[:, 2 * width + at : 2 * width + at + pair].astype(BF16)
        scores = jnp.where(is_open, mm(query, keys, NT) * SCALE, -1e9)
        top = jnp.max(scores, -1, keepdims=True)
        expo = jnp.where(is_open, jnp.exp(scores - top), 0.0)
        probs = (expo / jnp.sum(expo, -1, keepdims=True)).astype(BF16)
        probs_ref[0, n] = probs
        mix_s[:, at : at + pair] = join_pair(mm(probs, vals))
    mix = mix_s[...].astype(BF16)
    mix_ref[...] = mix
    mid = x + mm(mix, wout_ref[...])
    mid_ref[...] = mid
    unit, _ = stats(mid)
    routed_ref[...] = (unit * g2_ref[...]).astype(BF16)


def attend(own, other, is_open, g1, wqkv, wout, g2):
    imgs, half, width = own.shape
    seq = 2 * half
    rows = imgs * seq
    pairs = HEADS // 2
    one = lambda *s: pl.BlockSpec(s, lambda i: (i,) + (0,) * (len(s) - 1))
    fix = lambda *s: pl.BlockSpec(s, lambda i: (0,) * len(s))
    return pl.pallas_call(
        attend_kernel,
        grid=(imgs,),
        in_specs=[
            one(1, half, width), one(1, half, width), one(1, 1, seq), fix(1, width),
            fix(width, 3 * width), fix(width, width), fix(1, width),
        ],
        out_specs=[
            one(seq, width), one(seq, width), one(seq, 3 * width), one(1, pairs, 2 * seq, seq),
            one(seq, width), one(seq, width), one(seq, width),
        ],
        out_shape=[
            jax.ShapeDtypeStruct((rows, width), BF16),
            jax.ShapeDtypeStruct((rows, width), BF16),
            jax.ShapeDtypeStruct((rows, 3 * width), BF16),
            jax.ShapeDtypeStruct((imgs, pairs, 2 * seq, seq), BF16),
            jax.ShapeDtypeStruct((rows, width), BF16),
            jax.ShapeDtypeStruct((rows, width), F32),
            jax.ShapeDtypeStruct((rows, width), BF16),
        ],
        scratch_shapes=[
            pltpu.VMEM((seq, width), F32),
            pltpu.VMEM((seq, 3 * width), F32),
            pltpu.VMEM((seq, width), F32),
        ],
        compiler_params=pltpu.CompilerParams(vmem_limit_bytes=48 << 20),
        name="attend",
    )(own, other, is_open, g1, wqkv, wout, g2)


def expert_kernel(
    me_ref, rows_ref, dy_ref, ids_ref, wr_ref, win_ref, wback_ref,
    act_ref, dpre_ref, dout_ref, made_ref, din_ref, gg_ref,
    gate_s, made_s, din_s,
):
    step = pl.program_id(0)
    rows = rows_ref[...]

    @pl.when(step == 0)
    def _():
        logits = mm(rows, wr_ref[...])
        lane = lax.broadcasted_iota(jnp.int32, logits.shape, 1)
        pick = (lane == ids_ref[:, 0:1]) | (lane == ids_ref[:, 1:2])
        top = jnp.max(jnp.where(pick, logits, -jnp.inf), -1, keepdims=True)
        expo = jnp.where(pick, jnp.exp(logits - top), 0.0)
        gates = expo / jnp.sum(expo, -1, keepdims=True)
        gate = jnp.sum(jnp.where(lane == me_ref[0], gates, 0.0), -1, keepdims=True)
        gate_s[...] = jnp.broadcast_to(gate, gate_s.shape)
        dout_ref[...] = (gate * dy_ref[...].astype(F32)).astype(BF16)
        made_s[...] = jnp.zeros_like(made_s)
        din_s[...] = jnp.zeros_like(din_s)

    w_in = win_ref[0]
    w_back = wback_ref[0]
    pre = mm(rows, w_in)
    square = pre * pre
    inner = 0.7978845608 * (pre + 0.044715 * square * pre)
    th = jnp.tanh(inner)
    up = 0.5 * (1.0 + th)
    act = (pre * up).astype(BF16)
    slope = up + 0.5 * pre * (1.0 - th * th) * (0.7978845608 * (1.0 + 0.134145 * square))
    act_ref[...] = act
    made_s[...] += mm(act, w_back)
    dpre = (mm(dout_ref[...], w_back, NT) * slope).astype(BF16)
    dpre_ref[...] = dpre
    din_s[...] += mm(dpre, w_in, NT)

    @pl.when(step == pl.num_programs(0) - 1)
    def _():
        gate = gate_s[:, 0:1]
        made = made_s[...].astype(BF16).astype(F32)
        made_ref[...] = (gate * made).astype(BF16)
        din_ref[...] = din_s[...].astype(BF16)
        high, low = two_halves(made * dy_ref[...].astype(F32))
        ones = jnp.ones((16, made.shape[1]), BF16)
        gg_ref[...] = (mm(ones, high, NT) + mm(ones, low, NT))[0:8]


def expert(me, rows, dy, ids, wr, w_in, w_back):
    count, width = rows.shape
    hidden = w_in.shape[2]
    steps = 4
    part = hidden // steps
    fix = lambda *s: pl.BlockSpec(s, lambda j, m: (0,) * len(s))
    return pl.pallas_call(
        expert_kernel,
        grid_spec=pltpu.PrefetchScalarGridSpec(
            num_scalar_prefetch=1,
            grid=(steps,),
            in_specs=[
                fix(count, width), fix(count, width), fix(count, 2), fix(width, wr.shape[1]),
                pl.BlockSpec((1, width, part), lambda j, m: (0, 0, j)),
                pl.BlockSpec((1, part, width), lambda j, m: (0, j, 0)),
            ],
            out_specs=[
                pl.BlockSpec((count, part), lambda j, m: (0, j)),
                pl.BlockSpec((count, part), lambda j, m: (0, j)),
                fix(count, width), fix(count, width), fix(count, width), fix(8, count),
            ],
            scratch_shapes=[
                pltpu.VMEM((count, 128), F32),
                pltpu.VMEM((count, width), F32),
                pltpu.VMEM((count, width), F32),
            ],
        ),
        out_shape=[
            jax.ShapeDtypeStruct((count, hidden), BF16),
            jax.ShapeDtypeStruct((count, hidden), BF16),
            jax.ShapeDtypeStruct((count, width), BF16),
            jax.ShapeDtypeStruct((count, width), BF16),
            jax.ShapeDtypeStruct((count, width), BF16),
            jax.ShapeDtypeStruct((8, count), F32),
        ],
        compiler_params=pltpu.CompilerParams(vmem_limit_bytes=48 << 20),
        name="expert",
    )(me, rows, dy, ids, wr, w_in, w_back)


def weight_kernel(*refs):
    n = (len(refs) - 2) // 4
    rows, acts, dpres, douts = refs[:n], refs[n : 2 * n], refs[2 * n : 3 * n], refs[3 * n : 4 * n]
    gin_ref, gback_ref = refs[4 * n :]
    total = mm(rows[0][...], dpres[0][...], TN)
    for b in range(1, n):
        total += mm(rows[b][...], dpres[b][...], TN)
    gin_ref[0] = total.astype(BF16)
    total = mm(acts[0][...], douts[0][...], TN)
    for b in range(1, n):
        total += mm(acts[b][...], douts[b][...], TN)
    gback_ref[0] = total.astype(BF16)


def weight_grads(rows, acts, dpres, douts):
    count, width = rows[0].shape
    hidden = acts[0].shape[1]
    n = len(rows)
    steps = 8
    part = hidden // steps
    fix = pl.BlockSpec((count, width), lambda j: (0, 0))
    cut = pl.BlockSpec((count, part), lambda j: (0, j))
    return pl.pallas_call(
        weight_kernel,
        grid=(steps,),
        in_specs=[fix] * n + [cut] * (2 * n) + [fix] * n,
        out_specs=[
            pl.BlockSpec((1, width, part), lambda j: (0, 0, j)),
            pl.BlockSpec((1, part, width), lambda j: (0, j, 0)),
        ],
        out_shape=[
            jax.ShapeDtypeStruct((1, width, hidden), BF16),
            jax.ShapeDtypeStruct((1, hidden, width), BF16),
        ],
        compiler_params=pltpu.CompilerParams(vmem_limit_bytes=48 << 20),
        name="weight_grads",
    )(*rows, *acts, *dpres, *douts)


def back_kernel(
    me_ref, din0_ref, din1_ref, din2_ref, din3_ref, gg0_ref, gg1_ref, gg2_ref, gg3_ref,
    ids_ref, dy_ref, mid_ref, routed_ref, wr_ref, g2_ref, mix_ref, wout_ref,
    probs_ref, qkv_ref, x_ref, normed_ref, wqkv_ref, g1_ref,
    own_ref, other_ref, grad_ref, small_ref,
    dmid_s, dmix_s, dqkv_s, tok_s,
):
    step = pl.program_id(0)
    imgs = pl.num_programs(0)
    seq = qkv_ref.shape[0]
    width = x_ref.shape[1]
    half = seq // 2
    pair = 2 * HEAD_DIM

    @pl.when(step == 0)
    def _():
        routed = routed_ref[...]
        logits = mm(wr_ref[...], routed, NT)
        row = lax.broadcasted_iota(jnp.int32, logits.shape, 0)
        pick = (row == ids_ref[0:1, :]) | (row == ids_ref[1:2, :])
        top = jnp.max(jnp.where(pick, logits, -jnp.inf), 0, keepdims=True)
        expo = jnp.where(pick, jnp.exp(logits - top), 0.0)
        gates = expo / jnp.sum(expo, 0, keepdims=True)
        me = me_ref[0]
        d_gate = jnp.zeros_like(gates)
        for k, ref in enumerate((gg0_ref, gg1_ref, gg2_ref, gg3_ref)):
            there = me + k - 2 * (me & k)
            part = jnp.concatenate([ref[...]] * (gates.shape[0] // 8), axis=0)
            d_gate += jnp.where(row == there, part, 0.0)
        d_logits = gates * (d_gate - jnp.sum(gates * d_gate, 0, keepdims=True))
        high, low = two_halves(d_logits)
        wr = wr_ref[...]
        small_ref[0:16, :] = mm(high, routed) + mm(low, routed)
        d_routed = (
            din0_ref[...].astype(F32) + din1_ref[...].astype(F32)
            + din2_ref[...].astype(F32) + din3_ref[...].astype(F32)
            + mm(high, wr, TN) + mm(low, wr, TN)
        )
        unit, rstd = stats(mid_ref[...])
        small_ref[16:17, :] = jnp.sum(d_routed * unit, 0, keepdims=True)
        d_mid = dy_ref[...].astype(F32) + norm_vjp(d_routed, unit, rstd, g2_ref[...])
        dmid_s[...] = d_mid
        d_branch = d_mid.astype(BF16)
        grad_ref[:, 3 * width :] = mm(mix_ref[...], d_branch, TN).astype(BF16)
        dmix_s[...] = mm(d_branch, wout_ref[...], NT)

    base = pl.multiple_of(step * seq, 8)
    for n in range(width // pair):
        at = n * pair
        d_mix = head_pair(dmix_s[pl.ds(base, seq), at : at + pair])
        query = head_pair(qkv_ref[:, at : at + pair].astype(F32))
        keys = qkv_ref[:, width + at : width + at + pair]
        vals = qkv_ref[:, 2 * width + at : 2 * width + at + pair]
        low = probs_ref[0, n]
        probs = low.astype(F32)
        d_probs = mm(d_mix, vals, NT)
        d_scores = probs * (d_probs - jnp.sum(probs * d_probs, -1, keepdims=True))
        d_scores = d_scores.astype(BF16)
        d_query = join_pair(mm(d_scores, keys)) * SCALE
        d_keys = mm(d_scores, query, TN) * SCALE
        d_vals = mm(low, d_mix, TN)
        dqkv_s[pl.ds(base, seq), at : at + pair] = d_query.astype(BF16)
        dqkv_s[pl.ds(base, seq), width + at : width + at + pair] = d_keys.astype(BF16)
        dqkv_s[pl.ds(base, seq), 2 * width + at : 2 * width + at + pair] = d_vals.astype(BF16)

    @pl.when(step == imgs - 1)
    def _():
        d_qkv = dqkv_s[...]
        grad_ref[:, : 3 * width] = mm(normed_ref[...], d_qkv, TN).astype(BF16)
        d_normed = mm(d_qkv, wqkv_ref[...], NT)
        unit, rstd = stats(x_ref[...].astype(F32))
        small_ref[17:18, :] = jnp.sum(d_normed * unit, 0, keepdims=True)
        small_ref[18:24, :] = jnp.zeros((6, width), F32)
        tok_s[...] = dmid_s[...] + norm_vjp(d_normed, unit, rstd, g1_ref[...])
        for i in range(own_ref.shape[0]):
            own_ref[i] = tok_s[i * seq : i * seq + half, :].astype(BF16)
            other_ref[i] = tok_s[i * seq + half : (i + 1) * seq, :].astype(BF16)


def attend_back(me, dins, ggs, ids, dy, mid, routed, wr, g2, mix, wout, probs, qkv, x, normed, wqkv, g1):
    imgs = probs.shape[0]
    rows, width = x.shape
    seq = rows // imgs
    pairs = HEADS // 2
    fix = lambda *s: pl.BlockSpec(s, lambda i, m: (0,) * len(s))
    return pl.pallas_call(
        back_kernel,
        grid_spec=pltpu.PrefetchScalarGridSpec(
            num_scalar_prefetch=1,
            grid=(imgs,),
            in_specs=[fix(rows, width)] * 4 + [fix(8, rows)] * 4 + [
                fix(2, rows), fix(rows, width), fix(rows, width), fix(rows, width),
                fix(16, width), fix(1, width), fix(rows, width), fix(width, width),
                pl.BlockSpec((1, pairs, 2 * seq, seq), lambda i, m: (i, 0, 0, 0)),
                pl.BlockSpec((seq, 3 * width), lambda i, m: (i, 0)),
                fix(rows, width), fix(rows, width), fix(width, 3 * width), fix(1, width),
            ],
            out_specs=[
                fix(imgs, seq // 2, width), fix(imgs, seq // 2, width),
                fix(width, 4 * width), fix(24, width),
            ],
            scratch_shapes=[
                pltpu.VMEM((rows, width), F32),
                pltpu.VMEM((rows, width), F32),
                pltpu.VMEM((rows, 3 * width), BF16),
                pltpu.VMEM((rows, width), F32),
            ],
        ),
        out_shape=[
            jax.ShapeDtypeStruct((imgs, seq // 2, width), BF16),
            jax.ShapeDtypeStruct((imgs, seq // 2, width), BF16),
            jax.ShapeDtypeStruct((width, 4 * width), BF16),
            jax.ShapeDtypeStruct((24, width), F32),
        ],
        compiler_params=pltpu.CompilerParams(vmem_limit_bytes=56 << 20),
        name="attend_back",
    )(me, *dins, *ggs, ids, dy, mid, routed, wr, g2, mix, wout, probs, qkv, x, normed, wqkv, g1)


def combine_kernel(mid_ref, a_ref, b_ref, c_ref, d_ref, own_ref, other_ref, s_ref):
    half = own_ref.shape[1]
    s_ref[...] = mid_ref[...] + (
        a_ref[...].astype(F32) + b_ref[...].astype(F32)
        + c_ref[...].astype(F32) + d_ref[...].astype(F32)
    )
    own_ref[0] = s_ref[0:half, :].astype(BF16)
    other_ref[0] = s_ref[half : 2 * half, :].astype(BF16)


def combine(mid, parts, imgs):
    rows, width = mid.shape
    seq = rows // imgs
    spec = pl.BlockSpec((seq, width), lambda i: (i, 0))
    out = pl.BlockSpec((1, seq // 2, width), lambda i: (i, 0, 0))
    shape = jax.ShapeDtypeStruct((imgs, seq // 2, width), BF16)
    return pl.pallas_call(
        combine_kernel,
        grid=(imgs,),
        in_specs=[spec] * 5,
        out_specs=[out, out],
        out_shape=[shape, shape],
        scratch_shapes=[pltpu.VMEM((seq, width), F32)],
        name="combine",
    )(mid, *parts)


SWAP = [(0, 1), (1, 0)]


def xor(k, n=4):
    return [(i, i ^ k) for i in range(n)]


def keep_give(value, index):
    parts = value.shape[0] // 2
    return (
        lax.dynamic_slice_in_dim(value, index * parts, parts, 0),
        lax.dynamic_slice_in_dim(value, (1 - index) * parts, parts, 0),
    )


def order_two(mine, theirs, index, axis=0):
    return jnp.where(
        index == 0,
        jnp.concatenate([mine, theirs], axis),
        jnp.concatenate([theirs, mine], axis),
    )


def send(value, axis, pairs):
    return lax.ppermute(value, axis, pairs)


def halve(value, index, axis, pairs):
    mine, theirs = keep_give(value, index)
    return mine + send(theirs.astype(BF16), axis, pairs).astype(F32)


def reduce_shared(grads, small, core, y, x, z):
    total = halve(grads.astype(F32), core, "ctx", SWAP)
    cols = total.shape[1] // 2
    a, b = total[:, :cols], total[:, cols:]
    a = halve(a, x, "dp", xor(1))
    b = halve(b, y, "dp", xor(2))
    a = halve(a, y, "dp", xor(2))
    b = halve(b, x, "dp", xor(1))
    both = jnp.concatenate([a, b], 0)
    rows = both.shape[0] // 4
    piece = lambda k: lax.dynamic_slice_in_dim(both, (z ^ k) * rows, rows, 0)
    mine = piece(0)
    for k in (1, 2, 3):
        mine = mine + send(piece(k).astype(BF16), "expert", xor(k)).astype(F32)
    mine = mine.astype(BF16)
    slots = jnp.stack([mine] + [send(mine, "expert", xor(k)) for k in (1, 2, 3)])
    both = jnp.concatenate(
        [lax.dynamic_slice_in_dim(slots, z ^ k, 1, 0)[0] for k in range(4)], 0
    )
    a, b = both[: 2 * rows], both[2 * rows :]
    a = order_two(a, send(a, "dp", xor(2)), y)
    b = order_two(b, send(b, "dp", xor(1)), x)
    a = order_two(a, send(a, "dp", xor(1)), x)
    b = order_two(b, send(b, "dp", xor(2)), y)
    total = jnp.concatenate([a, b], 1)
    total = order_two(total, send(total, "ctx", SWAP), core)
    small = small + send(small, "ctx", SWAP)
    small = small + send(small, "dp", xor(1))
    small = small + send(small, "dp", xor(2))
    small = small + send(small, "expert", xor(1))
    small = small + send(small, "expert", xor(2))
    return total.astype(F32), small


def dense_shards(
    tokens, gain_one, w_qkv, w_out, gain_two, w_router, w_in, w_back, route_ids, key_mask, cotangent
):
    nimg, half, width = tokens.shape
    imgs = nimg // 2
    rows = imgs * 2 * half
    experts = w_router.shape[1]
    core = lax.axis_index("ctx")
    z = lax.axis_index("expert")
    place = lax.axis_index("dp")
    y, x = place // 2, place % 2

    dy_own, dy_give = keep_give(cotangent, core)
    tok_own, tok_give = keep_give(tokens, core)
    ids = route_ids.reshape(nimg, half, TOP)
    ids_own, ids_give = keep_give(ids, core)
    dy_other = send(dy_give, "ctx", SWAP)
    tok_other = send(tok_give, "ctx", SWAP)
    ids_flat = lambda v: jnp.transpose(v, (2, 0, 1))
    ids_other = send(ids_flat(ids_give), "ctx", SWAP)
    dy = jnp.concatenate([dy_own, dy_other], 1).reshape(rows, width)
    ids_row = jnp.concatenate([ids_flat(ids_own), ids_other], 2).reshape(TOP, rows)
    ids_all = lax.all_gather(ids_row, "expert", axis=0)
    ids_col = jnp.transpose(ids_all, (0, 2, 1))

    def spread(value):
        first = send(value, "expert", xor(1))
        second = send(value, "expert", [(1, 2), (2, 1)])
        inner = send(first, "expert", [(1, 2), (2, 1)])
        outer = send(second, "expert", [(1, 0), (2, 3)])
        far = send(first, "expert", [(2, 0), (1, 3)])
        middle = (z == 1) | (z == 2)
        return [
            value,
            first,
            jnp.where(middle, inner, outer),
            jnp.where(middle, second, far),
        ]

    dys = spread(dy)
    mask = lax.dynamic_slice_in_dim(key_mask, core * imgs, imgs, 0)
    is_open = order_two(mask[:, :half], mask[:, half:], core, 1)[:, None, :]
    g1, g2 = gain_one[None, :], gain_two[None, :]
    x_rows, normed, qkv, probs, mix, mid, routed = attend(
        tok_own, tok_other, is_open, g1, w_qkv, w_out, g2
    )
    routeds = spread(routed)
    me = z[None].astype(jnp.int32)
    wr = jnp.pad(w_router, ((0, 0), (0, 128 - experts)))
    wr_row = jnp.pad(w_router.T, ((0, 16 - experts), (0, 0)))
    parts = []
    for k in range(4):
        ids_k = lax.dynamic_slice_in_dim(ids_col, z ^ k, 1, 0)[0]
        parts.append(expert(me, routeds[k], dys[k], ids_k, wr, w_in, w_back))
    acts, dpres, douts, mades, dins, ggs = zip(*parts)
    back = lambda group: [group[0]] + [send(group[k], "expert", xor(k)) for k in (1, 2, 3)]
    dins, ggs = back(dins), back(ggs)
    grad_in, grad_back = weight_grads(routeds, acts, dpres, douts)
    mades = back(mades)
    tok_own, tok_give, shared, small = attend_back(
        me, dins, ggs, ids_row, dy, mid, routed, wr_row, g2, mix, w_out, probs, qkv, x_rows, normed, w_qkv, g1
    )
    mix_own, mix_give = combine(mid, mades, imgs)
    mixed = order_two(mix_own, send(mix_give, "ctx", SWAP), core)
    grad_tokens = order_two(tok_own, send(tok_give, "ctx", SWAP), core)
    shared, small = reduce_shared(shared, small, core, y, x, z)
    grad_in, grad_back = lax.psum((grad_in, grad_back), ("dp", "ctx"))
    return (
        mixed,
        grad_tokens,
        small[17],
        shared[:, : 3 * width],
        shared[:, 3 * width :],
        small[16],
        small[:experts].T,
        grad_in.astype(F32),
        grad_back.astype(F32),
    )


def norm_rows(value, gain):
    center = value - jnp.mean(value, -1, keepdims=True)
    spread = jnp.mean(center * center, -1, keepdims=True)
    return center * lax.rsqrt(spread + 1e-06) * gain


def smooth_gelu(value):
    return 0.5 * value * (1.0 + jnp.tanh(0.7978845608 * (value + 0.044715 * value * value * value)))


def forward(tokens, gain_one, w_qkv, w_out, gain_two, w_router, w_in, w_back, flat_ids, live):
    nimg, half, width = tokens.shape
    count = nimg * half
    experts_all = w_router.shape[1]
    capacity = max(2, 2 * TOP * count // experts_all)
    x_rows = tokens.astype(jnp.float32).reshape(count, width)
    normed = norm_rows(x_rows, gain_one).astype(jnp.bfloat16)
    qkv = jnp.dot(normed, w_qkv, preferred_element_type=jnp.float32).astype(jnp.bfloat16)
    qkv = qkv.reshape(nimg, half, 3 * width)
    query = qkv[..., :width]
    keys_local = qkv[..., width : 2 * width]
    vals_local = qkv[..., 2 * width :]
    keys, vals = (
        lax.all_gather(keys_local, "ctx", axis=1, tiled=True),
        lax.all_gather(vals_local, "ctx", axis=1, tiled=True),
    )
    seq = keys.shape[1]
    query4 = query.reshape(nimg, half, HEADS, HEAD_DIM)
    keys4 = keys.reshape(nimg, seq, HEADS, HEAD_DIM)
    vals4 = vals.reshape(nimg, seq, HEADS, HEAD_DIM)
    scale = HEAD_DIM ** (-0.5)
    scores = (
        jnp.einsum("iqhc,ikhc->ihqk", query4, keys4, preferred_element_type=jnp.float32) * scale
    )
    open_keys = live[:, None, None, :]
    masked = jnp.where(open_keys, scores, -1000000000.0)
    topmost = jnp.max(masked, -1, keepdims=True)
    expo = jnp.where(open_keys, jnp.exp(masked - topmost), 0.0)
    probs = expo / jnp.sum(expo, -1, keepdims=True)
    probs_low = probs.astype(jnp.bfloat16)
    mix = jnp.einsum("ihqk,ikhc->iqhc", probs_low, vals4, preferred_element_type=jnp.float32)
    mix = mix.reshape(count, width).astype(jnp.bfloat16)
    mid = x_rows + jnp.dot(mix, w_out, preferred_element_type=jnp.float32)
    routed = norm_rows(mid, gain_two).astype(jnp.bfloat16)
    logits = jnp.dot(routed, w_router, preferred_element_type=jnp.float32)
    pick = flat_ids[:, :, None] == jnp.arange(experts_all, dtype=jnp.int32)[None, None, :]
    chosen = jnp.sum(jnp.where(pick, logits[:, None, :], 0.0), -1)
    expo_gate = jnp.exp(chosen)
    gates = expo_gate / jnp.sum(expo_gate, -1, keepdims=True)
    pair_ids = flat_ids.reshape(-1)
    hits = (pair_ids[:, None] == jnp.arange(experts_all, dtype=jnp.int32)[None, :]).astype(
        jnp.int32
    )
    before = jnp.cumsum(hits, 0) - hits
    slots = jnp.sum(before * hits, 1)
    where_rows = pair_ids * capacity + slots
    sent = jnp.repeat(routed, TOP, axis=0)
    buffer = jnp.zeros((experts_all * capacity, width), jnp.bfloat16).at[where_rows].set(sent)
    buffer = buffer.reshape(experts_all, capacity, width)
    arrived = lax.all_to_all(buffer, "expert", split_axis=0, concat_axis=1, tiled=True)
    pre = jnp.einsum("erd,edf->erf", arrived, w_in, preferred_element_type=jnp.float32)
    act = smooth_gelu(pre).astype(jnp.bfloat16)
    made = jnp.einsum("erf,efd->erd", act, w_back, preferred_element_type=jnp.float32).astype(
        jnp.bfloat16
    )
    returned = lax.all_to_all(made, "expert", split_axis=1, concat_axis=0, tiled=True)
    picked = returned.reshape(experts_all * capacity, width)[where_rows].reshape(count, TOP, width)
    output = mid + jnp.sum(gates[:, :, None] * picked.astype(jnp.float32), 1)
    return (
        x_rows,
        normed,
        query4,
        keys4,
        vals4,
        probs,
        probs_low,
        mix,
        mid,
        routed,
        pick,
        gates,
        where_rows,
        arrived,
        pre,
        act,
        picked,
        output,
        capacity,
    )


def shards(
    tokens, gain_one, w_qkv, w_out, gain_two, w_router, w_in, w_back, route_ids, key_mask, cotangent
):
    nimg, half, width = tokens.shape
    count = nimg * half
    experts_all = w_router.shape[1]
    flat_ids = route_ids.reshape(count, TOP)
    live = key_mask > 0
    state = forward(
        tokens, gain_one, w_qkv, w_out, gain_two, w_router, w_in, w_back, flat_ids, live
    )
    mixed = state[17].reshape(nimg, half, width).astype(jnp.bfloat16)
    state = forward(
        tokens, gain_one, w_qkv, w_out, gain_two, w_router, w_in, w_back, flat_ids, live
    )
    (
        x_rows,
        normed,
        query4,
        keys4,
        vals4,
        probs,
        probs_low,
        mix,
        mid,
        routed,
        pick,
        gates,
        where_rows,
        arrived,
        pre,
        act,
        picked,
        output,
        capacity,
    ) = state
    scale = HEAD_DIM ** (-0.5)
    high = lax.Precision.HIGHEST
    grad_y = cotangent.astype(jnp.float32).reshape(count, width)
    grad_gate = jnp.sum(grad_y[:, None, :] * picked.astype(jnp.float32), -1)
    d_out = (
        (gates[:, :, None] * grad_y[:, None, :]).astype(jnp.bfloat16).reshape(count * TOP, width)
    )
    grad_buffer = jnp.zeros((experts_all * capacity, width), jnp.bfloat16).at[where_rows].set(d_out)
    grad_buffer = grad_buffer.reshape(experts_all, capacity, width)
    grad_arrived = lax.all_to_all(grad_buffer, "expert", split_axis=0, concat_axis=1, tiled=True)
    d_act = jnp.einsum("erd,efd->erf", grad_arrived, w_back, preferred_element_type=jnp.float32)
    grad_back = jnp.einsum("erf,erd->efd", act, grad_arrived, preferred_element_type=jnp.float32)
    _, gelu_pull = jax.vjp(smooth_gelu, pre)
    d_pre = gelu_pull(d_act)[0].astype(jnp.bfloat16)
    grad_in = jnp.einsum("erd,erf->edf", arrived, d_pre, preferred_element_type=jnp.float32)
    d_in = jnp.einsum("erf,edf->erd", d_pre, w_in, preferred_element_type=jnp.float32).astype(
        jnp.bfloat16
    )
    grad_returned = lax.all_to_all(d_in, "expert", split_axis=1, concat_axis=0, tiled=True)
    grad_rows = grad_returned.reshape(experts_all * capacity, width)[where_rows].reshape(
        count, TOP, width
    )
    d_experts = jnp.sum(grad_rows.astype(jnp.float32), 1)
    d_chosen = gates * (grad_gate - jnp.sum(gates * grad_gate, -1, keepdims=True))
    d_logits = jnp.sum(jnp.where(pick, d_chosen[:, :, None], 0.0), 1)
    grad_router = jnp.dot(routed.astype(jnp.float32).T, d_logits, precision=high)
    d_routed = d_experts + jnp.dot(d_logits, w_router.astype(jnp.float32).T, precision=high)
    _, norm_two_pull = jax.vjp(norm_rows, mid, gain_two)
    d_mid_norm, grad_gain_two = norm_two_pull(d_routed)
    d_mid = grad_y + d_mid_norm
    d_branch = d_mid.astype(jnp.bfloat16)
    grad_out = jnp.einsum("td,te->de", mix, d_branch, preferred_element_type=jnp.float32)
    d_mix = jnp.dot(d_branch, w_out.T, preferred_element_type=jnp.float32).astype(jnp.bfloat16)
    d_mix4 = d_mix.reshape(nimg, half, HEADS, HEAD_DIM)
    d_probs = jnp.einsum("iqhc,ikhc->ihqk", d_mix4, vals4, preferred_element_type=jnp.float32)
    d_scores = (probs * (d_probs - jnp.sum(probs * d_probs, -1, keepdims=True))).astype(
        jnp.bfloat16
    )
    d_query = (
        jnp.einsum("ihqk,ikhc->iqhc", d_scores, keys4, preferred_element_type=jnp.float32) * scale
    )
    d_keys = (
        jnp.einsum("ihqk,iqhc->ikhc", d_scores, query4, preferred_element_type=jnp.float32) * scale
    )
    d_vals = jnp.einsum("ihqk,iqhc->ikhc", probs_low, d_mix4, preferred_element_type=jnp.float32)
    seq = keys4.shape[1]
    d_keys_own, d_vals_own = (
        lax.psum_scatter(
            d_keys.reshape(nimg, seq, width).astype(jnp.bfloat16),
            "ctx",
            scatter_dimension=1,
            tiled=True,
        ).astype(jnp.float32),
        lax.psum_scatter(
            d_vals.reshape(nimg, seq, width).astype(jnp.bfloat16),
            "ctx",
            scatter_dimension=1,
            tiled=True,
        ).astype(jnp.float32),
    )
    d_qkv = jnp.concatenate(
        [
            d_query.reshape(count, width).astype(jnp.bfloat16),
            d_keys_own.reshape(count, width).astype(jnp.bfloat16),
            d_vals_own.reshape(count, width).astype(jnp.bfloat16),
        ],
        axis=1,
    )
    grad_qkv = jnp.einsum("td,te->de", normed, d_qkv, preferred_element_type=jnp.float32)
    d_normed = jnp.dot(d_qkv, w_qkv.T, preferred_element_type=jnp.float32)
    _, norm_one_pull = jax.vjp(norm_rows, x_rows, gain_one)
    d_x_norm, grad_gain_one = norm_one_pull(d_normed)
    grad_tokens = (d_mid + d_x_norm).reshape(nimg, half, width).astype(jnp.bfloat16)
    grad_gain_one, grad_qkv, grad_out, grad_gain_two, grad_router = lax.psum(
        (grad_gain_one, grad_qkv, grad_out, grad_gain_two, grad_router), ("dp", "ctx", "expert")
    )
    grad_in, grad_back = (
        lax.psum(grad_in.astype(jnp.bfloat16), ("dp", "ctx")).astype(jnp.float32),
        lax.psum(grad_back.astype(jnp.bfloat16), ("dp", "ctx")).astype(jnp.float32),
    )
    return (
        mixed,
        grad_tokens,
        grad_gain_one,
        grad_qkv,
        grad_out,
        grad_gain_two,
        grad_router,
        grad_in,
        grad_back,
    )


def solution(mesh):
    placed = (
        P(("dp", "expert"), "ctx", None),
        P(),
        P(),
        P(),
        P(),
        P(),
        P("expert", None, None),
        P("expert", None, None),
        P(("dp", "expert"), "ctx", None, None, None),
        P(("dp", "expert"), None),
        P(("dp", "expert"), "ctx", None),
    )
    sizes = dict(mesh.shape)
    dense = sizes == {"dp": 4, "ctx": 2, "expert": 4}
    return jax.shard_map(
        dense_shards if dense else shards,
        mesh=mesh,
        in_specs=placed,
        out_specs=(
            P(("dp", "expert"), "ctx", None),
            P(("dp", "expert"), "ctx", None),
            P(),
            P(),
            P(),
            P(),
            P(),
            P("expert", None, None),
            P("expert", None, None),
        ),
        check_vma=False,
    )
```

```python
import functools
import jax
import jax.numpy as jnp
from jax import lax
from jax.experimental import pallas as pl
from jax.experimental.pallas import tpu as pltpu
from jax.sharding import PartitionSpec as P

HEADS = 8
HEAD_DIM = 64
TOP = 2
EPS = 1e-06
SCALE = HEAD_DIM ** (-0.5)
F32 = jnp.float32
BF16 = jnp.bfloat16
HELD = pltpu.HBM
BRIEF = pl.CostEstimate(flops=1, bytes_accessed=1, transcendentals=0)
NT = (((1,), (1,)), ((), ()))
TN = (((0,), (0,)), ((), ()))
NN = (((1,), (0,)), ((), ()))


def mm(a, b, dims=NN):
    return lax.dot_general(a, b, dims, preferred_element_type=F32)


def two_halves(a):
    high = a.astype(BF16)
    return high, (a - high.astype(F32)).astype(BF16)


def stats(value):
    center = value - jnp.mean(value, -1, keepdims=True)
    rstd = lax.rsqrt(jnp.mean(center * center, -1, keepdims=True) + EPS)
    return center * rstd, rstd


def norm_vjp(d_value, unit, rstd, gain):
    d_unit = d_value * gain
    return rstd * (
        d_unit
        - jnp.mean(d_unit, -1, keepdims=True)
        - unit * jnp.mean(d_unit * unit, -1, keepdims=True)
    )


def head_pair(value):
    lane = lax.broadcasted_iota(jnp.int32, value.shape, 1)
    first = lane < HEAD_DIM
    return jnp.concatenate(
        [jnp.where(first, value, 0.0), jnp.where(first, 0.0, value)], axis=0
    ).astype(BF16)


def join_pair(value):
    rows = value.shape[0] // 2
    lane = lax.broadcasted_iota(jnp.int32, (rows, value.shape[1]), 1)
    return jnp.where(lane < HEAD_DIM, value[:rows], value[rows:])


def natural(core, mine, theirs):
    return jnp.where(core == 0, mine, theirs), jnp.where(core == 0, theirs, mine)


def attend_kernel(
    meta_ref, own_ref, other_ref, dyown_ref, dyother_ref, mask_ref, g1_ref, wqkv_ref, wout_ref, g2_ref,
    x_ref, dy_ref, normed_ref, qkv_ref, probs_ref, mix_ref, mid_ref, routed_ref,
    x_s, qkv_s, mix_s,
):
    half = own_ref.shape[1]
    width = own_ref.shape[2]
    pair = 2 * HEAD_DIM
    core = meta_ref[3]
    for mine, theirs, ref in ((dyown_ref, dyother_ref, dy_ref), (own_ref, other_ref, x_ref)):
        first, second = natural(core, mine[0].astype(F32), theirs[0].astype(F32))
        x_s[0:half, :] = first
        x_s[half : 2 * half, :] = second
        ref[...] = x_s[...].astype(BF16)
    x = x_s[...]
    unit, _ = stats(x)
    normed = (unit * g1_ref[...]).astype(BF16)
    normed_ref[...] = normed
    qkv_s[...] = mm(normed, wqkv_ref[...])
    qkv_ref[...] = qkv_s[...].astype(BF16)
    image = core * pl.num_programs(0) + pl.program_id(0)
    is_open = mask_ref[pl.ds(image, 1), :] > 0
    for n in range(width // pair):
        at = n * pair
        query = head_pair(qkv_s[:, at : at + pair])
        keys = qkv_s[:, width + at : width + at + pair].astype(BF16)
        vals = qkv_s[:, 2 * width + at : 2 * width + at + pair].astype(BF16)
        scores = jnp.where(is_open, mm(query, keys, NT) * SCALE, -1e9)
        top = jnp.max(scores, -1, keepdims=True)
        expo = jnp.where(is_open, jnp.exp(scores - top), 0.0)
        probs = (expo / jnp.sum(expo, -1, keepdims=True)).astype(BF16)
        probs_ref[0, n] = probs
        mix_s[:, at : at + pair] = join_pair(mm(probs, vals))
    mix = mix_s[...].astype(BF16)
    mix_ref[...] = mix
    mid = x + mm(mix, wout_ref[...])
    mid_ref[...] = mid
    unit, _ = stats(mid)
    routed_ref[...] = (unit * g2_ref[...]).astype(BF16)


def attend(meta, own, other, dy_own, dy_other, mask, g1, wqkv, wout, g2):
    imgs, half, width = own.shape
    imgs //= 2
    seq = 2 * half
    rows = imgs * seq
    pairs = HEADS // 2
    raw = pl.BlockSpec((1, half, width), lambda i, m: (m[3] * imgs + i, 0, 0))
    one = lambda *s: pl.BlockSpec(s, lambda i, m: (i,) + (0,) * (len(s) - 1))
    fix = lambda *s: pl.BlockSpec(s, lambda i, m: (0,) * len(s))
    late = lambda *s: HELD(s, BF16)
    return pl.pallas_call(
        attend_kernel,
        grid_spec=pltpu.PrefetchScalarGridSpec(
            num_scalar_prefetch=1,
            grid=(imgs,),
            in_specs=[
                raw, raw, raw, raw, fix(*mask.shape), fix(1, width),
                fix(width, 3 * width), fix(width, width), fix(1, width),
            ],
            out_specs=[
                one(seq, width), one(seq, width), one(seq, width), one(seq, 3 * width),
                one(1, pairs, 2 * seq, seq), one(seq, width), one(seq, width), one(seq, width),
            ],
            scratch_shapes=[
                pltpu.VMEM((seq, width), F32),
                pltpu.VMEM((seq, 3 * width), F32),
                pltpu.VMEM((seq, width), F32),
            ],
        ),
        out_shape=[
            late(rows, width),
            jax.ShapeDtypeStruct((rows, width), BF16),
            late(rows, width),
            late(rows, 3 * width),
            late(imgs, pairs, 2 * seq, seq),
            late(rows, width),
            HELD((rows, width), F32),
            jax.ShapeDtypeStruct((rows, width), BF16),
        ],
        compiler_params=pltpu.CompilerParams(vmem_limit_bytes=22 << 20),
        cost_estimate=BRIEF,
        name="attend",
    )(meta, own, other, dy_own, dy_other, mask, g1, wqkv, wout, g2)


def assemble_kernel(meta_ref, own_ref, other_ref, out_ref, out_s):
    half = own_ref.shape[1]
    first, second = natural(meta_ref[3], own_ref[0].astype(F32), other_ref[0].astype(F32))
    out_s[0:half, :] = first
    out_s[half : 2 * half, :] = second
    out_ref[...] = out_s[...].astype(BF16)


def assemble(meta, own, other):
    imgs, half, width = own.shape
    imgs //= 2
    raw = pl.BlockSpec((1, half, width), lambda i, m: (m[3] * imgs + i, 0, 0))
    return pl.pallas_call(
        assemble_kernel,
        grid_spec=pltpu.PrefetchScalarGridSpec(
            num_scalar_prefetch=1,
            grid=(imgs,),
            in_specs=[raw, raw],
            out_specs=pl.BlockSpec((2 * half, width), lambda i, m: (i, 0)),
            scratch_shapes=[pltpu.VMEM((2 * half, width), F32)],
        ),
        out_shape=jax.ShapeDtypeStruct((imgs * 2 * half, width), BF16),
        cost_estimate=BRIEF,
        name="assemble",
    )(meta, own, other)


def row_gates(rows, ids, wr):
    logits = mm(wr, rows, NT)
    row = lax.broadcasted_iota(jnp.int32, logits.shape, 0)
    pick = (row.astype(F32) == ids[0:1, :]) | (row.astype(F32) == ids[1:2, :])
    top = jnp.max(jnp.where(pick, logits, -jnp.inf), 0, keepdims=True)
    expo = jnp.where(pick, jnp.exp(logits - top), 0.0)
    return expo / jnp.sum(expo, 0, keepdims=True), row


def padded(count):
    return -(-count // 16) * 16


def expert_kernel(add, local, meta_ref, rows_ref, dy_ref, ids_ref, wr_ref, *rest):
    weights, rest = (rest[:4], rest[4:]) if local else (rest[:8], rest[8:])
    if add:
        pmade_ref, pdin_ref, *rest = rest
    act_ref, dpre_ref, dout_ref, made_ref, din_ref, gate_s, made_s, din_s, *rest = rest
    step = pl.program_id(0)
    count = act_ref.shape[0]
    width = rows_ref.shape[1]
    rows = rows_ref[0:count, :]

    @pl.when(step == 0)
    def _():
        if ids_ref.shape[0] == 2:
            ids = ids_ref[...].astype(F32)
        else:
            at = padded(count)
            ids = [ids_ref[at : at + 2, :], ids_ref[at + 2 : at + 4, 0 : count - width]]
            ids = jnp.concatenate([v.astype(F32) for v in ids], axis=1)
        gates, row = row_gates(rows, ids, wr_ref[...])
        high, low = two_halves(jnp.where(row == meta_ref[0], gates, 0.0))
        ones = jnp.ones((16, 128), BF16)
        gate_s[...] = mm(high, ones, TN) + mm(low, ones, TN)
        gate = gate_s[:, 0:1]
        dout_ref[...] = (gate * dy_ref[...].astype(F32)).astype(BF16)
        made_s[...] = jnp.zeros_like(made_s)
        din_s[...] = jnp.zeros_like(din_s)

    if local:
        w_in = jnp.concatenate([ref[0] for ref in weights[:2]], axis=1)
        w_back = jnp.concatenate([ref[0] for ref in weights[2:]], axis=0)
    else:
        wi_s, wb_s = rest
        part = wi_s.shape[0] // 2
        for side in range(2):

            @pl.when((step < pl.num_programs(0) // 2) == (side == 0))
            def _():
                for s in range(2):
                    for h in range(2):
                        wi_s[h * part : (h + 1) * part, s * part : (s + 1) * part] = weights[4 * side + s][0, h]
                        wb_s[s * part : (s + 1) * part, h * part : (h + 1) * part] = weights[4 * side + 2 + s][0, h]

        w_in, w_back = wi_s[...], wb_s[...]
    pre = mm(rows, w_in)
    square = pre * pre
    inner = pre * (0.7978845608 + 0.0356774081 * square)
    up = 0.5 + 0.5 * jnp.tanh(inner)
    value = pre * up
    act = value.astype(BF16)
    slope = up + value * (1.0 - up) * (1.5957691216 + 0.2140644488 * square)
    act_ref[...] = act
    made_s[...] += mm(act, w_back)
    dpre = (mm(dout_ref[...], w_back, NT) * slope).astype(BF16)
    dpre_ref[...] = dpre
    din_s[...] += mm(dpre, w_in, NT)

    @pl.when(step == pl.num_programs(0) - 1)
    def _():
        gate = gate_s[:, 0:1]
        made = made_s[...].astype(BF16).astype(F32)
        total = gate * made
        d_in = din_s[...]
        high, low = two_halves(made * dy_ref[...].astype(F32))
        ones = jnp.ones((16, made.shape[1]), BF16)
        d_gate = (mm(ones, high, NT) + mm(ones, low, NT))[0:8]
        row = lax.broadcasted_iota(jnp.int32, d_gate.shape, 0)
        d_gate = jnp.where(row == meta_ref[0], d_gate, 0.0)
        tail = padded(count)
        if add:
            total += pmade_ref[...].astype(F32)
            d_in += pdin_ref[0:count, :].astype(F32)
            d_gate += read_gate(pdin_ref, count)
        made_ref[...] = total.astype(BF16)
        din_ref[0:count, :] = d_in.astype(BF16)
        high = d_gate.astype(BF16).astype(F32)
        value = jnp.concatenate([high, d_gate - high], axis=0).astype(BF16)
        if count > d_in.shape[1]:
            cut = d_in.shape[1]
            din_ref[tail : tail + 16, :] = value[:, :cut]
            din_ref[tail + 16 : tail + 32, 0 : count - cut] = value[:, cut:]
        else:
            din_ref[tail : tail + 16, 0:count] = value


def read_gate(ref, count):
    tail = padded(count)
    width = ref.shape[1]
    value = ref[tail : tail + 16, 0 : min(count, width)].astype(F32)
    if count > width:
        value = jnp.concatenate([value, ref[tail + 16 : tail + 32, 0 : count - width].astype(F32)], axis=1)
    return value[0:8] + value[8:16]


PIECES = 8


def expert(meta, rows, dy, ids, wr, weights, prev=None):
    count = dy.shape[0]
    width = rows.shape[1]
    local = weights[0].ndim == 3
    piece = weights[0].shape[2] // PIECES if local else weights[0].shape[2]
    hidden = PIECES * piece
    steps = PIECES // 2
    deep = padded(count) + 16 * -(-count // width)
    fix = lambda *s: pl.BlockSpec(s, lambda q, m: (0,) * len(s))
    if local:
        cuts = [pl.BlockSpec((1, width, piece), lambda q, m, s=s: (0, 0, (2 * q + s) ^ m[1])) for s in (0, 1)]
        cuts += [pl.BlockSpec((1, piece, width), lambda q, m, s=s: (0, (2 * q + s) ^ m[1], 0)) for s in (0, 1)]
        weights = [weights[0]] * 2 + [weights[1]] * 2
    else:
        block = (1, 2, piece, piece)
        near = lambda q: jnp.minimum(q, steps // 2 - 1)
        away = lambda q: jnp.maximum(q - steps // 2, 0)
        cuts = [
            pl.BlockSpec(block, lambda q, m, s=s, g=g, at=at: (2 * at(q) + s, g, 0, 0))
            for at in (near, away) for g in (0, 1) for s in (0, 1)
        ]
        weights = [weights[0]] * 4 + [weights[1]] * 4
    more = [] if prev is None else [fix(count, width), fix(deep, width)]
    return pl.pallas_call(
        functools.partial(expert_kernel, prev is not None, local),
        grid_spec=pltpu.PrefetchScalarGridSpec(
            num_scalar_prefetch=1,
            grid=(steps,),
            in_specs=[
                fix(*rows.shape), fix(*dy.shape), fix(*ids.shape), fix(*wr.shape), *cuts, *more,
            ],
            out_specs=[
                pl.BlockSpec((count, 2 * piece), lambda q, m: (0, q)),
                pl.BlockSpec((count, 2 * piece), lambda q, m: (0, q)),
                fix(count, width), fix(count, width), fix(deep, width),
            ],
            scratch_shapes=[
                pltpu.VMEM((count, 128), F32),
                pltpu.VMEM((count, width), F32),
                pltpu.VMEM((count, width), F32),
            ] + ([] if local else [pltpu.VMEM((width, 2 * piece), BF16), pltpu.VMEM((2 * piece, width), BF16)]),
        ),
        out_shape=[
            jax.ShapeDtypeStruct((count, hidden), BF16),
            jax.ShapeDtypeStruct((count, hidden), BF16),
            jax.ShapeDtypeStruct((count, width), BF16),
            jax.ShapeDtypeStruct((count, width), BF16),
            jax.ShapeDtypeStruct((deep, width), BF16),
        ],
        compiler_params=pltpu.CompilerParams(vmem_limit_bytes=22 << 20),
        cost_estimate=BRIEF,
        name="expert",
    )(meta, rows, dy, ids, wr, *weights, *(prev or ()))


def weight_kernel(n, *refs):
    rows = refs[:n]
    sides = [[refs[n + (3 * e + g) * n : n + (3 * e + g + 1) * n] for g in range(3)] for e in range(2)]
    iown_ref, igive_ref, bown_ref, bgive_ref = refs[7 * n :]
    side, part = pl.program_id(0), pl.program_id(1)
    for e in range(2):
        acts, dpres, douts = sides[e]

        @pl.when(side == e)
        def _():
            results = []
            for left, right in ((dpres, rows), (acts, douts)):
                total = 0.0
                for b in range(n):
                    count = left[b].shape[0]
                    total = total + mm(left[b][...], right[b][0:count, :], TN)
                results.append(total.astype(BF16).reshape(iown_ref.shape[1:]))
            grad_in, grad_back = results

            @pl.when(part < pl.num_programs(1) // 2)
            def _():
                iown_ref[0] = grad_in
                bown_ref[0] = grad_back

            @pl.when(part >= pl.num_programs(1) // 2)
            def _():
                igive_ref[0] = grad_in
                bgive_ref[0] = grad_back


def weight_grads(rows, sides):
    n = len(rows)
    width = rows[0].shape[1]
    hidden = sides[0][0][0].shape[1]
    piece = hidden // PIECES
    upper = PIECES // 2
    steps = PIECES // 2
    fix = lambda a: pl.BlockSpec(a.shape, lambda e, q: (0, 0))
    cuts = [
        lambda a: pl.BlockSpec((a.shape[0], 2 * piece), lambda e, q: (0, jnp.where(e == 0, q, steps - 1))),
        lambda a: pl.BlockSpec((a.shape[0], 2 * piece), lambda e, q: (0, jnp.where(e == 1, q, 0))),
    ]
    specs = [fix(a) for a in rows]
    args = list(rows)
    for e, (acts, dpres, douts) in enumerate(sides):
        specs += [cuts[e](a) for a in acts] + [cuts[e](a) for a in dpres] + [fix(a) for a in douts]
        args += [*acts, *dpres, *douts]
    own = pl.BlockSpec((1, 2, piece, width), lambda e, q: (e, jnp.minimum(q, steps // 2 - 1), 0, 0))
    give = pl.BlockSpec((1, 2, piece, width), lambda e, q: (e, jnp.maximum(q - steps // 2, 0), 0, 0))
    return pl.pallas_call(
        functools.partial(weight_kernel, n),
        grid=(2, steps),
        in_specs=specs,
        out_specs=[own, give, own, give],
        out_shape=[jax.ShapeDtypeStruct((2, upper, piece, width), BF16)] * 4,
        compiler_params=pltpu.CompilerParams(vmem_limit_bytes=26 << 20),
        cost_estimate=BRIEF,
        name="weight_grads",
    )(*args)


def finish_kernel(meta_ref, im_ref, ir_ref, bm_ref, br_ref, gin_ref, gback_ref):
    mine = pl.program_id(0) < pl.num_programs(0) // 2
    flip = meta_ref[1] % 2 == 1
    piece, width = im_ref.shape[1:]
    for m_ref, r_ref, out_ref in ((im_ref, ir_ref, gin_ref), (bm_ref, br_ref, gback_ref)):
        value = jnp.where(mine, m_ref[...], r_ref[...]).astype(F32)
        first = jnp.where(flip, value[1], value[0])
        second = jnp.where(flip, value[0], value[1])
        if out_ref is gin_ref:
            out_ref[0, :, 0:piece] = jnp.transpose(first)
            out_ref[0, :, piece : 2 * piece] = jnp.transpose(second)
        else:
            out_ref[0, 0:piece, :] = first
            out_ref[0, piece : 2 * piece, :] = second


def finish_expert(meta, in_mine, in_recv, back_mine, back_recv):
    upper, piece, width = in_mine.shape
    steps = upper
    own = pl.BlockSpec((2, piece, width), lambda q, m: (jnp.minimum(q, steps // 2 - 1), 0, 0))
    give = pl.BlockSpec((2, piece, width), lambda q, m: (jnp.maximum(q - steps // 2, 0), 0, 0))
    return pl.pallas_call(
        finish_kernel,
        grid_spec=pltpu.PrefetchScalarGridSpec(
            num_scalar_prefetch=1,
            grid=(steps,),
            in_specs=[own, give, own, give],
            out_specs=[
                pl.BlockSpec((1, width, 2 * piece), lambda q, m: (0, 0, q ^ (m[1] // 2))),
                pl.BlockSpec((1, 2 * piece, width), lambda q, m: (0, q ^ (m[1] // 2), 0)),
            ],
        ),
        out_shape=[
            jax.ShapeDtypeStruct((1, width, PIECES * piece), F32),
            jax.ShapeDtypeStruct((1, PIECES * piece, width), F32),
        ],
        compiler_params=pltpu.CompilerParams(vmem_limit_bytes=24 << 20),
        cost_estimate=BRIEF,
        name="finish_expert",
    )(meta, in_mine, in_recv, back_mine, back_recv)


def split_halves(core, whole_ref, own_ref, other_ref):
    imgs, half, _ = own_ref.shape
    for i in range(imgs):
        at = 2 * half * i
        first, second = whole_ref[at : at + half, :], whole_ref[at + half : at + 2 * half, :]
        mine, theirs = natural(core, first, second)
        own_ref[i] = mine.astype(BF16)
        other_ref[i] = theirs.astype(BF16)


def back_kernel(
    meta_ref, din0_ref, din1_ref,
    ids_ref, dy_ref, mid_ref, routed_ref, wr_ref, g2_ref, mix_ref, wout_ref,
    probs_ref, qkv_ref, x_ref, normed_ref, wqkv_ref, g1_ref,
    own_ref, other_ref, gown_ref, ggive_ref,
    dmid_s, dmix_s, dqkv_s, tok_s, grad_s, small_s,
):
    step = pl.program_id(0)
    imgs = pl.num_programs(0)
    seq = qkv_ref.shape[0]
    width = x_ref.shape[1]
    half = seq // 2
    pair = 2 * HEAD_DIM
    rows = x_ref.shape[0]

    @pl.when(step == 0)
    def _():
        routed = routed_ref[...]
        wr = wr_ref[...]
        gates, _ = row_gates(routed, ids_ref[...].astype(F32), wr)
        d_gate = read_gate(din0_ref, rows) + read_gate(din1_ref, rows)
        d_gate = jnp.concatenate([d_gate, jnp.zeros_like(d_gate)], axis=0)
        d_logits = gates * (d_gate - jnp.sum(gates * d_gate, 0, keepdims=True))
        high, low = two_halves(d_logits)
        small_s[...] = jnp.zeros_like(small_s)
        small_s[0:16, :] = mm(high, routed) + mm(low, routed)
        d_routed = din0_ref[0:rows, :].astype(F32) + din1_ref[0:rows, :].astype(F32)
        d_routed = d_routed + mm(high, wr, TN) + mm(low, wr, TN)
        unit, rstd = stats(mid_ref[...])
        small_s[16:17, :] = jnp.sum(d_routed * unit, 0, keepdims=True)
        d_mid = dy_ref[...].astype(F32) + norm_vjp(d_routed, unit, rstd, g2_ref[...])
        dmid_s[...] = d_mid
        d_branch = d_mid.astype(BF16)
        grad_s[:, 3 * width : 4 * width] = mm(mix_ref[...], d_branch, TN).astype(BF16)
        dmix_s[...] = mm(d_branch, wout_ref[...], NT)

    base = pl.multiple_of(step * seq, 8)
    for n in range(width // pair):
        at = n * pair
        d_mix = head_pair(dmix_s[pl.ds(base, seq), at : at + pair])
        query = head_pair(qkv_ref[:, at : at + pair].astype(F32))
        keys = qkv_ref[:, width + at : width + at + pair]
        vals = qkv_ref[:, 2 * width + at : 2 * width + at + pair]
        low = probs_ref[0, n]
        probs = low.astype(F32)
        d_probs = mm(d_mix, vals, NT)
        d_scores = probs * (d_probs - jnp.sum(probs * d_probs, -1, keepdims=True))
        d_scores = d_scores.astype(BF16)
        d_query = join_pair(mm(d_scores, keys)) * SCALE
        d_keys = mm(d_scores, query, TN) * SCALE
        d_vals = mm(low, d_mix, TN)
        dqkv_s[pl.ds(base, seq), at : at + pair] = d_query.astype(BF16)
        dqkv_s[pl.ds(base, seq), width + at : width + at + pair] = d_keys.astype(BF16)
        dqkv_s[pl.ds(base, seq), 2 * width + at : 2 * width + at + pair] = d_vals.astype(BF16)

    @pl.when(step == imgs - 1)
    def _():
        d_qkv = dqkv_s[...]
        grad_s[:, : 3 * width] = mm(normed_ref[...], d_qkv, TN).astype(BF16)
        d_normed = mm(d_qkv, wqkv_ref[...], NT)
        unit, rstd = stats(x_ref[...].astype(F32))
        small_s[17:18, :] = jnp.sum(d_normed * unit, 0, keepdims=True)
        grad_s[:, 4 * width :] = jnp.transpose(small_s[...]).astype(BF16)
        tok_s[...] = dmid_s[...] + norm_vjp(d_normed, unit, rstd, g1_ref[...])
        split_halves(meta_ref[3], tok_s, own_ref, other_ref)
        part = width // SHARES
        for r in range(SHARES):
            ref = gown_ref if r < SHARES // 2 else ggive_ref
            to = (r % (SHARES // 2)) * part
            there = pl.multiple_of((r ^ meta_ref[2]) * part, part)
            ref[to : to + part, :] = grad_s[pl.ds(there, part), :]


SHARES = 32


def attend_back(meta, dins, ids, dy, mid, routed, wr, g2, mix, wout, probs, qkv, x, normed, wqkv, g1):
    imgs = probs.shape[0]
    rows, width = x.shape
    seq = rows // imgs
    pairs = HEADS // 2
    wide = 4 * width + 128
    fix = lambda *s: pl.BlockSpec(s, lambda i, m: (0,) * len(s))
    return pl.pallas_call(
        back_kernel,
        grid_spec=pltpu.PrefetchScalarGridSpec(
            num_scalar_prefetch=1,
            grid=(imgs,),
            in_specs=[fix(*a.shape) for a in dins] + [
                fix(2, rows), fix(rows, width), fix(rows, width), fix(rows, width),
                fix(16, width), fix(1, width), fix(rows, width), fix(width, width),
                pl.BlockSpec((1, pairs, 2 * seq, seq), lambda i, m: (i, 0, 0, 0)),
                pl.BlockSpec((seq, 3 * width), lambda i, m: (i, 0)),
                fix(rows, width), fix(rows, width), fix(width, 3 * width), fix(1, width),
            ],
            out_specs=[
                fix(imgs, seq // 2, width), fix(imgs, seq // 2, width),
                fix(width // 2, wide), fix(width // 2, wide),
            ],
            scratch_shapes=[
                pltpu.VMEM((rows, width), F32),
                pltpu.VMEM((rows, width), F32),
                pltpu.VMEM((rows, 3 * width), BF16),
                pltpu.VMEM((rows, width), F32),
                pltpu.VMEM((width, wide), BF16),
                pltpu.VMEM((128, width), F32),
            ],
        ),
        out_shape=[
            jax.ShapeDtypeStruct((imgs, seq // 2, width), BF16),
            jax.ShapeDtypeStruct((imgs, seq // 2, width), BF16),
            jax.ShapeDtypeStruct((width // 2, wide), BF16),
            jax.ShapeDtypeStruct((width // 2, wide), BF16),
        ],
        compiler_params=pltpu.CompilerParams(vmem_limit_bytes=32 << 20),
        cost_estimate=BRIEF,
        name="attend_back",
    )(meta, *dins, ids, dy, mid, routed, wr, g2, mix, wout, probs, qkv, x, normed, wqkv, g1)


def shared_kernel(meta_ref, mine_ref, recv_ref, gqkv_ref, gout_ref, small_ref, all_s):
    upper, wide = mine_ref.shape
    width = 2 * upper
    part = width // SHARES
    all_s[0:upper, :] = mine_ref[...]
    all_s[upper:width, :] = recv_ref[...]
    for i in range(SHARES):
        there = pl.multiple_of((i ^ meta_ref[2]) * part, part)
        value = all_s[pl.ds(there, part), :].astype(F32)
        at = i * part
        gqkv_ref[at : at + part, :] = value[:, : 3 * width]
        gout_ref[at : at + part, :] = value[:, 3 * width : 4 * width]
        small_ref[at : at + part, :] = value[:, 4 * width :]


def finish_shared(meta, mine, recv):
    upper, wide = mine.shape
    width = 2 * upper
    fix = lambda *s: pl.BlockSpec(s, lambda i, m: (0,) * len(s))
    return pl.pallas_call(
        shared_kernel,
        grid_spec=pltpu.PrefetchScalarGridSpec(
            num_scalar_prefetch=1,
            grid=(1,),
            in_specs=[fix(upper, wide), fix(upper, wide)],
            out_specs=[fix(width, 3 * width), fix(width, width), fix(width, wide - 4 * width)],
            scratch_shapes=[pltpu.VMEM((width, wide), BF16)],
        ),
        out_shape=[
            jax.ShapeDtypeStruct((width, 3 * width), F32),
            jax.ShapeDtypeStruct((width, width), F32),
            jax.ShapeDtypeStruct((width, wide - 4 * width), F32),
        ],
        compiler_params=pltpu.CompilerParams(vmem_limit_bytes=16 << 20),
        cost_estimate=BRIEF,
        name="finish_shared",
    )(meta, mine, recv)


def combine_kernel(meta_ref, mid_ref, a_ref, b_ref, own_ref, other_ref, s_ref):
    s_ref[...] = mid_ref[...] + (a_ref[...].astype(F32) + b_ref[...].astype(F32))
    split_halves(meta_ref[3], s_ref, own_ref, other_ref)


def combine(meta, mid, parts, imgs):
    rows, width = mid.shape
    seq = rows // imgs
    spec = pl.BlockSpec((seq, width), lambda i, m: (i, 0))
    out = pl.BlockSpec((1, seq // 2, width), lambda i, m: (i, 0, 0))
    shape = jax.ShapeDtypeStruct((imgs, seq // 2, width), BF16)
    return pl.pallas_call(
        combine_kernel,
        grid_spec=pltpu.PrefetchScalarGridSpec(
            num_scalar_prefetch=1,
            grid=(imgs,),
            in_specs=[spec] * 3,
            out_specs=[out, out],
            scratch_shapes=[pltpu.VMEM((seq, width), F32)],
        ),
        out_shape=[shape, shape],
        cost_estimate=BRIEF,
        name="combine",
    )(meta, mid, *parts)


def place_kernel(meta_ref, a_own_ref, a_recv_ref, b_own_ref, b_recv_ref, a_ref, b_ref):
    imgs = pl.num_programs(0) // 2
    mine = pl.program_id(0) // imgs == meta_ref[3]
    a_ref[...] = jnp.where(mine, a_own_ref[...], a_recv_ref[...])
    b_ref[...] = jnp.where(mine, b_own_ref[...], b_recv_ref[...])


def place(meta, *arrays):
    imgs, half, width = arrays[0].shape
    spec = pl.BlockSpec((1, half, width), lambda j, m: (j % imgs, 0, 0))
    out = pl.BlockSpec((1, half, width), lambda j, m: (j, 0, 0))
    shape = jax.ShapeDtypeStruct((2 * imgs, half, width), BF16)
    return pl.pallas_call(
        place_kernel,
        grid_spec=pltpu.PrefetchScalarGridSpec(
            num_scalar_prefetch=1, grid=(2 * imgs,), in_specs=[spec] * 4, out_specs=[out, out]
        ),
        out_shape=[shape, shape],
        cost_estimate=BRIEF,
        name="place",
    )(meta, *arrays)


SWAP = [(0, 1), (1, 0)]


def xor(k, n=4):
    return [(i, i ^ k) for i in range(n)]


def send(value, axis, pairs):
    return lax.ppermute(value, axis, pairs)


def add_low(a, b):
    return (a.astype(F32) + b.astype(F32)).astype(BF16)


def after(value, *earlier):
    return lax.optimization_barrier((value, *earlier))[0]


def tie(*values):
    return lax.optimization_barrier(values)


def fan(value, axis):
    rows = value.shape[0] // 4
    return [send(value[k * rows : (k + 1) * rows], axis, xor(k)) for k in (1, 2, 3)]


def add_fan(value, got):
    total = value[: value.shape[0] // 4].astype(F32)
    for v in got:
        total = total + v.astype(F32)
    return total.astype(BF16)


def dense_shards(
    tokens, gain_one, w_qkv, w_out, gain_two, w_router, w_in, w_back, route_ids, key_mask, cotangent
):
    nimg, half, width = tokens.shape
    imgs = nimg // 2
    rows = imgs * 2 * half
    experts = w_router.shape[1]
    piece = w_in.shape[2] // PIECES
    core = lax.axis_index("ctx")
    z = lax.axis_index("expert")
    me = core * 4 + lax.axis_index("dp")
    meta = jnp.stack([z, me, me * 4 + z, core]).astype(jnp.int32)
    meta_pair = jnp.stack([z ^ 1, me, me * 4 + z, core]).astype(jnp.int32)
    far = lambda v: send(v, "expert", xor(2))
    swap = lambda v: send(v, "ctx", SWAP)

    codes = route_ids.reshape(nimg, half, TOP)
    codes = codes[..., 0] + experts * codes[..., 1]
    tok_other, dy_other, codes_other = swap(tokens), swap(cotangent), swap(codes)
    mine_in = lax.dynamic_slice_in_dim(w_in[0], me * piece, piece, 1)
    mine_back = lax.dynamic_slice_in_dim(w_back[0], me * piece, piece, 0)
    pack = jnp.stack([mine_in[:piece], mine_in[piece:], mine_back[:, :piece], mine_back[:, piece:]])
    first = jnp.where(core == 0, codes, codes_other)
    second = jnp.where(core == 0, codes_other, codes)
    codes = lax.dynamic_slice_in_dim(jnp.concatenate([first, second], 1), core * imgs, imgs, 0)
    codes = codes.reshape(1, rows)
    ids = jnp.concatenate([codes % experts, codes // experts], 0)
    wide = jnp.pad(ids, ((0, 0), (0, 2 * width - rows))).reshape(TOP, 2, width)
    ids_pack = jnp.concatenate([wide[:, 0], wide[:, 1]], 0).astype(BF16)
    ids_pack = jnp.pad(ids_pack, ((padded(rows) - rows, 12), (0, 0)))
    wr = jnp.pad(w_router.T, ((0, 16 - experts), (0, 0)))
    g1, g2 = gain_one[None, :], gain_two[None, :]

    pack, far_raw = send(pack, "expert", xor(1)), far(cotangent)
    x_rows, dy, normed, qkv, probs, mix, mid, routed = attend(
        meta, tokens, tok_other, cotangent, dy_other, key_mask, g1, w_qkv, w_out, g2
    )
    own_one = expert(meta, routed, dy, ids, wr, (w_in, w_back))
    far_rows = jnp.concatenate([routed, ids_pack], 0)
    pack, far_raw, far_rows, own_din = tie(pack, far_raw, far_rows, own_one[4])
    own_one = [*own_one[:4], own_din]

    packs = [pack] + [send(pack, "dp", xor(k)) for k in (1, 2, 3)]
    far_other = swap(far_raw)
    *packs, far_rows, far_other = tie(*packs, far(far_rows), far_other)

    packs = jnp.stack(packs)
    far_dy = assemble(meta, far_raw, far_other)
    far_one = expert(meta, far_rows, far_dy, far_rows, wr, (w_in, w_back))
    packs_other, far_din = tie(swap(packs), far_one[4])
    pair = (packs, packs_other)
    far_two = expert(meta_pair, far_rows, far_dy, far_rows, wr, pair, [far_one[3], far_din])

    far_din, far_made = tie(far_two[4], far_two[3])
    own_two = expert(meta_pair, routed, dy, ids, wr, pair, [own_one[3], after(own_one[4], far_din)])
    sides = [list(zip(own_one[:3], far_one[:3])), list(zip(own_two[:3], far_two[:3]))]
    grads = weight_grads([routed, far_rows], sides)
    din_far, *grads = tie(far(far_din), *grads)

    a, a_give, b, b_give = grads
    a, b = tie(add_low(a, swap(a_give)), add_low(b, swap(b_give)))

    y_way, x_way = ("dp", xor(2)), ("dp", xor(1))
    a_got, b_got = send(a[:, 2:], *y_way), send(b[:, 1::2], *x_way)
    far_made = far(after(far_made, din_far))
    tok_own, tok_give, shared, shared_give = attend_back(
        meta, [after(own_two[4], a, b), din_far], ids, dy, mid, routed, wr, g2, mix, w_out, probs, qkv, x_rows, normed, w_qkv, g1
    )
    a, b, far_made, shared, shared_give, tok_give = tie(
        add_low(a[:, :2], a_got), add_low(b[:, 0::2], b_got), far_made, shared, shared_give, tok_give
    )
    others = lambda v, axis: [send(v, axis, xor(k)) for k in (1, 2, 3)]
    mix_own, mix_give = combine(meta, mid, [own_two[3], far_made], imgs)
    a, b, shared, tok_got, mix_give = tie(
        add_low(a[:, :1], send(a[:, 1:], *x_way)),
        add_low(b[:, :1], send(b[:, 1:], *y_way)),
        add_low(shared, swap(shared_give)),
        swap(tok_give),
        mix_give,
    )
    a, b, shared = tie(
        add_low(a[0], send(a[1], "expert", xor(1))),
        add_low(b[0], send(b[1], "expert", xor(1))),
        add_fan(shared, fan(shared, "dp")),
    )
    a, b, shared = tie(
        jnp.concatenate([a, send(a, *x_way)], 0),
        jnp.stack([b, send(b, *y_way)], 0),
        add_fan(shared, fan(shared, "expert")),
    )
    a, b, shared = tie(
        jnp.concatenate([a, send(a, *y_way)], 0),
        jnp.concatenate([b, send(b, *x_way)], 1).reshape(4, piece, width),
        jnp.concatenate([shared] + others(shared, "expert"), 0),
    )
    a_other, b_other, shared = tie(
        swap(a), swap(b), jnp.concatenate([shared] + others(shared, "dp"), 0)
    )
    shared_other, mix_got = swap(shared), swap(mix_give)
    grad_in, grad_back = finish_expert(meta, a, a_other, b, b_other)
    mixed, grad_tokens = place(meta, mix_own, mix_got, tok_own, tok_got)
    grad_qkv, grad_out, small = finish_shared(meta, shared, shared_other)
    return (
        mixed,
        grad_tokens,
        small[:, 17],
        grad_qkv,
        grad_out,
        small[:, 16],
        small[:, :experts],
        grad_in,
        grad_back,
    )


def norm_rows(value, gain):
    center = value - jnp.mean(value, -1, keepdims=True)
    spread = jnp.mean(center * center, -1, keepdims=True)
    return center * lax.rsqrt(spread + 1e-06) * gain


def smooth_gelu(value):
    return 0.5 * value * (1.0 + jnp.tanh(0.7978845608 * (value + 0.044715 * value * value * value)))


def forward(tokens, gain_one, w_qkv, w_out, gain_two, w_router, w_in, w_back, flat_ids, live):
    nimg, half, width = tokens.shape
    count = nimg * half
    experts_all = w_router.shape[1]
    capacity = max(2, 2 * TOP * count // experts_all)
    x_rows = tokens.astype(jnp.float32).reshape(count, width)
    normed = norm_rows(x_rows, gain_one).astype(jnp.bfloat16)
    qkv = jnp.dot(normed, w_qkv, preferred_element_type=jnp.float32).astype(jnp.bfloat16)
    qkv = qkv.reshape(nimg, half, 3 * width)
    query = qkv[..., :width]
    keys_local = qkv[..., width : 2 * width]
    vals_local = qkv[..., 2 * width :]
    keys, vals = (
        lax.all_gather(keys_local, "ctx", axis=1, tiled=True),
        lax.all_gather(vals_local, "ctx", axis=1, tiled=True),
    )
    seq = keys.shape[1]
    query4 = query.reshape(nimg, half, HEADS, HEAD_DIM)
    keys4 = keys.reshape(nimg, seq, HEADS, HEAD_DIM)
    vals4 = vals.reshape(nimg, seq, HEADS, HEAD_DIM)
    scale = HEAD_DIM ** (-0.5)
    scores = (
        jnp.einsum("iqhc,ikhc->ihqk", query4, keys4, preferred_element_type=jnp.float32) * scale
    )
    open_keys = live[:, None, None, :]
    masked = jnp.where(open_keys, scores, -1000000000.0)
    topmost = jnp.max(masked, -1, keepdims=True)
    expo = jnp.where(open_keys, jnp.exp(masked - topmost), 0.0)
    probs = expo / jnp.sum(expo, -1, keepdims=True)
    probs_low = probs.astype(jnp.bfloat16)
    mix = jnp.einsum("ihqk,ikhc->iqhc", probs_low, vals4, preferred_element_type=jnp.float32)
    mix = mix.reshape(count, width).astype(jnp.bfloat16)
    mid = x_rows + jnp.dot(mix, w_out, preferred_element_type=jnp.float32)
    routed = norm_rows(mid, gain_two).astype(jnp.bfloat16)
    logits = jnp.dot(routed, w_router, preferred_element_type=jnp.float32)
    pick = flat_ids[:, :, None] == jnp.arange(experts_all, dtype=jnp.int32)[None, None, :]
    chosen = jnp.sum(jnp.where(pick, logits[:, None, :], 0.0), -1)
    expo_gate = jnp.exp(chosen)
    gates = expo_gate / jnp.sum(expo_gate, -1, keepdims=True)
    pair_ids = flat_ids.reshape(-1)
    hits = (pair_ids[:, None] == jnp.arange(experts_all, dtype=jnp.int32)[None, :]).astype(
        jnp.int32
    )
    before = jnp.cumsum(hits, 0) - hits
    slots = jnp.sum(before * hits, 1)
    where_rows = pair_ids * capacity + slots
    sent = jnp.repeat(routed, TOP, axis=0)
    buffer = jnp.zeros((experts_all * capacity, width), jnp.bfloat16).at[where_rows].set(sent)
    buffer = buffer.reshape(experts_all, capacity, width)
    arrived = lax.all_to_all(buffer, "expert", split_axis=0, concat_axis=1, tiled=True)
    pre = jnp.einsum("erd,edf->erf", arrived, w_in, preferred_element_type=jnp.float32)
    act = smooth_gelu(pre).astype(jnp.bfloat16)
    made = jnp.einsum("erf,efd->erd", act, w_back, preferred_element_type=jnp.float32).astype(
        jnp.bfloat16
    )
    returned = lax.all_to_all(made, "expert", split_axis=1, concat_axis=0, tiled=True)
    picked = returned.reshape(experts_all * capacity, width)[where_rows].reshape(count, TOP, width)
    output = mid + jnp.sum(gates[:, :, None] * picked.astype(jnp.float32), 1)
    return (
        x_rows,
        normed,
        query4,
        keys4,
        vals4,
        probs,
        probs_low,
        mix,
        mid,
        routed,
        pick,
        gates,
        where_rows,
        arrived,
        pre,
        act,
        picked,
        output,
        capacity,
    )


def shards(
    tokens, gain_one, w_qkv, w_out, gain_two, w_router, w_in, w_back, route_ids, key_mask, cotangent
):
    nimg, half, width = tokens.shape
    count = nimg * half
    experts_all = w_router.shape[1]
    flat_ids = route_ids.reshape(count, TOP)
    live = key_mask > 0
    state = forward(
        tokens, gain_one, w_qkv, w_out, gain_two, w_router, w_in, w_back, flat_ids, live
    )
    mixed = state[17].reshape(nimg, half, width).astype(jnp.bfloat16)
    state = forward(
        tokens, gain_one, w_qkv, w_out, gain_two, w_router, w_in, w_back, flat_ids, live
    )
    (
        x_rows,
        normed,
        query4,
        keys4,
        vals4,
        probs,
        probs_low,
        mix,
        mid,
        routed,
        pick,
        gates,
        where_rows,
        arrived,
        pre,
        act,
        picked,
        output,
        capacity,
    ) = state
    scale = HEAD_DIM ** (-0.5)
    high = lax.Precision.HIGHEST
    grad_y = cotangent.astype(jnp.float32).reshape(count, width)
    grad_gate = jnp.sum(grad_y[:, None, :] * picked.astype(jnp.float32), -1)
    d_out = (
        (gates[:, :, None] * grad_y[:, None, :]).astype(jnp.bfloat16).reshape(count * TOP, width)
    )
    grad_buffer = jnp.zeros((experts_all * capacity, width), jnp.bfloat16).at[where_rows].set(d_out)
    grad_buffer = grad_buffer.reshape(experts_all, capacity, width)
    grad_arrived = lax.all_to_all(grad_buffer, "expert", split_axis=0, concat_axis=1, tiled=True)
    d_act = jnp.einsum("erd,efd->erf", grad_arrived, w_back, preferred_element_type=jnp.float32)
    grad_back = jnp.einsum("erf,erd->efd", act, grad_arrived, preferred_element_type=jnp.float32)
    _, gelu_pull = jax.vjp(smooth_gelu, pre)
    d_pre = gelu_pull(d_act)[0].astype(jnp.bfloat16)
    grad_in = jnp.einsum("erd,erf->edf", arrived, d_pre, preferred_element_type=jnp.float32)
    d_in = jnp.einsum("erf,edf->erd", d_pre, w_in, preferred_element_type=jnp.float32).astype(
        jnp.bfloat16
    )
    grad_returned = lax.all_to_all(d_in, "expert", split_axis=1, concat_axis=0, tiled=True)
    grad_rows = grad_returned.reshape(experts_all * capacity, width)[where_rows].reshape(
        count, TOP, width
    )
    d_experts = jnp.sum(grad_rows.astype(jnp.float32), 1)
    d_chosen = gates * (grad_gate - jnp.sum(gates * grad_gate, -1, keepdims=True))
    d_logits = jnp.sum(jnp.where(pick, d_chosen[:, :, None], 0.0), 1)
    grad_router = jnp.dot(routed.astype(jnp.float32).T, d_logits, precision=high)
    d_routed = d_experts + jnp.dot(d_logits, w_router.astype(jnp.float32).T, precision=high)
    _, norm_two_pull = jax.vjp(norm_rows, mid, gain_two)
    d_mid_norm, grad_gain_two = norm_two_pull(d_routed)
    d_mid = grad_y + d_mid_norm
    d_branch = d_mid.astype(jnp.bfloat16)
    grad_out = jnp.einsum("td,te->de", mix, d_branch, preferred_element_type=jnp.float32)
    d_mix = jnp.dot(d_branch, w_out.T, preferred_element_type=jnp.float32).astype(jnp.bfloat16)
    d_mix4 = d_mix.reshape(nimg, half, HEADS, HEAD_DIM)
    d_probs = jnp.einsum("iqhc,ikhc->ihqk", d_mix4, vals4, preferred_element_type=jnp.float32)
    d_scores = (probs * (d_probs - jnp.sum(probs * d_probs, -1, keepdims=True))).astype(
        jnp.bfloat16
    )
    d_query = (
        jnp.einsum("ihqk,ikhc->iqhc", d_scores, keys4, preferred_element_type=jnp.float32) * scale
    )
    d_keys = (
        jnp.einsum("ihqk,iqhc->ikhc", d_scores, query4, preferred_element_type=jnp.float32) * scale
    )
    d_vals = jnp.einsum("ihqk,iqhc->ikhc", probs_low, d_mix4, preferred_element_type=jnp.float32)
    seq = keys4.shape[1]
    d_keys_own, d_vals_own = (
        lax.psum_scatter(
            d_keys.reshape(nimg, seq, width).astype(jnp.bfloat16),
            "ctx",
            scatter_dimension=1,
            tiled=True,
        ).astype(jnp.float32),
        lax.psum_scatter(
            d_vals.reshape(nimg, seq, width).astype(jnp.bfloat16),
            "ctx",
            scatter_dimension=1,
            tiled=True,
        ).astype(jnp.float32),
    )
    d_qkv = jnp.concatenate(
        [
            d_query.reshape(count, width).astype(jnp.bfloat16),
            d_keys_own.reshape(count, width).astype(jnp.bfloat16),
            d_vals_own.reshape(count, width).astype(jnp.bfloat16),
        ],
        axis=1,
    )
    grad_qkv = jnp.einsum("td,te->de", normed, d_qkv, preferred_element_type=jnp.float32)
    d_normed = jnp.dot(d_qkv, w_qkv.T, preferred_element_type=jnp.float32)
    _, norm_one_pull = jax.vjp(norm_rows, x_rows, gain_one)
    d_x_norm, grad_gain_one = norm_one_pull(d_normed)
    grad_tokens = (d_mid + d_x_norm).reshape(nimg, half, width).astype(jnp.bfloat16)
    grad_gain_one, grad_qkv, grad_out, grad_gain_two, grad_router = lax.psum(
        (grad_gain_one, grad_qkv, grad_out, grad_gain_two, grad_router), ("dp", "ctx", "expert")
    )
    grad_in, grad_back = (
        lax.psum(grad_in.astype(jnp.bfloat16), ("dp", "ctx")).astype(jnp.float32),
        lax.psum(grad_back.astype(jnp.bfloat16), ("dp", "ctx")).astype(jnp.float32),
    )
    return (
        mixed,
        grad_tokens,
        grad_gain_one,
        grad_qkv,
        grad_out,
        grad_gain_two,
        grad_router,
        grad_in,
        grad_back,
    )


def solution(mesh):
    placed = (
        P(("dp", "expert"), "ctx", None),
        P(),
        P(),
        P(),
        P(),
        P(),
        P("expert", None, None),
        P("expert", None, None),
        P(("dp", "expert"), "ctx", None, None, None),
        P(("dp", "expert"), None),
        P(("dp", "expert"), "ctx", None),
    )
    sizes = dict(mesh.shape)
    dense = sizes == {"dp": 4, "ctx": 2, "expert": 4}
    return jax.shard_map(
        dense_shards if dense else shards,
        mesh=mesh,
        in_specs=placed,
        out_specs=(
            P(("dp", "expert"), "ctx", None),
            P(("dp", "expert"), "ctx", None),
            P(),
            P(),
            P(),
            P(),
            P(),
            P("expert", None, None),
            P("expert", None, None),
        ),
        check_vma=False,
    )
```

```python
import functools
import jax
import jax.numpy as jnp
from jax import lax
from jax.experimental import pallas as pl
from jax.experimental.pallas import tpu as pltpu
from jax.sharding import PartitionSpec as P

HEADS = 8
HEAD_DIM = 64
TOP = 2
EPS = 1e-06
SCALE = HEAD_DIM ** (-0.5)
F32 = jnp.float32
BF16 = jnp.bfloat16
HELD = pltpu.HBM
HERE = pl.BlockSpec(memory_space=pltpu.VMEM)
BRIEF = pl.CostEstimate(flops=1, bytes_accessed=1, transcendentals=0)
NT = (((1,), (1,)), ((), ()))
TN = (((0,), (0,)), ((), ()))
NN = (((1,), (0,)), ((), ()))


def mm(a, b, dims=NN):
    return lax.dot_general(a, b, dims, preferred_element_type=F32)


def two_halves(a):
    high = a.astype(BF16)
    return high, (a - high.astype(F32)).astype(BF16)


def stats(value):
    center = value - jnp.mean(value, -1, keepdims=True)
    rstd = lax.rsqrt(jnp.mean(center * center, -1, keepdims=True) + EPS)
    return center * rstd, rstd


def norm_vjp(d_value, unit, rstd, gain):
    d_unit = d_value * gain
    return rstd * (
        d_unit
        - jnp.mean(d_unit, -1, keepdims=True)
        - unit * jnp.mean(d_unit * unit, -1, keepdims=True)
    )


def head_pair(value):
    lane = lax.broadcasted_iota(jnp.int32, value.shape, 1)
    first = lane < HEAD_DIM
    return jnp.concatenate(
        [jnp.where(first, value, 0.0), jnp.where(first, 0.0, value)], axis=0
    ).astype(BF16)


def join_pair(value):
    rows = value.shape[0] // 2
    lane = lax.broadcasted_iota(jnp.int32, (rows, value.shape[1]), 1)
    return jnp.where(lane < HEAD_DIM, value[:rows], value[rows:])


def natural(core, mine, theirs):
    return jnp.where(core == 0, mine, theirs), jnp.where(core == 0, theirs, mine)


def attend_kernel(
    meta_ref, own_ref, other_ref, dyown_ref, dyother_ref, mask_ref, g1_ref, wqkv_ref, wout_ref, g2_ref,
    x_ref, dy_ref, normed_ref, qkv_ref, probs_ref, mix_ref, mid_ref, routed_ref,
    x_s, qkv_s, mix_s,
):
    half = own_ref.shape[1]
    width = own_ref.shape[2]
    pair = 2 * HEAD_DIM
    core = meta_ref[3]
    for mine, theirs, ref in ((dyown_ref, dyother_ref, dy_ref), (own_ref, other_ref, x_ref)):
        first, second = natural(core, mine[0].astype(F32), theirs[0].astype(F32))
        x_s[0:half, :] = first
        x_s[half : 2 * half, :] = second
        ref[...] = x_s[...].astype(BF16)
    x = x_s[...]
    unit, _ = stats(x)
    normed = (unit * g1_ref[...]).astype(BF16)
    normed_ref[...] = normed
    qkv_s[...] = mm(normed, wqkv_ref[...])
    qkv_ref[...] = qkv_s[...].astype(BF16)
    image = core * pl.num_programs(0) + pl.program_id(0)
    is_open = mask_ref[pl.ds(image, 1), :] > 0
    for n in range(width // pair):
        at = n * pair
        query = head_pair(qkv_s[:, at : at + pair])
        keys = qkv_s[:, width + at : width + at + pair].astype(BF16)
        vals = qkv_s[:, 2 * width + at : 2 * width + at + pair].astype(BF16)
        scores = jnp.where(is_open, mm(query, keys, NT) * SCALE, -1e9)
        top = jnp.max(scores, -1, keepdims=True)
        expo = jnp.where(is_open, jnp.exp(scores - top), 0.0)
        probs = (expo / jnp.sum(expo, -1, keepdims=True)).astype(BF16)
        probs_ref[0, n] = probs
        mix_s[:, at : at + pair] = join_pair(mm(probs, vals))
    mix = mix_s[...].astype(BF16)
    mix_ref[...] = mix
    mid = x + mm(mix, wout_ref[...])
    mid_ref[...] = mid
    unit, _ = stats(mid)
    routed_ref[...] = (unit * g2_ref[...]).astype(BF16)


def attend(meta, own, other, dy_own, dy_other, mask, g1, wqkv, wout, g2):
    imgs, half, width = own.shape
    imgs //= 2
    seq = 2 * half
    rows = imgs * seq
    pairs = HEADS // 2
    raw = pl.BlockSpec((1, half, width), lambda i, m: (m[3] * imgs + i, 0, 0))
    one = lambda *s: pl.BlockSpec(s, lambda i, m: (i,) + (0,) * (len(s) - 1))
    fix = lambda *s: pl.BlockSpec(s, lambda i, m: (0,) * len(s))
    late = lambda *s: HELD(s, BF16)
    return pl.pallas_call(
        attend_kernel,
        grid_spec=pltpu.PrefetchScalarGridSpec(
            num_scalar_prefetch=1,
            grid=(imgs,),
            in_specs=[
                raw, raw, raw, raw, fix(*mask.shape), fix(1, width),
                fix(width, 3 * width), fix(width, width), fix(1, width),
            ],
            out_specs=[
                one(seq, width), one(seq, width), one(seq, width), one(seq, 3 * width),
                one(1, pairs, 2 * seq, seq), one(seq, width), one(seq, width), one(seq, width),
            ],
            scratch_shapes=[
                pltpu.VMEM((seq, width), F32),
                pltpu.VMEM((seq, 3 * width), F32),
                pltpu.VMEM((seq, width), F32),
            ],
        ),
        out_shape=[
            late(rows, width),
            jax.ShapeDtypeStruct((rows, width), BF16),
            late(rows, width),
            late(rows, 3 * width),
            late(imgs, pairs, 2 * seq, seq),
            late(rows, width),
            HELD((rows, width), F32),
            jax.ShapeDtypeStruct((rows, width), BF16),
        ],
        compiler_params=pltpu.CompilerParams(vmem_limit_bytes=22 << 20),
        cost_estimate=BRIEF,
        name="attend",
    )(meta, *map(held, (own, other, dy_own, dy_other)), mask, g1, held(wqkv), held(wout), g2)


def assemble_kernel(meta_ref, own_ref, other_ref, out_ref, out_s):
    half = own_ref.shape[1]
    first, second = natural(meta_ref[3], own_ref[0].astype(F32), other_ref[0].astype(F32))
    out_s[0:half, :] = first
    out_s[half : 2 * half, :] = second
    out_ref[...] = out_s[...].astype(BF16)


def assemble(meta, own, other):
    imgs, half, width = own.shape
    imgs //= 2
    raw = pl.BlockSpec((1, half, width), lambda i, m: (m[3] * imgs + i, 0, 0))
    return pl.pallas_call(
        assemble_kernel,
        grid_spec=pltpu.PrefetchScalarGridSpec(
            num_scalar_prefetch=1,
            grid=(imgs,),
            in_specs=[raw, raw],
            out_specs=pl.BlockSpec((2 * half, width), lambda i, m: (i, 0)),
            scratch_shapes=[pltpu.VMEM((2 * half, width), F32)],
        ),
        out_shape=jax.ShapeDtypeStruct((imgs * 2 * half, width), BF16),
        compiler_params=pltpu.CompilerParams(vmem_limit_bytes=6 << 20),
        cost_estimate=BRIEF,
        name="assemble",
    )(meta, own, other)


def row_gates(rows, ids, wr):
    logits = mm(wr, rows, NT)
    row = lax.broadcasted_iota(jnp.int32, logits.shape, 0)
    pick = (row.astype(F32) == ids[0:1, :]) | (row.astype(F32) == ids[1:2, :])
    top = jnp.max(jnp.where(pick, logits, -jnp.inf), 0, keepdims=True)
    expo = jnp.where(pick, jnp.exp(logits - top), 0.0)
    return expo / jnp.sum(expo, 0, keepdims=True), row


def padded(count):
    return -(-count // 16) * 16


def expert_kernel(add, local, meta_ref, rows_ref, dy_ref, ids_ref, wr_ref, *rest):
    weights, rest = (rest[:4], rest[4:]) if local else (rest[:8], rest[8:])
    if add:
        pmade_ref, pdin_ref, *rest = rest
    act_ref, dpre_ref, dout_ref, made_ref, din_ref, gate_s, made_s, din_s, *rest = rest
    step = pl.program_id(0)
    count = act_ref.shape[0]
    width = rows_ref.shape[1]
    rows = rows_ref[0:count, :]

    @pl.when(step == 0)
    def _():
        if ids_ref.shape[0] == 2:
            ids = ids_ref[...].astype(F32)
        else:
            at = padded(count)
            ids = [ids_ref[at : at + 2, :], ids_ref[at + 2 : at + 4, 0 : count - width]]
            ids = jnp.concatenate([v.astype(F32) for v in ids], axis=1)
        gates, row = row_gates(rows, ids, wr_ref[...])
        high, low = two_halves(jnp.where(row == meta_ref[0], gates, 0.0))
        ones = jnp.ones((16, 128), BF16)
        gate_s[...] = mm(high, ones, TN) + mm(low, ones, TN)
        gate = gate_s[:, 0:1]
        dout_ref[...] = (gate * dy_ref[...].astype(F32)).astype(BF16)
        made_s[...] = jnp.zeros_like(made_s)
        din_s[...] = jnp.zeros_like(din_s)

    if local:
        w_in = jnp.concatenate([ref[0] for ref in weights[:2]], axis=1)
        w_back = jnp.concatenate([ref[0] for ref in weights[2:]], axis=0)
    else:
        wi_s, wb_s = rest
        part = wi_s.shape[0] // 2
        for side in range(2):

            @pl.when((step < pl.num_programs(0) // 2) == (side == 0))
            def _():
                for s in range(2):
                    for h in range(2):
                        wi_s[h * part : (h + 1) * part, s * part : (s + 1) * part] = weights[4 * side + s][0, h]
                        wb_s[s * part : (s + 1) * part, h * part : (h + 1) * part] = weights[4 * side + 2 + s][0, h]

        w_in, w_back = wi_s[...], wb_s[...]
    pre = mm(rows, w_in)
    square = pre * pre
    inner = pre * (0.7978845608 + 0.0356774081 * square)
    up = 0.5 + 0.5 * jnp.tanh(inner)
    value = pre * up
    act = value.astype(BF16)
    slope = up + value * (1.0 - up) * (1.5957691216 + 0.2140644488 * square)
    here = pl.ds(pl.multiple_of(step * pre.shape[1], pre.shape[1]), pre.shape[1])
    act_ref[:, here] = act
    made_s[...] += mm(act, w_back)
    dpre = (mm(dout_ref[...], w_back, NT) * slope).astype(BF16)
    dpre_ref[:, here] = dpre
    din_s[...] += mm(dpre, w_in, NT)

    @pl.when(step == pl.num_programs(0) - 1)
    def _():
        gate = gate_s[:, 0:1]
        made = made_s[...].astype(BF16).astype(F32)
        total = gate * made
        d_in = din_s[...]
        high, low = two_halves(made * dy_ref[...].astype(F32))
        ones = jnp.ones((16, made.shape[1]), BF16)
        d_gate = (mm(ones, high, NT) + mm(ones, low, NT))[0:8]
        row = lax.broadcasted_iota(jnp.int32, d_gate.shape, 0)
        d_gate = jnp.where(row == meta_ref[0], d_gate, 0.0)
        tail = padded(count)
        if add:
            total += pmade_ref[...].astype(F32)
            d_in += pdin_ref[0:count, :].astype(F32)
            d_gate += read_gate(pdin_ref, count)
        made_ref[...] = total.astype(BF16)
        din_ref[0:count, :] = d_in.astype(BF16)
        high = d_gate.astype(BF16).astype(F32)
        value = jnp.concatenate([high, d_gate - high], axis=0).astype(BF16)
        if count > d_in.shape[1]:
            cut = d_in.shape[1]
            din_ref[tail : tail + 16, :] = value[:, :cut]
            din_ref[tail + 16 : tail + 32, 0 : count - cut] = value[:, cut:]
        else:
            din_ref[tail : tail + 16, 0:count] = value


def read_gate(ref, count):
    tail = padded(count)
    width = ref.shape[1]
    value = ref[tail : tail + 16, 0 : min(count, width)].astype(F32)
    if count > width:
        value = jnp.concatenate([value, ref[tail + 16 : tail + 32, 0 : count - width].astype(F32)], axis=1)
    return value[0:8] + value[8:16]


PIECES = 8


def expert(meta, rows, dy, ids, wr, weights, prev=None):
    count = dy.shape[0]
    width = rows.shape[1]
    local = weights[0].ndim == 3
    piece = weights[0].shape[2] // PIECES if local else weights[0].shape[2]
    hidden = PIECES * piece
    steps = PIECES // 2
    deep = padded(count) + 16 * -(-count // width)
    if local:
        cuts = [pl.BlockSpec((1, width, piece), lambda q, m, s=s: (0, 0, (2 * q + s) ^ m[1])) for s in (0, 1)]
        cuts += [pl.BlockSpec((1, piece, width), lambda q, m, s=s: (0, (2 * q + s) ^ m[1], 0)) for s in (0, 1)]
        weights = [held(weights[0])] * 2 + [held(weights[1])] * 2
    else:
        block = (1, 2, piece, piece)
        near = lambda q: jnp.minimum(q, steps // 2 - 1)
        away = lambda q: jnp.maximum(q - steps // 2, 0)
        cuts = [
            pl.BlockSpec(block, lambda q, m, s=s, g=g, at=at: (2 * at(q) + s, g, 0, 0))
            for at in (near, away) for g in (0, 1) for s in (0, 1)
        ]
        weights = [weights[0]] * 4 + [weights[1]] * 4
    more = [] if prev is None else [HERE, HERE]
    return pl.pallas_call(
        functools.partial(expert_kernel, prev is not None, local),
        grid_spec=pltpu.PrefetchScalarGridSpec(
            num_scalar_prefetch=1,
            grid=(steps,),
            in_specs=[HERE] * 4 + [*cuts, *more],
            out_specs=[HERE] * 5,
            scratch_shapes=[
                pltpu.VMEM((count, 128), F32),
                pltpu.VMEM((count, width), F32),
                pltpu.VMEM((count, width), F32),
            ] + ([] if local else [pltpu.VMEM((width, 2 * piece), BF16), pltpu.VMEM((2 * piece, width), BF16)]),
        ),
        out_shape=[
            jax.ShapeDtypeStruct((count, hidden), BF16),
            jax.ShapeDtypeStruct((count, hidden), BF16),
            jax.ShapeDtypeStruct((count, width), BF16),
            jax.ShapeDtypeStruct((count, width), BF16),
            jax.ShapeDtypeStruct((deep, width), BF16),
        ],
        compiler_params=pltpu.CompilerParams(vmem_limit_bytes=20 << 20),
        cost_estimate=BRIEF,
        name="expert",
    )(meta, rows, dy, ids, wr, *weights, *(prev or ()))


def weight_kernel(n, *refs):
    rows, acts, dpres, douts = (refs[g * n : (g + 1) * n] for g in range(4))
    iown_ref, igive_ref, bown_ref, bgive_ref = refs[4 * n :]
    wide = iown_ref.shape[0] * iown_ref.shape[1]
    here = pl.ds(pl.multiple_of(pl.program_id(0) * wide, wide), wide)
    results = []
    for left, right in ((dpres, rows), (acts, douts)):
        total = 0.0
        for b in range(n):
            count = left[b].shape[0]
            total = total + mm(left[b][:, here], right[b][0:count, :], TN)
        results.append(total.astype(BF16).reshape(iown_ref.shape))
    grad_in, grad_back = results
    first = pl.program_id(0) < pl.num_programs(0) // 2

    @pl.when(first)
    def _():
        iown_ref[...] = grad_in
        bown_ref[...] = grad_back

    @pl.when(jnp.logical_not(first))
    def _():
        igive_ref[...] = grad_in
        bgive_ref[...] = grad_back


def weight_grads(rows, acts, dpres, douts, late=False):
    n = len(rows)
    width = rows[0].shape[1]
    piece = acts[0].shape[1] // PIECES
    steps = PIECES // 2
    own = pl.BlockSpec((2, piece, width), lambda q: (jnp.minimum(q, steps // 2 - 1), 0, 0))
    give = pl.BlockSpec((2, piece, width), lambda q: (jnp.maximum(q - steps // 2, 0), 0, 0))
    return pl.pallas_call(
        functools.partial(weight_kernel, n),
        grid=(steps,),
        in_specs=[HERE] * (4 * n),
        out_specs=[own, give, own, give],
        out_shape=[(HELD if late and g % 2 == 0 else jax.ShapeDtypeStruct)((PIECES // 2, piece, width), BF16) for g in range(4)],
        compiler_params=pltpu.CompilerParams(vmem_limit_bytes=14 << 20),
        cost_estimate=BRIEF,
        name="weight_grads",
    )(*rows, *acts, *dpres, *douts)


def finish_kernel(meta_ref, im_ref, ir_ref, bm_ref, br_ref, gin_ref, gback_ref):
    mine = pl.program_id(0) < pl.num_programs(0) // 2
    flip = meta_ref[1] % 2 == 1
    piece, width = im_ref.shape[1:]
    for m_ref, r_ref, out_ref in ((im_ref, ir_ref, gin_ref), (bm_ref, br_ref, gback_ref)):
        value = jnp.where(mine, m_ref[...], r_ref[...]).astype(F32)
        first = jnp.where(flip, value[1], value[0])
        second = jnp.where(flip, value[0], value[1])
        if out_ref is gin_ref:
            out_ref[0, :, 0:piece] = jnp.transpose(first)
            out_ref[0, :, piece : 2 * piece] = jnp.transpose(second)
        else:
            out_ref[0, 0:piece, :] = first
            out_ref[0, piece : 2 * piece, :] = second


def finish_expert(meta, in_mine, in_recv, back_mine, back_recv):
    upper, piece, width = in_mine.shape
    steps = upper
    own = pl.BlockSpec((2, piece, width), lambda q, m: (jnp.minimum(q, steps // 2 - 1), 0, 0))
    give = pl.BlockSpec((2, piece, width), lambda q, m: (jnp.maximum(q - steps // 2, 0), 0, 0))
    return pl.pallas_call(
        finish_kernel,
        grid_spec=pltpu.PrefetchScalarGridSpec(
            num_scalar_prefetch=1,
            grid=(steps,),
            in_specs=[own, give, own, give],
            out_specs=[
                pl.BlockSpec((1, width, 2 * piece), lambda q, m: (0, 0, q ^ (m[1] // 2))),
                pl.BlockSpec((1, 2 * piece, width), lambda q, m: (0, q ^ (m[1] // 2), 0)),
            ],
        ),
        out_shape=[
            jax.ShapeDtypeStruct((1, width, PIECES * piece), F32),
            jax.ShapeDtypeStruct((1, PIECES * piece, width), F32),
        ],
        compiler_params=pltpu.CompilerParams(vmem_limit_bytes=14 << 20),
        cost_estimate=BRIEF,
        name="finish_expert",
    )(meta, in_mine, in_recv, back_mine, back_recv)


def split_halves(core, whole_ref, own_ref, other_ref):
    imgs, half, _ = own_ref.shape
    for i in range(imgs):
        at = 2 * half * i
        first, second = whole_ref[at : at + half, :], whole_ref[at + half : at + 2 * half, :]
        mine, theirs = natural(core, first, second)
        own_ref[i] = mine.astype(BF16)
        other_ref[i] = theirs.astype(BF16)


def back_kernel(
    meta_ref, din0_ref, din1_ref,
    ids_ref, dy_ref, mid_ref, routed_ref, wr_ref, g2_ref, mix_ref, wout_ref,
    probs_ref, qkv_ref, x_ref, normed_ref, wqkv_ref, g1_ref,
    own_ref, other_ref, gown_ref, ggive_ref,
    dmid_s, dmix_s, dqkv_s, tok_s, grad_s, small_s,
):
    step = pl.program_id(0)
    imgs = pl.num_programs(0)
    seq = qkv_ref.shape[0]
    width = x_ref.shape[1]
    half = seq // 2
    pair = 2 * HEAD_DIM
    rows = x_ref.shape[0]

    @pl.when(step == 0)
    def _():
        routed = routed_ref[...]
        wr = wr_ref[...]
        gates, _ = row_gates(routed, ids_ref[...].astype(F32), wr)
        d_gate = read_gate(din0_ref, rows) + read_gate(din1_ref, rows)
        d_gate = jnp.concatenate([d_gate, jnp.zeros_like(d_gate)], axis=0)
        d_logits = gates * (d_gate - jnp.sum(gates * d_gate, 0, keepdims=True))
        high, low = two_halves(d_logits)
        small_s[...] = jnp.zeros_like(small_s)
        small_s[0:16, :] = mm(high, routed) + mm(low, routed)
        d_routed = din0_ref[0:rows, :].astype(F32) + din1_ref[0:rows, :].astype(F32)
        d_routed = d_routed + mm(high, wr, TN) + mm(low, wr, TN)
        unit, rstd = stats(mid_ref[...])
        small_s[16:17, :] = jnp.sum(d_routed * unit, 0, keepdims=True)
        d_mid = dy_ref[...].astype(F32) + norm_vjp(d_routed, unit, rstd, g2_ref[...])
        dmid_s[...] = d_mid
        d_branch = d_mid.astype(BF16)
        grad_s[:, 3 * width : 4 * width] = mm(mix_ref[...], d_branch, TN).astype(BF16)
        dmix_s[...] = mm(d_branch, wout_ref[...], NT)

    base = pl.multiple_of(step * seq, 8)
    for n in range(width // pair):
        at = n * pair
        d_mix = head_pair(dmix_s[pl.ds(base, seq), at : at + pair])
        query = head_pair(qkv_ref[:, at : at + pair].astype(F32))
        keys = qkv_ref[:, width + at : width + at + pair]
        vals = qkv_ref[:, 2 * width + at : 2 * width + at + pair]
        low = probs_ref[0, n]
        probs = low.astype(F32)
        d_probs = mm(d_mix, vals, NT)
        d_scores = probs * (d_probs - jnp.sum(probs * d_probs, -1, keepdims=True))
        d_scores = d_scores.astype(BF16)
        d_query = join_pair(mm(d_scores, keys)) * SCALE
        d_keys = mm(d_scores, query, TN) * SCALE
        d_vals = mm(low, d_mix, TN)
        dqkv_s[pl.ds(base, seq), at : at + pair] = d_query.astype(BF16)
        dqkv_s[pl.ds(base, seq), width + at : width + at + pair] = d_keys.astype(BF16)
        dqkv_s[pl.ds(base, seq), 2 * width + at : 2 * width + at + pair] = d_vals.astype(BF16)

    @pl.when(step == imgs - 1)
    def _():
        d_qkv = dqkv_s[...]
        grad_s[:, : 3 * width] = mm(normed_ref[...], d_qkv, TN).astype(BF16)
        d_normed = mm(d_qkv, wqkv_ref[...], NT)
        unit, rstd = stats(x_ref[...].astype(F32))
        small_s[17:18, :] = jnp.sum(d_normed * unit, 0, keepdims=True)
        grad_s[:, 4 * width :] = jnp.transpose(small_s[...]).astype(BF16)
        tok_s[...] = dmid_s[...] + norm_vjp(d_normed, unit, rstd, g1_ref[...])
        split_halves(meta_ref[3], tok_s, own_ref, other_ref)
        part = width // SHARES
        for r in range(SHARES):
            ref = gown_ref if r < SHARES // 2 else ggive_ref
            to = (r % (SHARES // 2)) * part
            there = pl.multiple_of((r ^ meta_ref[2]) * part, part)
            ref[to : to + part, :] = grad_s[pl.ds(there, part), :]


SHARES = 32


def attend_back(meta, dins, ids, dy, mid, routed, wr, g2, mix, wout, probs, qkv, x, normed, wqkv, g1):
    imgs = probs.shape[0]
    rows, width = x.shape
    seq = rows // imgs
    pairs = HEADS // 2
    wide = 4 * width + 128
    fix = lambda *s: pl.BlockSpec(s, lambda i, m: (0,) * len(s))
    return pl.pallas_call(
        back_kernel,
        grid_spec=pltpu.PrefetchScalarGridSpec(
            num_scalar_prefetch=1,
            grid=(imgs,),
            in_specs=[fix(*a.shape) for a in dins] + [
                fix(2, rows), fix(rows, width), fix(rows, width), fix(rows, width),
                fix(16, width), fix(1, width), fix(rows, width), fix(width, width),
                pl.BlockSpec((1, pairs, 2 * seq, seq), lambda i, m: (i, 0, 0, 0)),
                pl.BlockSpec((seq, 3 * width), lambda i, m: (i, 0)),
                fix(rows, width), fix(rows, width), fix(width, 3 * width), fix(1, width),
            ],
            out_specs=[
                fix(imgs, seq // 2, width), fix(imgs, seq // 2, width),
                fix(width // 2, wide), fix(width // 2, wide),
            ],
            scratch_shapes=[
                pltpu.VMEM((rows, width), F32),
                pltpu.VMEM((rows, width), F32),
                pltpu.VMEM((rows, 3 * width), BF16),
                pltpu.VMEM((rows, width), F32),
                pltpu.VMEM((width, wide), BF16),
                pltpu.VMEM((128, width), F32),
            ],
        ),
        out_shape=[
            jax.ShapeDtypeStruct((imgs, seq // 2, width), BF16),
            jax.ShapeDtypeStruct((imgs, seq // 2, width), BF16),
            jax.ShapeDtypeStruct((width // 2, wide), BF16),
            jax.ShapeDtypeStruct((width // 2, wide), BF16),
        ],
        compiler_params=pltpu.CompilerParams(vmem_limit_bytes=32 << 20),
        cost_estimate=BRIEF,
        name="attend_back",
    )(meta, *dins, ids, dy, mid, routed, wr, g2, mix, wout, probs, qkv, x, normed, wqkv, g1)


def shared_kernel(meta_ref, mine_ref, recv_ref, gqkv_ref, gout_ref, small_ref, all_s):
    upper, wide = mine_ref.shape
    width = 2 * upper
    part = width // SHARES
    all_s[0:upper, :] = mine_ref[...]
    all_s[upper:width, :] = recv_ref[...]
    for i in range(SHARES):
        there = pl.multiple_of((i ^ meta_ref[2]) * part, part)
        value = all_s[pl.ds(there, part), :].astype(F32)
        at = i * part
        gqkv_ref[at : at + part, :] = value[:, : 3 * width]
        gout_ref[at : at + part, :] = value[:, 3 * width : 4 * width]
        small_ref[at : at + part, :] = value[:, 4 * width :]


def finish_shared(meta, mine, recv):
    upper, wide = mine.shape
    width = 2 * upper
    fix = lambda *s: pl.BlockSpec(s, lambda i, m: (0,) * len(s))
    return pl.pallas_call(
        shared_kernel,
        grid_spec=pltpu.PrefetchScalarGridSpec(
            num_scalar_prefetch=1,
            grid=(1,),
            in_specs=[fix(upper, wide), fix(upper, wide)],
            out_specs=[fix(width, 3 * width), fix(width, width), fix(width, wide - 4 * width)],
            scratch_shapes=[pltpu.VMEM((width, wide), BF16)],
        ),
        out_shape=[
            jax.ShapeDtypeStruct((width, 3 * width), F32),
            jax.ShapeDtypeStruct((width, width), F32),
            jax.ShapeDtypeStruct((width, wide - 4 * width), F32),
        ],
        compiler_params=pltpu.CompilerParams(vmem_limit_bytes=16 << 20),
        cost_estimate=BRIEF,
        name="finish_shared",
    )(meta, mine, recv)


def combine_kernel(meta_ref, mid_ref, a_ref, b_ref, own_ref, other_ref, s_ref):
    s_ref[...] = mid_ref[...] + (a_ref[...].astype(F32) + b_ref[...].astype(F32))
    split_halves(meta_ref[3], s_ref, own_ref, other_ref)


def combine(meta, mid, parts, imgs):
    rows, width = mid.shape
    seq = rows // imgs
    spec = pl.BlockSpec((seq, width), lambda i, m: (i, 0))
    out = pl.BlockSpec((1, seq // 2, width), lambda i, m: (i, 0, 0))
    shape = jax.ShapeDtypeStruct((imgs, seq // 2, width), BF16)
    return pl.pallas_call(
        combine_kernel,
        grid_spec=pltpu.PrefetchScalarGridSpec(
            num_scalar_prefetch=1,
            grid=(imgs,),
            in_specs=[spec] * 3,
            out_specs=[out, out],
            scratch_shapes=[pltpu.VMEM((seq, width), F32)],
        ),
        out_shape=[shape, shape],
        compiler_params=pltpu.CompilerParams(vmem_limit_bytes=8 << 20),
        cost_estimate=BRIEF,
        name="combine",
    )(meta, mid, *parts)


def place_kernel(meta_ref, a_own_ref, a_recv_ref, b_own_ref, b_recv_ref, a_ref, b_ref):
    imgs = pl.num_programs(0) // 2
    mine = pl.program_id(0) // imgs == meta_ref[3]
    a_ref[...] = jnp.where(mine, a_own_ref[...], a_recv_ref[...])
    b_ref[...] = jnp.where(mine, b_own_ref[...], b_recv_ref[...])


def place(meta, *arrays):
    imgs, half, width = arrays[0].shape
    spec = pl.BlockSpec((1, half, width), lambda j, m: (j % imgs, 0, 0))
    out = pl.BlockSpec((1, half, width), lambda j, m: (j, 0, 0))
    shape = jax.ShapeDtypeStruct((2 * imgs, half, width), BF16)
    return pl.pallas_call(
        place_kernel,
        grid_spec=pltpu.PrefetchScalarGridSpec(
            num_scalar_prefetch=1, grid=(2 * imgs,), in_specs=[spec] * 4, out_specs=[out, out]
        ),
        out_shape=[shape, shape],
        compiler_params=pltpu.CompilerParams(vmem_limit_bytes=4 << 20),
        cost_estimate=BRIEF,
        name="place",
    )(meta, *arrays)


def merge_kernel(plan, *refs):
    refs = list(refs)
    takes = [[[refs.pop(0) for _ in range(n)] for n in sizes] for sizes, _, _ in plan]
    for groups, (_, axis, cuts) in zip(takes, plan):
        outs = [refs.pop(0) for _ in cuts]
        if axis is not None:
            size = groups[0][0].shape[axis]
            for k, ref in enumerate(groups[0]):
                at = slice(k * size, (k + 1) * size)
                outs[0][(slice(None),) * axis + (at,)] = ref[...]
            continue
        for g, take in enumerate(groups):
            total = take[0][...].astype(F32)
            for ref in take[1:]:
                total += ref[...].astype(F32)
            total = total.astype(BF16)
            for out, cut in zip(outs, cuts):
                if len(groups) > 1:
                    out[g] = total[cut]
                else:
                    out[...] = total[cut]


def merge(*items):
    plan, shapes, arrays = [], [], []
    for groups, axis, cuts in items:
        first = jax.ShapeDtypeStruct(groups[0][0].shape, BF16)
        if axis is not None:
            cuts = [None]
            shape = list(first.shape)
            shape[axis] *= len(groups[0])
            shapes.append(jax.ShapeDtypeStruct(tuple(shape), BF16))
        else:
            lead = (len(groups),) if len(groups) > 1 else ()
            shapes += [
                jax.ShapeDtypeStruct(lead + jax.eval_shape(lambda v, c=c: v[c], first).shape, BF16) for c in cuts
            ]
        plan.append(([len(g) for g in groups], axis, cuts))
        arrays += [v for g in groups for v in g]
    return pl.pallas_call(
        functools.partial(merge_kernel, plan),
        out_shape=shapes,
        compiler_params=pltpu.CompilerParams(vmem_limit_bytes=16 << 20),
        cost_estimate=BRIEF,
        name="merge",
    )(*arrays)


def held(value):
    return pltpu.with_memory_space_constraint(value, pltpu.HBM)


SWAP = [(0, 1), (1, 0)]


def xor(k, n=4):
    return [(i, i ^ k) for i in range(n)]


def send(value, axis, pairs):
    return lax.ppermute(value, axis, pairs)


def add_low(a, b):
    return (a.astype(F32) + b.astype(F32)).astype(BF16)


def after(value, *earlier):
    return lax.optimization_barrier((value, *earlier))[0]


def tie(*values):
    return lax.optimization_barrier(values)


def fan(value, axis):
    rows = value.shape[0] // 4
    return [send(value[k * rows : (k + 1) * rows], axis, xor(k)) for k in (1, 2, 3)]


def add_fan(value, got):
    total = value[: value.shape[0] // 4].astype(F32)
    for v in got:
        total = total + v.astype(F32)
    return total.astype(BF16)


def dense_shards(
    tokens, gain_one, w_qkv, w_out, gain_two, w_router, w_in, w_back, route_ids, key_mask, cotangent
):
    nimg, half, width = tokens.shape
    imgs = nimg // 2
    rows = imgs * 2 * half
    experts = w_router.shape[1]
    piece = w_in.shape[2] // PIECES
    core = lax.axis_index("ctx")
    z = lax.axis_index("expert")
    me = core * 4 + lax.axis_index("dp")
    meta = jnp.stack([z, me, me * 4 + z, core]).astype(jnp.int32)
    meta_pair = jnp.stack([z ^ 2, me, me * 4 + z, core]).astype(jnp.int32)
    far = lambda v: send(v, "expert", xor(1))
    swap = lambda v: send(v, "ctx", SWAP)

    codes = route_ids.reshape(nimg, half, TOP)
    codes = codes[..., 0] + experts * codes[..., 1]
    tok_other, dy_other, codes_other = swap(tokens), swap(cotangent), swap(codes)
    mine_in = lax.dynamic_slice_in_dim(w_in[0], me * piece, piece, 1)
    mine_back = lax.dynamic_slice_in_dim(w_back[0], me * piece, piece, 0)
    pack = jnp.stack([mine_in[:piece], mine_in[piece:], mine_back[:, :piece], mine_back[:, piece:]])
    first = jnp.where(core == 0, codes, codes_other)
    second = jnp.where(core == 0, codes_other, codes)
    codes = lax.dynamic_slice_in_dim(jnp.concatenate([first, second], 1), core * imgs, imgs, 0)
    codes = codes.reshape(1, rows)
    ids = jnp.concatenate([codes % experts, codes // experts], 0)
    wide = jnp.pad(ids, ((0, 0), (0, 2 * width - rows))).reshape(TOP, 2, width)
    ids_pack = jnp.concatenate([wide[:, 0], wide[:, 1]], 0).astype(BF16)
    ids_pack = jnp.pad(ids_pack, ((padded(rows) - rows, 12), (0, 0)))
    wr = jnp.pad(w_router.T, ((0, 16 - experts), (0, 0)))
    g1, g2 = gain_one[None, :], gain_two[None, :]

    far_raw, pack = far(after(cotangent, pack)), send(pack, "expert", xor(2))
    x_rows, dy, normed, qkv, probs, mix, mid, routed = attend(
        meta, tokens, tok_other, cotangent, dy_other, key_mask, g1, w_qkv, w_out, g2
    )
    far_rows = jnp.concatenate([routed, ids_pack], 0)
    pack, far_raw, far_rows, routed = tie(pack, far_raw, far_rows, routed)

    packs = [pack] + [send(pack, "dp", xor(k)) for k in (1, 2, 3)]
    far_rows = far(far_rows)
    far_dy = assemble(meta, far_raw, swap(far_raw))
    own_one = expert(meta, routed, dy, ids, wr, (w_in, w_back))
    far_one = expert(meta, after(far_rows, own_one[4]), far_dy, far_rows, wr, (w_in, w_back))
    *packs, far_din = tie(*packs, far_one[4])
    far_one = [*far_one[:4], far_din]

    packs = jnp.stack(packs)
    pair = [packs, swap(packs)]
    grads = weight_grads([routed, far_rows], *zip(own_one[:3], far_one[:3]), late=True)
    *pair, a, a_give, b, b_give = tie(*pair, *grads)

    far_two = expert(meta_pair, far_rows, far_dy, far_rows, wr, pair, far_one[3:])
    head, tail = slice(0, 2), slice(2, 4)
    even, odd = [(slice(None), slice(k, k + 1)) for k in (0, 1)]
    square = lambda v: v.reshape(2, 2, piece, width)

    def across(a, a_give, b, b_give):
        return merge(([[a, swap(a_give)]], None, [head, tail]), ([[square(b), square(swap(b_give))]], None, [even, odd]))

    *one, far_din, far_made = tie(*across(a, a_give, b, b_give), far_two[4], far_two[3])

    y_way, x_way = ("dp", xor(2)), ("dp", xor(1))
    own_two = expert(meta_pair, routed, dy, ids, wr, pair, [own_one[3], after(own_one[4], far_din)])
    grads = weight_grads([routed, far_rows], *zip(own_two[:3], far_two[:3]))
    din_far, a_got, b_got, *grads = tie(far(far_din), send(one[1], *y_way), send(one[3], *x_way), *grads)
    a_one, b_one = [one[0], a_got], [one[2], b_got]

    two = tie(*across(*grads))

    a_two, b_two = [two[0], send(two[1], *y_way)], [two[2], send(two[3], *x_way)]
    far_made = far(after(far_made, din_far))
    tok_own, tok_give, shared, shared_give = attend_back(
        meta, [after(own_two[4], *two), din_far], ids, dy, mid, routed, wr, g2, mix, w_out, probs, qkv, x_rows, normed, w_qkv, g1
    )
    halves = [slice(0, 1), slice(1, 2)]
    a, a_give, b, b_give, far_made, shared, shared_give, tok_give = tie(
        *merge(([a_one, a_two], None, halves), ([b_one, b_two], None, halves)),
        far_made,
        shared,
        shared_give,
        tok_give,
    )
    mix_own, mix_give = combine(meta, mid, [own_two[3], far_made], imgs)
    quarters = lambda n: [slice(k * n, (k + 1) * n) for k in range(4)]
    a, a_give, b, b_give, *shared, tok_got, mix_got = tie(
        *merge(
            ([[a, send(a_give, *x_way)]], None, [0, 1]),
            ([[b, send(b_give, *y_way)]], None, [0, 1]),
            ([[shared, swap(shared_give)]], None, quarters(width // 8)),
        ),
        swap(tok_give),
        swap(mix_give),
    )
    spread = lambda parts, axis: [send(v, axis, xor(k)) for k, v in zip((1, 2, 3), parts)]
    everything = [slice(None)]
    mixed, grad_tokens = place(meta, mix_own, mix_got, tok_own, tok_got)
    a, b, *shared, mixed, grad_tokens = tie(
        *merge(
            ([[a, send(a_give, "expert", xor(2))]], None, everything),
            ([[b, send(b_give, "expert", xor(2))]], None, everything),
            ([[shared[0], *spread(shared[1:], "dp")]], None, quarters(width // 32)),
        ),
        mixed,
        grad_tokens,
    )
    a, b, shared = tie(
        *merge(
            ([[a, send(a, *x_way)]], 0, None),
            ([[b, send(b, *y_way)]], 0, None),
            ([[shared[0], *spread(shared[1:], "expert")]], None, everything),
        )
    )
    a, b, shared = tie(
        *merge(
            ([[a, send(a, *y_way)]], 0, None),
            ([[b, send(b, *x_way)]], 1, None),
            ([[shared, *spread([shared] * 3, "expert")]], 0, None),
        )
    )
    b = b.reshape(a.shape)
    grad_in, grad_back = finish_expert(meta, a, swap(a), b, swap(b))
    (shared,) = merge(([[after(shared, grad_in, grad_back), *spread([shared] * 3, "dp")]], 0, None))
    grad_qkv, grad_out, small = finish_shared(meta, shared, swap(shared))
    return (
        mixed,
        grad_tokens,
        small[:, 17],
        grad_qkv,
        grad_out,
        small[:, 16],
        small[:, :experts],
        grad_in,
        grad_back,
    )


def norm_rows(value, gain):
    center = value - jnp.mean(value, -1, keepdims=True)
    spread = jnp.mean(center * center, -1, keepdims=True)
    return center * lax.rsqrt(spread + 1e-06) * gain


def smooth_gelu(value):
    return 0.5 * value * (1.0 + jnp.tanh(0.7978845608 * (value + 0.044715 * value * value * value)))


def forward(tokens, gain_one, w_qkv, w_out, gain_two, w_router, w_in, w_back, flat_ids, live):
    nimg, half, width = tokens.shape
    count = nimg * half
    experts_all = w_router.shape[1]
    capacity = max(2, 2 * TOP * count // experts_all)
    x_rows = tokens.astype(jnp.float32).reshape(count, width)
    normed = norm_rows(x_rows, gain_one).astype(jnp.bfloat16)
    qkv = jnp.dot(normed, w_qkv, preferred_element_type=jnp.float32).astype(jnp.bfloat16)
    qkv = qkv.reshape(nimg, half, 3 * width)
    query = qkv[..., :width]
    keys_local = qkv[..., width : 2 * width]
    vals_local = qkv[..., 2 * width :]
    keys, vals = (
        lax.all_gather(keys_local, "ctx", axis=1, tiled=True),
        lax.all_gather(vals_local, "ctx", axis=1, tiled=True),
    )
    seq = keys.shape[1]
    query4 = query.reshape(nimg, half, HEADS, HEAD_DIM)
    keys4 = keys.reshape(nimg, seq, HEADS, HEAD_DIM)
    vals4 = vals.reshape(nimg, seq, HEADS, HEAD_DIM)
    scale = HEAD_DIM ** (-0.5)
    scores = (
        jnp.einsum("iqhc,ikhc->ihqk", query4, keys4, preferred_element_type=jnp.float32) * scale
    )
    open_keys = live[:, None, None, :]
    masked = jnp.where(open_keys, scores, -1000000000.0)
    topmost = jnp.max(masked, -1, keepdims=True)
    expo = jnp.where(open_keys, jnp.exp(masked - topmost), 0.0)
    probs = expo / jnp.sum(expo, -1, keepdims=True)
    probs_low = probs.astype(jnp.bfloat16)
    mix = jnp.einsum("ihqk,ikhc->iqhc", probs_low, vals4, preferred_element_type=jnp.float32)
    mix = mix.reshape(count, width).astype(jnp.bfloat16)
    mid = x_rows + jnp.dot(mix, w_out, preferred_element_type=jnp.float32)
    routed = norm_rows(mid, gain_two).astype(jnp.bfloat16)
    logits = jnp.dot(routed, w_router, preferred_element_type=jnp.float32)
    pick = flat_ids[:, :, None] == jnp.arange(experts_all, dtype=jnp.int32)[None, None, :]
    chosen = jnp.sum(jnp.where(pick, logits[:, None, :], 0.0), -1)
    expo_gate = jnp.exp(chosen)
    gates = expo_gate / jnp.sum(expo_gate, -1, keepdims=True)
    pair_ids = flat_ids.reshape(-1)
    hits = (pair_ids[:, None] == jnp.arange(experts_all, dtype=jnp.int32)[None, :]).astype(
        jnp.int32
    )
    before = jnp.cumsum(hits, 0) - hits
    slots = jnp.sum(before * hits, 1)
    where_rows = pair_ids * capacity + slots
    sent = jnp.repeat(routed, TOP, axis=0)
    buffer = jnp.zeros((experts_all * capacity, width), jnp.bfloat16).at[where_rows].set(sent)
    buffer = buffer.reshape(experts_all, capacity, width)
    arrived = lax.all_to_all(buffer, "expert", split_axis=0, concat_axis=1, tiled=True)
    pre = jnp.einsum("erd,edf->erf", arrived, w_in, preferred_element_type=jnp.float32)
    act = smooth_gelu(pre).astype(jnp.bfloat16)
    made = jnp.einsum("erf,efd->erd", act, w_back, preferred_element_type=jnp.float32).astype(
        jnp.bfloat16
    )
    returned = lax.all_to_all(made, "expert", split_axis=1, concat_axis=0, tiled=True)
    picked = returned.reshape(experts_all * capacity, width)[where_rows].reshape(count, TOP, width)
    output = mid + jnp.sum(gates[:, :, None] * picked.astype(jnp.float32), 1)
    return (
        x_rows,
        normed,
        query4,
        keys4,
        vals4,
        probs,
        probs_low,
        mix,
        mid,
        routed,
        pick,
        gates,
        where_rows,
        arrived,
        pre,
        act,
        picked,
        output,
        capacity,
    )


def shards(
    tokens, gain_one, w_qkv, w_out, gain_two, w_router, w_in, w_back, route_ids, key_mask, cotangent
):
    nimg, half, width = tokens.shape
    count = nimg * half
    experts_all = w_router.shape[1]
    flat_ids = route_ids.reshape(count, TOP)
    live = key_mask > 0
    state = forward(
        tokens, gain_one, w_qkv, w_out, gain_two, w_router, w_in, w_back, flat_ids, live
    )
    mixed = state[17].reshape(nimg, half, width).astype(jnp.bfloat16)
    state = forward(
        tokens, gain_one, w_qkv, w_out, gain_two, w_router, w_in, w_back, flat_ids, live
    )
    (
        x_rows,
        normed,
        query4,
        keys4,
        vals4,
        probs,
        probs_low,
        mix,
        mid,
        routed,
        pick,
        gates,
        where_rows,
        arrived,
        pre,
        act,
        picked,
        output,
        capacity,
    ) = state
    scale = HEAD_DIM ** (-0.5)
    high = lax.Precision.HIGHEST
    grad_y = cotangent.astype(jnp.float32).reshape(count, width)
    grad_gate = jnp.sum(grad_y[:, None, :] * picked.astype(jnp.float32), -1)
    d_out = (
        (gates[:, :, None] * grad_y[:, None, :]).astype(jnp.bfloat16).reshape(count * TOP, width)
    )
    grad_buffer = jnp.zeros((experts_all * capacity, width), jnp.bfloat16).at[where_rows].set(d_out)
    grad_buffer = grad_buffer.reshape(experts_all, capacity, width)
    grad_arrived = lax.all_to_all(grad_buffer, "expert", split_axis=0, concat_axis=1, tiled=True)
    d_act = jnp.einsum("erd,efd->erf", grad_arrived, w_back, preferred_element_type=jnp.float32)
    grad_back = jnp.einsum("erf,erd->efd", act, grad_arrived, preferred_element_type=jnp.float32)
    _, gelu_pull = jax.vjp(smooth_gelu, pre)
    d_pre = gelu_pull(d_act)[0].astype(jnp.bfloat16)
    grad_in = jnp.einsum("erd,erf->edf", arrived, d_pre, preferred_element_type=jnp.float32)
    d_in = jnp.einsum("erf,edf->erd", d_pre, w_in, preferred_element_type=jnp.float32).astype(
        jnp.bfloat16
    )
    grad_returned = lax.all_to_all(d_in, "expert", split_axis=1, concat_axis=0, tiled=True)
    grad_rows = grad_returned.reshape(experts_all * capacity, width)[where_rows].reshape(
        count, TOP, width
    )
    d_experts = jnp.sum(grad_rows.astype(jnp.float32), 1)
    d_chosen = gates * (grad_gate - jnp.sum(gates * grad_gate, -1, keepdims=True))
    d_logits = jnp.sum(jnp.where(pick, d_chosen[:, :, None], 0.0), 1)
    grad_router = jnp.dot(routed.astype(jnp.float32).T, d_logits, precision=high)
    d_routed = d_experts + jnp.dot(d_logits, w_router.astype(jnp.float32).T, precision=high)
    _, norm_two_pull = jax.vjp(norm_rows, mid, gain_two)
    d_mid_norm, grad_gain_two = norm_two_pull(d_routed)
    d_mid = grad_y + d_mid_norm
    d_branch = d_mid.astype(jnp.bfloat16)
    grad_out = jnp.einsum("td,te->de", mix, d_branch, preferred_element_type=jnp.float32)
    d_mix = jnp.dot(d_branch, w_out.T, preferred_element_type=jnp.float32).astype(jnp.bfloat16)
    d_mix4 = d_mix.reshape(nimg, half, HEADS, HEAD_DIM)
    d_probs = jnp.einsum("iqhc,ikhc->ihqk", d_mix4, vals4, preferred_element_type=jnp.float32)
    d_scores = (probs * (d_probs - jnp.sum(probs * d_probs, -1, keepdims=True))).astype(
        jnp.bfloat16
    )
    d_query = (
        jnp.einsum("ihqk,ikhc->iqhc", d_scores, keys4, preferred_element_type=jnp.float32) * scale
    )
    d_keys = (
        jnp.einsum("ihqk,iqhc->ikhc", d_scores, query4, preferred_element_type=jnp.float32) * scale
    )
    d_vals = jnp.einsum("ihqk,iqhc->ikhc", probs_low, d_mix4, preferred_element_type=jnp.float32)
    seq = keys4.shape[1]
    d_keys_own, d_vals_own = (
        lax.psum_scatter(
            d_keys.reshape(nimg, seq, width).astype(jnp.bfloat16),
            "ctx",
            scatter_dimension=1,
            tiled=True,
        ).astype(jnp.float32),
        lax.psum_scatter(
            d_vals.reshape(nimg, seq, width).astype(jnp.bfloat16),
            "ctx",
            scatter_dimension=1,
            tiled=True,
        ).astype(jnp.float32),
    )
    d_qkv = jnp.concatenate(
        [
            d_query.reshape(count, width).astype(jnp.bfloat16),
            d_keys_own.reshape(count, width).astype(jnp.bfloat16),
            d_vals_own.reshape(count, width).astype(jnp.bfloat16),
        ],
        axis=1,
    )
    grad_qkv = jnp.einsum("td,te->de", normed, d_qkv, preferred_element_type=jnp.float32)
    d_normed = jnp.dot(d_qkv, w_qkv.T, preferred_element_type=jnp.float32)
    _, norm_one_pull = jax.vjp(norm_rows, x_rows, gain_one)
    d_x_norm, grad_gain_one = norm_one_pull(d_normed)
    grad_tokens = (d_mid + d_x_norm).reshape(nimg, half, width).astype(jnp.bfloat16)
    grad_gain_one, grad_qkv, grad_out, grad_gain_two, grad_router = lax.psum(
        (grad_gain_one, grad_qkv, grad_out, grad_gain_two, grad_router), ("dp", "ctx", "expert")
    )
    grad_in, grad_back = (
        lax.psum(grad_in.astype(jnp.bfloat16), ("dp", "ctx")).astype(jnp.float32),
        lax.psum(grad_back.astype(jnp.bfloat16), ("dp", "ctx")).astype(jnp.float32),
    )
    return (
        mixed,
        grad_tokens,
        grad_gain_one,
        grad_qkv,
        grad_out,
        grad_gain_two,
        grad_router,
        grad_in,
        grad_back,
    )


def solution(mesh):
    placed = (
        P(("dp", "expert"), "ctx", None),
        P(),
        P(),
        P(),
        P(),
        P(),
        P("expert", None, None),
        P("expert", None, None),
        P(("dp", "expert"), "ctx", None, None, None),
        P(("dp", "expert"), None),
        P(("dp", "expert"), "ctx", None),
    )
    sizes = dict(mesh.shape)
    dense = sizes == {"dp": 4, "ctx": 2, "expert": 4}
    return jax.shard_map(
        dense_shards if dense else shards,
        mesh=mesh,
        in_specs=placed,
        out_specs=(
            P(("dp", "expert"), "ctx", None),
            P(("dp", "expert"), "ctx", None),
            P(),
            P(),
            P(),
            P(),
            P(),
            P("expert", None, None),
            P("expert", None, None),
        ),
        check_vma=False,
    )
```

```python
import functools
import jax
import jax.numpy as jnp
from jax import lax
from jax.experimental import pallas as pl
from jax.experimental.pallas import tpu as pltpu
from jax.sharding import PartitionSpec as P

HEADS = 8
HEAD_DIM = 64
TOP = 2
EPS = 1e-06
SCALE = HEAD_DIM ** (-0.5)
F32 = jnp.float32
BF16 = jnp.bfloat16
HELD = pltpu.HBM
HERE = pl.BlockSpec(memory_space=pltpu.VMEM)
BRIEF = pl.CostEstimate(flops=1, bytes_accessed=1, transcendentals=0)
NT = (((1,), (1,)), ((), ()))
TN = (((0,), (0,)), ((), ()))
NN = (((1,), (0,)), ((), ()))


def mm(a, b, dims=NN):
    return lax.dot_general(a, b, dims, preferred_element_type=F32)


def two_halves(a):
    high = a.astype(BF16)
    return high, (a - high.astype(F32)).astype(BF16)


def stats(value):
    center = value - jnp.mean(value, -1, keepdims=True)
    rstd = lax.rsqrt(jnp.mean(center * center, -1, keepdims=True) + EPS)
    return center * rstd, rstd


def norm_vjp(d_value, unit, rstd, gain):
    d_unit = d_value * gain
    return rstd * (
        d_unit
        - jnp.mean(d_unit, -1, keepdims=True)
        - unit * jnp.mean(d_unit * unit, -1, keepdims=True)
    )


def head_pair(value):
    lane = lax.broadcasted_iota(jnp.int32, value.shape, 1)
    first = lane < HEAD_DIM
    return jnp.concatenate(
        [jnp.where(first, value, 0.0), jnp.where(first, 0.0, value)], axis=0
    ).astype(BF16)


def join_pair(value):
    rows = value.shape[0] // 2
    lane = lax.broadcasted_iota(jnp.int32, (rows, value.shape[1]), 1)
    return jnp.where(lane < HEAD_DIM, value[:rows], value[rows:])


def natural(core, mine, theirs):
    return jnp.where(core == 0, mine, theirs), jnp.where(core == 0, theirs, mine)


def attend_kernel(
    meta_ref, own_ref, other_ref, dyown_ref, dyother_ref, mask_ref, g1_ref, wqkv_ref, wout_ref, g2_ref,
    x_ref, dy_ref, normed_ref, qkv_ref, probs_ref, mix_ref, mid_ref, routed_ref,
    x_s, qkv_s, mix_s,
):
    half = own_ref.shape[1]
    width = own_ref.shape[2]
    pair = 2 * HEAD_DIM
    core = meta_ref[3]
    for mine, theirs, ref in ((dyown_ref, dyother_ref, dy_ref), (own_ref, other_ref, x_ref)):
        first, second = natural(core, mine[0].astype(F32), theirs[0].astype(F32))
        x_s[0:half, :] = first
        x_s[half : 2 * half, :] = second
        ref[...] = x_s[...].astype(BF16)
    x = x_s[...]
    unit, _ = stats(x)
    normed = (unit * g1_ref[...]).astype(BF16)
    normed_ref[...] = normed
    qkv_s[...] = mm(normed, wqkv_ref[...])
    qkv_ref[...] = qkv_s[...].astype(BF16)
    image = core * pl.num_programs(0) + pl.program_id(0)
    is_open = mask_ref[pl.ds(image, 1), :] > 0
    for n in range(width // pair):
        at = n * pair
        query = head_pair(qkv_s[:, at : at + pair])
        keys = qkv_s[:, width + at : width + at + pair].astype(BF16)
        vals = qkv_s[:, 2 * width + at : 2 * width + at + pair].astype(BF16)
        scores = jnp.where(is_open, mm(query, keys, NT) * SCALE, -1e9)
        top = jnp.max(scores, -1, keepdims=True)
        expo = jnp.where(is_open, jnp.exp(scores - top), 0.0)
        probs = (expo / jnp.sum(expo, -1, keepdims=True)).astype(BF16)
        probs_ref[0, n] = probs
        mix_s[:, at : at + pair] = join_pair(mm(probs, vals))
    mix = mix_s[...].astype(BF16)
    mix_ref[...] = mix
    mid = x + mm(mix, wout_ref[...])
    mid_ref[...] = mid
    unit, _ = stats(mid)
    routed_ref[...] = (unit * g2_ref[...]).astype(BF16)


def attend(meta, own, other, dy_own, dy_other, mask, g1, wqkv, wout, g2):
    imgs, half, width = own.shape
    imgs //= 2
    seq = 2 * half
    rows = imgs * seq
    pairs = HEADS // 2
    raw = pl.BlockSpec((1, half, width), lambda i, m: (m[3] * imgs + i, 0, 0))
    one = lambda *s: pl.BlockSpec(s, lambda i, m: (i,) + (0,) * (len(s) - 1))
    fix = lambda *s: pl.BlockSpec(s, lambda i, m: (0,) * len(s))
    late = lambda *s: HELD(s, BF16)
    return pl.pallas_call(
        attend_kernel,
        grid_spec=pltpu.PrefetchScalarGridSpec(
            num_scalar_prefetch=1,
            grid=(imgs,),
            in_specs=[
                raw, raw, raw, raw, fix(*mask.shape), fix(1, width),
                fix(width, 3 * width), fix(width, width), fix(1, width),
            ],
            out_specs=[
                one(seq, width), one(seq, width), one(seq, width), one(seq, 3 * width),
                one(1, pairs, 2 * seq, seq), one(seq, width), one(seq, width), one(seq, width),
            ],
            scratch_shapes=[
                pltpu.VMEM((seq, width), F32),
                pltpu.VMEM((seq, 3 * width), F32),
                pltpu.VMEM((seq, width), F32),
            ],
        ),
        out_shape=[
            late(rows, width),
            jax.ShapeDtypeStruct((rows, width), BF16),
            late(rows, width),
            late(rows, 3 * width),
            late(imgs, pairs, 2 * seq, seq),
            late(rows, width),
            HELD((rows, width), F32),
            jax.ShapeDtypeStruct((rows, width), BF16),
        ],
        compiler_params=pltpu.CompilerParams(vmem_limit_bytes=22 << 20),
        cost_estimate=BRIEF,
        name="attend",
    )(meta, *map(held, (own, other, dy_own, dy_other)), mask, g1, held(wqkv), held(wout), g2)


def assemble_kernel(meta_ref, own_ref, other_ref, out_ref, out_s):
    half = own_ref.shape[1]
    first, second = natural(meta_ref[3], own_ref[0].astype(F32), other_ref[0].astype(F32))
    out_s[0:half, :] = first
    out_s[half : 2 * half, :] = second
    out_ref[...] = out_s[...].astype(BF16)


def assemble(meta, own, other):
    imgs, half, width = own.shape
    imgs //= 2
    raw = pl.BlockSpec((1, half, width), lambda i, m: (m[3] * imgs + i, 0, 0))
    return pl.pallas_call(
        assemble_kernel,
        grid_spec=pltpu.PrefetchScalarGridSpec(
            num_scalar_prefetch=1,
            grid=(imgs,),
            in_specs=[raw, raw],
            out_specs=pl.BlockSpec((2 * half, width), lambda i, m: (i, 0)),
            scratch_shapes=[pltpu.VMEM((2 * half, width), F32)],
        ),
        out_shape=jax.ShapeDtypeStruct((imgs * 2 * half, width), BF16),
        compiler_params=pltpu.CompilerParams(vmem_limit_bytes=6 << 20),
        cost_estimate=BRIEF,
        name="assemble",
    )(meta, own, other)


def row_gates(rows, ids, wr):
    logits = mm(wr, rows, NT)
    row = lax.broadcasted_iota(jnp.int32, logits.shape, 0)
    pick = (row.astype(F32) == ids[0:1, :]) | (row.astype(F32) == ids[1:2, :])
    top = jnp.max(jnp.where(pick, logits, -jnp.inf), 0, keepdims=True)
    expo = jnp.where(pick, jnp.exp(logits - top), 0.0)
    return expo / jnp.sum(expo, 0, keepdims=True), row


def padded(count):
    return -(-count // 16) * 16


def expert_kernel(add, local, meta_ref, rows_ref, dy_ref, ids_ref, wr_ref, *rest):
    wi_ref, wb_ref, *rest = rest
    sources = [] if local else [wb_ref]
    if add:
        sources += rest[:2]
        rest = rest[2:]
    act_ref, dpre_ref, dout_ref, made_ref, din_ref, gate_s, made_s, din_s, *rest = rest
    step = pl.program_id(0)
    copies = []
    if sources:
        *rest, sems = rest
        landings = rest[len(rest) - len(sources) :]
        rest = rest[: len(rest) - len(sources)]
        copies = [pltpu.make_async_copy(v, w, sems.at[n]) for n, (v, w) in enumerate(zip(sources, landings))]
    if not local:
        wb_ref = landings[0]
    if add:
        pmade_ref, pdin_ref = landings[-2:]
    count = act_ref.shape[0]
    width = rows_ref.shape[1]
    rows = rows_ref[0:count, :]

    @pl.when(step == 0)
    def _():
        for copy in copies:
            copy.start()
        if ids_ref.shape[0] == 2:
            ids = ids_ref[...].astype(F32)
        else:
            at = padded(count)
            ids = [ids_ref[at : at + 2, :], ids_ref[at + 2 : at + 4, 0 : count - width]]
            ids = jnp.concatenate([v.astype(F32) for v in ids], axis=1)
        gates, row = row_gates(rows, ids, wr_ref[...])
        high, low = two_halves(jnp.where(row == meta_ref[0], gates, 0.0))
        ones = jnp.ones((16, 128), BF16)
        gate_s[...] = mm(high, ones, TN) + mm(low, ones, TN)
        gate = gate_s[:, 0:1]
        dout_ref[...] = (gate * dy_ref[...].astype(F32)).astype(BF16)
        made_s[...] = jnp.zeros_like(made_s)
        din_s[...] = jnp.zeros_like(din_s)

    if local:
        part = wi_ref.shape[2] // PIECES
        at = [pl.multiple_of(((2 * step + s) ^ meta_ref[1]) * part, part) for s in range(2)]
        w_in = jnp.concatenate([wi_ref[0, :, pl.ds(v, part)] for v in at], axis=1)
        w_back = jnp.concatenate([wb_ref[0, pl.ds(v, part), :] for v in at], axis=0)
    else:
        wi_s, wb_s = rest
        part = wi_s.shape[0] // 2
        upper = pl.num_programs(0) // 2

        @pl.when(step == upper)
        def _():
            copies[0].wait()

        for ref, first in ((wi_ref, 0), (wb_ref, upper)):

            @pl.when((step < upper) == (first == 0))
            def _():
                for s in range(2):
                    for h in range(2):
                        at = 2 * (step - first) + s
                        wi_s[h * part : (h + 1) * part, s * part : (s + 1) * part] = ref[at, h]
                        wb_s[s * part : (s + 1) * part, h * part : (h + 1) * part] = ref[at, 2 + h]

        w_in, w_back = wi_s[...], wb_s[...]
    pre = mm(rows, w_in)
    square = pre * pre
    inner = pre * (0.7978845608 + 0.0356774081 * square)
    up = 0.5 + 0.5 * jnp.tanh(inner)
    value = pre * up
    act = value.astype(BF16)
    slope = up + value * (1.0 - up) * (1.5957691216 + 0.2140644488 * square)
    here = pl.ds(pl.multiple_of(step * pre.shape[1], pre.shape[1]), pre.shape[1])
    act_ref[:, here] = act
    made_s[...] += mm(act, w_back)
    dpre = (mm(dout_ref[...], w_back, NT) * slope).astype(BF16)
    dpre_ref[:, here] = dpre
    din_s[...] += mm(dpre, w_in, NT)

    @pl.when(step == pl.num_programs(0) - 1)
    def _():
        gate = gate_s[:, 0:1]
        made = made_s[...].astype(BF16).astype(F32)
        total = gate * made
        d_in = din_s[...]
        high, low = two_halves(made * dy_ref[...].astype(F32))
        ones = jnp.ones((16, made.shape[1]), BF16)
        d_gate = (mm(ones, high, NT) + mm(ones, low, NT))[0:8]
        row = lax.broadcasted_iota(jnp.int32, d_gate.shape, 0)
        d_gate = jnp.where(row == meta_ref[0], d_gate, 0.0)
        tail = padded(count)
        for copy in copies[0 if local else 1 :]:
            copy.wait()
        if add:
            total += pmade_ref[...].astype(F32)
            d_in += pdin_ref[0:count, :].astype(F32)
            d_gate += read_gate(pdin_ref, count)
        made_ref[...] = total.astype(BF16)
        din_ref[0:count, :] = d_in.astype(BF16)
        high = d_gate.astype(BF16).astype(F32)
        value = jnp.concatenate([high, d_gate - high], axis=0).astype(BF16)
        if count > d_in.shape[1]:
            cut = d_in.shape[1]
            din_ref[tail : tail + 16, :] = value[:, :cut]
            din_ref[tail + 16 : tail + 32, 0 : count - cut] = value[:, cut:]
        else:
            din_ref[tail : tail + 16, 0:count] = value


def read_gate(ref, count):
    tail = padded(count)
    width = ref.shape[1]
    value = ref[tail : tail + 16, 0 : min(count, width)].astype(F32)
    if count > width:
        value = jnp.concatenate([value, ref[tail + 16 : tail + 32, 0 : count - width].astype(F32)], axis=1)
    return value[0:8] + value[8:16]


PIECES = 8


def expert(meta, rows, dy, ids, wr, weights, prev=None):
    count = dy.shape[0]
    width = rows.shape[1]
    local = weights[0].ndim == 3
    piece = weights[0].shape[2] // PIECES if local else weights[0].shape[2]
    hidden = PIECES * piece
    steps = PIECES // 2
    deep = padded(count) + 16 * -(-count // width)
    fix = lambda *s: pl.BlockSpec(s, lambda q, m: (0,) * len(s))
    first = prev is None
    away = pl.BlockSpec(memory_space=pl.ANY)
    more = [] if first else [away, away]
    landings = [] if local else [pltpu.VMEM(weights[1].shape, BF16)]
    if not first:
        landings += [pltpu.VMEM((count, width), BF16), pltpu.VMEM((deep, width), BF16)]
    if landings:
        landings.append(pltpu.SemaphoreType.DMA((len(landings),)))
    given = [] if first else [held(v) for v in prev]
    ends = [fix(count, width), fix(deep, width)] if first else [HERE, HERE]
    kept = HELD if first else jax.ShapeDtypeStruct
    return pl.pallas_call(
        functools.partial(expert_kernel, prev is not None, local),
        grid_spec=pltpu.PrefetchScalarGridSpec(
            num_scalar_prefetch=1,
            grid=(steps,),
            in_specs=[HERE, fix(*dy.shape), HERE, HERE, HERE, HERE if local else away, *more],
            out_specs=[HERE] * 3 + ends,
            scratch_shapes=[
                pltpu.VMEM((count, 128), F32),
                pltpu.VMEM((count, width), F32),
                pltpu.VMEM((count, width), F32),
            ]
            + ([] if local else [pltpu.VMEM((width, 2 * piece), BF16), pltpu.VMEM((2 * piece, width), BF16)])
            + landings,
        ),
        out_shape=[
            jax.ShapeDtypeStruct((count, hidden), BF16),
            jax.ShapeDtypeStruct((count, hidden), BF16),
            jax.ShapeDtypeStruct((count, width), BF16),
            kept((count, width), BF16),
            kept((deep, width), BF16),
        ],
        compiler_params=pltpu.CompilerParams(vmem_limit_bytes=20 << 20),
        cost_estimate=BRIEF,
        name="expert",
    )(meta, rows, dy if first else held(dy), ids, wr, weights[0], weights[1] if local else held(weights[1]), *given)


def weight_kernel(n, *refs):
    rows, acts, dpres, douts = (refs[g * n : (g + 1) * n] for g in range(4))
    iown_ref, igive_ref, bown_ref, bgive_ref = refs[4 * n :]
    wide = iown_ref.shape[0] * iown_ref.shape[1]
    here = pl.ds(pl.multiple_of(pl.program_id(0) * wide, wide), wide)
    results = []
    for left, right in ((dpres, rows), (acts, douts)):
        total = 0.0
        for b in range(n):
            count = left[b].shape[0]
            total = total + mm(left[b][:, here], right[b][0:count, :], TN)
        results.append(total.astype(BF16).reshape(iown_ref.shape))
    grad_in, grad_back = results
    first = pl.program_id(0) < pl.num_programs(0) // 2

    @pl.when(first)
    def _():
        iown_ref[...] = grad_in
        bown_ref[...] = grad_back

    @pl.when(jnp.logical_not(first))
    def _():
        igive_ref[...] = grad_in
        bgive_ref[...] = grad_back


def weight_grads(rows, acts, dpres, douts, late=False):
    n = len(rows)
    width = rows[0].shape[1]
    piece = acts[0].shape[1] // PIECES
    steps = PIECES // 2
    own = pl.BlockSpec((2, piece, width), lambda q: (jnp.minimum(q, steps // 2 - 1), 0, 0))
    give = pl.BlockSpec((2, piece, width), lambda q: (jnp.maximum(q - steps // 2, 0), 0, 0))
    return pl.pallas_call(
        functools.partial(weight_kernel, n),
        grid=(steps,),
        in_specs=[HERE] * (4 * n),
        out_specs=[own, give, own, give],
        out_shape=[(HELD if late and g % 2 == 0 else jax.ShapeDtypeStruct)((PIECES // 2, piece, width), BF16) for g in range(4)],
        compiler_params=pltpu.CompilerParams(vmem_limit_bytes=14 << 20),
        cost_estimate=BRIEF,
        name="weight_grads",
    )(*rows, *acts, *dpres, *douts)


def finish_kernel(meta_ref, im_ref, ir_ref, bm_ref, br_ref, gin_ref, gback_ref):
    mine = pl.program_id(0) < pl.num_programs(0) // 2
    flip = meta_ref[1] % 2 == 1
    piece, width = im_ref.shape[1:]
    for m_ref, r_ref, out_ref in ((im_ref, ir_ref, gin_ref), (bm_ref, br_ref, gback_ref)):
        value = jnp.where(mine, m_ref[...], r_ref[...]).astype(F32)
        first = jnp.where(flip, value[1], value[0])
        second = jnp.where(flip, value[0], value[1])
        if out_ref is gin_ref:
            out_ref[0, :, 0:piece] = jnp.transpose(first)
            out_ref[0, :, piece : 2 * piece] = jnp.transpose(second)
        else:
            out_ref[0, 0:piece, :] = first
            out_ref[0, piece : 2 * piece, :] = second


def finish_expert(meta, in_mine, in_recv, back_mine, back_recv):
    upper, piece, width = in_mine.shape
    steps = upper
    own = pl.BlockSpec((2, piece, width), lambda q, m: (jnp.minimum(q, steps // 2 - 1), 0, 0))
    give = pl.BlockSpec((2, piece, width), lambda q, m: (jnp.maximum(q - steps // 2, 0), 0, 0))
    return pl.pallas_call(
        finish_kernel,
        grid_spec=pltpu.PrefetchScalarGridSpec(
            num_scalar_prefetch=1,
            grid=(steps,),
            in_specs=[own, give, own, give],
            out_specs=[
                pl.BlockSpec((1, width, 2 * piece), lambda q, m: (0, 0, q ^ (m[1] // 2))),
                pl.BlockSpec((1, 2 * piece, width), lambda q, m: (0, q ^ (m[1] // 2), 0)),
            ],
        ),
        out_shape=[
            jax.ShapeDtypeStruct((1, width, PIECES * piece), F32),
            jax.ShapeDtypeStruct((1, PIECES * piece, width), F32),
        ],
        compiler_params=pltpu.CompilerParams(vmem_limit_bytes=14 << 20),
        cost_estimate=BRIEF,
        name="finish_expert",
    )(meta, in_mine, in_recv, back_mine, back_recv)


def split_halves(core, whole_ref, own_ref, other_ref):
    imgs, half, _ = own_ref.shape
    for i in range(imgs):
        at = 2 * half * i
        first, second = whole_ref[at : at + half, :], whole_ref[at + half : at + 2 * half, :]
        mine, theirs = natural(core, first, second)
        own_ref[i] = mine.astype(BF16)
        other_ref[i] = theirs.astype(BF16)


def back_kernel(
    meta_ref, din0_ref, din1_ref,
    ids_ref, dy_ref, mid_ref, routed_ref, wr_ref, g2_ref, mix_ref, wout_ref,
    probs_ref, qkv_ref, x_ref, normed_ref, wqkv_ref, g1_ref,
    own_ref, other_ref, gown_ref, ggive_ref,
    dmid_s, dmix_s, dqkv_s, tok_s, grad_s, small_s,
):
    step = pl.program_id(0)
    imgs = pl.num_programs(0)
    seq = qkv_ref.shape[0]
    width = x_ref.shape[1]
    half = seq // 2
    pair = 2 * HEAD_DIM
    rows = x_ref.shape[0]

    @pl.when(step == 0)
    def _():
        routed = routed_ref[...]
        wr = wr_ref[...]
        gates, _ = row_gates(routed, ids_ref[...].astype(F32), wr)
        d_gate = read_gate(din0_ref, rows) + read_gate(din1_ref, rows)
        d_gate = jnp.concatenate([d_gate, jnp.zeros_like(d_gate)], axis=0)
        d_logits = gates * (d_gate - jnp.sum(gates * d_gate, 0, keepdims=True))
        high, low = two_halves(d_logits)
        small_s[...] = jnp.zeros_like(small_s)
        small_s[0:16, :] = mm(high, routed) + mm(low, routed)
        d_routed = din0_ref[0:rows, :].astype(F32) + din1_ref[0:rows, :].astype(F32)
        d_routed = d_routed + mm(high, wr, TN) + mm(low, wr, TN)
        unit, rstd = stats(mid_ref[...])
        small_s[16:17, :] = jnp.sum(d_routed * unit, 0, keepdims=True)
        d_mid = dy_ref[...].astype(F32) + norm_vjp(d_routed, unit, rstd, g2_ref[...])
        dmid_s[...] = d_mid
        d_branch = d_mid.astype(BF16)
        grad_s[:, 3 * width : 4 * width] = mm(mix_ref[...], d_branch, TN).astype(BF16)
        dmix_s[...] = mm(d_branch, wout_ref[...], NT)

    base = pl.multiple_of(step * seq, 8)
    for n in range(width // pair):
        at = n * pair
        d_mix = head_pair(dmix_s[pl.ds(base, seq), at : at + pair])
        query = head_pair(qkv_ref[:, at : at + pair].astype(F32))
        keys = qkv_ref[:, width + at : width + at + pair]
        vals = qkv_ref[:, 2 * width + at : 2 * width + at + pair]
        low = probs_ref[0, n]
        probs = low.astype(F32)
        d_probs = mm(d_mix, vals, NT)
        d_scores = probs * (d_probs - jnp.sum(probs * d_probs, -1, keepdims=True))
        d_scores = d_scores.astype(BF16)
        d_query = join_pair(mm(d_scores, keys)) * SCALE
        d_keys = mm(d_scores, query, TN) * SCALE
        d_vals = mm(low, d_mix, TN)
        dqkv_s[pl.ds(base, seq), at : at + pair] = d_query.astype(BF16)
        dqkv_s[pl.ds(base, seq), width + at : width + at + pair] = d_keys.astype(BF16)
        dqkv_s[pl.ds(base, seq), 2 * width + at : 2 * width + at + pair] = d_vals.astype(BF16)

    @pl.when(step == imgs - 1)
    def _():
        d_qkv = dqkv_s[...]
        grad_s[:, : 3 * width] = mm(normed_ref[...], d_qkv, TN).astype(BF16)
        d_normed = mm(d_qkv, wqkv_ref[...], NT)
        unit, rstd = stats(x_ref[...].astype(F32))
        small_s[17:18, :] = jnp.sum(d_normed * unit, 0, keepdims=True)
        grad_s[:, 4 * width :] = jnp.transpose(small_s[...]).astype(BF16)
        tok_s[...] = dmid_s[...] + norm_vjp(d_normed, unit, rstd, g1_ref[...])
        split_halves(meta_ref[3], tok_s, own_ref, other_ref)
        part = width // SHARES
        for r in range(SHARES):
            ref = gown_ref if r < SHARES // 2 else ggive_ref
            to = (r % (SHARES // 2)) * part
            there = pl.multiple_of((r ^ meta_ref[2]) * part, part)
            ref[to : to + part, :] = grad_s[pl.ds(there, part), :]


SHARES = 32


def attend_back(meta, dins, ids, dy, mid, routed, wr, g2, mix, wout, probs, qkv, x, normed, wqkv, g1):
    imgs = probs.shape[0]
    rows, width = x.shape
    seq = rows // imgs
    pairs = HEADS // 2
    wide = 4 * width + 128
    fix = lambda *s: pl.BlockSpec(s, lambda i, m: (0,) * len(s))
    return pl.pallas_call(
        back_kernel,
        grid_spec=pltpu.PrefetchScalarGridSpec(
            num_scalar_prefetch=1,
            grid=(imgs,),
            in_specs=[fix(*a.shape) for a in dins] + [
                fix(2, rows), fix(rows, width), fix(rows, width), fix(rows, width),
                fix(16, width), fix(1, width), fix(rows, width), fix(width, width),
                pl.BlockSpec((1, pairs, 2 * seq, seq), lambda i, m: (i, 0, 0, 0)),
                pl.BlockSpec((seq, 3 * width), lambda i, m: (i, 0)),
                fix(rows, width), fix(rows, width), fix(width, 3 * width), fix(1, width),
            ],
            out_specs=[
                fix(imgs, seq // 2, width), fix(imgs, seq // 2, width),
                fix(width // 2, wide), fix(width // 2, wide),
            ],
            scratch_shapes=[
                pltpu.VMEM((rows, width), F32),
                pltpu.VMEM((rows, width), F32),
                pltpu.VMEM((rows, 3 * width), BF16),
                pltpu.VMEM((rows, width), F32),
                pltpu.VMEM((width, wide), BF16),
                pltpu.VMEM((128, width), F32),
            ],
        ),
        out_shape=[
            jax.ShapeDtypeStruct((imgs, seq // 2, width), BF16),
            jax.ShapeDtypeStruct((imgs, seq // 2, width), BF16),
            jax.ShapeDtypeStruct((width // 2, wide), BF16),
            jax.ShapeDtypeStruct((width // 2, wide), BF16),
        ],
        compiler_params=pltpu.CompilerParams(vmem_limit_bytes=32 << 20),
        cost_estimate=BRIEF,
        name="attend_back",
    )(meta, *dins, ids, dy, mid, routed, wr, g2, mix, wout, probs, qkv, x, normed, wqkv, g1)


def shared_kernel(meta_ref, mine_ref, recv_ref, gqkv_ref, gout_ref, small_ref, all_s):
    upper, wide = mine_ref.shape
    width = 2 * upper
    part = width // SHARES
    all_s[0:upper, :] = mine_ref[...]
    all_s[upper:width, :] = recv_ref[...]
    for i in range(SHARES):
        there = pl.multiple_of((i ^ meta_ref[2]) * part, part)
        value = all_s[pl.ds(there, part), :].astype(F32)
        at = i * part
        gqkv_ref[at : at + part, :] = value[:, : 3 * width]
        gout_ref[at : at + part, :] = value[:, 3 * width : 4 * width]
        small_ref[at : at + part, :] = value[:, 4 * width :]


def finish_shared(meta, mine, recv):
    upper, wide = mine.shape
    width = 2 * upper
    fix = lambda *s: pl.BlockSpec(s, lambda i, m: (0,) * len(s))
    return pl.pallas_call(
        shared_kernel,
        grid_spec=pltpu.PrefetchScalarGridSpec(
            num_scalar_prefetch=1,
            grid=(1,),
            in_specs=[fix(upper, wide), fix(upper, wide)],
            out_specs=[fix(width, 3 * width), fix(width, width), fix(width, wide - 4 * width)],
            scratch_shapes=[pltpu.VMEM((width, wide), BF16)],
        ),
        out_shape=[
            jax.ShapeDtypeStruct((width, 3 * width), F32),
            jax.ShapeDtypeStruct((width, width), F32),
            jax.ShapeDtypeStruct((width, wide - 4 * width), F32),
        ],
        compiler_params=pltpu.CompilerParams(vmem_limit_bytes=16 << 20),
        cost_estimate=BRIEF,
        name="finish_shared",
    )(meta, mine, recv)


def combine_kernel(meta_ref, mid_ref, a_ref, b_ref, own_ref, other_ref, s_ref):
    s_ref[...] = mid_ref[...] + (a_ref[...].astype(F32) + b_ref[...].astype(F32))
    split_halves(meta_ref[3], s_ref, own_ref, other_ref)


def combine(meta, mid, parts, imgs):
    rows, width = mid.shape
    seq = rows // imgs
    spec = pl.BlockSpec((seq, width), lambda i, m: (i, 0))
    out = pl.BlockSpec((1, seq // 2, width), lambda i, m: (i, 0, 0))
    shape = jax.ShapeDtypeStruct((imgs, seq // 2, width), BF16)
    return pl.pallas_call(
        combine_kernel,
        grid_spec=pltpu.PrefetchScalarGridSpec(
            num_scalar_prefetch=1,
            grid=(imgs,),
            in_specs=[spec] * 3,
            out_specs=[out, out],
            scratch_shapes=[pltpu.VMEM((seq, width), F32)],
        ),
        out_shape=[shape, shape],
        compiler_params=pltpu.CompilerParams(vmem_limit_bytes=8 << 20),
        cost_estimate=BRIEF,
        name="combine",
    )(meta, mid, *parts)


def place_kernel(meta_ref, a_own_ref, a_recv_ref, b_own_ref, b_recv_ref, a_ref, b_ref):
    imgs = pl.num_programs(0) // 2
    mine = pl.program_id(0) // imgs == meta_ref[3]
    a_ref[...] = jnp.where(mine, a_own_ref[...], a_recv_ref[...])
    b_ref[...] = jnp.where(mine, b_own_ref[...], b_recv_ref[...])


def place(meta, *arrays):
    imgs, half, width = arrays[0].shape
    spec = pl.BlockSpec((1, half, width), lambda j, m: (j % imgs, 0, 0))
    out = pl.BlockSpec((1, half, width), lambda j, m: (j, 0, 0))
    shape = jax.ShapeDtypeStruct((2 * imgs, half, width), BF16)
    return pl.pallas_call(
        place_kernel,
        grid_spec=pltpu.PrefetchScalarGridSpec(
            num_scalar_prefetch=1, grid=(2 * imgs,), in_specs=[spec] * 4, out_specs=[out, out]
        ),
        out_shape=[shape, shape],
        compiler_params=pltpu.CompilerParams(vmem_limit_bytes=4 << 20),
        cost_estimate=BRIEF,
        name="place",
    )(meta, *arrays)


def pack_kernel(meta_ref, wi_ref, wb_ref, out_ref):
    part = out_ref.shape[1]
    for h in range(2):
        at = slice(h * part, (h + 1) * part)
        out_ref[h] = wi_ref[0, at, :]
        out_ref[2 + h] = wb_ref[0, :, at]


def pack_piece(meta, w_in, w_back):
    width, hidden = w_in.shape[1:]
    piece = hidden // PIECES
    return pl.pallas_call(
        pack_kernel,
        grid_spec=pltpu.PrefetchScalarGridSpec(
            num_scalar_prefetch=1,
            grid=(1,),
            in_specs=[
                pl.BlockSpec((1, width, piece), lambda i, m: (0, 0, m[1])),
                pl.BlockSpec((1, piece, width), lambda i, m: (0, m[1], 0)),
            ],
            out_specs=pl.BlockSpec((4, piece, piece), lambda i, m: (0, 0, 0)),
        ),
        out_shape=jax.ShapeDtypeStruct((4, piece, piece), BF16),
        compiler_params=pltpu.CompilerParams(vmem_limit_bytes=4 << 20),
        cost_estimate=BRIEF,
        name="pack_piece",
    )(meta, held(w_in), held(w_back))


def merge_kernel(plan, *refs):
    refs = list(refs)
    takes = [[[(refs.pop(0), at) for at in views] for views in groups] for groups, _, _ in plan]
    for groups, (_, axis, cuts) in zip(takes, plan):
        outs = [refs.pop(0) for _ in cuts]
        if axis is not None:
            size = groups[0][0][0].shape[axis]
            for k, (ref, _) in enumerate(groups[0]):
                at = slice(k * size, (k + 1) * size)
                outs[0][(slice(None),) * axis + (at,)] = ref[...]
            continue
        for g, take in enumerate(groups):
            total = sum(ref[at].astype(F32) for ref, at in take).astype(BF16)
            for out, cut in zip(outs, cuts):
                if len(groups) > 1:
                    out[g] = total[cut]
                else:
                    out[...] = total[cut]


def merge(*items):
    plan, shapes, arrays = [], [], []
    for groups, axis, cuts in items:
        head = groups[0][0]
        shape = jax.eval_shape(lambda v: v[head[1]], head[0]).shape if isinstance(head, tuple) else head.shape
        first = jax.ShapeDtypeStruct(shape, BF16)
        if axis is not None:
            cuts = [None]
            shape = list(first.shape)
            shape[axis] *= len(groups[0])
            shapes.append(jax.ShapeDtypeStruct(tuple(shape), BF16))
        else:
            lead = (len(groups),) if len(groups) > 1 else ()
            shapes += [
                jax.ShapeDtypeStruct(lead + jax.eval_shape(lambda v, c=c: v[c], first).shape, BF16) for c in cuts
            ]
        pairs = [[v if isinstance(v, tuple) else (v, ...) for v in g] for g in groups]
        plan.append(([[at for _, at in g] for g in pairs], axis, cuts))
        arrays += [v for g in pairs for v, _ in g]
    return pl.pallas_call(
        functools.partial(merge_kernel, plan),
        out_shape=shapes,
        compiler_params=pltpu.CompilerParams(vmem_limit_bytes=16 << 20),
        cost_estimate=BRIEF,
        name="merge",
    )(*arrays)


def held(value):
    return pltpu.with_memory_space_constraint(value, pltpu.HBM)


SWAP = [(0, 1), (1, 0)]


def xor(k, n=4):
    return [(i, i ^ k) for i in range(n)]


def send(value, axis, pairs):
    return lax.ppermute(value, axis, pairs)


def add_low(a, b):
    return (a.astype(F32) + b.astype(F32)).astype(BF16)


def after(value, *earlier):
    return lax.optimization_barrier((value, *earlier))[0]


def tie(*values):
    return lax.optimization_barrier(values)


def fan(value, axis):
    rows = value.shape[0] // 4
    return [send(value[k * rows : (k + 1) * rows], axis, xor(k)) for k in (1, 2, 3)]


def add_fan(value, got):
    total = value[: value.shape[0] // 4].astype(F32)
    for v in got:
        total = total + v.astype(F32)
    return total.astype(BF16)


def dense_shards(
    tokens, gain_one, w_qkv, w_out, gain_two, w_router, w_in, w_back, route_ids, key_mask, cotangent
):
    nimg, half, width = tokens.shape
    imgs = nimg // 2
    rows = imgs * 2 * half
    experts = w_router.shape[1]
    piece = w_in.shape[2] // PIECES
    core = lax.axis_index("ctx")
    z = lax.axis_index("expert")
    me = core * 4 + lax.axis_index("dp")
    meta = jnp.stack([z, me, me * 4 + z, core]).astype(jnp.int32)
    meta_pair = jnp.stack([z ^ 2, me, me * 4 + z, core]).astype(jnp.int32)
    far = lambda v: send(v, "expert", xor(1))
    swap = lambda v: send(v, "ctx", SWAP)

    pack = pack_piece(meta, w_in, w_back)
    codes = after(route_ids, pack).reshape(nimg, half, TOP)
    codes = codes[..., 0] + experts * codes[..., 1]
    tok_other, dy_other, codes_other = swap(tokens), swap(cotangent), swap(codes)
    first = jnp.where(core == 0, codes, codes_other)
    second = jnp.where(core == 0, codes_other, codes)
    codes = lax.dynamic_slice_in_dim(jnp.concatenate([first, second], 1), core * imgs, imgs, 0)
    codes = codes.reshape(1, rows)
    ids = jnp.concatenate([codes % experts, codes // experts], 0)
    wide = jnp.pad(ids, ((0, 0), (0, 2 * width - rows))).reshape(TOP, 2, width)
    ids_pack = jnp.concatenate([wide[:, 0], wide[:, 1]], 0).astype(BF16)
    ids_pack = jnp.pad(ids_pack, ((padded(rows) - rows, 12), (0, 0)))
    wr = jnp.pad(w_router.T, ((0, 16 - experts), (0, 0)))
    g1, g2 = gain_one[None, :], gain_two[None, :]

    far_raw, pack = far(after(cotangent, pack)), send(pack, "expert", xor(2))
    x_rows, dy, normed, qkv, probs, mix, mid, routed = attend(
        meta, tokens, tok_other, cotangent, dy_other, key_mask, g1, w_qkv, w_out, g2
    )
    own_one = expert(meta, routed, dy, ids, wr, (w_in, w_back))
    far_rows = jnp.concatenate([routed, ids_pack], 0)
    pack, wr_far = after(pack, routed), after(wr, own_one[2])

    packs = [pack] + [send(pack, "dp", xor(k)) for k in (1, 2, 3)]
    far_rows = far(far_rows)
    far_raw = after(far_raw, own_one[2])
    far_dy = assemble(meta, far_raw, swap(far_raw))
    far_one = expert(meta, far_rows, far_dy, far_rows, wr_far, (w_in, w_back))
    *packs, wr_far = tie(*packs, after(wr, far_one[2]))
    packs = jnp.stack(packs)
    pair = [packs, swap(packs)]
    grads = weight_grads([routed, far_rows], *zip(own_one[:3], far_one[:3]), late=True)
    wr_far = after(wr_far, grads[0])

    far_two = expert(meta_pair, far_rows, far_dy, far_rows, wr_far, pair, far_one[3:])
    head, tail = slice(0, 2), slice(2, 4)
    even, odd = [(slice(None), slice(k, k + 1)) for k in (0, 1)]
    square = lambda v: v.reshape(2, 2, piece, width)

    def across(a, a_give, b, b_give):
        return merge(
            ([[a, swap(a_give)]], None, [head, tail]), ([[square(b), square(swap(b_give))]], None, [even, odd])
        )

    one = across(*grads)
    wr_own, *one = tie(after(wr, far_two[2]), *one)
    far_din, far_made = far_two[4], far_two[3]

    y_way, x_way = ("dp", xor(2)), ("dp", xor(1))
    own_two = expert(meta_pair, routed, dy, ids, wr_own, pair, own_one[3:])
    grads = weight_grads([routed, far_rows], *zip(own_two[:3], far_two[:3]))
    din_far, a_got, b_got, *grads = tie(far(far_din), send(one[1], *y_way), send(one[3], *x_way), *grads)
    a_one, b_one = [one[0], a_got], [one[2], b_got]

    two = tie(*across(*grads))

    a_two, b_two = [two[0], send(two[1], *y_way)], [two[2], send(two[3], *x_way)]
    far_made = far(after(far_made, din_far))
    tok_own, tok_give, shared, shared_give = attend_back(
        meta, [after(own_two[4], *two), din_far], ids, dy, mid, routed, wr, g2, mix, w_out, probs, qkv, x_rows, normed, w_qkv, g1
    )
    halves = [slice(0, 1), slice(1, 2)]
    line = lambda v: v.reshape(2, piece, width)
    flat = lambda group: [line(v) for v in group]
    one, one_give, two, two_give, far_made, shared, shared_give, tok_give = tie(
        *merge(([a_one, flat(b_one)], None, halves), ([a_two, flat(b_two)], None, halves)),
        far_made,
        shared,
        shared_give,
        tok_give,
    )
    mix_own, mix_give = combine(meta, mid, [own_two[3], far_made], imgs)
    quarters = lambda n: [slice(k * n, (k + 1) * n) for k in range(4)]
    everything = [slice(None)]
    second = lambda give: [send(give[0], *x_way), send(give[1], *y_way)]
    got = second(two_give)
    two, *shared, tok_got, mix_got = tie(
        *merge(
            ([[(two, 0), got[0]], [(two, 1), got[1]]], None, everything),
            ([[shared, swap(shared_give)]], None, quarters(width // 8)),
        ),
        swap(tok_give),
        swap(mix_give),
    )
    spread = lambda parts, axis: [send(v, axis, xor(k)) for k, v in zip((1, 2, 3), parts)]
    mixed, grad_tokens = place(meta, mix_own, mix_got, tok_own, tok_got)
    got, cross = second(one_give), send(two, "expert", xor(2))
    a, b, *shared, mixed, grad_tokens = tie(
        *merge(
            ([[(one, 0), got[0], (cross, 0)]], None, everything),
            ([[(one, 1), got[1], (cross, 1)]], None, everything),
            ([[shared[0], *spread(shared[1:], "dp")]], None, quarters(width // 32)),
        ),
        mixed,
        grad_tokens,
    )
    b = b[None]
    a, b, shared = tie(
        *merge(
            ([[a, send(a, *x_way)]], 0, None),
            ([[b, send(b, *y_way)]], 0, None),
            ([[shared[0], *spread(shared[1:], "expert")]], None, everything),
        )
    )
    a, b, shared = tie(
        *merge(
            ([[a, send(a, *y_way)]], 0, None),
            ([[b, send(b, *x_way)]], 1, None),
            ([[shared, *spread([shared] * 3, "expert")]], 0, None),
        )
    )
    b = b.reshape(a.shape)
    grad_in, grad_back = finish_expert(meta, a, swap(a), b, swap(b))
    (shared,) = merge(([[after(shared, grad_in, grad_back), *spread([shared] * 3, "dp")]], 0, None))
    grad_qkv, grad_out, small = finish_shared(meta, shared, swap(shared))
    return (
        mixed,
        grad_tokens,
        small[:, 17],
        grad_qkv,
        grad_out,
        small[:, 16],
        small[:, :experts],
        grad_in,
        grad_back,
    )


def norm_rows(value, gain):
    center = value - jnp.mean(value, -1, keepdims=True)
    spread = jnp.mean(center * center, -1, keepdims=True)
    return center * lax.rsqrt(spread + 1e-06) * gain


def smooth_gelu(value):
    return 0.5 * value * (1.0 + jnp.tanh(0.7978845608 * (value + 0.044715 * value * value * value)))


def forward(tokens, gain_one, w_qkv, w_out, gain_two, w_router, w_in, w_back, flat_ids, live):
    nimg, half, width = tokens.shape
    count = nimg * half
    experts_all = w_router.shape[1]
    capacity = max(2, 2 * TOP * count // experts_all)
    x_rows = tokens.astype(jnp.float32).reshape(count, width)
    normed = norm_rows(x_rows, gain_one).astype(jnp.bfloat16)
    qkv = jnp.dot(normed, w_qkv, preferred_element_type=jnp.float32).astype(jnp.bfloat16)
    qkv = qkv.reshape(nimg, half, 3 * width)
    query = qkv[..., :width]
    keys_local = qkv[..., width : 2 * width]
    vals_local = qkv[..., 2 * width :]
    keys, vals = (
        lax.all_gather(keys_local, "ctx", axis=1, tiled=True),
        lax.all_gather(vals_local, "ctx", axis=1, tiled=True),
    )
    seq = keys.shape[1]
    query4 = query.reshape(nimg, half, HEADS, HEAD_DIM)
    keys4 = keys.reshape(nimg, seq, HEADS, HEAD_DIM)
    vals4 = vals.reshape(nimg, seq, HEADS, HEAD_DIM)
    scale = HEAD_DIM ** (-0.5)
    scores = (
        jnp.einsum("iqhc,ikhc->ihqk", query4, keys4, preferred_element_type=jnp.float32) * scale
    )
    open_keys = live[:, None, None, :]
    masked = jnp.where(open_keys, scores, -1000000000.0)
    topmost = jnp.max(masked, -1, keepdims=True)
    expo = jnp.where(open_keys, jnp.exp(masked - topmost), 0.0)
    probs = expo / jnp.sum(expo, -1, keepdims=True)
    probs_low = probs.astype(jnp.bfloat16)
    mix = jnp.einsum("ihqk,ikhc->iqhc", probs_low, vals4, preferred_element_type=jnp.float32)
    mix = mix.reshape(count, width).astype(jnp.bfloat16)
    mid = x_rows + jnp.dot(mix, w_out, preferred_element_type=jnp.float32)
    routed = norm_rows(mid, gain_two).astype(jnp.bfloat16)
    logits = jnp.dot(routed, w_router, preferred_element_type=jnp.float32)
    pick = flat_ids[:, :, None] == jnp.arange(experts_all, dtype=jnp.int32)[None, None, :]
    chosen = jnp.sum(jnp.where(pick, logits[:, None, :], 0.0), -1)
    expo_gate = jnp.exp(chosen)
    gates = expo_gate / jnp.sum(expo_gate, -1, keepdims=True)
    pair_ids = flat_ids.reshape(-1)
    hits = (pair_ids[:, None] == jnp.arange(experts_all, dtype=jnp.int32)[None, :]).astype(
        jnp.int32
    )
    before = jnp.cumsum(hits, 0) - hits
    slots = jnp.sum(before * hits, 1)
    where_rows = pair_ids * capacity + slots
    sent = jnp.repeat(routed, TOP, axis=0)
    buffer = jnp.zeros((experts_all * capacity, width), jnp.bfloat16).at[where_rows].set(sent)
    buffer = buffer.reshape(experts_all, capacity, width)
    arrived = lax.all_to_all(buffer, "expert", split_axis=0, concat_axis=1, tiled=True)
    pre = jnp.einsum("erd,edf->erf", arrived, w_in, preferred_element_type=jnp.float32)
    act = smooth_gelu(pre).astype(jnp.bfloat16)
    made = jnp.einsum("erf,efd->erd", act, w_back, preferred_element_type=jnp.float32).astype(
        jnp.bfloat16
    )
    returned = lax.all_to_all(made, "expert", split_axis=1, concat_axis=0, tiled=True)
    picked = returned.reshape(experts_all * capacity, width)[where_rows].reshape(count, TOP, width)
    output = mid + jnp.sum(gates[:, :, None] * picked.astype(jnp.float32), 1)
    return (
        x_rows,
        normed,
        query4,
        keys4,
        vals4,
        probs,
        probs_low,
        mix,
        mid,
        routed,
        pick,
        gates,
        where_rows,
        arrived,
        pre,
        act,
        picked,
        output,
        capacity,
    )


def shards(
    tokens, gain_one, w_qkv, w_out, gain_two, w_router, w_in, w_back, route_ids, key_mask, cotangent
):
    nimg, half, width = tokens.shape
    count = nimg * half
    experts_all = w_router.shape[1]
    flat_ids = route_ids.reshape(count, TOP)
    live = key_mask > 0
    state = forward(
        tokens, gain_one, w_qkv, w_out, gain_two, w_router, w_in, w_back, flat_ids, live
    )
    mixed = state[17].reshape(nimg, half, width).astype(jnp.bfloat16)
    state = forward(
        tokens, gain_one, w_qkv, w_out, gain_two, w_router, w_in, w_back, flat_ids, live
    )
    (
        x_rows,
        normed,
        query4,
        keys4,
        vals4,
        probs,
        probs_low,
        mix,
        mid,
        routed,
        pick,
        gates,
        where_rows,
        arrived,
        pre,
        act,
        picked,
        output,
        capacity,
    ) = state
    scale = HEAD_DIM ** (-0.5)
    high = lax.Precision.HIGHEST
    grad_y = cotangent.astype(jnp.float32).reshape(count, width)
    grad_gate = jnp.sum(grad_y[:, None, :] * picked.astype(jnp.float32), -1)
    d_out = (
        (gates[:, :, None] * grad_y[:, None, :]).astype(jnp.bfloat16).reshape(count * TOP, width)
    )
    grad_buffer = jnp.zeros((experts_all * capacity, width), jnp.bfloat16).at[where_rows].set(d_out)
    grad_buffer = grad_buffer.reshape(experts_all, capacity, width)
    grad_arrived = lax.all_to_all(grad_buffer, "expert", split_axis=0, concat_axis=1, tiled=True)
    d_act = jnp.einsum("erd,efd->erf", grad_arrived, w_back, preferred_element_type=jnp.float32)
    grad_back = jnp.einsum("erf,erd->efd", act, grad_arrived, preferred_element_type=jnp.float32)
    _, gelu_pull = jax.vjp(smooth_gelu, pre)
    d_pre = gelu_pull(d_act)[0].astype(jnp.bfloat16)
    grad_in = jnp.einsum("erd,erf->edf", arrived, d_pre, preferred_element_type=jnp.float32)
    d_in = jnp.einsum("erf,edf->erd", d_pre, w_in, preferred_element_type=jnp.float32).astype(
        jnp.bfloat16
    )
    grad_returned = lax.all_to_all(d_in, "expert", split_axis=1, concat_axis=0, tiled=True)
    grad_rows = grad_returned.reshape(experts_all * capacity, width)[where_rows].reshape(
        count, TOP, width
    )
    d_experts = jnp.sum(grad_rows.astype(jnp.float32), 1)
    d_chosen = gates * (grad_gate - jnp.sum(gates * grad_gate, -1, keepdims=True))
    d_logits = jnp.sum(jnp.where(pick, d_chosen[:, :, None], 0.0), 1)
    grad_router = jnp.dot(routed.astype(jnp.float32).T, d_logits, precision=high)
    d_routed = d_experts + jnp.dot(d_logits, w_router.astype(jnp.float32).T, precision=high)
    _, norm_two_pull = jax.vjp(norm_rows, mid, gain_two)
    d_mid_norm, grad_gain_two = norm_two_pull(d_routed)
    d_mid = grad_y + d_mid_norm
    d_branch = d_mid.astype(jnp.bfloat16)
    grad_out = jnp.einsum("td,te->de", mix, d_branch, preferred_element_type=jnp.float32)
    d_mix = jnp.dot(d_branch, w_out.T, preferred_element_type=jnp.float32).astype(jnp.bfloat16)
    d_mix4 = d_mix.reshape(nimg, half, HEADS, HEAD_DIM)
    d_probs = jnp.einsum("iqhc,ikhc->ihqk", d_mix4, vals4, preferred_element_type=jnp.float32)
    d_scores = (probs * (d_probs - jnp.sum(probs * d_probs, -1, keepdims=True))).astype(
        jnp.bfloat16
    )
    d_query = (
        jnp.einsum("ihqk,ikhc->iqhc", d_scores, keys4, preferred_element_type=jnp.float32) * scale
    )
    d_keys = (
        jnp.einsum("ihqk,iqhc->ikhc", d_scores, query4, preferred_element_type=jnp.float32) * scale
    )
    d_vals = jnp.einsum("ihqk,iqhc->ikhc", probs_low, d_mix4, preferred_element_type=jnp.float32)
    seq = keys4.shape[1]
    d_keys_own, d_vals_own = (
        lax.psum_scatter(
            d_keys.reshape(nimg, seq, width).astype(jnp.bfloat16),
            "ctx",
            scatter_dimension=1,
            tiled=True,
        ).astype(jnp.float32),
        lax.psum_scatter(
            d_vals.reshape(nimg, seq, width).astype(jnp.bfloat16),
            "ctx",
            scatter_dimension=1,
            tiled=True,
        ).astype(jnp.float32),
    )
    d_qkv = jnp.concatenate(
        [
            d_query.reshape(count, width).astype(jnp.bfloat16),
            d_keys_own.reshape(count, width).astype(jnp.bfloat16),
            d_vals_own.reshape(count, width).astype(jnp.bfloat16),
        ],
        axis=1,
    )
    grad_qkv = jnp.einsum("td,te->de", normed, d_qkv, preferred_element_type=jnp.float32)
    d_normed = jnp.dot(d_qkv, w_qkv.T, preferred_element_type=jnp.float32)
    _, norm_one_pull = jax.vjp(norm_rows, x_rows, gain_one)
    d_x_norm, grad_gain_one = norm_one_pull(d_normed)
    grad_tokens = (d_mid + d_x_norm).reshape(nimg, half, width).astype(jnp.bfloat16)
    grad_gain_one, grad_qkv, grad_out, grad_gain_two, grad_router = lax.psum(
        (grad_gain_one, grad_qkv, grad_out, grad_gain_two, grad_router), ("dp", "ctx", "expert")
    )
    grad_in, grad_back = (
        lax.psum(grad_in.astype(jnp.bfloat16), ("dp", "ctx")).astype(jnp.float32),
        lax.psum(grad_back.astype(jnp.bfloat16), ("dp", "ctx")).astype(jnp.float32),
    )
    return (
        mixed,
        grad_tokens,
        grad_gain_one,
        grad_qkv,
        grad_out,
        grad_gain_two,
        grad_router,
        grad_in,
        grad_back,
    )


def solution(mesh):
    placed = (
        P(("dp", "expert"), "ctx", None),
        P(),
        P(),
        P(),
        P(),
        P(),
        P("expert", None, None),
        P("expert", None, None),
        P(("dp", "expert"), "ctx", None, None, None),
        P(("dp", "expert"), None),
        P(("dp", "expert"), "ctx", None),
    )
    sizes = dict(mesh.shape)
    dense = sizes == {"dp": 4, "ctx": 2, "expert": 4}
    return jax.shard_map(
        dense_shards if dense else shards,
        mesh=mesh,
        in_specs=placed,
        out_specs=(
            P(("dp", "expert"), "ctx", None),
            P(("dp", "expert"), "ctx", None),
            P(),
            P(),
            P(),
            P(),
            P(),
            P("expert", None, None),
            P("expert", None, None),
        ),
        check_vma=False,
    )
```

```python
import functools
import jax
import jax.numpy as jnp
from jax import lax
from jax.experimental import pallas as pl
from jax.experimental.pallas import tpu as pltpu
from jax.sharding import PartitionSpec as P

HEADS = 8
HEAD_DIM = 64
TOP = 2
EPS = 1e-06
SCALE = HEAD_DIM ** (-0.5)
F32 = jnp.float32
BF16 = jnp.bfloat16
HELD = pltpu.HBM
HERE = pl.BlockSpec(memory_space=pltpu.VMEM)
BRIEF = pl.CostEstimate(flops=1, bytes_accessed=1, transcendentals=0)
NT = (((1,), (1,)), ((), ()))
TN = (((0,), (0,)), ((), ()))
NN = (((1,), (0,)), ((), ()))


def mm(a, b, dims=NN):
    return lax.dot_general(a, b, dims, preferred_element_type=F32)


def two_halves(a):
    high = a.astype(BF16)
    return high, (a - high.astype(F32)).astype(BF16)


def stats(value):
    center = value - jnp.mean(value, -1, keepdims=True)
    rstd = lax.rsqrt(jnp.mean(center * center, -1, keepdims=True) + EPS)
    return center * rstd, rstd


def norm_vjp(d_value, unit, rstd, gain):
    d_unit = d_value * gain
    return rstd * (
        d_unit
        - jnp.mean(d_unit, -1, keepdims=True)
        - unit * jnp.mean(d_unit * unit, -1, keepdims=True)
    )


def head_pair(value):
    lane = lax.broadcasted_iota(jnp.int32, value.shape, 1)
    first = lane < HEAD_DIM
    return jnp.concatenate(
        [jnp.where(first, value, 0.0), jnp.where(first, 0.0, value)], axis=0
    ).astype(BF16)


def join_pair(value):
    rows = value.shape[0] // 2
    lane = lax.broadcasted_iota(jnp.int32, (rows, value.shape[1]), 1)
    return jnp.where(lane < HEAD_DIM, value[:rows], value[rows:])


def natural(core, mine, theirs):
    return jnp.where(core == 0, mine, theirs), jnp.where(core == 0, theirs, mine)


def attend_kernel(
    meta_ref, own_ref, other_ref, dyown_ref, dyother_ref, mask_ref, g1_ref, wqkv_ref, wout_ref, g2_ref,
    x_ref, dy_ref, normed_ref, qkv_ref, probs_ref, mix_ref, mid_ref, routed_ref,
    x_s, qkv_s, mix_s,
):
    half = own_ref.shape[1]
    width = own_ref.shape[2]
    pair = 2 * HEAD_DIM
    core = meta_ref[3]
    for mine, theirs, ref in ((dyown_ref, dyother_ref, dy_ref), (own_ref, other_ref, x_ref)):
        first, second = natural(core, mine[0].astype(F32), theirs[0].astype(F32))
        x_s[0:half, :] = first
        x_s[half : 2 * half, :] = second
        ref[...] = x_s[...].astype(BF16)
    x = x_s[...]
    unit, _ = stats(x)
    normed = (unit * g1_ref[...]).astype(BF16)
    normed_ref[...] = normed
    qkv_s[...] = mm(normed, wqkv_ref[...])
    qkv_ref[...] = qkv_s[...].astype(BF16)
    image = core * pl.num_programs(0) + pl.program_id(0)
    is_open = mask_ref[pl.ds(image, 1), :] > 0
    for n in range(width // pair):
        at = n * pair
        query = head_pair(qkv_s[:, at : at + pair])
        keys = qkv_s[:, width + at : width + at + pair].astype(BF16)
        vals = qkv_s[:, 2 * width + at : 2 * width + at + pair].astype(BF16)
        scores = jnp.where(is_open, mm(query, keys, NT) * SCALE, -1e9)
        top = jnp.max(scores, -1, keepdims=True)
        expo = jnp.where(is_open, jnp.exp(scores - top), 0.0)
        probs = (expo / jnp.sum(expo, -1, keepdims=True)).astype(BF16)
        probs_ref[0, n] = probs
        mix_s[:, at : at + pair] = join_pair(mm(probs, vals))
    mix = mix_s[...].astype(BF16)
    mix_ref[...] = mix
    mid = x + mm(mix, wout_ref[...])
    mid_ref[...] = mid
    unit, _ = stats(mid)
    routed_ref[...] = (unit * g2_ref[...]).astype(BF16)


def attend(meta, own, other, dy_own, dy_other, mask, g1, wqkv, wout, g2):
    imgs, half, width = own.shape
    imgs //= 2
    seq = 2 * half
    rows = imgs * seq
    pairs = HEADS // 2
    raw = pl.BlockSpec((1, half, width), lambda i, m: (m[3] * imgs + i, 0, 0))
    one = lambda *s: pl.BlockSpec(s, lambda i, m: (i,) + (0,) * (len(s) - 1))
    fix = lambda *s: pl.BlockSpec(s, lambda i, m: (0,) * len(s))
    late = lambda *s: HELD(s, BF16)
    return pl.pallas_call(
        attend_kernel,
        grid_spec=pltpu.PrefetchScalarGridSpec(
            num_scalar_prefetch=1,
            grid=(imgs,),
            in_specs=[
                raw, raw, raw, raw, fix(*mask.shape), fix(1, width),
                fix(width, 3 * width), fix(width, width), fix(1, width),
            ],
            out_specs=[
                one(seq, width), one(seq, width), one(seq, width), one(seq, 3 * width),
                one(1, pairs, 2 * seq, seq), one(seq, width), one(seq, width), one(seq, width),
            ],
            scratch_shapes=[
                pltpu.VMEM((seq, width), F32),
                pltpu.VMEM((seq, 3 * width), F32),
                pltpu.VMEM((seq, width), F32),
            ],
        ),
        out_shape=[
            late(rows, width),
            jax.ShapeDtypeStruct((rows, width), BF16),
            late(rows, width),
            late(rows, 3 * width),
            late(imgs, pairs, 2 * seq, seq),
            late(rows, width),
            HELD((rows, width), F32),
            jax.ShapeDtypeStruct((rows, width), BF16),
        ],
        compiler_params=pltpu.CompilerParams(vmem_limit_bytes=22 << 20),
        cost_estimate=BRIEF,
        name="attend",
    )(meta, *map(held, (own, other, dy_own, dy_other)), mask, g1, held(wqkv), held(wout), g2)


def assemble_kernel(meta_ref, own_ref, other_ref, out_ref, out_s):
    half = own_ref.shape[1]
    first, second = natural(meta_ref[3], own_ref[0].astype(F32), other_ref[0].astype(F32))
    out_s[0:half, :] = first
    out_s[half : 2 * half, :] = second
    out_ref[...] = out_s[...].astype(BF16)


def assemble(meta, own, other):
    imgs, half, width = own.shape
    imgs //= 2
    raw = pl.BlockSpec((1, half, width), lambda i, m: (m[3] * imgs + i, 0, 0))
    return pl.pallas_call(
        assemble_kernel,
        grid_spec=pltpu.PrefetchScalarGridSpec(
            num_scalar_prefetch=1,
            grid=(imgs,),
            in_specs=[raw, raw],
            out_specs=pl.BlockSpec((2 * half, width), lambda i, m: (i, 0)),
            scratch_shapes=[pltpu.VMEM((2 * half, width), F32)],
        ),
        out_shape=jax.ShapeDtypeStruct((imgs * 2 * half, width), BF16),
        compiler_params=pltpu.CompilerParams(vmem_limit_bytes=6 << 20),
        cost_estimate=BRIEF,
        name="assemble",
    )(meta, own, other)


def row_gates(rows, ids, wr):
    logits = mm(wr, rows, NT)
    row = lax.broadcasted_iota(jnp.int32, logits.shape, 0)
    pick = (row.astype(F32) == ids[0:1, :]) | (row.astype(F32) == ids[1:2, :])
    top = jnp.max(jnp.where(pick, logits, -jnp.inf), 0, keepdims=True)
    expo = jnp.where(pick, jnp.exp(logits - top), 0.0)
    return expo / jnp.sum(expo, 0, keepdims=True), row


def padded(count):
    return -(-count // 16) * 16


def expert_kernel(add, local, meta_ref, rows_ref, dy_ref, ids_ref, wr_ref, wi_ref, wb_ref, *rest):
    sources = [] if local else [wb_ref]
    if add:
        sources += rest[:2]
        rest = rest[2:]
    act_ref, dpre_ref, dout_ref, made_ref, din_ref, wi_s, wb_s, *rest = rest
    if sources:
        *landings, sems = rest
        copies = [pltpu.make_async_copy(v, w, sems.at[n]) for n, (v, w) in enumerate(zip(sources, landings))]
        for copy in copies:
            copy.start()
    count = act_ref.shape[0]
    width = rows_ref.shape[1]
    rows = rows_ref[0:count, :]
    part = wi_s.shape[1] // PIECES
    if local:
        for n in range(PIECES):
            at = pl.ds(pl.multiple_of((n ^ meta_ref[1]) * part, part), part)
            wi_s[:, n * part : (n + 1) * part] = wi_ref[0, :, at]
            wb_s[n * part : (n + 1) * part, :] = wb_ref[0, at, :]

    if ids_ref.shape[0] == 2:
        ids = ids_ref[...].astype(F32)
    else:
        at = padded(count)
        ids = [ids_ref[at : at + 2, :], ids_ref[at + 2 : at + 4, 0 : count - width]]
        ids = jnp.concatenate([v.astype(F32) for v in ids], axis=1)
    gates, row = row_gates(rows, ids, wr_ref[...])
    high, low = two_halves(jnp.where(row == meta_ref[0], gates, 0.0))
    ones = jnp.ones((16, 128), BF16)
    gate = (mm(high, ones, TN) + mm(low, ones, TN))[:, 0:1]
    dout_ref[...] = (gate * dy_ref[...].astype(F32)).astype(BF16)
    wide = wi_s.shape[1] // CHUNKS
    for q in range(CHUNKS):
        if not local and q % (CHUNKS // 2) == 0:
            ref, first = (landings[0], PIECES // 2) if q else (wi_ref, 0)
            if q:
                copies[0].wait()
            for n in range(PIECES // 2):
                to = slice((first + n) * part, (first + n + 1) * part)
                for h in range(2):
                    side = slice(h * part, (h + 1) * part)
                    wi_s[side, to] = ref[n, h]
                    wb_s[to, side] = ref[n, 2 + h]
        here = slice(q * wide, (q + 1) * wide)
        pre = mm(rows, wi_s[:, here])
        square = pre * pre
        inner = pre * (0.7978845608 + 0.0356774081 * square)
        up = 0.5 + 0.5 * jnp.tanh(inner)
        value = pre * up
        act_ref[:, here] = value.astype(BF16)
        slope = up + value * (1.0 - up) * (1.5957691216 + 0.2140644488 * square)
        dpre_ref[:, here] = (mm(dout_ref[...], wb_s[here, :], NT) * slope).astype(BF16)
    made = mm(act_ref[...], wb_s[...]).astype(BF16).astype(F32)
    d_in = mm(dpre_ref[...], wi_s[...], NT)
    total = gate * made
    high, low = two_halves(made * dy_ref[...].astype(F32))
    ones = jnp.ones((16, width), BF16)
    d_gate = (mm(ones, high, NT) + mm(ones, low, NT))[0:8]
    row = lax.broadcasted_iota(jnp.int32, d_gate.shape, 0)
    d_gate = jnp.where(row == meta_ref[0], d_gate, 0.0)
    tail = padded(count)
    if add:
        for copy in copies[-2:]:
            copy.wait()
        pmade_ref, pdin_ref = landings[-2:]
        total += pmade_ref[...].astype(F32)
        d_in += pdin_ref[0:count, :].astype(F32)
        d_gate += read_gate(pdin_ref, count)
    made_ref[...] = total.astype(BF16)
    din_ref[0:count, :] = d_in.astype(BF16)
    high = d_gate.astype(BF16).astype(F32)
    value = jnp.concatenate([high, d_gate - high], axis=0).astype(BF16)
    din_ref[tail : tail + 16, :] = value[:, :width]
    din_ref[tail + 16 : tail + 32, 0 : count - width] = value[:, width:]


CHUNKS = 4


def read_gate(ref, count):
    tail = padded(count)
    width = ref.shape[1]
    value = ref[tail : tail + 16, 0 : min(count, width)].astype(F32)
    if count > width:
        value = jnp.concatenate([value, ref[tail + 16 : tail + 32, 0 : count - width].astype(F32)], axis=1)
    return value[0:8] + value[8:16]


PIECES = 8


def expert(meta, rows, dy, ids, wr, weights, prev=None):
    count, width = dy.shape
    local = weights[0].ndim == 3
    hidden = weights[0].shape[2] if local else PIECES * weights[0].shape[2]
    deep = padded(count) + 32
    first = prev is None
    away = pl.BlockSpec(memory_space=pl.ANY)
    more = [] if first else [away, away]
    landings = [] if local else [pltpu.VMEM(weights[1].shape, BF16)]
    if not first:
        landings += [pltpu.VMEM((count, width), BF16), pltpu.VMEM((deep, width), BF16)]
    if landings:
        landings.append(pltpu.SemaphoreType.DMA((len(landings),)))
    shape = lambda *s: jax.ShapeDtypeStruct(s, BF16)
    return pl.pallas_call(
        functools.partial(expert_kernel, not first, local),
        grid_spec=pltpu.PrefetchScalarGridSpec(
            num_scalar_prefetch=1,
            grid=(1,),
            in_specs=[HERE] * 5 + [HERE if local else away, *more],
            out_specs=[HERE] * 5,
            scratch_shapes=[pltpu.VMEM((width, hidden), BF16), pltpu.VMEM((hidden, width), BF16), *landings],
        ),
        out_shape=[shape(count, hidden), shape(count, hidden), shape(count, width), shape(count, width), shape(deep, width)],
        compiler_params=pltpu.CompilerParams(vmem_limit_bytes=LIMIT << 20),
        cost_estimate=BRIEF,
        name="expert",
    )(meta, rows, dy, ids, wr, weights[0], weights[1] if local else held(weights[1]), *[held(v) for v in prev or ()])


LIMIT = 26


def weight_kernel(n, *refs):
    rows, acts, dpres, douts = (refs[g * n : (g + 1) * n] for g in range(4))
    iown_ref, igive_ref, bown_ref, bgive_ref = refs[4 * n :]
    pieces, piece, width = iown_ref.shape
    wide = piece * PIECES // WCHUNKS
    for q in range(WCHUNKS):
        at = q * wide // piece % pieces
        for left, right, own_ref, give_ref in ((dpres, rows, iown_ref, igive_ref), (acts, douts, bown_ref, bgive_ref)):
            total = 0.0
            for b in range(n):
                count = left[b].shape[0]
                total = total + mm(left[b][:, q * wide : (q + 1) * wide], right[b][0:count, :], TN)
            ref = own_ref if q < WCHUNKS // 2 else give_ref
            ref[at : at + wide // piece] = total.astype(BF16).reshape(wide // piece, piece, width)


WCHUNKS = 4


def weight_grads(rows, acts, dpres, douts, late=False):
    n = len(rows)
    width = rows[0].shape[1]
    piece = acts[0].shape[1] // PIECES
    return pl.pallas_call(
        functools.partial(weight_kernel, n),
        in_specs=[HERE] * (4 * n),
        out_specs=[HERE] * 4,
        out_shape=[jax.ShapeDtypeStruct((PIECES // 2, piece, width), BF16)] * 4,
        compiler_params=pltpu.CompilerParams(vmem_limit_bytes=14 << 20),
        cost_estimate=BRIEF,
        name="weight_grads",
    )(*rows, *acts, *dpres, *douts)


def finish_kernel(meta_ref, im_ref, ir_ref, bm_ref, br_ref, gin_ref, gback_ref):
    mine = pl.program_id(0) < pl.num_programs(0) // 2
    flip = meta_ref[1] % 2 == 1
    piece, width = im_ref.shape[1:]
    for m_ref, r_ref, out_ref in ((im_ref, ir_ref, gin_ref), (bm_ref, br_ref, gback_ref)):
        value = jnp.where(mine, m_ref[...], r_ref[...]).astype(F32)
        first = jnp.where(flip, value[1], value[0])
        second = jnp.where(flip, value[0], value[1])
        if out_ref is gin_ref:
            out_ref[0, :, 0:piece] = jnp.transpose(first)
            out_ref[0, :, piece : 2 * piece] = jnp.transpose(second)
        else:
            out_ref[0, 0:piece, :] = first
            out_ref[0, piece : 2 * piece, :] = second


def finish_expert(meta, in_mine, in_recv, back_mine, back_recv):
    upper, piece, width = in_mine.shape
    steps = upper
    own = pl.BlockSpec((2, piece, width), lambda q, m: (jnp.minimum(q, steps // 2 - 1), 0, 0))
    give = pl.BlockSpec((2, piece, width), lambda q, m: (jnp.maximum(q - steps // 2, 0), 0, 0))
    return pl.pallas_call(
        finish_kernel,
        grid_spec=pltpu.PrefetchScalarGridSpec(
            num_scalar_prefetch=1,
            grid=(steps,),
            in_specs=[own, give, own, give],
            out_specs=[
                pl.BlockSpec((1, width, 2 * piece), lambda q, m: (0, 0, q ^ (m[1] // 2))),
                pl.BlockSpec((1, 2 * piece, width), lambda q, m: (0, q ^ (m[1] // 2), 0)),
            ],
        ),
        out_shape=[
            jax.ShapeDtypeStruct((1, width, PIECES * piece), F32),
            jax.ShapeDtypeStruct((1, PIECES * piece, width), F32),
        ],
        compiler_params=pltpu.CompilerParams(vmem_limit_bytes=14 << 20),
        cost_estimate=BRIEF,
        name="finish_expert",
    )(meta, in_mine, in_recv, back_mine, back_recv)


def split_halves(core, whole_ref, own_ref, other_ref):
    imgs, half, _ = own_ref.shape
    for i in range(imgs):
        at = 2 * half * i
        first, second = whole_ref[at : at + half, :], whole_ref[at + half : at + 2 * half, :]
        mine, theirs = natural(core, first, second)
        own_ref[i] = mine.astype(BF16)
        other_ref[i] = theirs.astype(BF16)


def back_kernel(
    meta_ref, din0_ref, din1_ref,
    ids_ref, dy_ref, mid_ref, routed_ref, wr_ref, g2_ref, mix_ref, wout_ref,
    probs_ref, qkv_ref, x_ref, normed_ref, wqkv_ref, g1_ref,
    own_ref, other_ref, gown_ref, ggive_ref,
    dmid_s, dmix_s, dqkv_s, tok_s, grad_s, small_s,
):
    step = pl.program_id(0)
    imgs = pl.num_programs(0)
    seq = qkv_ref.shape[0]
    width = x_ref.shape[1]
    half = seq // 2
    pair = 2 * HEAD_DIM
    rows = x_ref.shape[0]

    @pl.when(step == 0)
    def _():
        routed = routed_ref[...]
        wr = wr_ref[...]
        gates, _ = row_gates(routed, ids_ref[...].astype(F32), wr)
        d_gate = read_gate(din0_ref, rows) + read_gate(din1_ref, rows)
        d_gate = jnp.concatenate([d_gate, jnp.zeros_like(d_gate)], axis=0)
        d_logits = gates * (d_gate - jnp.sum(gates * d_gate, 0, keepdims=True))
        high, low = two_halves(d_logits)
        small_s[...] = jnp.zeros_like(small_s)
        small_s[0:16, :] = mm(high, routed) + mm(low, routed)
        d_routed = din0_ref[0:rows, :].astype(F32) + din1_ref[0:rows, :].astype(F32)
        d_routed = d_routed + mm(high, wr, TN) + mm(low, wr, TN)
        unit, rstd = stats(mid_ref[...])
        small_s[16:17, :] = jnp.sum(d_routed * unit, 0, keepdims=True)
        d_mid = dy_ref[...].astype(F32) + norm_vjp(d_routed, unit, rstd, g2_ref[...])
        dmid_s[...] = d_mid
        d_branch = d_mid.astype(BF16)
        grad_s[:, 3 * width : 4 * width] = mm(mix_ref[...], d_branch, TN).astype(BF16)
        dmix_s[...] = mm(d_branch, wout_ref[...], NT)

    base = pl.multiple_of(step * seq, 8)
    for n in range(width // pair):
        at = n * pair
        d_mix = head_pair(dmix_s[pl.ds(base, seq), at : at + pair])
        query = head_pair(qkv_ref[:, at : at + pair].astype(F32))
        keys = qkv_ref[:, width + at : width + at + pair]
        vals = qkv_ref[:, 2 * width + at : 2 * width + at + pair]
        low = probs_ref[0, n]
        probs = low.astype(F32)
        d_probs = mm(d_mix, vals, NT)
        d_scores = probs * (d_probs - jnp.sum(probs * d_probs, -1, keepdims=True))
        d_scores = d_scores.astype(BF16)
        d_query = join_pair(mm(d_scores, keys)) * SCALE
        d_keys = mm(d_scores, query, TN) * SCALE
        d_vals = mm(low, d_mix, TN)
        dqkv_s[pl.ds(base, seq), at : at + pair] = d_query.astype(BF16)
        dqkv_s[pl.ds(base, seq), width + at : width + at + pair] = d_keys.astype(BF16)
        dqkv_s[pl.ds(base, seq), 2 * width + at : 2 * width + at + pair] = d_vals.astype(BF16)

    @pl.when(step == imgs - 1)
    def _():
        d_qkv = dqkv_s[...]
        grad_s[:, : 3 * width] = mm(normed_ref[...], d_qkv, TN).astype(BF16)
        d_normed = mm(d_qkv, wqkv_ref[...], NT)
        unit, rstd = stats(x_ref[...].astype(F32))
        small_s[17:18, :] = jnp.sum(d_normed * unit, 0, keepdims=True)
        grad_s[:, 4 * width :] = jnp.transpose(small_s[...]).astype(BF16)
        tok_s[...] = dmid_s[...] + norm_vjp(d_normed, unit, rstd, g1_ref[...])
        split_halves(meta_ref[3], tok_s, own_ref, other_ref)
        part = width // SHARES
        for r in range(SHARES):
            ref = gown_ref if r < SHARES // 2 else ggive_ref
            to = (r % (SHARES // 2)) * part
            there = pl.multiple_of((r ^ meta_ref[2]) * part, part)
            ref[to : to + part, :] = grad_s[pl.ds(there, part), :]


SHARES = 32


def attend_back(meta, dins, ids, dy, mid, routed, wr, g2, mix, wout, probs, qkv, x, normed, wqkv, g1):
    imgs = probs.shape[0]
    rows, width = x.shape
    seq = rows // imgs
    pairs = HEADS // 2
    wide = 4 * width + 128
    fix = lambda *s: pl.BlockSpec(s, lambda i, m: (0,) * len(s))
    return pl.pallas_call(
        back_kernel,
        grid_spec=pltpu.PrefetchScalarGridSpec(
            num_scalar_prefetch=1,
            grid=(imgs,),
            in_specs=[fix(*a.shape) for a in dins] + [
                fix(2, rows), fix(rows, width), fix(rows, width), fix(rows, width),
                fix(16, width), fix(1, width), fix(rows, width), fix(width, width),
                pl.BlockSpec((1, pairs, 2 * seq, seq), lambda i, m: (i, 0, 0, 0)),
                pl.BlockSpec((seq, 3 * width), lambda i, m: (i, 0)),
                fix(rows, width), fix(rows, width), fix(width, 3 * width), fix(1, width),
            ],
            out_specs=[
                fix(imgs, seq // 2, width), fix(imgs, seq // 2, width),
                fix(width // 2, wide), fix(width // 2, wide),
            ],
            scratch_shapes=[
                pltpu.VMEM((rows, width), F32),
                pltpu.VMEM((rows, width), F32),
                pltpu.VMEM((rows, 3 * width), BF16),
                pltpu.VMEM((rows, width), F32),
                pltpu.VMEM((width, wide), BF16),
                pltpu.VMEM((128, width), F32),
            ],
        ),
        out_shape=[
            jax.ShapeDtypeStruct((imgs, seq // 2, width), BF16),
            jax.ShapeDtypeStruct((imgs, seq // 2, width), BF16),
            jax.ShapeDtypeStruct((width // 2, wide), BF16),
            jax.ShapeDtypeStruct((width // 2, wide), BF16),
        ],
        compiler_params=pltpu.CompilerParams(vmem_limit_bytes=32 << 20),
        cost_estimate=BRIEF,
        name="attend_back",
    )(meta, *dins, ids, dy, mid, routed, wr, g2, mix, wout, probs, qkv, x, normed, wqkv, g1)


def shared_kernel(meta_ref, mine_ref, recv_ref, gqkv_ref, gout_ref, small_ref, all_s):
    upper, wide = mine_ref.shape
    width = 2 * upper
    part = width // SHARES
    all_s[0:upper, :] = mine_ref[...]
    all_s[upper:width, :] = recv_ref[...]
    for i in range(SHARES):
        there = pl.multiple_of((i ^ meta_ref[2]) * part, part)
        value = all_s[pl.ds(there, part), :].astype(F32)
        at = i * part
        gqkv_ref[at : at + part, :] = value[:, : 3 * width]
        gout_ref[at : at + part, :] = value[:, 3 * width : 4 * width]
        small_ref[at : at + part, :] = value[:, 4 * width :]


def finish_shared(meta, mine, recv):
    upper, wide = mine.shape
    width = 2 * upper
    fix = lambda *s: pl.BlockSpec(s, lambda i, m: (0,) * len(s))
    return pl.pallas_call(
        shared_kernel,
        grid_spec=pltpu.PrefetchScalarGridSpec(
            num_scalar_prefetch=1,
            grid=(1,),
            in_specs=[fix(upper, wide), fix(upper, wide)],
            out_specs=[fix(width, 3 * width), fix(width, width), fix(width, wide - 4 * width)],
            scratch_shapes=[pltpu.VMEM((width, wide), BF16)],
        ),
        out_shape=[
            jax.ShapeDtypeStruct((width, 3 * width), F32),
            jax.ShapeDtypeStruct((width, width), F32),
            jax.ShapeDtypeStruct((width, wide - 4 * width), F32),
        ],
        compiler_params=pltpu.CompilerParams(vmem_limit_bytes=16 << 20),
        cost_estimate=BRIEF,
        name="finish_shared",
    )(meta, mine, recv)


def combine_kernel(meta_ref, mid_ref, a_ref, b_ref, own_ref, other_ref, s_ref):
    s_ref[...] = mid_ref[...] + (a_ref[...].astype(F32) + b_ref[...].astype(F32))
    split_halves(meta_ref[3], s_ref, own_ref, other_ref)


def combine(meta, mid, parts, imgs):
    rows, width = mid.shape
    seq = rows // imgs
    spec = pl.BlockSpec((seq, width), lambda i, m: (i, 0))
    out = pl.BlockSpec((1, seq // 2, width), lambda i, m: (i, 0, 0))
    shape = jax.ShapeDtypeStruct((imgs, seq // 2, width), BF16)
    return pl.pallas_call(
        combine_kernel,
        grid_spec=pltpu.PrefetchScalarGridSpec(
            num_scalar_prefetch=1,
            grid=(imgs,),
            in_specs=[spec] * 3,
            out_specs=[out, out],
            scratch_shapes=[pltpu.VMEM((seq, width), F32)],
        ),
        out_shape=[shape, shape],
        compiler_params=pltpu.CompilerParams(vmem_limit_bytes=8 << 20),
        cost_estimate=BRIEF,
        name="combine",
    )(meta, mid, *parts)


def place_kernel(meta_ref, a_own_ref, a_recv_ref, b_own_ref, b_recv_ref, a_ref, b_ref):
    imgs = pl.num_programs(0) // 2
    mine = pl.program_id(0) // imgs == meta_ref[3]
    a_ref[...] = jnp.where(mine, a_own_ref[...], a_recv_ref[...])
    b_ref[...] = jnp.where(mine, b_own_ref[...], b_recv_ref[...])


def place(meta, *arrays):
    imgs, half, width = arrays[0].shape
    spec = pl.BlockSpec((1, half, width), lambda j, m: (j % imgs, 0, 0))
    out = pl.BlockSpec((1, half, width), lambda j, m: (j, 0, 0))
    shape = jax.ShapeDtypeStruct((2 * imgs, half, width), BF16)
    return pl.pallas_call(
        place_kernel,
        grid_spec=pltpu.PrefetchScalarGridSpec(
            num_scalar_prefetch=1, grid=(2 * imgs,), in_specs=[spec] * 4, out_specs=[out, out]
        ),
        out_shape=[shape, shape],
        compiler_params=pltpu.CompilerParams(vmem_limit_bytes=4 << 20),
        cost_estimate=BRIEF,
        name="place",
    )(meta, *arrays)


def pack_kernel(meta_ref, wi_ref, wb_ref, out_ref):
    part = out_ref.shape[1]
    for h in range(2):
        at = slice(h * part, (h + 1) * part)
        out_ref[h] = wi_ref[0, at, :]
        out_ref[2 + h] = wb_ref[0, :, at]


def pack_piece(meta, w_in, w_back):
    width, hidden = w_in.shape[1:]
    piece = hidden // PIECES
    return pl.pallas_call(
        pack_kernel,
        grid_spec=pltpu.PrefetchScalarGridSpec(
            num_scalar_prefetch=1,
            grid=(1,),
            in_specs=[
                pl.BlockSpec((1, width, piece), lambda i, m: (0, 0, m[1])),
                pl.BlockSpec((1, piece, width), lambda i, m: (0, m[1], 0)),
            ],
            out_specs=pl.BlockSpec((4, piece, piece), lambda i, m: (0, 0, 0)),
        ),
        out_shape=jax.ShapeDtypeStruct((4, piece, piece), BF16),
        compiler_params=pltpu.CompilerParams(vmem_limit_bytes=4 << 20),
        cost_estimate=BRIEF,
        name="pack_piece",
    )(meta, held(w_in), held(w_back))


def merge_kernel(plan, *refs):
    refs = list(refs)
    takes = [[[(refs.pop(0), at) for at in views] for views in groups] for groups, _, _ in plan]
    for groups, (_, axis, cuts) in zip(takes, plan):
        outs = [refs.pop(0) for _ in cuts]
        if axis is not None:
            size = groups[0][0][0].shape[axis]
            for k, (ref, _) in enumerate(groups[0]):
                at = slice(k * size, (k + 1) * size)
                outs[0][(slice(None),) * axis + (at,)] = ref[...]
            continue
        for g, take in enumerate(groups):
            total = sum(ref[at].astype(F32) for ref, at in take).astype(BF16)
            for out, cut in zip(outs, cuts):
                if len(groups) > 1:
                    out[g] = total[cut]
                else:
                    out[...] = total[cut]


def merge(*items):
    plan, shapes, arrays = [], [], []
    for groups, axis, cuts in items:
        head = groups[0][0]
        shape = jax.eval_shape(lambda v: v[head[1]], head[0]).shape if isinstance(head, tuple) else head.shape
        first = jax.ShapeDtypeStruct(shape, BF16)
        if axis is not None:
            cuts = [None]
            shape = list(first.shape)
            shape[axis] *= len(groups[0])
            shapes.append(jax.ShapeDtypeStruct(tuple(shape), BF16))
        else:
            lead = (len(groups),) if len(groups) > 1 else ()
            shapes += [
                jax.ShapeDtypeStruct(lead + jax.eval_shape(lambda v, c=c: v[c], first).shape, BF16) for c in cuts
            ]
        pairs = [[v if isinstance(v, tuple) else (v, ...) for v in g] for g in groups]
        plan.append(([[at for _, at in g] for g in pairs], axis, cuts))
        arrays += [v for g in pairs for v, _ in g]
    return pl.pallas_call(
        functools.partial(merge_kernel, plan),
        out_shape=shapes,
        compiler_params=pltpu.CompilerParams(vmem_limit_bytes=16 << 20),
        cost_estimate=BRIEF,
        name="merge",
    )(*arrays)


def held(value):
    return pltpu.with_memory_space_constraint(value, pltpu.HBM)


SWAP = [(0, 1), (1, 0)]


def xor(k, n=4):
    return [(i, i ^ k) for i in range(n)]


def send(value, axis, pairs):
    return lax.ppermute(value, axis, pairs)


def add_low(a, b):
    return (a.astype(F32) + b.astype(F32)).astype(BF16)


def after(value, *earlier):
    return lax.optimization_barrier((value, *earlier))[0]


def tie(*values):
    return lax.optimization_barrier(values)


def fan(value, axis):
    rows = value.shape[0] // 4
    return [send(value[k * rows : (k + 1) * rows], axis, xor(k)) for k in (1, 2, 3)]


def add_fan(value, got):
    total = value[: value.shape[0] // 4].astype(F32)
    for v in got:
        total = total + v.astype(F32)
    return total.astype(BF16)


def dense_shards(
    tokens, gain_one, w_qkv, w_out, gain_two, w_router, w_in, w_back, route_ids, key_mask, cotangent
):
    nimg, half, width = tokens.shape
    imgs = nimg // 2
    rows = imgs * 2 * half
    experts = w_router.shape[1]
    piece = w_in.shape[2] // PIECES
    core = lax.axis_index("ctx")
    z = lax.axis_index("expert")
    me = core * 4 + lax.axis_index("dp")
    meta = jnp.stack([z, me, me * 4 + z, core]).astype(jnp.int32)
    meta_pair = jnp.stack([z ^ 2, me, me * 4 + z, core]).astype(jnp.int32)
    far = lambda v: send(v, "expert", xor(1))
    swap = lambda v: send(v, "ctx", SWAP)

    pack = pack_piece(meta, w_in, w_back)
    codes = after(route_ids, pack).reshape(nimg, half, TOP)
    codes = codes[..., 0] + experts * codes[..., 1]
    tok_other, dy_other, codes_other = swap(tokens), swap(cotangent), swap(codes)
    first = jnp.where(core == 0, codes, codes_other)
    second = jnp.where(core == 0, codes_other, codes)
    codes = lax.dynamic_slice_in_dim(jnp.concatenate([first, second], 1), core * imgs, imgs, 0)
    codes = codes.reshape(1, rows)
    ids = jnp.concatenate([codes % experts, codes // experts], 0)
    wide = jnp.pad(ids, ((0, 0), (0, 2 * width - rows))).reshape(TOP, 2, width)
    ids_pack = jnp.concatenate([wide[:, 0], wide[:, 1]], 0).astype(BF16)
    ids_pack = jnp.pad(ids_pack, ((padded(rows) - rows, 12), (0, 0)))
    wr = jnp.pad(w_router.T, ((0, 16 - experts), (0, 0)))
    g1, g2 = gain_one[None, :], gain_two[None, :]

    far_raw, pack = far(after(cotangent, pack)), send(pack, "expert", xor(2))
    x_rows, dy, normed, qkv, probs, mix, mid, routed = attend(
        meta, tokens, tok_other, cotangent, dy_other, key_mask, g1, w_qkv, w_out, g2
    )
    own_one = expert(meta, routed, dy, ids, wr, (w_in, w_back))
    far_rows = jnp.concatenate([routed, ids_pack], 0)
    pack, wr_far = after(pack, routed), after(wr, own_one[2])

    packs = [pack] + [send(pack, "dp", xor(k)) for k in (1, 2, 3)]
    far_rows = far(far_rows)
    far_raw = after(far_raw, own_one[2])
    far_dy = assemble(meta, far_raw, swap(far_raw))
    far_one = expert(meta, far_rows, far_dy, far_rows, wr_far, (w_in, w_back))
    *packs, wr_far = tie(*packs, after(wr, far_one[2]))
    packs = jnp.stack(packs)
    pair = [packs, swap(packs)]
    grads = weight_grads([routed, far_rows], *zip(own_one[:3], far_one[:3]), late=True)
    wr_far = after(wr_far, grads[0])

    far_two = expert(meta_pair, far_rows, far_dy, far_rows, wr_far, pair, far_one[3:])
    head, tail = slice(0, 2), slice(2, 4)
    even, odd = [(slice(None), slice(k, k + 1)) for k in (0, 1)]
    square = lambda v: v.reshape(2, 2, piece, width)

    def across(a, a_give, b, b_give):
        return merge(
            ([[a, swap(a_give)]], None, [head, tail]), ([[square(b), square(swap(b_give))]], None, [even, odd])
        )

    one = across(*grads)
    wr_own, *one = tie(after(wr, far_two[2]), *one)
    far_din, far_made = far_two[4], far_two[3]

    y_way, x_way = ("dp", xor(2)), ("dp", xor(1))
    own_two = expert(meta_pair, routed, dy, ids, wr_own, pair, own_one[3:])
    grads = weight_grads([routed, far_rows], *zip(own_two[:3], far_two[:3]))
    din_far, a_got, b_got, *grads = tie(far(far_din), send(one[1], *y_way), send(one[3], *x_way), *grads)
    a_one, b_one = [one[0], a_got], [one[2], b_got]

    two = tie(*across(*grads))

    a_two, b_two = [two[0], send(two[1], *y_way)], [two[2], send(two[3], *x_way)]
    far_made = far(after(far_made, din_far))
    tok_own, tok_give, shared, shared_give = attend_back(
        meta, [after(own_two[4], *two), din_far], ids, dy, mid, routed, wr, g2, mix, w_out, probs, qkv, x_rows, normed, w_qkv, g1
    )
    halves = [slice(0, 1), slice(1, 2)]
    line = lambda v: v.reshape(2, piece, width)
    flat = lambda group: [line(v) for v in group]
    one, one_give, two, two_give, far_made, shared, shared_give, tok_give = tie(
        *merge(([a_one, flat(b_one)], None, halves), ([a_two, flat(b_two)], None, halves)),
        far_made,
        shared,
        shared_give,
        tok_give,
    )
    mix_own, mix_give = combine(meta, mid, [own_two[3], far_made], imgs)
    quarters = lambda n: [slice(k * n, (k + 1) * n) for k in range(4)]
    everything = [slice(None)]
    second = lambda give: [send(give[0], *x_way), send(give[1], *y_way)]
    got = second(two_give)
    two, *shared, tok_got, mix_got = tie(
        *merge(
            ([[(two, 0), got[0]], [(two, 1), got[1]]], None, everything),
            ([[shared, swap(shared_give)]], None, quarters(width // 8)),
        ),
        swap(tok_give),
        swap(mix_give),
    )
    spread = lambda parts, axis: [send(v, axis, xor(k)) for k, v in zip((1, 2, 3), parts)]
    mixed, grad_tokens = place(meta, mix_own, mix_got, tok_own, tok_got)
    got, cross = second(one_give), send(two, "expert", xor(2))
    a, b, *shared, mixed, grad_tokens = tie(
        *merge(
            ([[(one, 0), got[0], (cross, 0)]], None, everything),
            ([[(one, 1), got[1], (cross, 1)]], None, everything),
            ([[shared[0], *spread(shared[1:], "dp")]], None, quarters(width // 32)),
        ),
        mixed,
        grad_tokens,
    )
    b = b[None]
    a, b, shared = tie(
        *merge(
            ([[a, send(a, *x_way)]], 0, None),
            ([[b, send(b, *y_way)]], 0, None),
            ([[shared[0], *spread(shared[1:], "expert")]], None, everything),
        )
    )
    a, b, shared = tie(
        *merge(
            ([[a, send(a, *y_way)]], 0, None),
            ([[b, send(b, *x_way)]], 1, None),
            ([[shared, *spread([shared] * 3, "expert")]], 0, None),
        )
    )
    b = b.reshape(a.shape)
    grad_in, grad_back = finish_expert(meta, a, swap(a), b, swap(b))
    (shared,) = merge(([[after(shared, grad_in, grad_back), *spread([shared] * 3, "dp")]], 0, None))
    grad_qkv, grad_out, small = finish_shared(meta, shared, swap(shared))
    return (
        mixed,
        grad_tokens,
        small[:, 17],
        grad_qkv,
        grad_out,
        small[:, 16],
        small[:, :experts],
        grad_in,
        grad_back,
    )


def norm_rows(value, gain):
    center = value - jnp.mean(value, -1, keepdims=True)
    spread = jnp.mean(center * center, -1, keepdims=True)
    return center * lax.rsqrt(spread + 1e-06) * gain


def smooth_gelu(value):
    return 0.5 * value * (1.0 + jnp.tanh(0.7978845608 * (value + 0.044715 * value * value * value)))


def forward(tokens, gain_one, w_qkv, w_out, gain_two, w_router, w_in, w_back, flat_ids, live):
    nimg, half, width = tokens.shape
    count = nimg * half
    experts_all = w_router.shape[1]
    capacity = max(2, 2 * TOP * count // experts_all)
    x_rows = tokens.astype(jnp.float32).reshape(count, width)
    normed = norm_rows(x_rows, gain_one).astype(jnp.bfloat16)
    qkv = jnp.dot(normed, w_qkv, preferred_element_type=jnp.float32).astype(jnp.bfloat16)
    qkv = qkv.reshape(nimg, half, 3 * width)
    query = qkv[..., :width]
    keys_local = qkv[..., width : 2 * width]
    vals_local = qkv[..., 2 * width :]
    keys, vals = (
        lax.all_gather(keys_local, "ctx", axis=1, tiled=True),
        lax.all_gather(vals_local, "ctx", axis=1, tiled=True),
    )
    seq = keys.shape[1]
    query4 = query.reshape(nimg, half, HEADS, HEAD_DIM)
    keys4 = keys.reshape(nimg, seq, HEADS, HEAD_DIM)
    vals4 = vals.reshape(nimg, seq, HEADS, HEAD_DIM)
    scale = HEAD_DIM ** (-0.5)
    scores = (
        jnp.einsum("iqhc,ikhc->ihqk", query4, keys4, preferred_element_type=jnp.float32) * scale
    )
    open_keys = live[:, None, None, :]
    masked = jnp.where(open_keys, scores, -1000000000.0)
    topmost = jnp.max(masked, -1, keepdims=True)
    expo = jnp.where(open_keys, jnp.exp(masked - topmost), 0.0)
    probs = expo / jnp.sum(expo, -1, keepdims=True)
    probs_low = probs.astype(jnp.bfloat16)
    mix = jnp.einsum("ihqk,ikhc->iqhc", probs_low, vals4, preferred_element_type=jnp.float32)
    mix = mix.reshape(count, width).astype(jnp.bfloat16)
    mid = x_rows + jnp.dot(mix, w_out, preferred_element_type=jnp.float32)
    routed = norm_rows(mid, gain_two).astype(jnp.bfloat16)
    logits = jnp.dot(routed, w_router, preferred_element_type=jnp.float32)
    pick = flat_ids[:, :, None] == jnp.arange(experts_all, dtype=jnp.int32)[None, None, :]
    chosen = jnp.sum(jnp.where(pick, logits[:, None, :], 0.0), -1)
    expo_gate = jnp.exp(chosen)
    gates = expo_gate / jnp.sum(expo_gate, -1, keepdims=True)
    pair_ids = flat_ids.reshape(-1)
    hits = (pair_ids[:, None] == jnp.arange(experts_all, dtype=jnp.int32)[None, :]).astype(
        jnp.int32
    )
    before = jnp.cumsum(hits, 0) - hits
    slots = jnp.sum(before * hits, 1)
    where_rows = pair_ids * capacity + slots
    sent = jnp.repeat(routed, TOP, axis=0)
    buffer = jnp.zeros((experts_all * capacity, width), jnp.bfloat16).at[where_rows].set(sent)
    buffer = buffer.reshape(experts_all, capacity, width)
    arrived = lax.all_to_all(buffer, "expert", split_axis=0, concat_axis=1, tiled=True)
    pre = jnp.einsum("erd,edf->erf", arrived, w_in, preferred_element_type=jnp.float32)
    act = smooth_gelu(pre).astype(jnp.bfloat16)
    made = jnp.einsum("erf,efd->erd", act, w_back, preferred_element_type=jnp.float32).astype(
        jnp.bfloat16
    )
    returned = lax.all_to_all(made, "expert", split_axis=1, concat_axis=0, tiled=True)
    picked = returned.reshape(experts_all * capacity, width)[where_rows].reshape(count, TOP, width)
    output = mid + jnp.sum(gates[:, :, None] * picked.astype(jnp.float32), 1)
    return (
        x_rows,
        normed,
        query4,
        keys4,
        vals4,
        probs,
        probs_low,
        mix,
        mid,
        routed,
        pick,
        gates,
        where_rows,
        arrived,
        pre,
        act,
        picked,
        output,
        capacity,
    )


def shards(
    tokens, gain_one, w_qkv, w_out, gain_two, w_router, w_in, w_back, route_ids, key_mask, cotangent
):
    nimg, half, width = tokens.shape
    count = nimg * half
    experts_all = w_router.shape[1]
    flat_ids = route_ids.reshape(count, TOP)
    live = key_mask > 0
    state = forward(
        tokens, gain_one, w_qkv, w_out, gain_two, w_router, w_in, w_back, flat_ids, live
    )
    mixed = state[17].reshape(nimg, half, width).astype(jnp.bfloat16)
    state = forward(
        tokens, gain_one, w_qkv, w_out, gain_two, w_router, w_in, w_back, flat_ids, live
    )
    (
        x_rows,
        normed,
        query4,
        keys4,
        vals4,
        probs,
        probs_low,
        mix,
        mid,
        routed,
        pick,
        gates,
        where_rows,
        arrived,
        pre,
        act,
        picked,
        output,
        capacity,
    ) = state
    scale = HEAD_DIM ** (-0.5)
    high = lax.Precision.HIGHEST
    grad_y = cotangent.astype(jnp.float32).reshape(count, width)
    grad_gate = jnp.sum(grad_y[:, None, :] * picked.astype(jnp.float32), -1)
    d_out = (
        (gates[:, :, None] * grad_y[:, None, :]).astype(jnp.bfloat16).reshape(count * TOP, width)
    )
    grad_buffer = jnp.zeros((experts_all * capacity, width), jnp.bfloat16).at[where_rows].set(d_out)
    grad_buffer = grad_buffer.reshape(experts_all, capacity, width)
    grad_arrived = lax.all_to_all(grad_buffer, "expert", split_axis=0, concat_axis=1, tiled=True)
    d_act = jnp.einsum("erd,efd->erf", grad_arrived, w_back, preferred_element_type=jnp.float32)
    grad_back = jnp.einsum("erf,erd->efd", act, grad_arrived, preferred_element_type=jnp.float32)
    _, gelu_pull = jax.vjp(smooth_gelu, pre)
    d_pre = gelu_pull(d_act)[0].astype(jnp.bfloat16)
    grad_in = jnp.einsum("erd,erf->edf", arrived, d_pre, preferred_element_type=jnp.float32)
    d_in = jnp.einsum("erf,edf->erd", d_pre, w_in, preferred_element_type=jnp.float32).astype(
        jnp.bfloat16
    )
    grad_returned = lax.all_to_all(d_in, "expert", split_axis=1, concat_axis=0, tiled=True)
    grad_rows = grad_returned.reshape(experts_all * capacity, width)[where_rows].reshape(
        count, TOP, width
    )
    d_experts = jnp.sum(grad_rows.astype(jnp.float32), 1)
    d_chosen = gates * (grad_gate - jnp.sum(gates * grad_gate, -1, keepdims=True))
    d_logits = jnp.sum(jnp.where(pick, d_chosen[:, :, None], 0.0), 1)
    grad_router = jnp.dot(routed.astype(jnp.float32).T, d_logits, precision=high)
    d_routed = d_experts + jnp.dot(d_logits, w_router.astype(jnp.float32).T, precision=high)
    _, norm_two_pull = jax.vjp(norm_rows, mid, gain_two)
    d_mid_norm, grad_gain_two = norm_two_pull(d_routed)
    d_mid = grad_y + d_mid_norm
    d_branch = d_mid.astype(jnp.bfloat16)
    grad_out = jnp.einsum("td,te->de", mix, d_branch, preferred_element_type=jnp.float32)
    d_mix = jnp.dot(d_branch, w_out.T, preferred_element_type=jnp.float32).astype(jnp.bfloat16)
    d_mix4 = d_mix.reshape(nimg, half, HEADS, HEAD_DIM)
    d_probs = jnp.einsum("iqhc,ikhc->ihqk", d_mix4, vals4, preferred_element_type=jnp.float32)
    d_scores = (probs * (d_probs - jnp.sum(probs * d_probs, -1, keepdims=True))).astype(
        jnp.bfloat16
    )
    d_query = (
        jnp.einsum("ihqk,ikhc->iqhc", d_scores, keys4, preferred_element_type=jnp.float32) * scale
    )
    d_keys = (
        jnp.einsum("ihqk,iqhc->ikhc", d_scores, query4, preferred_element_type=jnp.float32) * scale
    )
    d_vals = jnp.einsum("ihqk,iqhc->ikhc", probs_low, d_mix4, preferred_element_type=jnp.float32)
    seq = keys4.shape[1]
    d_keys_own, d_vals_own = (
        lax.psum_scatter(
            d_keys.reshape(nimg, seq, width).astype(jnp.bfloat16),
            "ctx",
            scatter_dimension=1,
            tiled=True,
        ).astype(jnp.float32),
        lax.psum_scatter(
            d_vals.reshape(nimg, seq, width).astype(jnp.bfloat16),
            "ctx",
            scatter_dimension=1,
            tiled=True,
        ).astype(jnp.float32),
    )
    d_qkv = jnp.concatenate(
        [
            d_query.reshape(count, width).astype(jnp.bfloat16),
            d_keys_own.reshape(count, width).astype(jnp.bfloat16),
            d_vals_own.reshape(count, width).astype(jnp.bfloat16),
        ],
        axis=1,
    )
    grad_qkv = jnp.einsum("td,te->de", normed, d_qkv, preferred_element_type=jnp.float32)
    d_normed = jnp.dot(d_qkv, w_qkv.T, preferred_element_type=jnp.float32)
    _, norm_one_pull = jax.vjp(norm_rows, x_rows, gain_one)
    d_x_norm, grad_gain_one = norm_one_pull(d_normed)
    grad_tokens = (d_mid + d_x_norm).reshape(nimg, half, width).astype(jnp.bfloat16)
    grad_gain_one, grad_qkv, grad_out, grad_gain_two, grad_router = lax.psum(
        (grad_gain_one, grad_qkv, grad_out, grad_gain_two, grad_router), ("dp", "ctx", "expert")
    )
    grad_in, grad_back = (
        lax.psum(grad_in.astype(jnp.bfloat16), ("dp", "ctx")).astype(jnp.float32),
        lax.psum(grad_back.astype(jnp.bfloat16), ("dp", "ctx")).astype(jnp.float32),
    )
    return (
        mixed,
        grad_tokens,
        grad_gain_one,
        grad_qkv,
        grad_out,
        grad_gain_two,
        grad_router,
        grad_in,
        grad_back,
    )


def solution(mesh):
    placed = (
        P(("dp", "expert"), "ctx", None),
        P(),
        P(),
        P(),
        P(),
        P(),
        P("expert", None, None),
        P("expert", None, None),
        P(("dp", "expert"), "ctx", None, None, None),
        P(("dp", "expert"), None),
        P(("dp", "expert"), "ctx", None),
    )
    sizes = dict(mesh.shape)
    dense = sizes == {"dp": 4, "ctx": 2, "expert": 4}
    return jax.shard_map(
        dense_shards if dense else shards,
        mesh=mesh,
        in_specs=placed,
        out_specs=(
            P(("dp", "expert"), "ctx", None),
            P(("dp", "expert"), "ctx", None),
            P(),
            P(),
            P(),
            P(),
            P(),
            P("expert", None, None),
            P("expert", None, None),
        ),
        check_vma=False,
    )
```

```python
import functools
import jax
import jax.numpy as jnp
from jax import lax
from jax.experimental import pallas as pl
from jax.experimental.pallas import tpu as pltpu
from jax.sharding import PartitionSpec as P

HEADS = 8
HEAD_DIM = 64
TOP = 2
EPS = 1e-06
SCALE = HEAD_DIM ** (-0.5)
F32 = jnp.float32
BF16 = jnp.bfloat16
HELD = pltpu.HBM
HERE = pl.BlockSpec(memory_space=pltpu.VMEM)
BRIEF = pl.CostEstimate(flops=1, bytes_accessed=1, transcendentals=0)
NT = (((1,), (1,)), ((), ()))
TN = (((0,), (0,)), ((), ()))
NN = (((1,), (0,)), ((), ()))


def mm(a, b, dims=NN):
    return lax.dot_general(a, b, dims, preferred_element_type=F32)


def two_halves(a):
    high = a.astype(BF16)
    return high, (a - high.astype(F32)).astype(BF16)


def stats(value):
    center = value - jnp.mean(value, -1, keepdims=True)
    rstd = lax.rsqrt(jnp.mean(center * center, -1, keepdims=True) + EPS)
    return center * rstd, rstd


def norm_vjp(d_value, unit, rstd, gain):
    d_unit = d_value * gain
    return rstd * (
        d_unit
        - jnp.mean(d_unit, -1, keepdims=True)
        - unit * jnp.mean(d_unit * unit, -1, keepdims=True)
    )


def head_pair(value):
    lane = lax.broadcasted_iota(jnp.int32, value.shape, 1)
    first = lane < HEAD_DIM
    return jnp.concatenate(
        [jnp.where(first, value, 0.0), jnp.where(first, 0.0, value)], axis=0
    ).astype(BF16)


def join_pair(value):
    rows = value.shape[0] // 2
    lane = lax.broadcasted_iota(jnp.int32, (rows, value.shape[1]), 1)
    return jnp.where(lane < HEAD_DIM, value[:rows], value[rows:])


def natural(core, mine, theirs):
    return jnp.where(core == 0, mine, theirs), jnp.where(core == 0, theirs, mine)


def attend_kernel(
    meta_ref, own_ref, other_ref, dyown_ref, dyother_ref, mask_ref, g1_ref, wqkv_ref, wout_ref, g2_ref,
    x_ref, dy_ref, normed_ref, qkv_ref, probs_ref, mix_ref, mid_ref, routed_ref,
    x_s, qkv_s, mix_s,
):
    half = own_ref.shape[1]
    width = own_ref.shape[2]
    pair = 2 * HEAD_DIM
    core = meta_ref[3]
    for mine, theirs, ref in ((dyown_ref, dyother_ref, dy_ref), (own_ref, other_ref, x_ref)):
        first, second = natural(core, mine[0].astype(F32), theirs[0].astype(F32))
        x_s[0:half, :] = first
        x_s[half : 2 * half, :] = second
        ref[...] = x_s[...].astype(BF16)
    x = x_s[...]
    unit, _ = stats(x)
    normed = (unit * g1_ref[...]).astype(BF16)
    normed_ref[...] = normed
    qkv_s[...] = mm(normed, wqkv_ref[...])
    qkv_ref[...] = qkv_s[...].astype(BF16)
    image = core * pl.num_programs(0) + pl.program_id(0)
    is_open = mask_ref[pl.ds(image, 1), :] > 0
    for n in range(width // pair):
        at = n * pair
        query = head_pair(qkv_s[:, at : at + pair])
        keys = qkv_s[:, width + at : width + at + pair].astype(BF16)
        vals = qkv_s[:, 2 * width + at : 2 * width + at + pair].astype(BF16)
        scores = jnp.where(is_open, mm(query, keys, NT) * SCALE, -1e9)
        top = jnp.max(scores, -1, keepdims=True)
        expo = jnp.where(is_open, jnp.exp(scores - top), 0.0)
        probs = (expo / jnp.sum(expo, -1, keepdims=True)).astype(BF16)
        probs_ref[0, n] = probs
        mix_s[:, at : at + pair] = join_pair(mm(probs, vals))
    mix = mix_s[...].astype(BF16)
    mix_ref[...] = mix
    mid = x + mm(mix, wout_ref[...])
    mid_ref[...] = mid
    unit, _ = stats(mid)
    routed_ref[...] = (unit * g2_ref[...]).astype(BF16)


def attend(meta, own, other, dy_own, dy_other, mask, g1, wqkv, wout, g2):
    imgs, half, width = own.shape
    imgs //= 2
    seq = 2 * half
    rows = imgs * seq
    pairs = HEADS // 2
    raw = pl.BlockSpec((1, half, width), lambda i, m: (m[3] * imgs + i, 0, 0))
    one = lambda *s: pl.BlockSpec(s, lambda i, m: (i,) + (0,) * (len(s) - 1))
    fix = lambda *s: pl.BlockSpec(s, lambda i, m: (0,) * len(s))
    late = lambda *s: HELD(s, BF16)
    return pl.pallas_call(
        attend_kernel,
        grid_spec=pltpu.PrefetchScalarGridSpec(
            num_scalar_prefetch=1,
            grid=(imgs,),
            in_specs=[
                raw, raw, raw, raw, fix(*mask.shape), fix(1, width),
                fix(width, 3 * width), fix(width, width), fix(1, width),
            ],
            out_specs=[
                one(seq, width), one(seq, width), one(seq, width), one(seq, 3 * width),
                one(1, pairs, 2 * seq, seq), one(seq, width), one(seq, width), one(seq, width),
            ],
            scratch_shapes=[
                pltpu.VMEM((seq, width), F32),
                pltpu.VMEM((seq, 3 * width), F32),
                pltpu.VMEM((seq, width), F32),
            ],
        ),
        out_shape=[
            late(rows, width),
            jax.ShapeDtypeStruct((rows, width), BF16),
            late(rows, width),
            late(rows, 3 * width),
            late(imgs, pairs, 2 * seq, seq),
            late(rows, width),
            HELD((rows, width), F32),
            jax.ShapeDtypeStruct((rows, width), BF16),
        ],
        compiler_params=pltpu.CompilerParams(vmem_limit_bytes=22 << 20),
        cost_estimate=BRIEF,
        name="attend",
    )(meta, *map(held, (own, other, dy_own, dy_other)), mask, g1, held(wqkv), held(wout), g2)


def assemble_kernel(meta_ref, own_ref, other_ref, out_ref, out_s):
    half = own_ref.shape[1]
    first, second = natural(meta_ref[3], own_ref[0].astype(F32), other_ref[0].astype(F32))
    out_s[0:half, :] = first
    out_s[half : 2 * half, :] = second
    out_ref[...] = out_s[...].astype(BF16)


def assemble(meta, own, other):
    imgs, half, width = own.shape
    imgs //= 2
    raw = pl.BlockSpec((1, half, width), lambda i, m: (m[3] * imgs + i, 0, 0))
    return pl.pallas_call(
        assemble_kernel,
        grid_spec=pltpu.PrefetchScalarGridSpec(
            num_scalar_prefetch=1,
            grid=(imgs,),
            in_specs=[raw, raw],
            out_specs=pl.BlockSpec((2 * half, width), lambda i, m: (i, 0)),
            scratch_shapes=[pltpu.VMEM((2 * half, width), F32)],
        ),
        out_shape=jax.ShapeDtypeStruct((imgs * 2 * half, width), BF16),
        compiler_params=pltpu.CompilerParams(vmem_limit_bytes=6 << 20),
        cost_estimate=BRIEF,
        name="assemble",
    )(meta, own, other)


def row_gates(rows, ids, wr):
    logits = mm(wr, rows, NT)
    row = lax.broadcasted_iota(jnp.int32, logits.shape, 0)
    pick = (row.astype(F32) == ids[0:1, :]) | (row.astype(F32) == ids[1:2, :])
    top = jnp.max(jnp.where(pick, logits, -jnp.inf), 0, keepdims=True)
    expo = jnp.where(pick, jnp.exp(logits - top), 0.0)
    return expo / jnp.sum(expo, 0, keepdims=True), row


def padded(count):
    return -(-count // 16) * 16


def expert_kernel(add, local, meta_ref, rows_ref, dy_ref, ids_ref, wr_ref, wi_ref, wb_ref, *rest):
    sources = [] if local else [wb_ref]
    if add:
        sources += rest[:2]
        rest = rest[2:]
    act_ref, dpre_ref, dout_ref, made_ref, din_ref, wi_s, wb_s, *rest = rest
    if sources:
        *landings, sems = rest
        copies = [pltpu.make_async_copy(v, w, sems.at[n]) for n, (v, w) in enumerate(zip(sources, landings))]
        for copy in copies:
            copy.start()
    count = act_ref.shape[0]
    width = rows_ref.shape[1]
    rows = rows_ref[0:count, :]
    part = wi_s.shape[1] // PIECES
    if local:
        for n in range(PIECES):
            at = pl.ds(pl.multiple_of((n ^ meta_ref[1]) * part, part), part)
            wi_s[:, n * part : (n + 1) * part] = wi_ref[0, :, at]
            wb_s[n * part : (n + 1) * part, :] = wb_ref[0, at, :]

    if ids_ref.shape[0] == 2:
        ids = ids_ref[...].astype(F32)
    else:
        at = padded(count)
        ids = [ids_ref[at : at + 2, :], ids_ref[at + 2 : at + 4, 0 : count - width]]
        ids = jnp.concatenate([v.astype(F32) for v in ids], axis=1)
    gates, row = row_gates(rows, ids, wr_ref[...])
    high, low = two_halves(jnp.where(row == meta_ref[0], gates, 0.0))
    ones = jnp.ones((16, 128), BF16)
    gate = (mm(high, ones, TN) + mm(low, ones, TN))[:, 0:1]
    dout_ref[...] = (gate * dy_ref[...].astype(F32)).astype(BF16)
    wide = wi_s.shape[1] // CHUNKS
    for q in range(CHUNKS):
        if not local and q % (CHUNKS // 2) == 0:
            ref, first = (landings[0], PIECES // 2) if q else (wi_ref, 0)
            if q:
                copies[0].wait()
            for n in range(PIECES // 2):
                to = slice((first + n) * part, (first + n + 1) * part)
                for h in range(2):
                    side = slice(h * part, (h + 1) * part)
                    wi_s[side, to] = ref[n, h]
                    wb_s[to, side] = ref[n, 2 + h]
        here = slice(q * wide, (q + 1) * wide)
        pre = mm(rows, wi_s[:, here])
        square = pre * pre
        inner = pre * (0.7978845608 + 0.0356774081 * square)
        up = 0.5 + 0.5 * jnp.tanh(inner)
        value = pre * up
        act_ref[:, here] = value.astype(BF16)
        slope = up + value * (1.0 - up) * (1.5957691216 + 0.2140644488 * square)
        dpre_ref[:, here] = (mm(dout_ref[...], wb_s[here, :], NT) * slope).astype(BF16)
    made = mm(act_ref[...], wb_s[...]).astype(BF16).astype(F32)
    d_in = mm(dpre_ref[...], wi_s[...], NT)
    total = gate * made
    high, low = two_halves(made * dy_ref[...].astype(F32))
    ones = jnp.ones((16, width), BF16)
    d_gate = (mm(ones, high, NT) + mm(ones, low, NT))[0:8]
    row = lax.broadcasted_iota(jnp.int32, d_gate.shape, 0)
    d_gate = jnp.where(row == meta_ref[0], d_gate, 0.0)
    tail = padded(count)
    if add:
        for copy in copies[-2:]:
            copy.wait()
        pmade_ref, pdin_ref = landings[-2:]
        total += pmade_ref[...].astype(F32)
        d_in += pdin_ref[0:count, :].astype(F32)
        d_gate += read_gate(pdin_ref, count)
    made_ref[...] = total.astype(BF16)
    din_ref[0:count, :] = d_in.astype(BF16)
    high = d_gate.astype(BF16).astype(F32)
    value = jnp.concatenate([high, d_gate - high], axis=0).astype(BF16)
    din_ref[tail : tail + 16, :] = value[:, :width]
    din_ref[tail + 16 : tail + 32, 0 : count - width] = value[:, width:]


CHUNKS = 4


def read_gate(ref, count):
    tail = padded(count)
    width = ref.shape[1]
    value = ref[tail : tail + 16, 0 : min(count, width)].astype(F32)
    if count > width:
        value = jnp.concatenate([value, ref[tail + 16 : tail + 32, 0 : count - width].astype(F32)], axis=1)
    return value[0:8] + value[8:16]


PIECES = 8


def expert(meta, rows, dy, ids, wr, weights, prev=None):
    count, width = dy.shape
    local = weights[0].ndim == 3
    hidden = weights[0].shape[2] if local else PIECES * weights[0].shape[2]
    deep = padded(count) + 32
    first = prev is None
    away = pl.BlockSpec(memory_space=pl.ANY)
    more = [] if first else [away, away]
    landings = [] if local else [pltpu.VMEM(weights[1].shape, BF16)]
    if not first:
        landings += [pltpu.VMEM((count, width), BF16), pltpu.VMEM((deep, width), BF16)]
    if landings:
        landings.append(pltpu.SemaphoreType.DMA((len(landings),)))
    shape = lambda *s: jax.ShapeDtypeStruct(s, BF16)
    return pl.pallas_call(
        functools.partial(expert_kernel, not first, local),
        grid_spec=pltpu.PrefetchScalarGridSpec(
            num_scalar_prefetch=1,
            grid=(1,),
            in_specs=[HERE] * 5 + [HERE if local else away, *more],
            out_specs=[HERE] * 5,
            scratch_shapes=[pltpu.VMEM((width, hidden), BF16), pltpu.VMEM((hidden, width), BF16), *landings],
        ),
        out_shape=[shape(count, hidden), shape(count, hidden), shape(count, width), shape(count, width), shape(deep, width)],
        compiler_params=pltpu.CompilerParams(vmem_limit_bytes=LIMIT << 20),
        cost_estimate=BRIEF,
        name="expert",
    )(meta, rows, dy, ids, wr, weights[0], weights[1] if local else held(weights[1]), *[held(v) for v in prev or ()])


LIMIT = 26


def expert_steps_kernel(add, local, meta_ref, rows_ref, dy_ref, ids_ref, wr_ref, *rest):
    wi_ref, wb_ref, *rest = rest
    sources = [] if local else [wb_ref]
    if add:
        sources += rest[:2]
        rest = rest[2:]
    act_ref, dpre_ref, dout_ref, made_ref, din_ref, gate_s, made_s, din_s, *rest = rest
    step = pl.program_id(0)
    copies = []
    if sources:
        *rest, sems = rest
        landings = rest[len(rest) - len(sources) :]
        rest = rest[: len(rest) - len(sources)]
        copies = [pltpu.make_async_copy(v, w, sems.at[n]) for n, (v, w) in enumerate(zip(sources, landings))]
    if not local:
        wb_ref = landings[0]
    if add:
        pmade_ref, pdin_ref = landings[-2:]
    count = act_ref.shape[0]
    width = rows_ref.shape[1]
    rows = rows_ref[0:count, :]

    @pl.when(step == 0)
    def _():
        for copy in copies:
            copy.start()
        if ids_ref.shape[0] == 2:
            ids = ids_ref[...].astype(F32)
        else:
            at = padded(count)
            ids = [ids_ref[at : at + 2, :], ids_ref[at + 2 : at + 4, 0 : count - width]]
            ids = jnp.concatenate([v.astype(F32) for v in ids], axis=1)
        gates, row = row_gates(rows, ids, wr_ref[...])
        high, low = two_halves(jnp.where(row == meta_ref[0], gates, 0.0))
        ones = jnp.ones((16, 128), BF16)
        gate_s[...] = mm(high, ones, TN) + mm(low, ones, TN)
        gate = gate_s[:, 0:1]
        dout_ref[...] = (gate * dy_ref[...].astype(F32)).astype(BF16)
        made_s[...] = jnp.zeros_like(made_s)
        din_s[...] = jnp.zeros_like(din_s)

    if local:
        part = wi_ref.shape[2] // PIECES
        at = [pl.multiple_of(((2 * step + s) ^ meta_ref[1]) * part, part) for s in range(2)]
        w_in = jnp.concatenate([wi_ref[0, :, pl.ds(v, part)] for v in at], axis=1)
        w_back = jnp.concatenate([wb_ref[0, pl.ds(v, part), :] for v in at], axis=0)
    else:
        wi_s, wb_s = rest
        part = wi_s.shape[0] // 2
        upper = pl.num_programs(0) // 2

        @pl.when(step == upper)
        def _():
            copies[0].wait()

        for ref, first in ((wi_ref, 0), (wb_ref, upper)):

            @pl.when((step < upper) == (first == 0))
            def _():
                for s in range(2):
                    for h in range(2):
                        at = 2 * (step - first) + s
                        wi_s[h * part : (h + 1) * part, s * part : (s + 1) * part] = ref[at, h]
                        wb_s[s * part : (s + 1) * part, h * part : (h + 1) * part] = ref[at, 2 + h]

        w_in, w_back = wi_s[...], wb_s[...]
    pre = mm(rows, w_in)
    square = pre * pre
    inner = pre * (0.7978845608 + 0.0356774081 * square)
    up = 0.5 + 0.5 * jnp.tanh(inner)
    value = pre * up
    act = value.astype(BF16)
    slope = up + value * (1.0 - up) * (1.5957691216 + 0.2140644488 * square)
    here = pl.ds(pl.multiple_of(step * pre.shape[1], pre.shape[1]), pre.shape[1])
    act_ref[:, here] = act
    made_s[...] += mm(act, w_back)
    dpre = (mm(dout_ref[...], w_back, NT) * slope).astype(BF16)
    dpre_ref[:, here] = dpre
    din_s[...] += mm(dpre, w_in, NT)

    @pl.when(step == pl.num_programs(0) - 1)
    def _():
        gate = gate_s[:, 0:1]
        made = made_s[...].astype(BF16).astype(F32)
        total = gate * made
        d_in = din_s[...]
        high, low = two_halves(made * dy_ref[...].astype(F32))
        ones = jnp.ones((16, made.shape[1]), BF16)
        d_gate = (mm(ones, high, NT) + mm(ones, low, NT))[0:8]
        row = lax.broadcasted_iota(jnp.int32, d_gate.shape, 0)
        d_gate = jnp.where(row == meta_ref[0], d_gate, 0.0)
        tail = padded(count)
        for copy in copies[0 if local else 1 :]:
            copy.wait()
        if add:
            total += pmade_ref[...].astype(F32)
            d_in += pdin_ref[0:count, :].astype(F32)
            d_gate += read_gate(pdin_ref, count)
        made_ref[...] = total.astype(BF16)
        din_ref[0:count, :] = d_in.astype(BF16)
        high = d_gate.astype(BF16).astype(F32)
        value = jnp.concatenate([high, d_gate - high], axis=0).astype(BF16)
        if count > d_in.shape[1]:
            cut = d_in.shape[1]
            din_ref[tail : tail + 16, :] = value[:, :cut]
            din_ref[tail + 16 : tail + 32, 0 : count - cut] = value[:, cut:]
        else:
            din_ref[tail : tail + 16, 0:count] = value


def expert_steps(meta, rows, dy, ids, wr, weights, prev=None):
    count = dy.shape[0]
    width = rows.shape[1]
    local = weights[0].ndim == 3
    piece = weights[0].shape[2] // PIECES if local else weights[0].shape[2]
    hidden = PIECES * piece
    steps = PIECES // 2
    deep = padded(count) + 16 * -(-count // width)
    fix = lambda *s: pl.BlockSpec(s, lambda q, m: (0,) * len(s))
    first = prev is None
    away = pl.BlockSpec(memory_space=pl.ANY)
    more = [] if first else [away, away]
    landings = [] if local else [pltpu.VMEM(weights[1].shape, BF16)]
    if not first:
        landings += [pltpu.VMEM((count, width), BF16), pltpu.VMEM((deep, width), BF16)]
    if landings:
        landings.append(pltpu.SemaphoreType.DMA((len(landings),)))
    given = [] if first else [held(v) for v in prev]
    ends = [fix(count, width), fix(deep, width)] if first else [HERE, HERE]
    kept = HELD if first else jax.ShapeDtypeStruct
    return pl.pallas_call(
        functools.partial(expert_steps_kernel, prev is not None, local),
        grid_spec=pltpu.PrefetchScalarGridSpec(
            num_scalar_prefetch=1,
            grid=(steps,),
            in_specs=[HERE, fix(*dy.shape), HERE, HERE, HERE, HERE if local else away, *more],
            out_specs=[HERE] * 3 + ends,
            scratch_shapes=[
                pltpu.VMEM((count, 128), F32),
                pltpu.VMEM((count, width), F32),
                pltpu.VMEM((count, width), F32),
            ]
            + ([] if local else [pltpu.VMEM((width, 2 * piece), BF16), pltpu.VMEM((2 * piece, width), BF16)])
            + landings,
        ),
        out_shape=[
            jax.ShapeDtypeStruct((count, hidden), BF16),
            jax.ShapeDtypeStruct((count, hidden), BF16),
            jax.ShapeDtypeStruct((count, width), BF16),
            kept((count, width), BF16),
            kept((deep, width), BF16),
        ],
        compiler_params=pltpu.CompilerParams(vmem_limit_bytes=20 << 20),
        cost_estimate=BRIEF,
        name="expert_steps",
    )(meta, rows, dy if first else held(dy), ids, wr, weights[0], weights[1] if local else held(weights[1]), *given)


def weight_kernel(n, *refs):
    rows, acts, dpres, douts = (refs[g * n : (g + 1) * n] for g in range(4))
    iown_ref, igive_ref, bown_ref, bgive_ref = refs[4 * n :]
    wide = iown_ref.shape[0] * iown_ref.shape[1]
    here = pl.ds(pl.multiple_of(pl.program_id(0) * wide, wide), wide)
    results = []
    for left, right in ((dpres, rows), (acts, douts)):
        total = 0.0
        for b in range(n):
            count = left[b].shape[0]
            total = total + mm(left[b][:, here], right[b][0:count, :], TN)
        results.append(total.astype(BF16).reshape(iown_ref.shape))
    grad_in, grad_back = results
    first = pl.program_id(0) < pl.num_programs(0) // 2

    @pl.when(first)
    def _():
        iown_ref[...] = grad_in
        bown_ref[...] = grad_back

    @pl.when(jnp.logical_not(first))
    def _():
        igive_ref[...] = grad_in
        bgive_ref[...] = grad_back


def weight_grads(rows, acts, dpres, douts, late=False):
    n = len(rows)
    width = rows[0].shape[1]
    piece = acts[0].shape[1] // PIECES
    steps = PIECES // 2
    own = pl.BlockSpec((2, piece, width), lambda q: (jnp.minimum(q, steps // 2 - 1), 0, 0))
    give = pl.BlockSpec((2, piece, width), lambda q: (jnp.maximum(q - steps // 2, 0), 0, 0))
    return pl.pallas_call(
        functools.partial(weight_kernel, n),
        grid=(steps,),
        in_specs=[HERE] * (4 * n),
        out_specs=[own, give, own, give],
        out_shape=[(HELD if late and g % 2 == 0 else jax.ShapeDtypeStruct)((PIECES // 2, piece, width), BF16) for g in range(4)],
        compiler_params=pltpu.CompilerParams(vmem_limit_bytes=14 << 20),
        cost_estimate=BRIEF,
        name="weight_grads",
    )(*rows, *acts, *dpres, *douts)


def finish_kernel(meta_ref, im_ref, ir_ref, bm_ref, br_ref, gin_ref, gback_ref):
    mine = pl.program_id(0) < pl.num_programs(0) // 2
    flip = meta_ref[1] % 2 == 1
    piece, width = im_ref.shape[1:]
    for m_ref, r_ref, out_ref in ((im_ref, ir_ref, gin_ref), (bm_ref, br_ref, gback_ref)):
        value = jnp.where(mine, m_ref[...], r_ref[...]).astype(F32)
        first = jnp.where(flip, value[1], value[0])
        second = jnp.where(flip, value[0], value[1])
        if out_ref is gin_ref:
            out_ref[0, :, 0:piece] = jnp.transpose(first)
            out_ref[0, :, piece : 2 * piece] = jnp.transpose(second)
        else:
            out_ref[0, 0:piece, :] = first
            out_ref[0, piece : 2 * piece, :] = second


def finish_expert(meta, in_mine, in_recv, back_mine, back_recv):
    upper, piece, width = in_mine.shape
    steps = upper
    own = pl.BlockSpec((2, piece, width), lambda q, m: (jnp.minimum(q, steps // 2 - 1), 0, 0))
    give = pl.BlockSpec((2, piece, width), lambda q, m: (jnp.maximum(q - steps // 2, 0), 0, 0))
    return pl.pallas_call(
        finish_kernel,
        grid_spec=pltpu.PrefetchScalarGridSpec(
            num_scalar_prefetch=1,
            grid=(steps,),
            in_specs=[own, give, own, give],
            out_specs=[
                pl.BlockSpec((1, width, 2 * piece), lambda q, m: (0, 0, q ^ (m[1] // 2))),
                pl.BlockSpec((1, 2 * piece, width), lambda q, m: (0, q ^ (m[1] // 2), 0)),
            ],
        ),
        out_shape=[
            jax.ShapeDtypeStruct((1, width, PIECES * piece), F32),
            jax.ShapeDtypeStruct((1, PIECES * piece, width), F32),
        ],
        compiler_params=pltpu.CompilerParams(vmem_limit_bytes=14 << 20),
        cost_estimate=BRIEF,
        name="finish_expert",
    )(meta, in_mine, in_recv, back_mine, back_recv)


def split_halves(core, whole_ref, own_ref, other_ref):
    imgs, half, _ = own_ref.shape
    for i in range(imgs):
        at = 2 * half * i
        first, second = whole_ref[at : at + half, :], whole_ref[at + half : at + 2 * half, :]
        mine, theirs = natural(core, first, second)
        own_ref[i] = mine.astype(BF16)
        other_ref[i] = theirs.astype(BF16)


def back_kernel(
    meta_ref, din0_ref, din1_ref,
    ids_ref, dy_ref, mid_ref, routed_ref, wr_ref, g2_ref, mix_ref, wout_ref,
    probs_ref, qkv_ref, x_ref, normed_ref, wqkv_ref, g1_ref,
    own_ref, other_ref, gown_ref, ggive_ref,
    dmid_s, dmix_s, dqkv_s, tok_s, grad_s, small_s,
):
    step = pl.program_id(0)
    imgs = pl.num_programs(0)
    seq = qkv_ref.shape[0]
    width = x_ref.shape[1]
    half = seq // 2
    pair = 2 * HEAD_DIM
    rows = x_ref.shape[0]

    @pl.when(step == 0)
    def _():
        routed = routed_ref[...]
        wr = wr_ref[...]
        gates, _ = row_gates(routed, ids_ref[...].astype(F32), wr)
        d_gate = read_gate(din0_ref, rows) + read_gate(din1_ref, rows)
        d_gate = jnp.concatenate([d_gate, jnp.zeros_like(d_gate)], axis=0)
        d_logits = gates * (d_gate - jnp.sum(gates * d_gate, 0, keepdims=True))
        high, low = two_halves(d_logits)
        small_s[...] = jnp.zeros_like(small_s)
        small_s[0:16, :] = mm(high, routed) + mm(low, routed)
        d_routed = din0_ref[0:rows, :].astype(F32) + din1_ref[0:rows, :].astype(F32)
        d_routed = d_routed + mm(high, wr, TN) + mm(low, wr, TN)
        unit, rstd = stats(mid_ref[...])
        small_s[16:17, :] = jnp.sum(d_routed * unit, 0, keepdims=True)
        d_mid = dy_ref[...].astype(F32) + norm_vjp(d_routed, unit, rstd, g2_ref[...])
        dmid_s[...] = d_mid
        d_branch = d_mid.astype(BF16)
        grad_s[:, 3 * width : 4 * width] = mm(mix_ref[...], d_branch, TN).astype(BF16)
        dmix_s[...] = mm(d_branch, wout_ref[...], NT)

    base = pl.multiple_of(step * seq, 8)
    for n in range(width // pair):
        at = n * pair
        d_mix = head_pair(dmix_s[pl.ds(base, seq), at : at + pair])
        query = head_pair(qkv_ref[:, at : at + pair].astype(F32))
        keys = qkv_ref[:, width + at : width + at + pair]
        vals = qkv_ref[:, 2 * width + at : 2 * width + at + pair]
        low = probs_ref[0, n]
        probs = low.astype(F32)
        d_probs = mm(d_mix, vals, NT)
        d_scores = probs * (d_probs - jnp.sum(probs * d_probs, -1, keepdims=True))
        d_scores = d_scores.astype(BF16)
        d_query = join_pair(mm(d_scores, keys)) * SCALE
        d_keys = mm(d_scores, query, TN) * SCALE
        d_vals = mm(low, d_mix, TN)
        dqkv_s[pl.ds(base, seq), at : at + pair] = d_query.astype(BF16)
        dqkv_s[pl.ds(base, seq), width + at : width + at + pair] = d_keys.astype(BF16)
        dqkv_s[pl.ds(base, seq), 2 * width + at : 2 * width + at + pair] = d_vals.astype(BF16)

    @pl.when(step == imgs - 1)
    def _():
        d_qkv = dqkv_s[...]
        grad_s[:, : 3 * width] = mm(normed_ref[...], d_qkv, TN).astype(BF16)
        d_normed = mm(d_qkv, wqkv_ref[...], NT)
        unit, rstd = stats(x_ref[...].astype(F32))
        small_s[17:18, :] = jnp.sum(d_normed * unit, 0, keepdims=True)
        grad_s[:, 4 * width :] = jnp.transpose(small_s[...]).astype(BF16)
        tok_s[...] = dmid_s[...] + norm_vjp(d_normed, unit, rstd, g1_ref[...])
        split_halves(meta_ref[3], tok_s, own_ref, other_ref)
        part = width // SHARES

        @pl.loop(0, SHARES // 2)
        def _(r):
            to = pl.ds(pl.multiple_of(r * part, part), part)
            for ref, first in ((gown_ref, 0), (ggive_ref, SHARES // 2)):
                there = pl.multiple_of(((r + first) ^ meta_ref[2]) * part, part)
                ref[to, :] = grad_s[pl.ds(there, part), :]


SHARES = 32


def attend_back(meta, dins, ids, dy, mid, routed, wr, g2, mix, wout, probs, qkv, x, normed, wqkv, g1):
    imgs = probs.shape[0]
    rows, width = x.shape
    seq = rows // imgs
    pairs = HEADS // 2
    wide = 4 * width + 128
    fix = lambda *s: pl.BlockSpec(s, lambda i, m: (0,) * len(s))
    return pl.pallas_call(
        back_kernel,
        grid_spec=pltpu.PrefetchScalarGridSpec(
            num_scalar_prefetch=1,
            grid=(imgs,),
            in_specs=[fix(*a.shape) for a in dins] + [
                fix(2, rows), fix(rows, width), fix(rows, width), fix(rows, width),
                fix(16, width), fix(1, width), fix(rows, width), fix(width, width),
                pl.BlockSpec((1, pairs, 2 * seq, seq), lambda i, m: (i, 0, 0, 0)),
                pl.BlockSpec((seq, 3 * width), lambda i, m: (i, 0)),
                fix(rows, width), fix(rows, width), fix(width, 3 * width), fix(1, width),
            ],
            out_specs=[
                fix(imgs, seq // 2, width), fix(imgs, seq // 2, width),
                fix(width // 2, wide), fix(width // 2, wide),
            ],
            scratch_shapes=[
                pltpu.VMEM((rows, width), F32),
                pltpu.VMEM((rows, width), F32),
                pltpu.VMEM((rows, 3 * width), BF16),
                pltpu.VMEM((rows, width), F32),
                pltpu.VMEM((width, wide), BF16),
                pltpu.VMEM((128, width), F32),
            ],
        ),
        out_shape=[
            jax.ShapeDtypeStruct((imgs, seq // 2, width), BF16),
            jax.ShapeDtypeStruct((imgs, seq // 2, width), BF16),
            jax.ShapeDtypeStruct((width // 2, wide), BF16),
            jax.ShapeDtypeStruct((width // 2, wide), BF16),
        ],
        compiler_params=pltpu.CompilerParams(vmem_limit_bytes=32 << 20),
        cost_estimate=BRIEF,
        name="attend_back",
    )(meta, *dins, ids, dy, mid, routed, wr, g2, mix, wout, probs, qkv, x, normed, wqkv, g1)


def shared_kernel(meta_ref, mine_ref, recv_ref, gqkv_ref, gout_ref, small_ref, all_s):
    upper, wide = mine_ref.shape
    width = 2 * upper
    part = width // SHARES
    all_s[0:upper, :] = mine_ref[...]
    all_s[upper:width, :] = recv_ref[...]

    @pl.loop(0, SHARES)
    def _(i):
        there = pl.multiple_of((i ^ meta_ref[2]) * part, part)
        value = all_s[pl.ds(there, part), :].astype(F32)
        at = pl.ds(pl.multiple_of(i * part, part), part)
        gqkv_ref[at, :] = value[:, : 3 * width]
        gout_ref[at, :] = value[:, 3 * width : 4 * width]
        small_ref[at, :] = value[:, 4 * width :]


def finish_shared(meta, mine, recv):
    upper, wide = mine.shape
    width = 2 * upper
    fix = lambda *s: pl.BlockSpec(s, lambda i, m: (0,) * len(s))
    return pl.pallas_call(
        shared_kernel,
        grid_spec=pltpu.PrefetchScalarGridSpec(
            num_scalar_prefetch=1,
            grid=(1,),
            in_specs=[fix(upper, wide), fix(upper, wide)],
            out_specs=[fix(width, 3 * width), fix(width, width), fix(width, wide - 4 * width)],
            scratch_shapes=[pltpu.VMEM((width, wide), BF16)],
        ),
        out_shape=[
            jax.ShapeDtypeStruct((width, 3 * width), F32),
            jax.ShapeDtypeStruct((width, width), F32),
            jax.ShapeDtypeStruct((width, wide - 4 * width), F32),
        ],
        compiler_params=pltpu.CompilerParams(vmem_limit_bytes=16 << 20),
        cost_estimate=BRIEF,
        name="finish_shared",
    )(meta, mine, recv)


def combine_kernel(meta_ref, mid_ref, a_ref, b_ref, own_ref, other_ref, s_ref):
    s_ref[...] = mid_ref[...] + (a_ref[...].astype(F32) + b_ref[...].astype(F32))
    split_halves(meta_ref[3], s_ref, own_ref, other_ref)


def combine(meta, mid, parts, imgs):
    rows, width = mid.shape
    seq = rows // imgs
    spec = pl.BlockSpec((seq, width), lambda i, m: (i, 0))
    out = pl.BlockSpec((1, seq // 2, width), lambda i, m: (i, 0, 0))
    shape = jax.ShapeDtypeStruct((imgs, seq // 2, width), BF16)
    return pl.pallas_call(
        combine_kernel,
        grid_spec=pltpu.PrefetchScalarGridSpec(
            num_scalar_prefetch=1,
            grid=(imgs,),
            in_specs=[spec] * 3,
            out_specs=[out, out],
            scratch_shapes=[pltpu.VMEM((seq, width), F32)],
        ),
        out_shape=[shape, shape],
        compiler_params=pltpu.CompilerParams(vmem_limit_bytes=8 << 20),
        cost_estimate=BRIEF,
        name="combine",
    )(meta, mid, *parts)


def place_kernel(meta_ref, a_own_ref, a_recv_ref, b_own_ref, b_recv_ref, a_ref, b_ref):
    imgs = pl.num_programs(0) // 2
    mine = pl.program_id(0) // imgs == meta_ref[3]
    a_ref[...] = jnp.where(mine, a_own_ref[...], a_recv_ref[...])
    b_ref[...] = jnp.where(mine, b_own_ref[...], b_recv_ref[...])


def place(meta, *arrays):
    imgs, half, width = arrays[0].shape
    spec = pl.BlockSpec((1, half, width), lambda j, m: (j % imgs, 0, 0))
    out = pl.BlockSpec((1, half, width), lambda j, m: (j, 0, 0))
    shape = jax.ShapeDtypeStruct((2 * imgs, half, width), BF16)
    return pl.pallas_call(
        place_kernel,
        grid_spec=pltpu.PrefetchScalarGridSpec(
            num_scalar_prefetch=1, grid=(2 * imgs,), in_specs=[spec] * 4, out_specs=[out, out]
        ),
        out_shape=[shape, shape],
        compiler_params=pltpu.CompilerParams(vmem_limit_bytes=4 << 20),
        cost_estimate=BRIEF,
        name="place",
    )(meta, *arrays)


def pack_kernel(meta_ref, wi_ref, wb_ref, out_ref):
    part = out_ref.shape[1]
    for h in range(2):
        at = slice(h * part, (h + 1) * part)
        out_ref[h] = wi_ref[0, at, :]
        out_ref[2 + h] = wb_ref[0, :, at]


def pack_piece(meta, w_in, w_back):
    width, hidden = w_in.shape[1:]
    piece = hidden // PIECES
    return pl.pallas_call(
        pack_kernel,
        grid_spec=pltpu.PrefetchScalarGridSpec(
            num_scalar_prefetch=1,
            grid=(1,),
            in_specs=[
                pl.BlockSpec((1, width, piece), lambda i, m: (0, 0, m[1])),
                pl.BlockSpec((1, piece, width), lambda i, m: (0, m[1], 0)),
            ],
            out_specs=pl.BlockSpec((4, piece, piece), lambda i, m: (0, 0, 0)),
        ),
        out_shape=jax.ShapeDtypeStruct((4, piece, piece), BF16),
        compiler_params=pltpu.CompilerParams(vmem_limit_bytes=4 << 20),
        cost_estimate=BRIEF,
        name="pack_piece",
    )(meta, held(w_in), held(w_back))


def by_rows(count, step, body):
    @pl.loop(0, count // step)
    def _(n):
        body(n * step if isinstance(n, int) else pl.multiple_of(n * step, step))


def merge_kernel(plan, *refs):
    refs = list(refs)
    takes = [[[(refs.pop(0), at) for at in views] for views in groups] for groups, _, _ in plan]
    full = lambda n: (slice(None),) * n

    def rows_of(ref, lead, at, size):
        return lead + full(len(ref.shape) - 2 - len(lead)) + (pl.ds(at, size), slice(None))

    for groups, (_, axis, cuts) in zip(takes, plan):
        outs = [refs.pop(0) for _ in cuts]
        head = groups[0][0][0]
        count = head.shape[-2]
        step = 16 if len(head.shape) == 2 else 64
        if axis is not None:
            size = head.shape[axis]
            for k, (ref, _) in enumerate(groups[0]):

                def copy(at, k=k, ref=ref):
                    if len(ref.shape) == 2:
                        outs[0][pl.ds(k * size + at, step), :] = ref[pl.ds(at, step), :]
                    else:
                        lead = full(axis) + (slice(k * size, (k + 1) * size),)
                        outs[0][rows_of(outs[0], lead, at, step)] = ref[rows_of(ref, (), at, step)]

                by_rows(count, step, copy)
            continue
        for g, take in enumerate(groups):
            place = (g,) if len(groups) > 1 else ()
            if len(head.shape) == 2:
                for out, cut in zip(outs, cuts):
                    start = cut.start or 0

                    def add(at, out=out, start=start):
                        total = sum(ref[pl.ds(start + at, step), :].astype(F32) for ref, _ in take)
                        out[pl.ds(at, step), :] = total.astype(BF16)

                    by_rows(out.shape[0], step, add)
                continue

            def add(at, take=take, place=place):
                parts = [ref[rows_of(ref, () if view is ... else (view,), at, step)] for ref, view in take]
                total = sum(v.astype(F32) for v in parts).astype(BF16)
                for out, cut in zip(outs, cuts):
                    out[rows_of(out, place, at, step)] = total[cut]

            by_rows(count, step, add)


def merge(*items):
    plan, shapes, arrays = [], [], []
    for groups, axis, cuts in items:
        head = groups[0][0]
        shape = jax.eval_shape(lambda v: v[head[1]], head[0]).shape if isinstance(head, tuple) else head.shape
        first = jax.ShapeDtypeStruct(shape, BF16)
        if axis is not None:
            cuts = [None]
            shape = list(first.shape)
            shape[axis] *= len(groups[0])
            shapes.append(jax.ShapeDtypeStruct(tuple(shape), BF16))
        else:
            lead = (len(groups),) if len(groups) > 1 else ()
            shapes += [
                jax.ShapeDtypeStruct(lead + jax.eval_shape(lambda v, c=c: v[c], first).shape, BF16) for c in cuts
            ]
        pairs = [[v if isinstance(v, tuple) else (v, ...) for v in g] for g in groups]
        plan.append(([[at for _, at in g] for g in pairs], axis, cuts))
        arrays += [v for g in pairs for v, _ in g]
    return pl.pallas_call(
        functools.partial(merge_kernel, plan),
        out_shape=shapes,
        compiler_params=pltpu.CompilerParams(vmem_limit_bytes=16 << 20),
        cost_estimate=BRIEF,
        name="merge",
    )(*arrays)


def held(value):
    return pltpu.with_memory_space_constraint(value, pltpu.HBM)


SWAP = [(0, 1), (1, 0)]


def xor(k, n=4):
    return [(i, i ^ k) for i in range(n)]


def send(value, axis, pairs):
    return lax.ppermute(value, axis, pairs)


def add_low(a, b):
    return (a.astype(F32) + b.astype(F32)).astype(BF16)


def after(value, *earlier):
    return lax.optimization_barrier((value, *earlier))[0]


def tie(*values):
    return lax.optimization_barrier(values)


def fan(value, axis):
    rows = value.shape[0] // 4
    return [send(value[k * rows : (k + 1) * rows], axis, xor(k)) for k in (1, 2, 3)]


def add_fan(value, got):
    total = value[: value.shape[0] // 4].astype(F32)
    for v in got:
        total = total + v.astype(F32)
    return total.astype(BF16)


def dense_shards(
    tokens, gain_one, w_qkv, w_out, gain_two, w_router, w_in, w_back, route_ids, key_mask, cotangent
):
    nimg, half, width = tokens.shape
    imgs = nimg // 2
    rows = imgs * 2 * half
    experts = w_router.shape[1]
    piece = w_in.shape[2] // PIECES
    core = lax.axis_index("ctx")
    z = lax.axis_index("expert")
    me = core * 4 + lax.axis_index("dp")
    meta = jnp.stack([z, me, me * 4 + z, core]).astype(jnp.int32)
    meta_pair = jnp.stack([z ^ 2, me, me * 4 + z, core]).astype(jnp.int32)
    far = lambda v: send(v, "expert", xor(1))
    swap = lambda v: send(v, "ctx", SWAP)

    pack = pack_piece(meta, w_in, w_back)
    codes = after(route_ids, pack).reshape(nimg, half, TOP)
    codes = codes[..., 0] + experts * codes[..., 1]
    tok_other, dy_other, codes_other = swap(tokens), swap(cotangent), swap(codes)
    first = jnp.where(core == 0, codes, codes_other)
    second = jnp.where(core == 0, codes_other, codes)
    codes = lax.dynamic_slice_in_dim(jnp.concatenate([first, second], 1), core * imgs, imgs, 0)
    codes = codes.reshape(1, rows)
    ids = jnp.concatenate([codes % experts, codes // experts], 0)
    wide = jnp.pad(ids, ((0, 0), (0, 2 * width - rows))).reshape(TOP, 2, width)
    ids_pack = jnp.concatenate([wide[:, 0], wide[:, 1]], 0).astype(BF16)
    ids_pack = jnp.pad(ids_pack, ((padded(rows) - rows, 12), (0, 0)))
    wr = jnp.pad(w_router.T, ((0, 16 - experts), (0, 0)))
    g1, g2 = gain_one[None, :], gain_two[None, :]

    far_raw, pack = far(after(cotangent, pack)), send(pack, "expert", xor(2))
    x_rows, dy, normed, qkv, probs, mix, mid, routed = attend(
        meta, tokens, tok_other, cotangent, dy_other, key_mask, g1, w_qkv, w_out, g2
    )
    own_one = expert_steps(meta, routed, dy, ids, wr, (w_in, w_back))
    far_rows = jnp.concatenate([routed, ids_pack], 0)
    pack, wr_far = after(pack, routed), after(wr, own_one[2])

    packs = [pack] + [send(pack, "dp", xor(k)) for k in (1, 2, 3)]
    far_rows = far(far_rows)
    far_raw = after(far_raw, own_one[2])
    far_dy = assemble(meta, far_raw, swap(far_raw))
    far_one = expert_steps(meta, far_rows, far_dy, far_rows, wr_far, (w_in, w_back))
    *packs, wr_far = tie(*packs, after(wr, far_one[2]))
    packs = jnp.stack(packs)
    pair = [packs, swap(packs)]
    grads = weight_grads([routed, far_rows], *zip(own_one[:3], far_one[:3]), late=True)
    wr_far = after(wr_far, grads[0])

    far_two = expert(meta_pair, far_rows, far_dy, far_rows, wr_far, pair, far_one[3:])
    head, tail = slice(0, 2), slice(2, 4)
    even, odd = [(slice(None), slice(k, k + 1)) for k in (0, 1)]
    square = lambda v: v.reshape(2, 2, piece, width)

    def across(a, a_give, b, b_give):
        return merge(
            ([[a, swap(a_give)]], None, [head, tail]), ([[square(b), square(swap(b_give))]], None, [even, odd])
        )

    one = across(*grads)
    wr_own, *one = tie(after(wr, far_two[2]), *one)
    far_din, far_made = far_two[4], far_two[3]

    y_way, x_way = ("dp", xor(2)), ("dp", xor(1))
    own_two = expert(meta_pair, routed, dy, ids, wr_own, pair, own_one[3:])
    grads = weight_grads([routed, far_rows], *zip(own_two[:3], far_two[:3]))
    din_far, a_got, b_got, *grads = tie(far(far_din), send(one[1], *y_way), send(one[3], *x_way), *grads)
    a_one, b_one = [one[0], a_got], [one[2], b_got]

    two = tie(*across(*grads))

    a_two, b_two = [two[0], send(two[1], *y_way)], [two[2], send(two[3], *x_way)]
    far_made = far(after(far_made, din_far))
    tok_own, tok_give, shared, shared_give = attend_back(
        meta, [after(own_two[4], *two), din_far], ids, dy, mid, routed, wr, g2, mix, w_out, probs, qkv, x_rows, normed, w_qkv, g1
    )
    halves = [slice(0, 1), slice(1, 2)]
    line = lambda v: v.reshape(2, piece, width)
    flat = lambda group: [line(v) for v in group]
    one, one_give, two, two_give, far_made, shared, shared_give, tok_give = tie(
        *merge(([a_one, flat(b_one)], None, halves), ([a_two, flat(b_two)], None, halves)),
        far_made,
        shared,
        shared_give,
        tok_give,
    )
    mix_own, mix_give = combine(meta, mid, [own_two[3], far_made], imgs)
    quarters = lambda n: [slice(k * n, (k + 1) * n) for k in range(4)]
    everything = [slice(None)]
    second = lambda give: [send(give[0], *x_way), send(give[1], *y_way)]
    got = second(two_give)
    two, *shared, tok_got, mix_got = tie(
        *merge(
            ([[(two, 0), got[0]], [(two, 1), got[1]]], None, everything),
            ([[shared, swap(shared_give)]], None, quarters(width // 8)),
        ),
        swap(tok_give),
        swap(mix_give),
    )
    spread = lambda parts, axis: [send(v, axis, xor(k)) for k, v in zip((1, 2, 3), parts)]
    mixed, grad_tokens = place(meta, mix_own, mix_got, tok_own, tok_got)
    got, cross = second(one_give), send(two, "expert", xor(2))
    a, b, *shared, mixed, grad_tokens = tie(
        *merge(
            ([[(one, 0), got[0], (cross, 0)]], None, everything),
            ([[(one, 1), got[1], (cross, 1)]], None, everything),
            ([[shared[0], *spread(shared[1:], "dp")]], None, quarters(width // 32)),
        ),
        mixed,
        grad_tokens,
    )
    b = b[None]
    a, b, shared = tie(
        *merge(
            ([[a, send(a, *x_way)]], 0, None),
            ([[b, send(b, *y_way)]], 0, None),
            ([[shared[0], *spread(shared[1:], "expert")]], None, everything),
        )
    )
    a, b, shared = tie(
        *merge(
            ([[a, send(a, *y_way)]], 0, None),
            ([[b, send(b, *x_way)]], 1, None),
            ([[shared, *spread([shared] * 3, "expert")]], 0, None),
        )
    )
    b = b.reshape(a.shape)
    grad_in, grad_back = finish_expert(meta, a, swap(a), b, swap(b))
    (shared,) = merge(([[after(shared, grad_in, grad_back), *spread([shared] * 3, "dp")]], 0, None))
    grad_qkv, grad_out, small = finish_shared(meta, shared, swap(shared))
    return (
        mixed,
        grad_tokens,
        small[:, 17],
        grad_qkv,
        grad_out,
        small[:, 16],
        small[:, :experts],
        grad_in,
        grad_back,
    )


def norm_rows(value, gain):
    center = value - jnp.mean(value, -1, keepdims=True)
    spread = jnp.mean(center * center, -1, keepdims=True)
    return center * lax.rsqrt(spread + 1e-06) * gain


def smooth_gelu(value):
    return 0.5 * value * (1.0 + jnp.tanh(0.7978845608 * (value + 0.044715 * value * value * value)))


def forward(tokens, gain_one, w_qkv, w_out, gain_two, w_router, w_in, w_back, flat_ids, live):
    nimg, half, width = tokens.shape
    count = nimg * half
    experts_all = w_router.shape[1]
    capacity = max(2, 2 * TOP * count // experts_all)
    x_rows = tokens.astype(jnp.float32).reshape(count, width)
    normed = norm_rows(x_rows, gain_one).astype(jnp.bfloat16)
    qkv = jnp.dot(normed, w_qkv, preferred_element_type=jnp.float32).astype(jnp.bfloat16)
    qkv = qkv.reshape(nimg, half, 3 * width)
    query = qkv[..., :width]
    keys_local = qkv[..., width : 2 * width]
    vals_local = qkv[..., 2 * width :]
    keys, vals = (
        lax.all_gather(keys_local, "ctx", axis=1, tiled=True),
        lax.all_gather(vals_local, "ctx", axis=1, tiled=True),
    )
    seq = keys.shape[1]
    query4 = query.reshape(nimg, half, HEADS, HEAD_DIM)
    keys4 = keys.reshape(nimg, seq, HEADS, HEAD_DIM)
    vals4 = vals.reshape(nimg, seq, HEADS, HEAD_DIM)
    scale = HEAD_DIM ** (-0.5)
    scores = (
        jnp.einsum("iqhc,ikhc->ihqk", query4, keys4, preferred_element_type=jnp.float32) * scale
    )
    open_keys = live[:, None, None, :]
    masked = jnp.where(open_keys, scores, -1000000000.0)
    topmost = jnp.max(masked, -1, keepdims=True)
    expo = jnp.where(open_keys, jnp.exp(masked - topmost), 0.0)
    probs = expo / jnp.sum(expo, -1, keepdims=True)
    probs_low = probs.astype(jnp.bfloat16)
    mix = jnp.einsum("ihqk,ikhc->iqhc", probs_low, vals4, preferred_element_type=jnp.float32)
    mix = mix.reshape(count, width).astype(jnp.bfloat16)
    mid = x_rows + jnp.dot(mix, w_out, preferred_element_type=jnp.float32)
    routed = norm_rows(mid, gain_two).astype(jnp.bfloat16)
    logits = jnp.dot(routed, w_router, preferred_element_type=jnp.float32)
    pick = flat_ids[:, :, None] == jnp.arange(experts_all, dtype=jnp.int32)[None, None, :]
    chosen = jnp.sum(jnp.where(pick, logits[:, None, :], 0.0), -1)
    expo_gate = jnp.exp(chosen)
    gates = expo_gate / jnp.sum(expo_gate, -1, keepdims=True)
    pair_ids = flat_ids.reshape(-1)
    hits = (pair_ids[:, None] == jnp.arange(experts_all, dtype=jnp.int32)[None, :]).astype(
        jnp.int32
    )
    before = jnp.cumsum(hits, 0) - hits
    slots = jnp.sum(before * hits, 1)
    where_rows = pair_ids * capacity + slots
    sent = jnp.repeat(routed, TOP, axis=0)
    buffer = jnp.zeros((experts_all * capacity, width), jnp.bfloat16).at[where_rows].set(sent)
    buffer = buffer.reshape(experts_all, capacity, width)
    arrived = lax.all_to_all(buffer, "expert", split_axis=0, concat_axis=1, tiled=True)
    pre = jnp.einsum("erd,edf->erf", arrived, w_in, preferred_element_type=jnp.float32)
    act = smooth_gelu(pre).astype(jnp.bfloat16)
    made = jnp.einsum("erf,efd->erd", act, w_back, preferred_element_type=jnp.float32).astype(
        jnp.bfloat16
    )
    returned = lax.all_to_all(made, "expert", split_axis=1, concat_axis=0, tiled=True)
    picked = returned.reshape(experts_all * capacity, width)[where_rows].reshape(count, TOP, width)
    output = mid + jnp.sum(gates[:, :, None] * picked.astype(jnp.float32), 1)
    return (
        x_rows,
        normed,
        query4,
        keys4,
        vals4,
        probs,
        probs_low,
        mix,
        mid,
        routed,
        pick,
        gates,
        where_rows,
        arrived,
        pre,
        act,
        picked,
        output,
        capacity,
    )


def shards(
    tokens, gain_one, w_qkv, w_out, gain_two, w_router, w_in, w_back, route_ids, key_mask, cotangent
):
    nimg, half, width = tokens.shape
    count = nimg * half
    experts_all = w_router.shape[1]
    flat_ids = route_ids.reshape(count, TOP)
    live = key_mask > 0
    state = forward(
        tokens, gain_one, w_qkv, w_out, gain_two, w_router, w_in, w_back, flat_ids, live
    )
    mixed = state[17].reshape(nimg, half, width).astype(jnp.bfloat16)
    state = forward(
        tokens, gain_one, w_qkv, w_out, gain_two, w_router, w_in, w_back, flat_ids, live
    )
    (
        x_rows,
        normed,
        query4,
        keys4,
        vals4,
        probs,
        probs_low,
        mix,
        mid,
        routed,
        pick,
        gates,
        where_rows,
        arrived,
        pre,
        act,
        picked,
        output,
        capacity,
    ) = state
    scale = HEAD_DIM ** (-0.5)
    high = lax.Precision.HIGHEST
    grad_y = cotangent.astype(jnp.float32).reshape(count, width)
    grad_gate = jnp.sum(grad_y[:, None, :] * picked.astype(jnp.float32), -1)
    d_out = (
        (gates[:, :, None] * grad_y[:, None, :]).astype(jnp.bfloat16).reshape(count * TOP, width)
    )
    grad_buffer = jnp.zeros((experts_all * capacity, width), jnp.bfloat16).at[where_rows].set(d_out)
    grad_buffer = grad_buffer.reshape(experts_all, capacity, width)
    grad_arrived = lax.all_to_all(grad_buffer, "expert", split_axis=0, concat_axis=1, tiled=True)
    d_act = jnp.einsum("erd,efd->erf", grad_arrived, w_back, preferred_element_type=jnp.float32)
    grad_back = jnp.einsum("erf,erd->efd", act, grad_arrived, preferred_element_type=jnp.float32)
    _, gelu_pull = jax.vjp(smooth_gelu, pre)
    d_pre = gelu_pull(d_act)[0].astype(jnp.bfloat16)
    grad_in = jnp.einsum("erd,erf->edf", arrived, d_pre, preferred_element_type=jnp.float32)
    d_in = jnp.einsum("erf,edf->erd", d_pre, w_in, preferred_element_type=jnp.float32).astype(
        jnp.bfloat16
    )
    grad_returned = lax.all_to_all(d_in, "expert", split_axis=1, concat_axis=0, tiled=True)
    grad_rows = grad_returned.reshape(experts_all * capacity, width)[where_rows].reshape(
        count, TOP, width
    )
    d_experts = jnp.sum(grad_rows.astype(jnp.float32), 1)
    d_chosen = gates * (grad_gate - jnp.sum(gates * grad_gate, -1, keepdims=True))
    d_logits = jnp.sum(jnp.where(pick, d_chosen[:, :, None], 0.0), 1)
    grad_router = jnp.dot(routed.astype(jnp.float32).T, d_logits, precision=high)
    d_routed = d_experts + jnp.dot(d_logits, w_router.astype(jnp.float32).T, precision=high)
    _, norm_two_pull = jax.vjp(norm_rows, mid, gain_two)
    d_mid_norm, grad_gain_two = norm_two_pull(d_routed)
    d_mid = grad_y + d_mid_norm
    d_branch = d_mid.astype(jnp.bfloat16)
    grad_out = jnp.einsum("td,te->de", mix, d_branch, preferred_element_type=jnp.float32)
    d_mix = jnp.dot(d_branch, w_out.T, preferred_element_type=jnp.float32).astype(jnp.bfloat16)
    d_mix4 = d_mix.reshape(nimg, half, HEADS, HEAD_DIM)
    d_probs = jnp.einsum("iqhc,ikhc->ihqk", d_mix4, vals4, preferred_element_type=jnp.float32)
    d_scores = (probs * (d_probs - jnp.sum(probs * d_probs, -1, keepdims=True))).astype(
        jnp.bfloat16
    )
    d_query = (
        jnp.einsum("ihqk,ikhc->iqhc", d_scores, keys4, preferred_element_type=jnp.float32) * scale
    )
    d_keys = (
        jnp.einsum("ihqk,iqhc->ikhc", d_scores, query4, preferred_element_type=jnp.float32) * scale
    )
    d_vals = jnp.einsum("ihqk,iqhc->ikhc", probs_low, d_mix4, preferred_element_type=jnp.float32)
    seq = keys4.shape[1]
    d_keys_own, d_vals_own = (
        lax.psum_scatter(
            d_keys.reshape(nimg, seq, width).astype(jnp.bfloat16),
            "ctx",
            scatter_dimension=1,
            tiled=True,
        ).astype(jnp.float32),
        lax.psum_scatter(
            d_vals.reshape(nimg, seq, width).astype(jnp.bfloat16),
            "ctx",
            scatter_dimension=1,
            tiled=True,
        ).astype(jnp.float32),
    )
    d_qkv = jnp.concatenate(
        [
            d_query.reshape(count, width).astype(jnp.bfloat16),
            d_keys_own.reshape(count, width).astype(jnp.bfloat16),
            d_vals_own.reshape(count, width).astype(jnp.bfloat16),
        ],
        axis=1,
    )
    grad_qkv = jnp.einsum("td,te->de", normed, d_qkv, preferred_element_type=jnp.float32)
    d_normed = jnp.dot(d_qkv, w_qkv.T, preferred_element_type=jnp.float32)
    _, norm_one_pull = jax.vjp(norm_rows, x_rows, gain_one)
    d_x_norm, grad_gain_one = norm_one_pull(d_normed)
    grad_tokens = (d_mid + d_x_norm).reshape(nimg, half, width).astype(jnp.bfloat16)
    grad_gain_one, grad_qkv, grad_out, grad_gain_two, grad_router = lax.psum(
        (grad_gain_one, grad_qkv, grad_out, grad_gain_two, grad_router), ("dp", "ctx", "expert")
    )
    grad_in, grad_back = (
        lax.psum(grad_in.astype(jnp.bfloat16), ("dp", "ctx")).astype(jnp.float32),
        lax.psum(grad_back.astype(jnp.bfloat16), ("dp", "ctx")).astype(jnp.float32),
    )
    return (
        mixed,
        grad_tokens,
        grad_gain_one,
        grad_qkv,
        grad_out,
        grad_gain_two,
        grad_router,
        grad_in,
        grad_back,
    )


def solution(mesh):
    placed = (
        P(("dp", "expert"), "ctx", None),
        P(),
        P(),
        P(),
        P(),
        P(),
        P("expert", None, None),
        P("expert", None, None),
        P(("dp", "expert"), "ctx", None, None, None),
        P(("dp", "expert"), None),
        P(("dp", "expert"), "ctx", None),
    )
    sizes = dict(mesh.shape)
    dense = sizes == {"dp": 4, "ctx": 2, "expert": 4}
    return jax.shard_map(
        dense_shards if dense else shards,
        mesh=mesh,
        in_specs=placed,
        out_specs=(
            P(("dp", "expert"), "ctx", None),
            P(("dp", "expert"), "ctx", None),
            P(),
            P(),
            P(),
            P(),
            P(),
            P("expert", None, None),
            P("expert", None, None),
        ),
        check_vma=False,
    )
```

```python
import functools
import jax
import jax.numpy as jnp
from jax import lax
from jax.experimental import pallas as pl
from jax.experimental.pallas import tpu as pltpu
from jax.sharding import PartitionSpec as P

HEADS = 8
HEAD_DIM = 64
TOP = 2
EPS = 1e-06
SCALE = HEAD_DIM ** (-0.5)
F32 = jnp.float32
BF16 = jnp.bfloat16
HELD = pltpu.HBM
HERE = pl.BlockSpec(memory_space=pltpu.VMEM)
BRIEF = pl.CostEstimate(flops=1, bytes_accessed=1, transcendentals=0)
NT = (((1,), (1,)), ((), ()))
TN = (((0,), (0,)), ((), ()))
NN = (((1,), (0,)), ((), ()))


def mm(a, b, dims=NN):
    return lax.dot_general(a, b, dims, preferred_element_type=F32)


def two_halves(a):
    high = a.astype(BF16)
    return high, (a - high.astype(F32)).astype(BF16)


def stats(value):
    center = value - jnp.mean(value, -1, keepdims=True)
    rstd = lax.rsqrt(jnp.mean(center * center, -1, keepdims=True) + EPS)
    return center * rstd, rstd


def norm_vjp(d_value, unit, rstd, gain):
    d_unit = d_value * gain
    return rstd * (
        d_unit
        - jnp.mean(d_unit, -1, keepdims=True)
        - unit * jnp.mean(d_unit * unit, -1, keepdims=True)
    )


def head_pair(value):
    lane = lax.broadcasted_iota(jnp.int32, value.shape, 1)
    first = lane < HEAD_DIM
    return jnp.concatenate(
        [jnp.where(first, value, 0.0), jnp.where(first, 0.0, value)], axis=0
    ).astype(BF16)


def join_pair(value):
    rows = value.shape[0] // 2
    lane = lax.broadcasted_iota(jnp.int32, (rows, value.shape[1]), 1)
    return jnp.where(lane < HEAD_DIM, value[:rows], value[rows:])


def natural(core, mine, theirs):
    return jnp.where(core == 0, mine, theirs), jnp.where(core == 0, theirs, mine)


def attend_kernel(
    meta_ref, own_ref, other_ref, dyown_ref, dyother_ref, mask_ref, g1_ref, wqkv_ref, wout_ref, g2_ref,
    x_ref, dy_ref, normed_ref, qkv_ref, probs_ref, mix_ref, mid_ref, routed_ref,
    x_s, qkv_s, mix_s,
):
    half = own_ref.shape[1]
    width = own_ref.shape[2]
    pair = 2 * HEAD_DIM
    core = meta_ref[3]
    for mine, theirs, ref in ((dyown_ref, dyother_ref, dy_ref), (own_ref, other_ref, x_ref)):
        first, second = natural(core, mine[0].astype(F32), theirs[0].astype(F32))
        x_s[0:half, :] = first
        x_s[half : 2 * half, :] = second
        ref[...] = x_s[...].astype(BF16)
    x = x_s[...]
    unit, _ = stats(x)
    normed = (unit * g1_ref[...]).astype(BF16)
    normed_ref[...] = normed
    qkv_s[...] = mm(normed, wqkv_ref[...])
    qkv_ref[...] = qkv_s[...].astype(BF16)
    image = core * pl.num_programs(0) + pl.program_id(0)
    is_open = mask_ref[pl.ds(image, 1), :] > 0
    for n in range(width // pair):
        at = n * pair
        query = head_pair(qkv_s[:, at : at + pair])
        keys = qkv_s[:, width + at : width + at + pair].astype(BF16)
        vals = qkv_s[:, 2 * width + at : 2 * width + at + pair].astype(BF16)
        scores = jnp.where(is_open, mm(query, keys, NT) * SCALE, -1e9)
        top = jnp.max(scores, -1, keepdims=True)
        expo = jnp.where(is_open, jnp.exp(scores - top), 0.0)
        probs = (expo / jnp.sum(expo, -1, keepdims=True)).astype(BF16)
        probs_ref[0, n] = probs
        mix_s[:, at : at + pair] = join_pair(mm(probs, vals))
    mix = mix_s[...].astype(BF16)
    mix_ref[...] = mix
    mid = x + mm(mix, wout_ref[...])
    mid_ref[...] = mid
    unit, _ = stats(mid)
    routed_ref[...] = (unit * g2_ref[...]).astype(BF16)


def attend(meta, own, other, dy_own, dy_other, mask, g1, wqkv, wout, g2):
    imgs, half, width = own.shape
    imgs //= 2
    seq = 2 * half
    rows = imgs * seq
    pairs = HEADS // 2
    raw = pl.BlockSpec((1, half, width), lambda i, m: (m[3] * imgs + i, 0, 0))
    one = lambda *s: pl.BlockSpec(s, lambda i, m: (i,) + (0,) * (len(s) - 1))
    fix = lambda *s: pl.BlockSpec(s, lambda i, m: (0,) * len(s))
    late = lambda *s: HELD(s, BF16)
    return pl.pallas_call(
        attend_kernel,
        grid_spec=pltpu.PrefetchScalarGridSpec(
            num_scalar_prefetch=1,
            grid=(imgs,),
            in_specs=[
                raw, raw, raw, raw, fix(*mask.shape), fix(1, width),
                fix(width, 3 * width), fix(width, width), fix(1, width),
            ],
            out_specs=[
                one(seq, width), one(seq, width), one(seq, width), one(seq, 3 * width),
                one(1, pairs, 2 * seq, seq), one(seq, width), one(seq, width), one(seq, width),
            ],
            scratch_shapes=[
                pltpu.VMEM((seq, width), F32),
                pltpu.VMEM((seq, 3 * width), F32),
                pltpu.VMEM((seq, width), F32),
            ],
        ),
        out_shape=[
            late(rows, width),
            jax.ShapeDtypeStruct((rows, width), BF16),
            late(rows, width),
            late(rows, 3 * width),
            late(imgs, pairs, 2 * seq, seq),
            late(rows, width),
            HELD((rows, width), F32),
            jax.ShapeDtypeStruct((rows, width), BF16),
        ],
        compiler_params=pltpu.CompilerParams(vmem_limit_bytes=22 << 20),
        cost_estimate=BRIEF,
        name="attend",
    )(meta, *map(held, (own, other, dy_own, dy_other)), mask, g1, held(wqkv), held(wout), g2)


def assemble_kernel(meta_ref, own_ref, other_ref, out_ref, out_s):
    half = own_ref.shape[1]
    first, second = natural(meta_ref[3], own_ref[0].astype(F32), other_ref[0].astype(F32))
    out_s[0:half, :] = first
    out_s[half : 2 * half, :] = second
    out_ref[...] = out_s[...].astype(BF16)


def assemble(meta, own, other):
    imgs, half, width = own.shape
    imgs //= 2
    raw = pl.BlockSpec((1, half, width), lambda i, m: (m[3] * imgs + i, 0, 0))
    return pl.pallas_call(
        assemble_kernel,
        grid_spec=pltpu.PrefetchScalarGridSpec(
            num_scalar_prefetch=1,
            grid=(imgs,),
            in_specs=[raw, raw],
            out_specs=pl.BlockSpec((2 * half, width), lambda i, m: (i, 0)),
            scratch_shapes=[pltpu.VMEM((2 * half, width), F32)],
        ),
        out_shape=jax.ShapeDtypeStruct((imgs * 2 * half, width), BF16),
        compiler_params=pltpu.CompilerParams(vmem_limit_bytes=6 << 20),
        cost_estimate=BRIEF,
        name="assemble",
    )(meta, own, other)


def row_gates(rows, ids, wr):
    logits = mm(wr, rows, NT)
    row = lax.broadcasted_iota(jnp.int32, logits.shape, 0)
    pick = (row.astype(F32) == ids[0:1, :]) | (row.astype(F32) == ids[1:2, :])
    top = jnp.max(jnp.where(pick, logits, -jnp.inf), 0, keepdims=True)
    expo = jnp.where(pick, jnp.exp(logits - top), 0.0)
    return expo / jnp.sum(expo, 0, keepdims=True), row


def padded(count):
    return -(-count // 16) * 16


def expert_kernel(add, local, meta_ref, rows_ref, dy_ref, ids_ref, wr_ref, wi_ref, wb_ref, *rest):
    sources = [] if local else [wb_ref]
    if add:
        sources += rest[:2]
        rest = rest[2:]
    act_ref, dpre_ref, dout_ref, made_ref, din_ref, wi_s, wb_s, *rest = rest
    if sources:
        *landings, sems = rest
        copies = [pltpu.make_async_copy(v, w, sems.at[n]) for n, (v, w) in enumerate(zip(sources, landings))]
        for copy in copies:
            copy.start()
    count = act_ref.shape[0]
    width = rows_ref.shape[1]
    rows = rows_ref[0:count, :]
    part = wi_s.shape[1] // PIECES
    if local:
        for n in range(PIECES):
            at = pl.ds(pl.multiple_of((n ^ meta_ref[1]) * part, part), part)
            wi_s[:, n * part : (n + 1) * part] = wi_ref[0, :, at]
            wb_s[n * part : (n + 1) * part, :] = wb_ref[0, at, :]

    if ids_ref.shape[0] == 2:
        ids = ids_ref[...].astype(F32)
    else:
        at = padded(count)
        ids = [ids_ref[at : at + 2, :], ids_ref[at + 2 : at + 4, 0 : count - width]]
        ids = jnp.concatenate([v.astype(F32) for v in ids], axis=1)
    gates, row = row_gates(rows, ids, wr_ref[...])
    high, low = two_halves(jnp.where(row == meta_ref[0], gates, 0.0))
    ones = jnp.ones((16, 128), BF16)
    gate = (mm(high, ones, TN) + mm(low, ones, TN))[:, 0:1]
    dout_ref[...] = (gate * dy_ref[...].astype(F32)).astype(BF16)
    wide = wi_s.shape[1] // CHUNKS
    for q in range(CHUNKS):
        if not local and q % (CHUNKS // 2) == 0:
            ref, first = (landings[0], PIECES // 2) if q else (wi_ref, 0)
            if q:
                copies[0].wait()
            for n in range(PIECES // 2):
                to = slice((first + n) * part, (first + n + 1) * part)
                for h in range(2):
                    side = slice(h * part, (h + 1) * part)
                    wi_s[side, to] = ref[n, h]
                    wb_s[to, side] = ref[n, 2 + h]
        here = slice(q * wide, (q + 1) * wide)
        pre = mm(rows, wi_s[:, here])
        square = pre * pre
        inner = pre * (0.7978845608 + 0.0356774081 * square)
        up = 0.5 + 0.5 * jnp.tanh(inner)
        value = pre * up
        act_ref[:, here] = value.astype(BF16)
        slope = up + value * (1.0 - up) * (1.5957691216 + 0.2140644488 * square)
        dpre_ref[:, here] = (mm(dout_ref[...], wb_s[here, :], NT) * slope).astype(BF16)
    made = mm(act_ref[...], wb_s[...]).astype(BF16).astype(F32)
    d_in = mm(dpre_ref[...], wi_s[...], NT)
    total = gate * made
    high, low = two_halves(made * dy_ref[...].astype(F32))
    ones = jnp.ones((16, width), BF16)
    d_gate = (mm(ones, high, NT) + mm(ones, low, NT))[0:8]
    row = lax.broadcasted_iota(jnp.int32, d_gate.shape, 0)
    d_gate = jnp.where(row == meta_ref[0], d_gate, 0.0)
    tail = padded(count)
    if add:
        for copy in copies[-2:]:
            copy.wait()
        pmade_ref, pdin_ref = landings[-2:]
        total += pmade_ref[...].astype(F32)
        d_in += pdin_ref[0:count, :].astype(F32)
        d_gate += read_gate(pdin_ref, count)
    made_ref[...] = total.astype(BF16)
    din_ref[0:count, :] = d_in.astype(BF16)
    high = d_gate.astype(BF16).astype(F32)
    value = jnp.concatenate([high, d_gate - high], axis=0).astype(BF16)
    din_ref[tail : tail + 16, :] = value[:, :width]
    din_ref[tail + 16 : tail + 32, 0 : count - width] = value[:, width:]


CHUNKS = 4


def read_gate(ref, count):
    tail = padded(count)
    width = ref.shape[1]
    value = ref[tail : tail + 16, 0 : min(count, width)].astype(F32)
    if count > width:
        value = jnp.concatenate([value, ref[tail + 16 : tail + 32, 0 : count - width].astype(F32)], axis=1)
    return value[0:8] + value[8:16]


PIECES = 8


def expert(meta, rows, dy, ids, wr, weights, prev=None):
    count, width = dy.shape
    local = weights[0].ndim == 3
    hidden = weights[0].shape[2] if local else PIECES * weights[0].shape[2]
    deep = padded(count) + 32
    first = prev is None
    away = pl.BlockSpec(memory_space=pl.ANY)
    more = [] if first else [away, away]
    landings = [] if local else [pltpu.VMEM(weights[1].shape, BF16)]
    if not first:
        landings += [pltpu.VMEM((count, width), BF16), pltpu.VMEM((deep, width), BF16)]
    if landings:
        landings.append(pltpu.SemaphoreType.DMA((len(landings),)))
    shape = lambda *s: jax.ShapeDtypeStruct(s, BF16)
    return pl.pallas_call(
        functools.partial(expert_kernel, not first, local),
        grid_spec=pltpu.PrefetchScalarGridSpec(
            num_scalar_prefetch=1,
            grid=(1,),
            in_specs=[HERE] * 5 + [HERE if local else away, *more],
            out_specs=[HERE] * 5,
            scratch_shapes=[pltpu.VMEM((width, hidden), BF16), pltpu.VMEM((hidden, width), BF16), *landings],
        ),
        out_shape=[shape(count, hidden), shape(count, hidden), shape(count, width), shape(count, width), shape(deep, width)],
        compiler_params=pltpu.CompilerParams(vmem_limit_bytes=LIMIT << 20),
        cost_estimate=BRIEF,
        name="expert",
    )(meta, rows, dy, ids, wr, weights[0], weights[1] if local else held(weights[1]), *[held(v) for v in prev or ()])


LIMIT = 26


def expert_steps_kernel(add, local, meta_ref, rows_ref, dy_ref, ids_ref, wr_ref, *rest):
    wi_ref, wb_ref, *rest = rest
    sources = [] if local else [wb_ref]
    if add:
        sources += rest[:2]
        rest = rest[2:]
    act_ref, dpre_ref, dout_ref, made_ref, din_ref, gate_s, made_s, din_s, *rest = rest
    step = pl.program_id(0)
    copies = []
    if sources:
        *rest, sems = rest
        landings = rest[len(rest) - len(sources) :]
        rest = rest[: len(rest) - len(sources)]
        copies = [pltpu.make_async_copy(v, w, sems.at[n]) for n, (v, w) in enumerate(zip(sources, landings))]
    if not local:
        wb_ref = landings[0]
    if add:
        pmade_ref, pdin_ref = landings[-2:]
    count = act_ref.shape[0]
    width = rows_ref.shape[1]
    rows = rows_ref[0:count, :]

    @pl.when(step == 0)
    def _():
        for copy in copies:
            copy.start()
        if ids_ref.shape[0] == 2:
            ids = ids_ref[...].astype(F32)
        else:
            at = padded(count)
            ids = [ids_ref[at : at + 2, :], ids_ref[at + 2 : at + 4, 0 : count - width]]
            ids = jnp.concatenate([v.astype(F32) for v in ids], axis=1)
        gates, row = row_gates(rows, ids, wr_ref[...])
        high, low = two_halves(jnp.where(row == meta_ref[0], gates, 0.0))
        ones = jnp.ones((16, 128), BF16)
        gate_s[...] = mm(high, ones, TN) + mm(low, ones, TN)
        gate = gate_s[:, 0:1]
        dout_ref[...] = (gate * dy_ref[...].astype(F32)).astype(BF16)
        made_s[...] = jnp.zeros_like(made_s)
        din_s[...] = jnp.zeros_like(din_s)

    if local:
        part = wi_ref.shape[2] // PIECES
        at = [pl.multiple_of(((2 * step + s) ^ meta_ref[1]) * part, part) for s in range(2)]
        w_in = jnp.concatenate([wi_ref[0, :, pl.ds(v, part)] for v in at], axis=1)
        w_back = jnp.concatenate([wb_ref[0, pl.ds(v, part), :] for v in at], axis=0)
    else:
        wi_s, wb_s = rest
        part = wi_s.shape[0] // 2
        upper = pl.num_programs(0) // 2

        @pl.when(step == upper)
        def _():
            copies[0].wait()

        for ref, first in ((wi_ref, 0), (wb_ref, upper)):

            @pl.when((step < upper) == (first == 0))
            def _():
                for s in range(2):
                    for h in range(2):
                        at = 2 * (step - first) + s
                        wi_s[h * part : (h + 1) * part, s * part : (s + 1) * part] = ref[at, h]
                        wb_s[s * part : (s + 1) * part, h * part : (h + 1) * part] = ref[at, 2 + h]

        w_in, w_back = wi_s[...], wb_s[...]
    pre = mm(rows, w_in)
    square = pre * pre
    inner = pre * (0.7978845608 + 0.0356774081 * square)
    up = 0.5 + 0.5 * jnp.tanh(inner)
    value = pre * up
    act = value.astype(BF16)
    slope = up + value * (1.0 - up) * (1.5957691216 + 0.2140644488 * square)
    here = pl.ds(pl.multiple_of(step * pre.shape[1], pre.shape[1]), pre.shape[1])
    act_ref[:, here] = act
    made_s[...] += mm(act, w_back)
    dpre = (mm(dout_ref[...], w_back, NT) * slope).astype(BF16)
    dpre_ref[:, here] = dpre
    din_s[...] += mm(dpre, w_in, NT)

    @pl.when(step == pl.num_programs(0) - 1)
    def _():
        gate = gate_s[:, 0:1]
        made = made_s[...].astype(BF16).astype(F32)
        total = gate * made
        d_in = din_s[...]
        high, low = two_halves(made * dy_ref[...].astype(F32))
        ones = jnp.ones((16, made.shape[1]), BF16)
        d_gate = (mm(ones, high, NT) + mm(ones, low, NT))[0:8]
        row = lax.broadcasted_iota(jnp.int32, d_gate.shape, 0)
        d_gate = jnp.where(row == meta_ref[0], d_gate, 0.0)
        tail = padded(count)
        for copy in copies[0 if local else 1 :]:
            copy.wait()
        if add:
            total += pmade_ref[...].astype(F32)
            d_in += pdin_ref[0:count, :].astype(F32)
            d_gate += read_gate(pdin_ref, count)
        made_ref[...] = total.astype(BF16)
        din_ref[0:count, :] = d_in.astype(BF16)
        high = d_gate.astype(BF16).astype(F32)
        value = jnp.concatenate([high, d_gate - high], axis=0).astype(BF16)
        if count > d_in.shape[1]:
            cut = d_in.shape[1]
            din_ref[tail : tail + 16, :] = value[:, :cut]
            din_ref[tail + 16 : tail + 32, 0 : count - cut] = value[:, cut:]
        else:
            din_ref[tail : tail + 16, 0:count] = value


def expert_steps(meta, rows, dy, ids, wr, weights, prev=None):
    count = dy.shape[0]
    width = rows.shape[1]
    local = weights[0].ndim == 3
    piece = weights[0].shape[2] // PIECES if local else weights[0].shape[2]
    hidden = PIECES * piece
    steps = PIECES // 2
    deep = padded(count) + 16 * -(-count // width)
    fix = lambda *s: pl.BlockSpec(s, lambda q, m: (0,) * len(s))
    first = prev is None
    away = pl.BlockSpec(memory_space=pl.ANY)
    more = [] if first else [away, away]
    landings = [] if local else [pltpu.VMEM(weights[1].shape, BF16)]
    if not first:
        landings += [pltpu.VMEM((count, width), BF16), pltpu.VMEM((deep, width), BF16)]
    if landings:
        landings.append(pltpu.SemaphoreType.DMA((len(landings),)))
    given = [] if first else [held(v) for v in prev]
    ends = [fix(count, width), fix(deep, width)] if first else [HERE, HERE]
    kept = HELD if first else jax.ShapeDtypeStruct
    return pl.pallas_call(
        functools.partial(expert_steps_kernel, prev is not None, local),
        grid_spec=pltpu.PrefetchScalarGridSpec(
            num_scalar_prefetch=1,
            grid=(steps,),
            in_specs=[HERE, fix(*dy.shape), HERE, HERE, HERE, HERE if local else away, *more],
            out_specs=[HERE] * 3 + ends,
            scratch_shapes=[
                pltpu.VMEM((count, 128), F32),
                pltpu.VMEM((count, width), F32),
                pltpu.VMEM((count, width), F32),
            ]
            + ([] if local else [pltpu.VMEM((width, 2 * piece), BF16), pltpu.VMEM((2 * piece, width), BF16)])
            + landings,
        ),
        out_shape=[
            jax.ShapeDtypeStruct((count, hidden), BF16),
            jax.ShapeDtypeStruct((count, hidden), BF16),
            jax.ShapeDtypeStruct((count, width), BF16),
            kept((count, width), BF16),
            kept((deep, width), BF16),
        ],
        compiler_params=pltpu.CompilerParams(vmem_limit_bytes=20 << 20),
        cost_estimate=BRIEF,
        name="expert_steps",
    )(meta, rows, dy if first else held(dy), ids, wr, weights[0], weights[1] if local else held(weights[1]), *given)


def weight_kernel(n, *refs):
    rows, acts, dpres, douts = (refs[g * n : (g + 1) * n] for g in range(4))
    iown_ref, igive_ref, bown_ref, bgive_ref = refs[4 * n :]
    wide = iown_ref.shape[0] * iown_ref.shape[1]
    here = pl.ds(pl.multiple_of(pl.program_id(0) * wide, wide), wide)
    results = []
    for left, right in ((dpres, rows), (acts, douts)):
        total = 0.0
        for b in range(n):
            count = left[b].shape[0]
            total = total + mm(left[b][:, here], right[b][0:count, :], TN)
        results.append(total.astype(BF16).reshape(iown_ref.shape))
    grad_in, grad_back = results
    first = pl.program_id(0) < pl.num_programs(0) // 2

    @pl.when(first)
    def _():
        iown_ref[...] = grad_in
        bown_ref[...] = grad_back

    @pl.when(jnp.logical_not(first))
    def _():
        igive_ref[...] = grad_in
        bgive_ref[...] = grad_back


def weight_grads(rows, acts, dpres, douts, late=False):
    n = len(rows)
    width = rows[0].shape[1]
    piece = acts[0].shape[1] // PIECES
    steps = PIECES // 2
    own = pl.BlockSpec((2, piece, width), lambda q: (jnp.minimum(q, steps // 2 - 1), 0, 0))
    give = pl.BlockSpec((2, piece, width), lambda q: (jnp.maximum(q - steps // 2, 0), 0, 0))
    return pl.pallas_call(
        functools.partial(weight_kernel, n),
        grid=(steps,),
        in_specs=[HERE] * (4 * n),
        out_specs=[own, give, own, give],
        out_shape=[(HELD if late and g % 2 == 0 else jax.ShapeDtypeStruct)((PIECES // 2, piece, width), BF16) for g in range(4)],
        compiler_params=pltpu.CompilerParams(vmem_limit_bytes=14 << 20),
        cost_estimate=BRIEF,
        name="weight_grads",
    )(*rows, *acts, *dpres, *douts)


def finish_kernel(meta_ref, im_ref, ir_ref, bm_ref, br_ref, gin_ref, gback_ref):
    mine = pl.program_id(0) < pl.num_programs(0) // 2
    flip = meta_ref[1] % 2 == 1
    piece, width = im_ref.shape[1:]
    for m_ref, r_ref, out_ref in ((im_ref, ir_ref, gin_ref), (bm_ref, br_ref, gback_ref)):
        value = jnp.where(mine, m_ref[...], r_ref[...]).astype(F32)
        first = jnp.where(flip, value[1], value[0])
        second = jnp.where(flip, value[0], value[1])
        if out_ref is gin_ref:
            out_ref[0, :, 0:piece] = jnp.transpose(first)
            out_ref[0, :, piece : 2 * piece] = jnp.transpose(second)
        else:
            out_ref[0, 0:piece, :] = first
            out_ref[0, piece : 2 * piece, :] = second


def finish_expert(meta, in_mine, in_recv, back_mine, back_recv):
    upper, piece, width = in_mine.shape
    steps = upper
    own = pl.BlockSpec((2, piece, width), lambda q, m: (jnp.minimum(q, steps // 2 - 1), 0, 0))
    give = pl.BlockSpec((2, piece, width), lambda q, m: (jnp.maximum(q - steps // 2, 0), 0, 0))
    return pl.pallas_call(
        finish_kernel,
        grid_spec=pltpu.PrefetchScalarGridSpec(
            num_scalar_prefetch=1,
            grid=(steps,),
            in_specs=[own, give, own, give],
            out_specs=[
                pl.BlockSpec((1, width, 2 * piece), lambda q, m: (0, 0, q ^ (m[1] // 2))),
                pl.BlockSpec((1, 2 * piece, width), lambda q, m: (0, q ^ (m[1] // 2), 0)),
            ],
        ),
        out_shape=[
            jax.ShapeDtypeStruct((1, width, PIECES * piece), F32),
            jax.ShapeDtypeStruct((1, PIECES * piece, width), F32),
        ],
        compiler_params=pltpu.CompilerParams(vmem_limit_bytes=14 << 20),
        cost_estimate=BRIEF,
        name="finish_expert",
    )(meta, in_mine, in_recv, back_mine, back_recv)


def split_halves(core, whole_ref, own_ref, other_ref):
    imgs, half, _ = own_ref.shape
    for i in range(imgs):
        at = 2 * half * i
        first, second = whole_ref[at : at + half, :], whole_ref[at + half : at + 2 * half, :]
        mine, theirs = natural(core, first, second)
        own_ref[i] = mine.astype(BF16)
        other_ref[i] = theirs.astype(BF16)


def back_kernel(
    meta_ref, din0_ref, din1_ref,
    ids_ref, dy_ref, mid_ref, routed_ref, wr_ref, g2_ref, mix_ref, wout_ref,
    probs_ref, qkv_ref, x_ref, normed_ref, wqkv_ref, g1_ref,
    own_ref, other_ref, gown_ref, ggive_ref,
    dmid_s, dmix_s, dqkv_s, tok_s, grad_s, small_s,
):
    step = pl.program_id(0)
    imgs = pl.num_programs(0)
    seq = qkv_ref.shape[0]
    width = x_ref.shape[1]
    half = seq // 2
    pair = 2 * HEAD_DIM
    rows = x_ref.shape[0]

    @pl.when(step == 0)
    def _():
        routed = routed_ref[...]
        wr = wr_ref[...]
        gates, _ = row_gates(routed, ids_ref[...].astype(F32), wr)
        d_gate = read_gate(din0_ref, rows) + read_gate(din1_ref, rows)
        d_gate = jnp.concatenate([d_gate, jnp.zeros_like(d_gate)], axis=0)
        d_logits = gates * (d_gate - jnp.sum(gates * d_gate, 0, keepdims=True))
        high, low = two_halves(d_logits)
        small_s[...] = jnp.zeros_like(small_s)
        small_s[0:16, :] = mm(high, routed) + mm(low, routed)
        d_routed = din0_ref[0:rows, :].astype(F32) + din1_ref[0:rows, :].astype(F32)
        d_routed = d_routed + mm(high, wr, TN) + mm(low, wr, TN)
        unit, rstd = stats(mid_ref[...])
        small_s[16:17, :] = jnp.sum(d_routed * unit, 0, keepdims=True)
        d_mid = dy_ref[...].astype(F32) + norm_vjp(d_routed, unit, rstd, g2_ref[...])
        dmid_s[...] = d_mid
        d_branch = d_mid.astype(BF16)
        grad_s[:, 3 * width : 4 * width] = mm(mix_ref[...], d_branch, TN).astype(BF16)
        dmix_s[...] = mm(d_branch, wout_ref[...], NT)

    base = pl.multiple_of(step * seq, 8)
    for n in range(width // pair):
        at = n * pair
        d_mix = head_pair(dmix_s[pl.ds(base, seq), at : at + pair])
        query = head_pair(qkv_ref[:, at : at + pair].astype(F32))
        keys = qkv_ref[:, width + at : width + at + pair]
        vals = qkv_ref[:, 2 * width + at : 2 * width + at + pair]
        low = probs_ref[0, n]
        probs = low.astype(F32)
        d_probs = mm(d_mix, vals, NT)
        d_scores = probs * (d_probs - jnp.sum(probs * d_probs, -1, keepdims=True))
        d_scores = d_scores.astype(BF16)
        d_query = join_pair(mm(d_scores, keys)) * SCALE
        d_keys = mm(d_scores, query, TN) * SCALE
        d_vals = mm(low, d_mix, TN)
        dqkv_s[pl.ds(base, seq), at : at + pair] = d_query.astype(BF16)
        dqkv_s[pl.ds(base, seq), width + at : width + at + pair] = d_keys.astype(BF16)
        dqkv_s[pl.ds(base, seq), 2 * width + at : 2 * width + at + pair] = d_vals.astype(BF16)

    @pl.when(step == imgs - 1)
    def _():
        d_qkv = dqkv_s[...]
        grad_s[:, : 3 * width] = mm(normed_ref[...], d_qkv, TN).astype(BF16)
        d_normed = mm(d_qkv, wqkv_ref[...], NT)
        unit, rstd = stats(x_ref[...].astype(F32))
        small_s[17:18, :] = jnp.sum(d_normed * unit, 0, keepdims=True)
        grad_s[:, 4 * width :] = jnp.transpose(small_s[...]).astype(BF16)
        tok_s[...] = dmid_s[...] + norm_vjp(d_normed, unit, rstd, g1_ref[...])
        split_halves(meta_ref[3], tok_s, own_ref, other_ref)
        part = width // SHARES

        @pl.loop(0, SHARES // 2)
        def _(r):
            to = pl.ds(pl.multiple_of(r * part, part), part)
            for ref, first in ((gown_ref, 0), (ggive_ref, SHARES // 2)):
                there = pl.multiple_of(((r + first) ^ meta_ref[2]) * part, part)
                ref[to, :] = grad_s[pl.ds(there, part), :]


SHARES = 32


def attend_back(meta, dins, ids, dy, mid, routed, wr, g2, mix, wout, probs, qkv, x, normed, wqkv, g1):
    imgs = probs.shape[0]
    rows, width = x.shape
    seq = rows // imgs
    pairs = HEADS // 2
    wide = 4 * width + 128
    fix = lambda *s: pl.BlockSpec(s, lambda i, m: (0,) * len(s))
    return pl.pallas_call(
        back_kernel,
        grid_spec=pltpu.PrefetchScalarGridSpec(
            num_scalar_prefetch=1,
            grid=(imgs,),
            in_specs=[fix(*a.shape) for a in dins] + [
                fix(2, rows), fix(rows, width), fix(rows, width), fix(rows, width),
                fix(16, width), fix(1, width), fix(rows, width), fix(width, width),
                pl.BlockSpec((1, pairs, 2 * seq, seq), lambda i, m: (i, 0, 0, 0)),
                pl.BlockSpec((seq, 3 * width), lambda i, m: (i, 0)),
                fix(rows, width), fix(rows, width), fix(width, 3 * width), fix(1, width),
            ],
            out_specs=[
                fix(imgs, seq // 2, width), fix(imgs, seq // 2, width),
                fix(width // 2, wide), fix(width // 2, wide),
            ],
            scratch_shapes=[
                pltpu.VMEM((rows, width), F32),
                pltpu.VMEM((rows, width), F32),
                pltpu.VMEM((rows, 3 * width), BF16),
                pltpu.VMEM((rows, width), F32),
                pltpu.VMEM((width, wide), BF16),
                pltpu.VMEM((128, width), F32),
            ],
        ),
        out_shape=[
            jax.ShapeDtypeStruct((imgs, seq // 2, width), BF16),
            jax.ShapeDtypeStruct((imgs, seq // 2, width), BF16),
            jax.ShapeDtypeStruct((width // 2, wide), BF16),
            jax.ShapeDtypeStruct((width // 2, wide), BF16),
        ],
        compiler_params=pltpu.CompilerParams(vmem_limit_bytes=32 << 20),
        cost_estimate=BRIEF,
        name="attend_back",
    )(meta, *dins, ids, dy, mid, routed, wr, g2, mix, wout, probs, qkv, x, normed, wqkv, g1)


def shared_kernel(meta_ref, half_ref, *refs):
    gqkv_ref, gout_ref, small_ref = refs[-3:]
    upper = half_ref.shape[0]
    width = 2 * upper
    part = width // SHARES

    @pl.loop(0, SHARES // 2)
    def _(i):
        there = pl.multiple_of((i ^ (meta_ref[2] % (SHARES // 2))) * part, part)
        value = half_ref[pl.ds(there, part), :].astype(F32)
        at = pl.ds(pl.multiple_of(i * part, part), part)
        gqkv_ref[at, :] = value[:, : 3 * width]
        gout_ref[at, :] = value[:, 3 * width : 4 * width]
        small_ref[at, :] = value[:, 4 * width :]


def finish_shared(meta, half, earlier=()):
    upper, wide = half.shape
    width = 2 * upper
    at = (lambda i, m: (1 - m[3], 0)) if earlier else (lambda i, m: (m[3], 0))
    columns = (3 * width, width, wide - 4 * width)
    return pl.pallas_call(
        shared_kernel,
        grid_spec=pltpu.PrefetchScalarGridSpec(
            num_scalar_prefetch=1,
            grid=(1,),
            in_specs=[pl.BlockSpec((upper, wide), lambda i, m: (0, 0))] + [pl.BlockSpec(memory_space=pl.ANY)] * len(earlier),
            out_specs=[pl.BlockSpec((upper, c), at) for c in columns],
        ),
        out_shape=[jax.ShapeDtypeStruct((width, c), F32) for c in columns],
        input_output_aliases={2 + n: n for n in range(len(earlier))},
        compiler_params=pltpu.CompilerParams(vmem_limit_bytes=12 << 20),
        cost_estimate=BRIEF,
        name="finish_shared",
    )(meta, half, *earlier)


def combine_kernel(meta_ref, mid_ref, a_ref, b_ref, own_ref, other_ref, s_ref):
    s_ref[...] = mid_ref[...] + (a_ref[...].astype(F32) + b_ref[...].astype(F32))
    split_halves(meta_ref[3], s_ref, own_ref, other_ref)


def combine(meta, mid, parts, imgs):
    rows, width = mid.shape
    seq = rows // imgs
    spec = pl.BlockSpec((seq, width), lambda i, m: (i, 0))
    out = pl.BlockSpec((1, seq // 2, width), lambda i, m: (i, 0, 0))
    shape = jax.ShapeDtypeStruct((imgs, seq // 2, width), BF16)
    return pl.pallas_call(
        combine_kernel,
        grid_spec=pltpu.PrefetchScalarGridSpec(
            num_scalar_prefetch=1,
            grid=(imgs,),
            in_specs=[spec] * 3,
            out_specs=[out, out],
            scratch_shapes=[pltpu.VMEM((seq, width), F32)],
        ),
        out_shape=[shape, shape],
        compiler_params=pltpu.CompilerParams(vmem_limit_bytes=8 << 20),
        cost_estimate=BRIEF,
        name="combine",
    )(meta, mid, *parts)


def place_kernel(meta_ref, a_own_ref, a_recv_ref, b_own_ref, b_recv_ref, a_ref, b_ref):
    imgs = pl.num_programs(0) // 2
    mine = pl.program_id(0) // imgs == meta_ref[3]
    a_ref[...] = jnp.where(mine, a_own_ref[...], a_recv_ref[...])
    b_ref[...] = jnp.where(mine, b_own_ref[...], b_recv_ref[...])


def place(meta, *arrays):
    imgs, half, width = arrays[0].shape
    spec = pl.BlockSpec((1, half, width), lambda j, m: (j % imgs, 0, 0))
    out = pl.BlockSpec((1, half, width), lambda j, m: (j, 0, 0))
    shape = jax.ShapeDtypeStruct((2 * imgs, half, width), BF16)
    return pl.pallas_call(
        place_kernel,
        grid_spec=pltpu.PrefetchScalarGridSpec(
            num_scalar_prefetch=1, grid=(2 * imgs,), in_specs=[spec] * 4, out_specs=[out, out]
        ),
        out_shape=[shape, shape],
        compiler_params=pltpu.CompilerParams(vmem_limit_bytes=4 << 20),
        cost_estimate=BRIEF,
        name="place",
    )(meta, *arrays)


def pack_kernel(meta_ref, wi_ref, wb_ref, out_ref):
    part = out_ref.shape[1]
    for h in range(2):
        at = slice(h * part, (h + 1) * part)
        out_ref[h] = wi_ref[0, at, :]
        out_ref[2 + h] = wb_ref[0, :, at]


def pack_piece(meta, w_in, w_back):
    width, hidden = w_in.shape[1:]
    piece = hidden // PIECES
    return pl.pallas_call(
        pack_kernel,
        grid_spec=pltpu.PrefetchScalarGridSpec(
            num_scalar_prefetch=1,
            grid=(1,),
            in_specs=[
                pl.BlockSpec((1, width, piece), lambda i, m: (0, 0, m[1])),
                pl.BlockSpec((1, piece, width), lambda i, m: (0, m[1], 0)),
            ],
            out_specs=pl.BlockSpec((4, piece, piece), lambda i, m: (0, 0, 0)),
        ),
        out_shape=jax.ShapeDtypeStruct((4, piece, piece), BF16),
        compiler_params=pltpu.CompilerParams(vmem_limit_bytes=4 << 20),
        cost_estimate=BRIEF,
        name="pack_piece",
    )(meta, held(w_in), held(w_back))


def by_rows(count, step, body):
    @pl.loop(0, count // step)
    def _(n):
        body(n * step if isinstance(n, int) else pl.multiple_of(n * step, step))


def merge_kernel(plan, *refs):
    refs = list(refs)
    takes = [[[(refs.pop(0), at) for at in views] for views in groups] for groups, _, _ in plan]
    full = lambda n: (slice(None),) * n

    def rows_of(ref, lead, at, size):
        return lead + full(len(ref.shape) - 2 - len(lead)) + (pl.ds(at, size), slice(None))

    for groups, (_, axis, cuts) in zip(takes, plan):
        outs = [refs.pop(0) for _ in cuts]
        head = groups[0][0][0]
        count = head.shape[-2]
        step = 16 if len(head.shape) == 2 else 64
        if axis is not None:
            size = head.shape[axis]
            for k, (ref, _) in enumerate(groups[0]):

                def copy(at, k=k, ref=ref):
                    if len(ref.shape) == 2:
                        outs[0][pl.ds(k * size + at, step), :] = ref[pl.ds(at, step), :]
                    else:
                        lead = full(axis) + (slice(k * size, (k + 1) * size),)
                        outs[0][rows_of(outs[0], lead, at, step)] = ref[rows_of(ref, (), at, step)]

                by_rows(count, step, copy)
            continue
        for g, take in enumerate(groups):
            place = (g,) if len(groups) > 1 else ()
            if len(head.shape) == 2:
                for out, cut in zip(outs, cuts):
                    start = cut.start or 0

                    def add(at, out=out, start=start):
                        total = sum(ref[pl.ds(start + at, step), :].astype(F32) for ref, _ in take)
                        out[pl.ds(at, step), :] = total.astype(BF16)

                    by_rows(out.shape[0], step, add)
                continue

            def add(at, take=take, place=place):
                parts = [ref[rows_of(ref, () if view is ... else (view,), at, step)] for ref, view in take]
                total = sum(v.astype(F32) for v in parts).astype(BF16)
                for out, cut in zip(outs, cuts):
                    out[rows_of(out, place, at, step)] = total[cut]

            by_rows(count, step, add)


def merge(*items):
    plan, shapes, arrays = [], [], []
    for groups, axis, cuts in items:
        head = groups[0][0]
        shape = jax.eval_shape(lambda v: v[head[1]], head[0]).shape if isinstance(head, tuple) else head.shape
        first = jax.ShapeDtypeStruct(shape, BF16)
        if axis is not None:
            cuts = [None]
            shape = list(first.shape)
            shape[axis] *= len(groups[0])
            shapes.append(jax.ShapeDtypeStruct(tuple(shape), BF16))
        else:
            lead = (len(groups),) if len(groups) > 1 else ()
            shapes += [
                jax.ShapeDtypeStruct(lead + jax.eval_shape(lambda v, c=c: v[c], first).shape, BF16) for c in cuts
            ]
        pairs = [[v if isinstance(v, tuple) else (v, ...) for v in g] for g in groups]
        plan.append(([[at for _, at in g] for g in pairs], axis, cuts))
        arrays += [v for g in pairs for v, _ in g]
    return pl.pallas_call(
        functools.partial(merge_kernel, plan),
        out_shape=shapes,
        compiler_params=pltpu.CompilerParams(vmem_limit_bytes=16 << 20),
        cost_estimate=BRIEF,
        name="merge",
    )(*arrays)


def held(value):
    return pltpu.with_memory_space_constraint(value, pltpu.HBM)


SWAP = [(0, 1), (1, 0)]


def xor(k, n=4):
    return [(i, i ^ k) for i in range(n)]


def send(value, axis, pairs):
    return lax.ppermute(value, axis, pairs)


def add_low(a, b):
    return (a.astype(F32) + b.astype(F32)).astype(BF16)


def after(value, *earlier):
    return lax.optimization_barrier((value, *earlier))[0]


def tie(*values):
    return lax.optimization_barrier(values)


def fan(value, axis):
    rows = value.shape[0] // 4
    return [send(value[k * rows : (k + 1) * rows], axis, xor(k)) for k in (1, 2, 3)]


def add_fan(value, got):
    total = value[: value.shape[0] // 4].astype(F32)
    for v in got:
        total = total + v.astype(F32)
    return total.astype(BF16)


def dense_shards(
    tokens, gain_one, w_qkv, w_out, gain_two, w_router, w_in, w_back, route_ids, key_mask, cotangent
):
    nimg, half, width = tokens.shape
    imgs = nimg // 2
    rows = imgs * 2 * half
    experts = w_router.shape[1]
    piece = w_in.shape[2] // PIECES
    core = lax.axis_index("ctx")
    z = lax.axis_index("expert")
    me = core * 4 + lax.axis_index("dp")
    meta = jnp.stack([z, me, me * 4 + z, core]).astype(jnp.int32)
    meta_pair = jnp.stack([z ^ 2, me, me * 4 + z, core]).astype(jnp.int32)
    far = lambda v: send(v, "expert", xor(1))
    swap = lambda v: send(v, "ctx", SWAP)

    pack = pack_piece(meta, w_in, w_back)
    codes = after(route_ids, pack).reshape(nimg, half, TOP)
    codes = codes[..., 0] + experts * codes[..., 1]
    tok_other, dy_other, codes_other = swap(tokens), swap(cotangent), swap(codes)
    first = jnp.where(core == 0, codes, codes_other)
    second = jnp.where(core == 0, codes_other, codes)
    codes = lax.dynamic_slice_in_dim(jnp.concatenate([first, second], 1), core * imgs, imgs, 0)
    codes = codes.reshape(1, rows)
    ids = jnp.concatenate([codes % experts, codes // experts], 0)
    wide = jnp.pad(ids, ((0, 0), (0, 2 * width - rows))).reshape(TOP, 2, width)
    ids_pack = jnp.concatenate([wide[:, 0], wide[:, 1]], 0).astype(BF16)
    ids_pack = jnp.pad(ids_pack, ((padded(rows) - rows, 12), (0, 0)))
    wr = jnp.pad(w_router.T, ((0, 16 - experts), (0, 0)))
    g1, g2 = gain_one[None, :], gain_two[None, :]

    far_raw, pack = far(after(cotangent, pack)), send(pack, "expert", xor(2))
    x_rows, dy, normed, qkv, probs, mix, mid, routed = attend(
        meta, tokens, tok_other, cotangent, dy_other, key_mask, g1, w_qkv, w_out, g2
    )
    own_one = expert_steps(meta, routed, dy, ids, wr, (w_in, w_back))
    far_rows = jnp.concatenate([routed, ids_pack], 0)
    pack, wr_far = after(pack, routed), after(wr, own_one[2])

    packs = [pack] + [send(pack, "dp", xor(k)) for k in (1, 2, 3)]
    far_rows = far(far_rows)
    far_raw = after(far_raw, own_one[2])
    far_dy = assemble(meta, far_raw, swap(far_raw))
    far_one = expert_steps(meta, far_rows, far_dy, far_rows, wr_far, (w_in, w_back))
    *packs, wr_far = tie(*packs, after(wr, far_one[2]))
    packs = jnp.stack(packs)
    pair = [packs, swap(packs)]
    grads = weight_grads([routed, far_rows], *zip(own_one[:3], far_one[:3]), late=True)
    wr_far = after(wr_far, grads[0])

    far_two = expert(meta_pair, far_rows, far_dy, far_rows, wr_far, pair, far_one[3:])
    head, tail = slice(0, 2), slice(2, 4)
    even, odd = [(slice(None), slice(k, k + 1)) for k in (0, 1)]
    square = lambda v: v.reshape(2, 2, piece, width)

    def across(a, a_give, b, b_give):
        return merge(
            ([[a, swap(a_give)]], None, [head, tail]), ([[square(b), square(swap(b_give))]], None, [even, odd])
        )

    one = across(*grads)
    wr_own, *one = tie(after(wr, far_two[2]), *one)
    far_din, far_made = far_two[4], far_two[3]

    y_way, x_way = ("dp", xor(2)), ("dp", xor(1))
    own_two = expert(meta_pair, routed, dy, ids, wr_own, pair, own_one[3:])
    grads = weight_grads([routed, far_rows], *zip(own_two[:3], far_two[:3]))
    din_far, a_got, b_got, *grads = tie(far(far_din), send(one[1], *y_way), send(one[3], *x_way), *grads)
    a_one, b_one = [one[0], a_got], [one[2], b_got]

    two = tie(*across(*grads))

    a_two, b_two = [two[0], send(two[1], *y_way)], [two[2], send(two[3], *x_way)]
    far_made = far(after(far_made, din_far))
    tok_own, tok_give, shared, shared_give = attend_back(
        meta, [after(own_two[4], *two), din_far], ids, dy, mid, routed, wr, g2, mix, w_out, probs, qkv, x_rows, normed, w_qkv, g1
    )
    halves = [slice(0, 1), slice(1, 2)]
    line = lambda v: v.reshape(2, piece, width)
    flat = lambda group: [line(v) for v in group]
    one, one_give, two, two_give, far_made, shared, shared_give, tok_give = tie(
        *merge(([a_one, flat(b_one)], None, halves), ([a_two, flat(b_two)], None, halves)),
        far_made,
        shared,
        shared_give,
        tok_give,
    )
    mix_own, mix_give = combine(meta, mid, [own_two[3], far_made], imgs)
    quarters = lambda n: [slice(k * n, (k + 1) * n) for k in range(4)]
    everything = [slice(None)]
    second = lambda give: [send(give[0], *x_way), send(give[1], *y_way)]
    got = second(two_give)
    two, *shared, tok_got, mix_got = tie(
        *merge(
            ([[(two, 0), got[0]], [(two, 1), got[1]]], None, everything),
            ([[shared, swap(shared_give)]], None, quarters(width // 8)),
        ),
        swap(tok_give),
        swap(mix_give),
    )
    spread = lambda parts, axis: [send(v, axis, xor(k)) for k, v in zip((1, 2, 3), parts)]
    mixed, grad_tokens = place(meta, mix_own, mix_got, tok_own, tok_got)
    got, cross = second(one_give), send(two, "expert", xor(2))
    a, b, *shared, mixed, grad_tokens = tie(
        *merge(
            ([[(one, 0), got[0], (cross, 0)]], None, everything),
            ([[(one, 1), got[1], (cross, 1)]], None, everything),
            ([[shared[0], *spread(shared[1:], "dp")]], None, quarters(width // 32)),
        ),
        mixed,
        grad_tokens,
    )
    b = b[None]
    a, b, shared = tie(
        *merge(
            ([[a, send(a, *x_way)]], 0, None),
            ([[b, send(b, *y_way)]], 0, None),
            ([[shared[0], *spread(shared[1:], "expert")]], None, everything),
        )
    )
    a, b, shared = tie(
        *merge(
            ([[a, send(a, *y_way)]], 0, None),
            ([[b, send(b, *x_way)]], 1, None),
            ([[shared, *spread([shared] * 3, "expert")]], 0, None),
        )
    )
    b = b.reshape(a.shape)
    grad_in, grad_back = finish_expert(meta, a, swap(a), b, swap(b))
    (shared,) = merge(([[after(shared, grad_in, grad_back), *spread([shared] * 3, "dp")]], 0, None))
    earlier = finish_shared(meta, shared)
    grad_qkv, grad_out, small = finish_shared(meta, swap(shared), earlier)
    return (
        mixed,
        grad_tokens,
        small[:, 17],
        grad_qkv,
        grad_out,
        small[:, 16],
        small[:, :experts],
        grad_in,
        grad_back,
    )


def norm_rows(value, gain):
    center = value - jnp.mean(value, -1, keepdims=True)
    spread = jnp.mean(center * center, -1, keepdims=True)
    return center * lax.rsqrt(spread + 1e-06) * gain


def smooth_gelu(value):
    return 0.5 * value * (1.0 + jnp.tanh(0.7978845608 * (value + 0.044715 * value * value * value)))


def forward(tokens, gain_one, w_qkv, w_out, gain_two, w_router, w_in, w_back, flat_ids, live):
    nimg, half, width = tokens.shape
    count = nimg * half
    experts_all = w_router.shape[1]
    capacity = max(2, 2 * TOP * count // experts_all)
    x_rows = tokens.astype(jnp.float32).reshape(count, width)
    normed = norm_rows(x_rows, gain_one).astype(jnp.bfloat16)
    qkv = jnp.dot(normed, w_qkv, preferred_element_type=jnp.float32).astype(jnp.bfloat16)
    qkv = qkv.reshape(nimg, half, 3 * width)
    query = qkv[..., :width]
    keys_local = qkv[..., width : 2 * width]
    vals_local = qkv[..., 2 * width :]
    keys, vals = (
        lax.all_gather(keys_local, "ctx", axis=1, tiled=True),
        lax.all_gather(vals_local, "ctx", axis=1, tiled=True),
    )
    seq = keys.shape[1]
    query4 = query.reshape(nimg, half, HEADS, HEAD_DIM)
    keys4 = keys.reshape(nimg, seq, HEADS, HEAD_DIM)
    vals4 = vals.reshape(nimg, seq, HEADS, HEAD_DIM)
    scale = HEAD_DIM ** (-0.5)
    scores = (
        jnp.einsum("iqhc,ikhc->ihqk", query4, keys4, preferred_element_type=jnp.float32) * scale
    )
    open_keys = live[:, None, None, :]
    masked = jnp.where(open_keys, scores, -1000000000.0)
    topmost = jnp.max(masked, -1, keepdims=True)
    expo = jnp.where(open_keys, jnp.exp(masked - topmost), 0.0)
    probs = expo / jnp.sum(expo, -1, keepdims=True)
    probs_low = probs.astype(jnp.bfloat16)
    mix = jnp.einsum("ihqk,ikhc->iqhc", probs_low, vals4, preferred_element_type=jnp.float32)
    mix = mix.reshape(count, width).astype(jnp.bfloat16)
    mid = x_rows + jnp.dot(mix, w_out, preferred_element_type=jnp.float32)
    routed = norm_rows(mid, gain_two).astype(jnp.bfloat16)
    logits = jnp.dot(routed, w_router, preferred_element_type=jnp.float32)
    pick = flat_ids[:, :, None] == jnp.arange(experts_all, dtype=jnp.int32)[None, None, :]
    chosen = jnp.sum(jnp.where(pick, logits[:, None, :], 0.0), -1)
    expo_gate = jnp.exp(chosen)
    gates = expo_gate / jnp.sum(expo_gate, -1, keepdims=True)
    pair_ids = flat_ids.reshape(-1)
    hits = (pair_ids[:, None] == jnp.arange(experts_all, dtype=jnp.int32)[None, :]).astype(
        jnp.int32
    )
    before = jnp.cumsum(hits, 0) - hits
    slots = jnp.sum(before * hits, 1)
    where_rows = pair_ids * capacity + slots
    sent = jnp.repeat(routed, TOP, axis=0)
    buffer = jnp.zeros((experts_all * capacity, width), jnp.bfloat16).at[where_rows].set(sent)
    buffer = buffer.reshape(experts_all, capacity, width)
    arrived = lax.all_to_all(buffer, "expert", split_axis=0, concat_axis=1, tiled=True)
    pre = jnp.einsum("erd,edf->erf", arrived, w_in, preferred_element_type=jnp.float32)
    act = smooth_gelu(pre).astype(jnp.bfloat16)
    made = jnp.einsum("erf,efd->erd", act, w_back, preferred_element_type=jnp.float32).astype(
        jnp.bfloat16
    )
    returned = lax.all_to_all(made, "expert", split_axis=1, concat_axis=0, tiled=True)
    picked = returned.reshape(experts_all * capacity, width)[where_rows].reshape(count, TOP, width)
    output = mid + jnp.sum(gates[:, :, None] * picked.astype(jnp.float32), 1)
    return (
        x_rows,
        normed,
        query4,
        keys4,
        vals4,
        probs,
        probs_low,
        mix,
        mid,
        routed,
        pick,
        gates,
        where_rows,
        arrived,
        pre,
        act,
        picked,
        output,
        capacity,
    )


def shards(
    tokens, gain_one, w_qkv, w_out, gain_two, w_router, w_in, w_back, route_ids, key_mask, cotangent
):
    nimg, half, width = tokens.shape
    count = nimg * half
    experts_all = w_router.shape[1]
    flat_ids = route_ids.reshape(count, TOP)
    live = key_mask > 0
    state = forward(
        tokens, gain_one, w_qkv, w_out, gain_two, w_router, w_in, w_back, flat_ids, live
    )
    mixed = state[17].reshape(nimg, half, width).astype(jnp.bfloat16)
    state = forward(
        tokens, gain_one, w_qkv, w_out, gain_two, w_router, w_in, w_back, flat_ids, live
    )
    (
        x_rows,
        normed,
        query4,
        keys4,
        vals4,
        probs,
        probs_low,
        mix,
        mid,
        routed,
        pick,
        gates,
        where_rows,
        arrived,
        pre,
        act,
        picked,
        output,
        capacity,
    ) = state
    scale = HEAD_DIM ** (-0.5)
    high = lax.Precision.HIGHEST
    grad_y = cotangent.astype(jnp.float32).reshape(count, width)
    grad_gate = jnp.sum(grad_y[:, None, :] * picked.astype(jnp.float32), -1)
    d_out = (
        (gates[:, :, None] * grad_y[:, None, :]).astype(jnp.bfloat16).reshape(count * TOP, width)
    )
    grad_buffer = jnp.zeros((experts_all * capacity, width), jnp.bfloat16).at[where_rows].set(d_out)
    grad_buffer = grad_buffer.reshape(experts_all, capacity, width)
    grad_arrived = lax.all_to_all(grad_buffer, "expert", split_axis=0, concat_axis=1, tiled=True)
    d_act = jnp.einsum("erd,efd->erf", grad_arrived, w_back, preferred_element_type=jnp.float32)
    grad_back = jnp.einsum("erf,erd->efd", act, grad_arrived, preferred_element_type=jnp.float32)
    _, gelu_pull = jax.vjp(smooth_gelu, pre)
    d_pre = gelu_pull(d_act)[0].astype(jnp.bfloat16)
    grad_in = jnp.einsum("erd,erf->edf", arrived, d_pre, preferred_element_type=jnp.float32)
    d_in = jnp.einsum("erf,edf->erd", d_pre, w_in, preferred_element_type=jnp.float32).astype(
        jnp.bfloat16
    )
    grad_returned = lax.all_to_all(d_in, "expert", split_axis=1, concat_axis=0, tiled=True)
    grad_rows = grad_returned.reshape(experts_all * capacity, width)[where_rows].reshape(
        count, TOP, width
    )
    d_experts = jnp.sum(grad_rows.astype(jnp.float32), 1)
    d_chosen = gates * (grad_gate - jnp.sum(gates * grad_gate, -1, keepdims=True))
    d_logits = jnp.sum(jnp.where(pick, d_chosen[:, :, None], 0.0), 1)
    grad_router = jnp.dot(routed.astype(jnp.float32).T, d_logits, precision=high)
    d_routed = d_experts + jnp.dot(d_logits, w_router.astype(jnp.float32).T, precision=high)
    _, norm_two_pull = jax.vjp(norm_rows, mid, gain_two)
    d_mid_norm, grad_gain_two = norm_two_pull(d_routed)
    d_mid = grad_y + d_mid_norm
    d_branch = d_mid.astype(jnp.bfloat16)
    grad_out = jnp.einsum("td,te->de", mix, d_branch, preferred_element_type=jnp.float32)
    d_mix = jnp.dot(d_branch, w_out.T, preferred_element_type=jnp.float32).astype(jnp.bfloat16)
    d_mix4 = d_mix.reshape(nimg, half, HEADS, HEAD_DIM)
    d_probs = jnp.einsum("iqhc,ikhc->ihqk", d_mix4, vals4, preferred_element_type=jnp.float32)
    d_scores = (probs * (d_probs - jnp.sum(probs * d_probs, -1, keepdims=True))).astype(
        jnp.bfloat16
    )
    d_query = (
        jnp.einsum("ihqk,ikhc->iqhc", d_scores, keys4, preferred_element_type=jnp.float32) * scale
    )
    d_keys = (
        jnp.einsum("ihqk,iqhc->ikhc", d_scores, query4, preferred_element_type=jnp.float32) * scale
    )
    d_vals = jnp.einsum("ihqk,iqhc->ikhc", probs_low, d_mix4, preferred_element_type=jnp.float32)
    seq = keys4.shape[1]
    d_keys_own, d_vals_own = (
        lax.psum_scatter(
            d_keys.reshape(nimg, seq, width).astype(jnp.bfloat16),
            "ctx",
            scatter_dimension=1,
            tiled=True,
        ).astype(jnp.float32),
        lax.psum_scatter(
            d_vals.reshape(nimg, seq, width).astype(jnp.bfloat16),
            "ctx",
            scatter_dimension=1,
            tiled=True,
        ).astype(jnp.float32),
    )
    d_qkv = jnp.concatenate(
        [
            d_query.reshape(count, width).astype(jnp.bfloat16),
            d_keys_own.reshape(count, width).astype(jnp.bfloat16),
            d_vals_own.reshape(count, width).astype(jnp.bfloat16),
        ],
        axis=1,
    )
    grad_qkv = jnp.einsum("td,te->de", normed, d_qkv, preferred_element_type=jnp.float32)
    d_normed = jnp.dot(d_qkv, w_qkv.T, preferred_element_type=jnp.float32)
    _, norm_one_pull = jax.vjp(norm_rows, x_rows, gain_one)
    d_x_norm, grad_gain_one = norm_one_pull(d_normed)
    grad_tokens = (d_mid + d_x_norm).reshape(nimg, half, width).astype(jnp.bfloat16)
    grad_gain_one, grad_qkv, grad_out, grad_gain_two, grad_router = lax.psum(
        (grad_gain_one, grad_qkv, grad_out, grad_gain_two, grad_router), ("dp", "ctx", "expert")
    )
    grad_in, grad_back = (
        lax.psum(grad_in.astype(jnp.bfloat16), ("dp", "ctx")).astype(jnp.float32),
        lax.psum(grad_back.astype(jnp.bfloat16), ("dp", "ctx")).astype(jnp.float32),
    )
    return (
        mixed,
        grad_tokens,
        grad_gain_one,
        grad_qkv,
        grad_out,
        grad_gain_two,
        grad_router,
        grad_in,
        grad_back,
    )


def solution(mesh):
    placed = (
        P(("dp", "expert"), "ctx", None),
        P(),
        P(),
        P(),
        P(),
        P(),
        P("expert", None, None),
        P("expert", None, None),
        P(("dp", "expert"), "ctx", None, None, None),
        P(("dp", "expert"), None),
        P(("dp", "expert"), "ctx", None),
    )
    sizes = dict(mesh.shape)
    dense = sizes == {"dp": 4, "ctx": 2, "expert": 4}
    return jax.shard_map(
        dense_shards if dense else shards,
        mesh=mesh,
        in_specs=placed,
        out_specs=(
            P(("dp", "expert"), "ctx", None),
            P(("dp", "expert"), "ctx", None),
            P(),
            P(),
            P(),
            P(),
            P(),
            P("expert", None, None),
            P("expert", None, None),
        ),
        check_vma=False,
    )
```

```python
import functools
import jax
import jax.numpy as jnp
from jax import lax
from jax.experimental import pallas as pl
from jax.experimental.pallas import tpu as pltpu
from jax.sharding import PartitionSpec as P

HEADS = 8
HEAD_DIM = 64
TOP = 2
EPS = 1e-06
SCALE = HEAD_DIM ** (-0.5)
F32 = jnp.float32
BF16 = jnp.bfloat16
HELD = pltpu.HBM
HERE = pl.BlockSpec(memory_space=pltpu.VMEM)
BRIEF = pl.CostEstimate(flops=1, bytes_accessed=1, transcendentals=0)
NT = (((1,), (1,)), ((), ()))
TN = (((0,), (0,)), ((), ()))
NN = (((1,), (0,)), ((), ()))


def mm(a, b, dims=NN):
    return lax.dot_general(a, b, dims, preferred_element_type=F32)


def two_halves(a):
    high = a.astype(BF16)
    return high, (a - high.astype(F32)).astype(BF16)


def stats(value):
    center = value - jnp.mean(value, -1, keepdims=True)
    rstd = lax.rsqrt(jnp.mean(center * center, -1, keepdims=True) + EPS)
    return center * rstd, rstd


def norm_vjp(d_value, unit, rstd, gain):
    d_unit = d_value * gain
    return rstd * (
        d_unit
        - jnp.mean(d_unit, -1, keepdims=True)
        - unit * jnp.mean(d_unit * unit, -1, keepdims=True)
    )


def head_pair(value):
    lane = lax.broadcasted_iota(jnp.int32, value.shape, 1)
    first = lane < HEAD_DIM
    return jnp.concatenate(
        [jnp.where(first, value, 0.0), jnp.where(first, 0.0, value)], axis=0
    ).astype(BF16)


def join_pair(value):
    rows = value.shape[0] // 2
    lane = lax.broadcasted_iota(jnp.int32, (rows, value.shape[1]), 1)
    return jnp.where(lane < HEAD_DIM, value[:rows], value[rows:])


def natural(core, mine, theirs):
    return jnp.where(core == 0, mine, theirs), jnp.where(core == 0, theirs, mine)


def attend_kernel(
    meta_ref, own_ref, other_ref, dyown_ref, dyother_ref, mask_ref, g1_ref, wqkv_ref, wout_ref, g2_ref,
    x_ref, dy_ref, normed_ref, qkv_ref, probs_ref, mix_ref, mid_ref, routed_ref,
    x_s, qkv_s, mix_s,
):
    half = own_ref.shape[1]
    width = own_ref.shape[2]
    pair = 2 * HEAD_DIM
    core = meta_ref[3]
    for mine, theirs, ref in ((dyown_ref, dyother_ref, dy_ref), (own_ref, other_ref, x_ref)):
        first, second = natural(core, mine[0].astype(F32), theirs[0].astype(F32))
        x_s[0:half, :] = first
        x_s[half : 2 * half, :] = second
        ref[...] = x_s[...].astype(BF16)
    x = x_s[...]
    unit, _ = stats(x)
    normed = (unit * g1_ref[...]).astype(BF16)
    normed_ref[...] = normed
    qkv_s[...] = mm(normed, wqkv_ref[...])
    qkv_ref[...] = qkv_s[...].astype(BF16)
    image = core * pl.num_programs(0) + pl.program_id(0)
    is_open = mask_ref[pl.ds(image, 1), :] > 0
    for n in range(width // pair):
        at = n * pair
        query = head_pair(qkv_s[:, at : at + pair])
        keys = qkv_s[:, width + at : width + at + pair].astype(BF16)
        vals = qkv_s[:, 2 * width + at : 2 * width + at + pair].astype(BF16)
        scores = jnp.where(is_open, mm(query, keys, NT) * SCALE, -1e9)
        top = jnp.max(scores, -1, keepdims=True)
        expo = jnp.where(is_open, jnp.exp(scores - top), 0.0)
        probs = (expo / jnp.sum(expo, -1, keepdims=True)).astype(BF16)
        probs_ref[0, n] = probs
        mix_s[:, at : at + pair] = join_pair(mm(probs, vals))
    mix = mix_s[...].astype(BF16)
    mix_ref[...] = mix
    mid = x + mm(mix, wout_ref[...])
    mid_ref[...] = mid
    unit, _ = stats(mid)
    routed_ref[...] = (unit * g2_ref[...]).astype(BF16)


def attend(meta, own, other, dy_own, dy_other, mask, g1, wqkv, wout, g2):
    imgs, half, width = own.shape
    imgs //= 2
    seq = 2 * half
    rows = imgs * seq
    pairs = HEADS // 2
    raw = pl.BlockSpec((1, half, width), lambda i, m: (m[3] * imgs + i, 0, 0))
    one = lambda *s: pl.BlockSpec(s, lambda i, m: (i,) + (0,) * (len(s) - 1))
    fix = lambda *s: pl.BlockSpec(s, lambda i, m: (0,) * len(s))
    late = lambda *s: HELD(s, BF16)
    return pl.pallas_call(
        attend_kernel,
        grid_spec=pltpu.PrefetchScalarGridSpec(
            num_scalar_prefetch=1,
            grid=(imgs,),
            in_specs=[
                raw, raw, raw, raw, fix(*mask.shape), fix(1, width),
                fix(width, 3 * width), fix(width, width), fix(1, width),
            ],
            out_specs=[
                one(seq, width), one(seq, width), one(seq, width), one(seq, 3 * width),
                one(1, pairs, 2 * seq, seq), one(seq, width), one(seq, width), one(seq, width),
            ],
            scratch_shapes=[
                pltpu.VMEM((seq, width), F32),
                pltpu.VMEM((seq, 3 * width), F32),
                pltpu.VMEM((seq, width), F32),
            ],
        ),
        out_shape=[
            late(rows, width),
            jax.ShapeDtypeStruct((rows, width), BF16),
            late(rows, width),
            late(rows, 3 * width),
            late(imgs, pairs, 2 * seq, seq),
            late(rows, width),
            HELD((rows, width), F32),
            jax.ShapeDtypeStruct((rows, width), BF16),
        ],
        compiler_params=pltpu.CompilerParams(vmem_limit_bytes=22 << 20),
        cost_estimate=BRIEF,
        name="attend",
    )(meta, *map(held, (own, other, dy_own, dy_other)), mask, g1, held(wqkv), held(wout), g2)


def assemble_kernel(meta_ref, own_ref, other_ref, out_ref, out_s):
    half = own_ref.shape[1]
    first, second = natural(meta_ref[3], own_ref[0].astype(F32), other_ref[0].astype(F32))
    out_s[0:half, :] = first
    out_s[half : 2 * half, :] = second
    out_ref[...] = out_s[...].astype(BF16)


def assemble(meta, own, other):
    imgs, half, width = own.shape
    imgs //= 2
    raw = pl.BlockSpec((1, half, width), lambda i, m: (m[3] * imgs + i, 0, 0))
    return pl.pallas_call(
        assemble_kernel,
        grid_spec=pltpu.PrefetchScalarGridSpec(
            num_scalar_prefetch=1,
            grid=(imgs,),
            in_specs=[raw, raw],
            out_specs=pl.BlockSpec((2 * half, width), lambda i, m: (i, 0)),
            scratch_shapes=[pltpu.VMEM((2 * half, width), F32)],
        ),
        out_shape=jax.ShapeDtypeStruct((imgs * 2 * half, width), BF16),
        compiler_params=pltpu.CompilerParams(vmem_limit_bytes=6 << 20),
        cost_estimate=BRIEF,
        name="assemble",
    )(meta, own, other)


def row_gates(rows, ids, wr):
    logits = mm(wr, rows, NT)
    row = lax.broadcasted_iota(jnp.int32, logits.shape, 0)
    pick = (row.astype(F32) == ids[0:1, :]) | (row.astype(F32) == ids[1:2, :])
    top = jnp.max(jnp.where(pick, logits, -jnp.inf), 0, keepdims=True)
    expo = jnp.where(pick, jnp.exp(logits - top), 0.0)
    return expo / jnp.sum(expo, 0, keepdims=True), row


def padded(count):
    return -(-count // 16) * 16


def expert_kernel(add, local, meta_ref, rows_ref, dy_ref, ids_ref, wr_ref, wi_ref, wb_ref, *rest):
    sources = [] if local else [wb_ref]
    if add:
        sources += rest[:2]
        rest = rest[2:]
    act_ref, dpre_ref, dout_ref, made_ref, din_ref, wi_s, wb_s, *rest = rest
    if sources:
        *landings, sems = rest
        copies = [pltpu.make_async_copy(v, w, sems.at[n]) for n, (v, w) in enumerate(zip(sources, landings))]
        for copy in copies:
            copy.start()
    count = act_ref.shape[0]
    width = rows_ref.shape[1]
    rows = rows_ref[0:count, :]
    part = wi_s.shape[1] // PIECES
    if local:
        for n in range(PIECES):
            at = pl.ds(pl.multiple_of((n ^ meta_ref[1]) * part, part), part)
            wi_s[:, n * part : (n + 1) * part] = wi_ref[0, :, at]
            wb_s[n * part : (n + 1) * part, :] = wb_ref[0, at, :]

    if ids_ref.shape[0] == 2:
        ids = ids_ref[...].astype(F32)
    else:
        at = padded(count)
        ids = [ids_ref[at : at + 2, :], ids_ref[at + 2 : at + 4, 0 : count - width]]
        ids = jnp.concatenate([v.astype(F32) for v in ids], axis=1)
    gates, row = row_gates(rows, ids, wr_ref[...])
    high, low = two_halves(jnp.where(row == meta_ref[0], gates, 0.0))
    ones = jnp.ones((16, 128), BF16)
    gate = (mm(high, ones, TN) + mm(low, ones, TN))[:, 0:1]
    dout_ref[...] = (gate * dy_ref[...].astype(F32)).astype(BF16)
    wide = wi_s.shape[1] // CHUNKS
    for q in range(CHUNKS):
        if not local and q % (CHUNKS // 2) == 0:
            ref, first = (landings[0], PIECES // 2) if q else (wi_ref, 0)
            if q:
                copies[0].wait()
            for n in range(PIECES // 2):
                to = slice((first + n) * part, (first + n + 1) * part)
                for h in range(2):
                    side = slice(h * part, (h + 1) * part)
                    wi_s[side, to] = ref[n, h]
                    wb_s[to, side] = ref[n, 2 + h]
        here = slice(q * wide, (q + 1) * wide)
        pre = mm(rows, wi_s[:, here])
        square = pre * pre
        inner = pre * (0.7978845608 + 0.0356774081 * square)
        up = 0.5 + 0.5 * jnp.tanh(inner)
        value = pre * up
        act_ref[:, here] = value.astype(BF16)
        slope = up + value * (1.0 - up) * (1.5957691216 + 0.2140644488 * square)
        dpre_ref[:, here] = (mm(dout_ref[...], wb_s[here, :], NT) * slope).astype(BF16)
    made = mm(act_ref[...], wb_s[...]).astype(BF16).astype(F32)
    d_in = mm(dpre_ref[...], wi_s[...], NT)
    total = gate * made
    high, low = two_halves(made * dy_ref[...].astype(F32))
    ones = jnp.ones((16, width), BF16)
    d_gate = (mm(ones, high, NT) + mm(ones, low, NT))[0:8]
    row = lax.broadcasted_iota(jnp.int32, d_gate.shape, 0)
    d_gate = jnp.where(row == meta_ref[0], d_gate, 0.0)
    tail = padded(count)
    if add:
        for copy in copies[-2:]:
            copy.wait()
        pmade_ref, pdin_ref = landings[-2:]
        total += pmade_ref[...].astype(F32)
        d_in += pdin_ref[0:count, :].astype(F32)
        d_gate += read_gate(pdin_ref, count)
    made_ref[...] = total.astype(BF16)
    din_ref[0:count, :] = d_in.astype(BF16)
    high = d_gate.astype(BF16).astype(F32)
    value = jnp.concatenate([high, d_gate - high], axis=0).astype(BF16)
    din_ref[tail : tail + 16, :] = value[:, :width]
    din_ref[tail + 16 : tail + 32, 0 : count - width] = value[:, width:]


CHUNKS = 4


def read_gate(ref, count):
    tail = padded(count)
    width = ref.shape[1]
    value = ref[tail : tail + 16, 0 : min(count, width)].astype(F32)
    if count > width:
        value = jnp.concatenate([value, ref[tail + 16 : tail + 32, 0 : count - width].astype(F32)], axis=1)
    return value[0:8] + value[8:16]


PIECES = 8


def expert(meta, rows, dy, ids, wr, weights, prev=None):
    count, width = dy.shape
    local = weights[0].ndim == 3
    hidden = weights[0].shape[2] if local else PIECES * weights[0].shape[2]
    deep = padded(count) + 32
    first = prev is None
    away = pl.BlockSpec(memory_space=pl.ANY)
    more = [] if first else [away, away]
    landings = [] if local else [pltpu.VMEM(weights[1].shape, BF16)]
    if not first:
        landings += [pltpu.VMEM((count, width), BF16), pltpu.VMEM((deep, width), BF16)]
    if landings:
        landings.append(pltpu.SemaphoreType.DMA((len(landings),)))
    shape = lambda *s: jax.ShapeDtypeStruct(s, BF16)
    return pl.pallas_call(
        functools.partial(expert_kernel, not first, local),
        grid_spec=pltpu.PrefetchScalarGridSpec(
            num_scalar_prefetch=1,
            grid=(1,),
            in_specs=[HERE] * 5 + [HERE if local else away, *more],
            out_specs=[HERE] * 5,
            scratch_shapes=[pltpu.VMEM((width, hidden), BF16), pltpu.VMEM((hidden, width), BF16), *landings],
        ),
        out_shape=[shape(count, hidden), shape(count, hidden), shape(count, width), shape(count, width), shape(deep, width)],
        compiler_params=pltpu.CompilerParams(vmem_limit_bytes=LIMIT << 20),
        cost_estimate=BRIEF,
        name="expert",
    )(meta, rows, dy, ids, wr, weights[0], weights[1] if local else held(weights[1]), *[held(v) for v in prev or ()])


LIMIT = 26


def expert_steps_kernel(add, local, meta_ref, rows_ref, dy_ref, ids_ref, wr_ref, *rest):
    wi_ref, wb_ref, *rest = rest
    sources = [] if local else [wb_ref]
    if add:
        sources += rest[:2]
        rest = rest[2:]
    act_ref, dpre_ref, dout_ref, made_ref, din_ref, gate_s, made_s, din_s, *rest = rest
    step = pl.program_id(0)
    copies = []
    if sources:
        *rest, sems = rest
        landings = rest[len(rest) - len(sources) :]
        rest = rest[: len(rest) - len(sources)]
        copies = [pltpu.make_async_copy(v, w, sems.at[n]) for n, (v, w) in enumerate(zip(sources, landings))]
    if not local:
        wb_ref = landings[0]
    if add:
        pmade_ref, pdin_ref = landings[-2:]
    count = act_ref.shape[0]
    width = rows_ref.shape[1]
    rows = rows_ref[0:count, :]

    @pl.when(step == 0)
    def _():
        for copy in copies:
            copy.start()
        if ids_ref.shape[0] == 2:
            ids = ids_ref[...].astype(F32)
        else:
            at = padded(count)
            ids = [ids_ref[at : at + 2, :], ids_ref[at + 2 : at + 4, 0 : count - width]]
            ids = jnp.concatenate([v.astype(F32) for v in ids], axis=1)
        gates, row = row_gates(rows, ids, wr_ref[...])
        high, low = two_halves(jnp.where(row == meta_ref[0], gates, 0.0))
        ones = jnp.ones((16, 128), BF16)
        gate_s[...] = mm(high, ones, TN) + mm(low, ones, TN)
        gate = gate_s[:, 0:1]
        dout_ref[...] = (gate * dy_ref[...].astype(F32)).astype(BF16)
        made_s[...] = jnp.zeros_like(made_s)
        din_s[...] = jnp.zeros_like(din_s)

    if local:
        part = wi_ref.shape[2] // PIECES
        at = [pl.multiple_of(((2 * step + s) ^ meta_ref[1]) * part, part) for s in range(2)]
        w_in = jnp.concatenate([wi_ref[0, :, pl.ds(v, part)] for v in at], axis=1)
        w_back = jnp.concatenate([wb_ref[0, pl.ds(v, part), :] for v in at], axis=0)
    else:
        wi_s, wb_s = rest
        part = wi_s.shape[0] // 2
        upper = pl.num_programs(0) // 2

        @pl.when(step == upper)
        def _():
            copies[0].wait()

        for ref, first in ((wi_ref, 0), (wb_ref, upper)):

            @pl.when((step < upper) == (first == 0))
            def _():
                for s in range(2):
                    for h in range(2):
                        at = 2 * (step - first) + s
                        wi_s[h * part : (h + 1) * part, s * part : (s + 1) * part] = ref[at, h]
                        wb_s[s * part : (s + 1) * part, h * part : (h + 1) * part] = ref[at, 2 + h]

        w_in, w_back = wi_s[...], wb_s[...]
    pre = mm(rows, w_in)
    square = pre * pre
    inner = pre * (0.7978845608 + 0.0356774081 * square)
    up = 0.5 + 0.5 * jnp.tanh(inner)
    value = pre * up
    act = value.astype(BF16)
    slope = up + value * (1.0 - up) * (1.5957691216 + 0.2140644488 * square)
    here = pl.ds(pl.multiple_of(step * pre.shape[1], pre.shape[1]), pre.shape[1])
    act_ref[:, here] = act
    made_s[...] += mm(act, w_back)
    dpre = (mm(dout_ref[...], w_back, NT) * slope).astype(BF16)
    dpre_ref[:, here] = dpre
    din_s[...] += mm(dpre, w_in, NT)

    @pl.when(step == pl.num_programs(0) - 1)
    def _():
        gate = gate_s[:, 0:1]
        made = made_s[...].astype(BF16).astype(F32)
        total = gate * made
        d_in = din_s[...]
        high, low = two_halves(made * dy_ref[...].astype(F32))
        ones = jnp.ones((16, made.shape[1]), BF16)
        d_gate = (mm(ones, high, NT) + mm(ones, low, NT))[0:8]
        row = lax.broadcasted_iota(jnp.int32, d_gate.shape, 0)
        d_gate = jnp.where(row == meta_ref[0], d_gate, 0.0)
        tail = padded(count)
        for copy in copies[0 if local else 1 :]:
            copy.wait()
        if add:
            total += pmade_ref[...].astype(F32)
            d_in += pdin_ref[0:count, :].astype(F32)
            d_gate += read_gate(pdin_ref, count)
        made_ref[...] = total.astype(BF16)
        din_ref[0:count, :] = d_in.astype(BF16)
        high = d_gate.astype(BF16).astype(F32)
        value = jnp.concatenate([high, d_gate - high], axis=0).astype(BF16)
        if count > d_in.shape[1]:
            cut = d_in.shape[1]
            din_ref[tail : tail + 16, :] = value[:, :cut]
            din_ref[tail + 16 : tail + 32, 0 : count - cut] = value[:, cut:]
        else:
            din_ref[tail : tail + 16, 0:count] = value


def expert_steps(meta, rows, dy, ids, wr, weights, prev=None):
    count = dy.shape[0]
    width = rows.shape[1]
    local = weights[0].ndim == 3
    piece = weights[0].shape[2] // PIECES if local else weights[0].shape[2]
    hidden = PIECES * piece
    steps = PIECES // 2
    deep = padded(count) + 16 * -(-count // width)
    fix = lambda *s: pl.BlockSpec(s, lambda q, m: (0,) * len(s))
    first = prev is None
    away = pl.BlockSpec(memory_space=pl.ANY)
    more = [] if first else [away, away]
    landings = [] if local else [pltpu.VMEM(weights[1].shape, BF16)]
    if not first:
        landings += [pltpu.VMEM((count, width), BF16), pltpu.VMEM((deep, width), BF16)]
    if landings:
        landings.append(pltpu.SemaphoreType.DMA((len(landings),)))
    given = [] if first else [held(v) for v in prev]
    ends = [fix(count, width), fix(deep, width)] if first else [HERE, HERE]
    kept = HELD if first else jax.ShapeDtypeStruct
    return pl.pallas_call(
        functools.partial(expert_steps_kernel, prev is not None, local),
        grid_spec=pltpu.PrefetchScalarGridSpec(
            num_scalar_prefetch=1,
            grid=(steps,),
            in_specs=[HERE, fix(*dy.shape), HERE, HERE, HERE, HERE if local else away, *more],
            out_specs=[HERE] * 3 + ends,
            scratch_shapes=[
                pltpu.VMEM((count, 128), F32),
                pltpu.VMEM((count, width), F32),
                pltpu.VMEM((count, width), F32),
            ]
            + ([] if local else [pltpu.VMEM((width, 2 * piece), BF16), pltpu.VMEM((2 * piece, width), BF16)])
            + landings,
        ),
        out_shape=[
            jax.ShapeDtypeStruct((count, hidden), BF16),
            jax.ShapeDtypeStruct((count, hidden), BF16),
            jax.ShapeDtypeStruct((count, width), BF16),
            kept((count, width), BF16),
            kept((deep, width), BF16),
        ],
        compiler_params=pltpu.CompilerParams(vmem_limit_bytes=20 << 20),
        cost_estimate=BRIEF,
        name="expert_steps",
    )(meta, rows, dy if first else held(dy), ids, wr, weights[0], weights[1] if local else held(weights[1]), *given)


def weight_kernel(n, *refs):
    rows, acts, dpres, douts = (refs[g * n : (g + 1) * n] for g in range(4))
    iown_ref, igive_ref, bown_ref, bgive_ref = refs[4 * n :]
    wide = iown_ref.shape[0] * iown_ref.shape[1]
    here = pl.ds(pl.multiple_of(pl.program_id(0) * wide, wide), wide)
    results = []
    for left, right in ((dpres, rows), (acts, douts)):
        total = 0.0
        for b in range(n):
            count = left[b].shape[0]
            total = total + mm(left[b][:, here], right[b][0:count, :], TN)
        results.append(total.astype(BF16).reshape(iown_ref.shape))
    grad_in, grad_back = results
    first = pl.program_id(0) < pl.num_programs(0) // 2

    @pl.when(first)
    def _():
        iown_ref[...] = grad_in
        bown_ref[...] = grad_back

    @pl.when(jnp.logical_not(first))
    def _():
        igive_ref[...] = grad_in
        bgive_ref[...] = grad_back


def weight_grads(rows, acts, dpres, douts, late=False):
    n = len(rows)
    width = rows[0].shape[1]
    piece = acts[0].shape[1] // PIECES
    steps = PIECES // 2
    own = pl.BlockSpec((2, piece, width), lambda q: (jnp.minimum(q, steps // 2 - 1), 0, 0))
    give = pl.BlockSpec((2, piece, width), lambda q: (jnp.maximum(q - steps // 2, 0), 0, 0))
    return pl.pallas_call(
        functools.partial(weight_kernel, n),
        grid=(steps,),
        in_specs=[HERE] * (4 * n),
        out_specs=[own, give, own, give],
        out_shape=[(HELD if late and g % 2 == 0 else jax.ShapeDtypeStruct)((PIECES // 2, piece, width), BF16) for g in range(4)],
        compiler_params=pltpu.CompilerParams(vmem_limit_bytes=14 << 20),
        cost_estimate=BRIEF,
        name="weight_grads",
    )(*rows, *acts, *dpres, *douts)


def finish_kernel(meta_ref, im_ref, ir_ref, bm_ref, br_ref, gin_ref, gback_ref):
    mine = pl.program_id(0) < pl.num_programs(0) // 2
    flip = meta_ref[1] % 2 == 1
    piece, width = im_ref.shape[1:]
    for m_ref, r_ref, out_ref in ((im_ref, ir_ref, gin_ref), (bm_ref, br_ref, gback_ref)):
        value = jnp.where(mine, m_ref[...], r_ref[...]).astype(F32)
        first = jnp.where(flip, value[1], value[0])
        second = jnp.where(flip, value[0], value[1])
        if out_ref is gin_ref:
            out_ref[0, :, 0:piece] = jnp.transpose(first)
            out_ref[0, :, piece : 2 * piece] = jnp.transpose(second)
        else:
            out_ref[0, 0:piece, :] = first
            out_ref[0, piece : 2 * piece, :] = second


def finish_expert(meta, in_mine, in_recv, back_mine, back_recv):
    upper, piece, width = in_mine.shape
    steps = upper
    own = pl.BlockSpec((2, piece, width), lambda q, m: (jnp.minimum(q, steps // 2 - 1), 0, 0))
    give = pl.BlockSpec((2, piece, width), lambda q, m: (jnp.maximum(q - steps // 2, 0), 0, 0))
    return pl.pallas_call(
        finish_kernel,
        grid_spec=pltpu.PrefetchScalarGridSpec(
            num_scalar_prefetch=1,
            grid=(steps,),
            in_specs=[own, give, own, give],
            out_specs=[
                pl.BlockSpec((1, width, 2 * piece), lambda q, m: (0, 0, q ^ (m[1] // 2))),
                pl.BlockSpec((1, 2 * piece, width), lambda q, m: (0, q ^ (m[1] // 2), 0)),
            ],
        ),
        out_shape=[
            jax.ShapeDtypeStruct((1, width, PIECES * piece), F32),
            jax.ShapeDtypeStruct((1, PIECES * piece, width), F32),
        ],
        compiler_params=pltpu.CompilerParams(vmem_limit_bytes=14 << 20),
        cost_estimate=BRIEF,
        name="finish_expert",
    )(meta, in_mine, in_recv, back_mine, back_recv)


def split_halves(core, whole_ref, own_ref, other_ref):
    imgs, half, _ = own_ref.shape
    for i in range(imgs):
        at = 2 * half * i
        first, second = whole_ref[at : at + half, :], whole_ref[at + half : at + 2 * half, :]
        mine, theirs = natural(core, first, second)
        own_ref[i] = mine.astype(BF16)
        other_ref[i] = theirs.astype(BF16)


def back_kernel(
    meta_ref, din0_ref, din1_ref,
    ids_ref, dy_ref, mid_ref, routed_ref, wr_ref, g2_ref, mix_ref, wout_ref,
    probs_ref, qkv_ref, x_ref, normed_ref, wqkv_ref, g1_ref,
    own_ref, other_ref, gown_ref, ggive_ref,
    dmid_s, dmix_s, dqkv_s, tok_s, grad_s, small_s,
):
    step = pl.program_id(0)
    imgs = pl.num_programs(0)
    seq = qkv_ref.shape[0]
    width = x_ref.shape[1]
    half = seq // 2
    pair = 2 * HEAD_DIM
    rows = x_ref.shape[0]

    @pl.when(step == 0)
    def _():
        routed = routed_ref[...]
        wr = wr_ref[...]
        gates, _ = row_gates(routed, ids_ref[...].astype(F32), wr)
        d_gate = read_gate(din0_ref, rows) + read_gate(din1_ref, rows)
        d_gate = jnp.concatenate([d_gate, jnp.zeros_like(d_gate)], axis=0)
        d_logits = gates * (d_gate - jnp.sum(gates * d_gate, 0, keepdims=True))
        high, low = two_halves(d_logits)
        small_s[...] = jnp.zeros_like(small_s)
        small_s[0:16, :] = mm(high, routed) + mm(low, routed)
        d_routed = din0_ref[0:rows, :].astype(F32) + din1_ref[0:rows, :].astype(F32)
        d_routed = d_routed + mm(high, wr, TN) + mm(low, wr, TN)
        unit, rstd = stats(mid_ref[...])
        small_s[16:17, :] = jnp.sum(d_routed * unit, 0, keepdims=True)
        d_mid = dy_ref[...].astype(F32) + norm_vjp(d_routed, unit, rstd, g2_ref[...])
        dmid_s[...] = d_mid
        d_branch = d_mid.astype(BF16)
        grad_s[:, 3 * width : 4 * width] = mm(mix_ref[...], d_branch, TN).astype(BF16)
        dmix_s[...] = mm(d_branch, wout_ref[...], NT)

    base = pl.multiple_of(step * seq, 8)
    for n in range(width // pair):
        at = n * pair
        d_mix = head_pair(dmix_s[pl.ds(base, seq), at : at + pair])
        query = head_pair(qkv_ref[:, at : at + pair].astype(F32))
        keys = qkv_ref[:, width + at : width + at + pair]
        vals = qkv_ref[:, 2 * width + at : 2 * width + at + pair]
        low = probs_ref[0, n]
        probs = low.astype(F32)
        d_probs = mm(d_mix, vals, NT)
        d_scores = probs * (d_probs - jnp.sum(probs * d_probs, -1, keepdims=True))
        d_scores = d_scores.astype(BF16)
        d_query = join_pair(mm(d_scores, keys)) * SCALE
        d_keys = mm(d_scores, query, TN) * SCALE
        d_vals = mm(low, d_mix, TN)
        dqkv_s[pl.ds(base, seq), at : at + pair] = d_query.astype(BF16)
        dqkv_s[pl.ds(base, seq), width + at : width + at + pair] = d_keys.astype(BF16)
        dqkv_s[pl.ds(base, seq), 2 * width + at : 2 * width + at + pair] = d_vals.astype(BF16)

    @pl.when(step == imgs - 1)
    def _():
        d_qkv = dqkv_s[...]
        grad_s[:, : 3 * width] = mm(normed_ref[...], d_qkv, TN).astype(BF16)
        d_normed = mm(d_qkv, wqkv_ref[...], NT)
        unit, rstd = stats(x_ref[...].astype(F32))
        small_s[17:18, :] = jnp.sum(d_normed * unit, 0, keepdims=True)
        grad_s[:, 4 * width :] = jnp.transpose(small_s[...]).astype(BF16)
        tok_s[...] = dmid_s[...] + norm_vjp(d_normed, unit, rstd, g1_ref[...])
        split_halves(meta_ref[3], tok_s, own_ref, other_ref)
        part = width // SHARES

        @pl.loop(0, SHARES // 2)
        def _(r):
            to = pl.ds(pl.multiple_of(r * part, part), part)
            for ref, first in ((gown_ref, 0), (ggive_ref, SHARES // 2)):
                there = pl.multiple_of(((r + first) ^ meta_ref[2]) * part, part)
                ref[to, :] = grad_s[pl.ds(there, part), :]


SHARES = 32


def attend_back(meta, dins, ids, dy, mid, routed, wr, g2, mix, wout, probs, qkv, x, normed, wqkv, g1):
    imgs = probs.shape[0]
    rows, width = x.shape
    seq = rows // imgs
    pairs = HEADS // 2
    wide = 4 * width + 128
    fix = lambda *s: pl.BlockSpec(s, lambda i, m: (0,) * len(s))
    return pl.pallas_call(
        back_kernel,
        grid_spec=pltpu.PrefetchScalarGridSpec(
            num_scalar_prefetch=1,
            grid=(imgs,),
            in_specs=[fix(*a.shape) for a in dins] + [
                fix(2, rows), fix(rows, width), fix(rows, width), fix(rows, width),
                fix(16, width), fix(1, width), fix(rows, width), fix(width, width),
                pl.BlockSpec((1, pairs, 2 * seq, seq), lambda i, m: (i, 0, 0, 0)),
                pl.BlockSpec((seq, 3 * width), lambda i, m: (i, 0)),
                fix(rows, width), fix(rows, width), fix(width, 3 * width), fix(1, width),
            ],
            out_specs=[
                fix(imgs, seq // 2, width), fix(imgs, seq // 2, width),
                fix(width // 2, wide), fix(width // 2, wide),
            ],
            scratch_shapes=[
                pltpu.VMEM((rows, width), F32),
                pltpu.VMEM((rows, width), F32),
                pltpu.VMEM((rows, 3 * width), BF16),
                pltpu.VMEM((rows, width), F32),
                pltpu.VMEM((width, wide), BF16),
                pltpu.VMEM((128, width), F32),
            ],
        ),
        out_shape=[
            jax.ShapeDtypeStruct((imgs, seq // 2, width), BF16),
            jax.ShapeDtypeStruct((imgs, seq // 2, width), BF16),
            jax.ShapeDtypeStruct((width // 2, wide), BF16),
            jax.ShapeDtypeStruct((width // 2, wide), BF16),
        ],
        compiler_params=pltpu.CompilerParams(vmem_limit_bytes=32 << 20),
        cost_estimate=BRIEF,
        name="attend_back",
    )(meta, *dins, ids, dy, mid, routed, wr, g2, mix, wout, probs, qkv, x, normed, wqkv, g1)


def shared_kernel(meta_ref, half_ref, *refs):
    gqkv_ref, gout_ref, small_ref = refs[-3:]
    upper = half_ref.shape[0]
    width = 2 * upper
    part = width // SHARES

    @pl.loop(0, SHARES // 2)
    def _(i):
        there = pl.multiple_of((i ^ (meta_ref[2] % (SHARES // 2))) * part, part)
        value = half_ref[pl.ds(there, part), :].astype(F32)
        at = pl.ds(pl.multiple_of(i * part, part), part)
        gqkv_ref[at, :] = value[:, : 3 * width]
        gout_ref[at, :] = value[:, 3 * width : 4 * width]
        small_ref[at, :] = value[:, 4 * width :]


def finish_shared(meta, half, earlier=()):
    upper, wide = half.shape
    width = 2 * upper
    at = (lambda i, m: (1 - m[3], 0)) if earlier else (lambda i, m: (m[3], 0))
    columns = (3 * width, width, wide - 4 * width)
    return pl.pallas_call(
        shared_kernel,
        grid_spec=pltpu.PrefetchScalarGridSpec(
            num_scalar_prefetch=1,
            grid=(1,),
            in_specs=[pl.BlockSpec((upper, wide), lambda i, m: (0, 0))] + [pl.BlockSpec(memory_space=pl.ANY)] * len(earlier),
            out_specs=[pl.BlockSpec((upper, c), at) for c in columns],
        ),
        out_shape=[jax.ShapeDtypeStruct((width, c), F32) for c in columns],
        input_output_aliases={2 + n: n for n in range(len(earlier))},
        compiler_params=pltpu.CompilerParams(vmem_limit_bytes=12 << 20),
        cost_estimate=BRIEF,
        name="finish_shared",
    )(meta, half, *earlier)


def combine_kernel(meta_ref, mid_ref, a_ref, b_ref, own_ref, other_ref, s_ref):
    s_ref[...] = mid_ref[...] + (a_ref[...].astype(F32) + b_ref[...].astype(F32))
    split_halves(meta_ref[3], s_ref, own_ref, other_ref)


def combine(meta, mid, parts, imgs):
    rows, width = mid.shape
    seq = rows // imgs
    spec = pl.BlockSpec((seq, width), lambda i, m: (i, 0))
    out = pl.BlockSpec((1, seq // 2, width), lambda i, m: (i, 0, 0))
    shape = jax.ShapeDtypeStruct((imgs, seq // 2, width), BF16)
    return pl.pallas_call(
        combine_kernel,
        grid_spec=pltpu.PrefetchScalarGridSpec(
            num_scalar_prefetch=1,
            grid=(imgs,),
            in_specs=[spec] * 3,
            out_specs=[out, out],
            scratch_shapes=[pltpu.VMEM((seq, width), F32)],
        ),
        out_shape=[shape, shape],
        compiler_params=pltpu.CompilerParams(vmem_limit_bytes=8 << 20),
        cost_estimate=BRIEF,
        name="combine",
    )(meta, mid, *parts)


def place_kernel(meta_ref, a_own_ref, a_recv_ref, b_own_ref, b_recv_ref, a_ref, b_ref):
    imgs = pl.num_programs(0) // 2
    mine = pl.program_id(0) // imgs == meta_ref[3]
    a_ref[...] = jnp.where(mine, a_own_ref[...], a_recv_ref[...])
    b_ref[...] = jnp.where(mine, b_own_ref[...], b_recv_ref[...])


def place(meta, *arrays):
    imgs, half, width = arrays[0].shape
    spec = pl.BlockSpec((1, half, width), lambda j, m: (j % imgs, 0, 0))
    out = pl.BlockSpec((1, half, width), lambda j, m: (j, 0, 0))
    shape = jax.ShapeDtypeStruct((2 * imgs, half, width), BF16)
    return pl.pallas_call(
        place_kernel,
        grid_spec=pltpu.PrefetchScalarGridSpec(
            num_scalar_prefetch=1, grid=(2 * imgs,), in_specs=[spec] * 4, out_specs=[out, out]
        ),
        out_shape=[shape, shape],
        compiler_params=pltpu.CompilerParams(vmem_limit_bytes=4 << 20),
        cost_estimate=BRIEF,
        name="place",
    )(meta, *arrays)


def pack_kernel(meta_ref, wi_ref, wb_ref, out_ref):
    part = out_ref.shape[1]
    for h in range(2):
        at = slice(h * part, (h + 1) * part)
        out_ref[h] = wi_ref[0, at, :]
        out_ref[2 + h] = wb_ref[0, :, at]


def pack_piece(meta, w_in, w_back):
    width, hidden = w_in.shape[1:]
    piece = hidden // PIECES
    return pl.pallas_call(
        pack_kernel,
        grid_spec=pltpu.PrefetchScalarGridSpec(
            num_scalar_prefetch=1,
            grid=(1,),
            in_specs=[
                pl.BlockSpec((1, width, piece), lambda i, m: (0, 0, m[1])),
                pl.BlockSpec((1, piece, width), lambda i, m: (0, m[1], 0)),
            ],
            out_specs=pl.BlockSpec((4, piece, piece), lambda i, m: (0, 0, 0)),
        ),
        out_shape=jax.ShapeDtypeStruct((4, piece, piece), BF16),
        compiler_params=pltpu.CompilerParams(vmem_limit_bytes=4 << 20),
        cost_estimate=BRIEF,
        name="pack_piece",
    )(meta, held(w_in), held(w_back))


def by_rows(count, step, body):
    @pl.loop(0, count // step)
    def _(n):
        body(n * step if isinstance(n, int) else pl.multiple_of(n * step, step))


def merge_kernel(plan, *refs):
    refs = list(refs)
    takes = [[[(refs.pop(0), at) for at in views] for views in groups] for groups, _, _ in plan]
    full = lambda n: (slice(None),) * n

    def rows_of(ref, lead, at, size):
        return lead + full(len(ref.shape) - 2 - len(lead)) + (pl.ds(at, size), slice(None))

    for groups, (_, axis, cuts) in zip(takes, plan):
        outs = [refs.pop(0) for _ in cuts]
        head = groups[0][0][0]
        count = head.shape[-2]
        step = 16 if len(head.shape) == 2 else 64
        if axis is not None:
            size = head.shape[axis]
            for k, (ref, _) in enumerate(groups[0]):

                def copy(at, k=k, ref=ref):
                    if len(ref.shape) == 2:
                        outs[0][pl.ds(k * size + at, step), :] = ref[pl.ds(at, step), :]
                    else:
                        lead = full(axis) + (slice(k * size, (k + 1) * size),)
                        outs[0][rows_of(outs[0], lead, at, step)] = ref[rows_of(ref, (), at, step)]

                by_rows(count, step, copy)
            continue
        for g, take in enumerate(groups):
            place = (g,) if len(groups) > 1 else ()
            if len(head.shape) == 2:
                for out, cut in zip(outs, cuts):
                    start = cut.start or 0

                    def add(at, out=out, start=start):
                        total = sum(ref[pl.ds(start + at, step), :].astype(F32) for ref, _ in take)
                        out[pl.ds(at, step), :] = total.astype(BF16)

                    by_rows(out.shape[0], step, add)
                continue

            def add(at, take=take, place=place):
                parts = [ref[rows_of(ref, () if view is ... else (view,), at, step)] for ref, view in take]
                total = sum(v.astype(F32) for v in parts).astype(BF16)
                for out, cut in zip(outs, cuts):
                    out[rows_of(out, place, at, step)] = total[cut]

            by_rows(count, step, add)


def merge(*items):
    plan, shapes, arrays = [], [], []
    for groups, axis, cuts in items:
        head = groups[0][0]
        shape = jax.eval_shape(lambda v: v[head[1]], head[0]).shape if isinstance(head, tuple) else head.shape
        first = jax.ShapeDtypeStruct(shape, BF16)
        if axis is not None:
            cuts = [None]
            shape = list(first.shape)
            shape[axis] *= len(groups[0])
            shapes.append(jax.ShapeDtypeStruct(tuple(shape), BF16))
        else:
            lead = (len(groups),) if len(groups) > 1 else ()
            shapes += [
                jax.ShapeDtypeStruct(lead + jax.eval_shape(lambda v, c=c: v[c], first).shape, BF16) for c in cuts
            ]
        pairs = [[v if isinstance(v, tuple) else (v, ...) for v in g] for g in groups]
        plan.append(([[at for _, at in g] for g in pairs], axis, cuts))
        arrays += [v for g in pairs for v, _ in g]
    return pl.pallas_call(
        functools.partial(merge_kernel, plan),
        out_shape=shapes,
        compiler_params=pltpu.CompilerParams(vmem_limit_bytes=16 << 20),
        cost_estimate=BRIEF,
        name="merge",
    )(*arrays)


def held(value):
    return pltpu.with_memory_space_constraint(value, pltpu.HBM)


SWAP = [(0, 1), (1, 0)]


def xor(k, n=4):
    return [(i, i ^ k) for i in range(n)]


def send(value, axis, pairs):
    return lax.ppermute(value, axis, pairs)


def add_low(a, b):
    return (a.astype(F32) + b.astype(F32)).astype(BF16)


def after(value, *earlier):
    return lax.optimization_barrier((value, *earlier))[0]


def tie(*values):
    return lax.optimization_barrier(values)


def fan(value, axis):
    rows = value.shape[0] // 4
    return [send(value[k * rows : (k + 1) * rows], axis, xor(k)) for k in (1, 2, 3)]


def add_fan(value, got):
    total = value[: value.shape[0] // 4].astype(F32)
    for v in got:
        total = total + v.astype(F32)
    return total.astype(BF16)


def dense_shards(
    tokens, gain_one, w_qkv, w_out, gain_two, w_router, w_in, w_back, route_ids, key_mask, cotangent
):
    nimg, half, width = tokens.shape
    imgs = nimg // 2
    rows = imgs * 2 * half
    experts = w_router.shape[1]
    piece = w_in.shape[2] // PIECES
    core = lax.axis_index("ctx")
    z = lax.axis_index("expert")
    me = core * 4 + lax.axis_index("dp")
    meta = jnp.stack([z, me, me * 4 + z, core]).astype(jnp.int32)
    meta_pair = jnp.stack([z ^ 2, me, me * 4 + z, core]).astype(jnp.int32)
    far = lambda v: send(v, "expert", xor(1))
    swap = lambda v: send(v, "ctx", SWAP)

    pack = pack_piece(meta, w_in, w_back)
    codes = after(route_ids, pack).reshape(nimg, half, TOP)
    codes = codes[..., 0] + experts * codes[..., 1]
    tok_other, dy_other, codes_other = swap(tokens), swap(cotangent), swap(codes)
    first = jnp.where(core == 0, codes, codes_other)
    second = jnp.where(core == 0, codes_other, codes)
    codes = lax.dynamic_slice_in_dim(jnp.concatenate([first, second], 1), core * imgs, imgs, 0)
    codes = codes.reshape(1, rows)
    ids = jnp.concatenate([codes % experts, codes // experts], 0)
    wide = jnp.pad(ids, ((0, 0), (0, 2 * width - rows))).reshape(TOP, 2, width)
    ids_pack = jnp.concatenate([wide[:, 0], wide[:, 1]], 0).astype(BF16)
    ids_pack = jnp.pad(ids_pack, ((padded(rows) - rows, 12), (0, 0)))
    wr = jnp.pad(w_router.T, ((0, 16 - experts), (0, 0)))
    g1, g2 = gain_one[None, :], gain_two[None, :]

    far_raw, pack = far(after(cotangent, pack)), send(pack, "expert", xor(2))
    x_rows, dy, normed, qkv, probs, mix, mid, routed = attend(
        meta, tokens, tok_other, cotangent, dy_other, key_mask, g1, w_qkv, w_out, g2
    )
    own_one = expert_steps(meta, routed, dy, ids, wr, (w_in, w_back))
    far_rows = jnp.concatenate([routed, ids_pack], 0)
    pack, wr_far = after(pack, routed), after(wr, own_one[2])

    packs = [pack] + [send(pack, "dp", xor(k)) for k in (1, 2, 3)]
    far_rows = far(far_rows)
    far_raw = after(far_raw, own_one[2])
    far_dy = assemble(meta, far_raw, swap(far_raw))
    far_one = expert_steps(meta, far_rows, far_dy, far_rows, wr_far, (w_in, w_back))
    *packs, wr_far = tie(*packs, after(wr, far_one[2]))
    packs = jnp.stack(packs)
    pair = [packs, swap(packs)]
    grads = weight_grads([routed, far_rows], *zip(own_one[:3], far_one[:3]), late=True)
    wr_far = after(wr_far, grads[0])

    far_two = expert(meta_pair, far_rows, far_dy, far_rows, wr_far, pair, far_one[3:])
    head, tail = slice(0, 2), slice(2, 4)
    even, odd = [(slice(None), slice(k, k + 1)) for k in (0, 1)]
    square = lambda v: v.reshape(2, 2, piece, width)

    def across(a, a_give, b, b_give):
        return merge(
            ([[a, swap(a_give)]], None, [head, tail]), ([[square(b), square(swap(b_give))]], None, [even, odd])
        )

    one = across(*grads)
    wr_own, *one = tie(after(wr, far_two[2]), *one)
    far_din, far_made = far_two[4], far_two[3]

    y_way, x_way = ("dp", xor(2)), ("dp", xor(1))
    own_two = expert(meta_pair, routed, dy, ids, wr_own, pair, own_one[3:])
    grads = weight_grads([routed, far_rows], *zip(own_two[:3], far_two[:3]))
    din_far, a_got, b_got, give_a = tie(far(far_din), send(one[1], *y_way), send(one[3], *x_way), grads[1])
    grads = [grads[0], give_a, *grads[2:]]
    a_one, b_one = [one[0], a_got], [one[2], b_got]

    two = tie(*across(*grads))

    a_two, b_two = [two[0], send(two[1], *y_way)], [two[2], send(two[3], *x_way)]
    far_made = far(after(far_made, din_far))
    tok_own, tok_give, shared, shared_give = attend_back(
        meta, [after(own_two[4], *two), din_far], ids, dy, mid, routed, wr, g2, mix, w_out, probs, qkv, x_rows, normed, w_qkv, g1
    )
    halves = [slice(0, 1), slice(1, 2)]
    line = lambda v: v.reshape(2, piece, width)
    flat = lambda group: [line(v) for v in group]
    one, one_give, two, two_give, far_made, shared, shared_give, tok_give = tie(
        *merge(([a_one, flat(b_one)], None, halves), ([a_two, flat(b_two)], None, halves)),
        far_made,
        shared,
        shared_give,
        tok_give,
    )
    mix_own, mix_give = combine(meta, mid, [own_two[3], far_made], imgs)
    quarters = lambda n: [slice(k * n, (k + 1) * n) for k in range(4)]
    everything = [slice(None)]
    second = lambda give: [send(give[0], *x_way), send(give[1], *y_way)]
    got = second(two_give)
    two, *shared, tok_got, mix_got = tie(
        *merge(
            ([[(two, 0), got[0]], [(two, 1), got[1]]], None, everything),
            ([[shared, swap(shared_give)]], None, quarters(width // 8)),
        ),
        swap(tok_give),
        swap(mix_give),
    )
    spread = lambda parts, axis: [send(v, axis, xor(k)) for k, v in zip((1, 2, 3), parts)]
    mixed, grad_tokens = place(meta, mix_own, mix_got, tok_own, tok_got)
    got, cross = second(one_give), send(two, "expert", xor(2))
    a, b, *shared, mixed, grad_tokens = tie(
        *merge(
            ([[(one, 0), got[0], (cross, 0)]], None, everything),
            ([[(one, 1), got[1], (cross, 1)]], None, everything),
            ([[shared[0], *spread(shared[1:], "dp")]], None, quarters(width // 32)),
        ),
        mixed,
        grad_tokens,
    )
    b = b[None]
    a, b, shared = tie(
        *merge(
            ([[a, send(a, *x_way)]], 0, None),
            ([[b, send(b, *y_way)]], 0, None),
            ([[shared[0], *spread(shared[1:], "expert")]], None, everything),
        )
    )
    a, b, shared = tie(
        *merge(
            ([[a, send(a, *y_way)]], 0, None),
            ([[b, send(b, *x_way)]], 1, None),
            ([[shared, *spread([shared] * 3, "expert")]], 0, None),
        )
    )
    b = b.reshape(a.shape)
    grad_in, grad_back = finish_expert(meta, a, swap(a), b, swap(b))
    (shared,) = merge(([[after(shared, grad_in, grad_back), *spread([shared] * 3, "dp")]], 0, None))
    earlier = finish_shared(meta, shared)
    grad_qkv, grad_out, small = finish_shared(meta, swap(shared), earlier)
    return (
        mixed,
        grad_tokens,
        small[:, 17],
        grad_qkv,
        grad_out,
        small[:, 16],
        small[:, :experts],
        grad_in,
        grad_back,
    )


def norm_rows(value, gain):
    center = value - jnp.mean(value, -1, keepdims=True)
    spread = jnp.mean(center * center, -1, keepdims=True)
    return center * lax.rsqrt(spread + 1e-06) * gain


def smooth_gelu(value):
    return 0.5 * value * (1.0 + jnp.tanh(0.7978845608 * (value + 0.044715 * value * value * value)))


def forward(tokens, gain_one, w_qkv, w_out, gain_two, w_router, w_in, w_back, flat_ids, live):
    nimg, half, width = tokens.shape
    count = nimg * half
    experts_all = w_router.shape[1]
    capacity = max(2, 2 * TOP * count // experts_all)
    x_rows = tokens.astype(jnp.float32).reshape(count, width)
    normed = norm_rows(x_rows, gain_one).astype(jnp.bfloat16)
    qkv = jnp.dot(normed, w_qkv, preferred_element_type=jnp.float32).astype(jnp.bfloat16)
    qkv = qkv.reshape(nimg, half, 3 * width)
    query = qkv[..., :width]
    keys_local = qkv[..., width : 2 * width]
    vals_local = qkv[..., 2 * width :]
    keys, vals = (
        lax.all_gather(keys_local, "ctx", axis=1, tiled=True),
        lax.all_gather(vals_local, "ctx", axis=1, tiled=True),
    )
    seq = keys.shape[1]
    query4 = query.reshape(nimg, half, HEADS, HEAD_DIM)
    keys4 = keys.reshape(nimg, seq, HEADS, HEAD_DIM)
    vals4 = vals.reshape(nimg, seq, HEADS, HEAD_DIM)
    scale = HEAD_DIM ** (-0.5)
    scores = (
        jnp.einsum("iqhc,ikhc->ihqk", query4, keys4, preferred_element_type=jnp.float32) * scale
    )
    open_keys = live[:, None, None, :]
    masked = jnp.where(open_keys, scores, -1000000000.0)
    topmost = jnp.max(masked, -1, keepdims=True)
    expo = jnp.where(open_keys, jnp.exp(masked - topmost), 0.0)
    probs = expo / jnp.sum(expo, -1, keepdims=True)
    probs_low = probs.astype(jnp.bfloat16)
    mix = jnp.einsum("ihqk,ikhc->iqhc", probs_low, vals4, preferred_element_type=jnp.float32)
    mix = mix.reshape(count, width).astype(jnp.bfloat16)
    mid = x_rows + jnp.dot(mix, w_out, preferred_element_type=jnp.float32)
    routed = norm_rows(mid, gain_two).astype(jnp.bfloat16)
    logits = jnp.dot(routed, w_router, preferred_element_type=jnp.float32)
    pick = flat_ids[:, :, None] == jnp.arange(experts_all, dtype=jnp.int32)[None, None, :]
    chosen = jnp.sum(jnp.where(pick, logits[:, None, :], 0.0), -1)
    expo_gate = jnp.exp(chosen)
    gates = expo_gate / jnp.sum(expo_gate, -1, keepdims=True)
    pair_ids = flat_ids.reshape(-1)
    hits = (pair_ids[:, None] == jnp.arange(experts_all, dtype=jnp.int32)[None, :]).astype(
        jnp.int32
    )
    before = jnp.cumsum(hits, 0) - hits
    slots = jnp.sum(before * hits, 1)
    where_rows = pair_ids * capacity + slots
    sent = jnp.repeat(routed, TOP, axis=0)
    buffer = jnp.zeros((experts_all * capacity, width), jnp.bfloat16).at[where_rows].set(sent)
    buffer = buffer.reshape(experts_all, capacity, width)
    arrived = lax.all_to_all(buffer, "expert", split_axis=0, concat_axis=1, tiled=True)
    pre = jnp.einsum("erd,edf->erf", arrived, w_in, preferred_element_type=jnp.float32)
    act = smooth_gelu(pre).astype(jnp.bfloat16)
    made = jnp.einsum("erf,efd->erd", act, w_back, preferred_element_type=jnp.float32).astype(
        jnp.bfloat16
    )
    returned = lax.all_to_all(made, "expert", split_axis=1, concat_axis=0, tiled=True)
    picked = returned.reshape(experts_all * capacity, width)[where_rows].reshape(count, TOP, width)
    output = mid + jnp.sum(gates[:, :, None] * picked.astype(jnp.float32), 1)
    return (
        x_rows,
        normed,
        query4,
        keys4,
        vals4,
        probs,
        probs_low,
        mix,
        mid,
        routed,
        pick,
        gates,
        where_rows,
        arrived,
        pre,
        act,
        picked,
        output,
        capacity,
    )


def shards(
    tokens, gain_one, w_qkv, w_out, gain_two, w_router, w_in, w_back, route_ids, key_mask, cotangent
):
    nimg, half, width = tokens.shape
    count = nimg * half
    experts_all = w_router.shape[1]
    flat_ids = route_ids.reshape(count, TOP)
    live = key_mask > 0
    state = forward(
        tokens, gain_one, w_qkv, w_out, gain_two, w_router, w_in, w_back, flat_ids, live
    )
    mixed = state[17].reshape(nimg, half, width).astype(jnp.bfloat16)
    state = forward(
        tokens, gain_one, w_qkv, w_out, gain_two, w_router, w_in, w_back, flat_ids, live
    )
    (
        x_rows,
        normed,
        query4,
        keys4,
        vals4,
        probs,
        probs_low,
        mix,
        mid,
        routed,
        pick,
        gates,
        where_rows,
        arrived,
        pre,
        act,
        picked,
        output,
        capacity,
    ) = state
    scale = HEAD_DIM ** (-0.5)
    high = lax.Precision.HIGHEST
    grad_y = cotangent.astype(jnp.float32).reshape(count, width)
    grad_gate = jnp.sum(grad_y[:, None, :] * picked.astype(jnp.float32), -1)
    d_out = (
        (gates[:, :, None] * grad_y[:, None, :]).astype(jnp.bfloat16).reshape(count * TOP, width)
    )
    grad_buffer = jnp.zeros((experts_all * capacity, width), jnp.bfloat16).at[where_rows].set(d_out)
    grad_buffer = grad_buffer.reshape(experts_all, capacity, width)
    grad_arrived = lax.all_to_all(grad_buffer, "expert", split_axis=0, concat_axis=1, tiled=True)
    d_act = jnp.einsum("erd,efd->erf", grad_arrived, w_back, preferred_element_type=jnp.float32)
    grad_back = jnp.einsum("erf,erd->efd", act, grad_arrived, preferred_element_type=jnp.float32)
    _, gelu_pull = jax.vjp(smooth_gelu, pre)
    d_pre = gelu_pull(d_act)[0].astype(jnp.bfloat16)
    grad_in = jnp.einsum("erd,erf->edf", arrived, d_pre, preferred_element_type=jnp.float32)
    d_in = jnp.einsum("erf,edf->erd", d_pre, w_in, preferred_element_type=jnp.float32).astype(
        jnp.bfloat16
    )
    grad_returned = lax.all_to_all(d_in, "expert", split_axis=1, concat_axis=0, tiled=True)
    grad_rows = grad_returned.reshape(experts_all * capacity, width)[where_rows].reshape(
        count, TOP, width
    )
    d_experts = jnp.sum(grad_rows.astype(jnp.float32), 1)
    d_chosen = gates * (grad_gate - jnp.sum(gates * grad_gate, -1, keepdims=True))
    d_logits = jnp.sum(jnp.where(pick, d_chosen[:, :, None], 0.0), 1)
    grad_router = jnp.dot(routed.astype(jnp.float32).T, d_logits, precision=high)
    d_routed = d_experts + jnp.dot(d_logits, w_router.astype(jnp.float32).T, precision=high)
    _, norm_two_pull = jax.vjp(norm_rows, mid, gain_two)
    d_mid_norm, grad_gain_two = norm_two_pull(d_routed)
    d_mid = grad_y + d_mid_norm
    d_branch = d_mid.astype(jnp.bfloat16)
    grad_out = jnp.einsum("td,te->de", mix, d_branch, preferred_element_type=jnp.float32)
    d_mix = jnp.dot(d_branch, w_out.T, preferred_element_type=jnp.float32).astype(jnp.bfloat16)
    d_mix4 = d_mix.reshape(nimg, half, HEADS, HEAD_DIM)
    d_probs = jnp.einsum("iqhc,ikhc->ihqk", d_mix4, vals4, preferred_element_type=jnp.float32)
    d_scores = (probs * (d_probs - jnp.sum(probs * d_probs, -1, keepdims=True))).astype(
        jnp.bfloat16
    )
    d_query = (
        jnp.einsum("ihqk,ikhc->iqhc", d_scores, keys4, preferred_element_type=jnp.float32) * scale
    )
    d_keys = (
        jnp.einsum("ihqk,iqhc->ikhc", d_scores, query4, preferred_element_type=jnp.float32) * scale
    )
    d_vals = jnp.einsum("ihqk,iqhc->ikhc", probs_low, d_mix4, preferred_element_type=jnp.float32)
    seq = keys4.shape[1]
    d_keys_own, d_vals_own = (
        lax.psum_scatter(
            d_keys.reshape(nimg, seq, width).astype(jnp.bfloat16),
            "ctx",
            scatter_dimension=1,
            tiled=True,
        ).astype(jnp.float32),
        lax.psum_scatter(
            d_vals.reshape(nimg, seq, width).astype(jnp.bfloat16),
            "ctx",
            scatter_dimension=1,
            tiled=True,
        ).astype(jnp.float32),
    )
    d_qkv = jnp.concatenate(
        [
            d_query.reshape(count, width).astype(jnp.bfloat16),
            d_keys_own.reshape(count, width).astype(jnp.bfloat16),
            d_vals_own.reshape(count, width).astype(jnp.bfloat16),
        ],
        axis=1,
    )
    grad_qkv = jnp.einsum("td,te->de", normed, d_qkv, preferred_element_type=jnp.float32)
    d_normed = jnp.dot(d_qkv, w_qkv.T, preferred_element_type=jnp.float32)
    _, norm_one_pull = jax.vjp(norm_rows, x_rows, gain_one)
    d_x_norm, grad_gain_one = norm_one_pull(d_normed)
    grad_tokens = (d_mid + d_x_norm).reshape(nimg, half, width).astype(jnp.bfloat16)
    grad_gain_one, grad_qkv, grad_out, grad_gain_two, grad_router = lax.psum(
        (grad_gain_one, grad_qkv, grad_out, grad_gain_two, grad_router), ("dp", "ctx", "expert")
    )
    grad_in, grad_back = (
        lax.psum(grad_in.astype(jnp.bfloat16), ("dp", "ctx")).astype(jnp.float32),
        lax.psum(grad_back.astype(jnp.bfloat16), ("dp", "ctx")).astype(jnp.float32),
    )
    return (
        mixed,
        grad_tokens,
        grad_gain_one,
        grad_qkv,
        grad_out,
        grad_gain_two,
        grad_router,
        grad_in,
        grad_back,
    )


def solution(mesh):
    placed = (
        P(("dp", "expert"), "ctx", None),
        P(),
        P(),
        P(),
        P(),
        P(),
        P("expert", None, None),
        P("expert", None, None),
        P(("dp", "expert"), "ctx", None, None, None),
        P(("dp", "expert"), None),
        P(("dp", "expert"), "ctx", None),
    )
    sizes = dict(mesh.shape)
    dense = sizes == {"dp": 4, "ctx": 2, "expert": 4}
    return jax.shard_map(
        dense_shards if dense else shards,
        mesh=mesh,
        in_specs=placed,
        out_specs=(
            P(("dp", "expert"), "ctx", None),
            P(("dp", "expert"), "ctx", None),
            P(),
            P(),
            P(),
            P(),
            P(),
            P("expert", None, None),
            P("expert", None, None),
        ),
        check_vma=False,
    )
```
